32 devices in a mesh: rep: 16 (over z, x, core), shard: 2 (over y).
Axes of the slice: x: 2, y: 2, z: 4, core: 2. Of those that a mesh axis runs over, the one named last changes fastest.
Arguments:
- prompt_x: bfloat16 [2, 32, 256, 768], P(None, ('rep', 'shard')), may hold values from -6 to 6
- cont_x: bfloat16 [2, 32, 2, 128, 768], P(None, ('rep', 'shard')), may hold values from -6 to 6
- prompt_cot: bfloat16 [2, 32, 256, 768], P(None, ('rep', 'shard')), may hold values from -6 to 6
- cont_cot: bfloat16 [2, 32, 2, 128, 768], P(None, ('rep', 'shard')), may hold values from -6 to 6
- norm1_gain: bfloat16 [768], P('shard'), may hold values from 0.25 to 1.75
- norm1_bias: bfloat16 [768], P('shard'), may hold values from -1.75 to 1.75
- in_weight: bfloat16 [768, 2304], P('shard'), may hold values from -0.21875 to 0.21875
- in_bias: bfloat16 [2304], P('shard'), may hold values from -1.75 to 1.75
- short_weight: bfloat16 [3, 2304], P(None, 'shard'), may hold values from -3 to 3
- short_bias: bfloat16 [2304], P('shard'), may hold values from -1.75 to 1.75
- long_bias: bfloat16 [2, 768], P(None, 'shard'), may hold values from -6 to 6
- filter_w1: bfloat16 [33, 64], P(None, 'shard'), may hold values from -1 to 1
- filter_b1: bfloat16 [64], P('shard'), may hold values from -6 to 6
- filter_w2: bfloat16 [64, 64], P(None, 'shard'), may hold values from -0.75 to 0.75
- filter_b2: bfloat16 [64], P('shard'), may hold values from -6 to 6
- filter_w3: bfloat16 [64, 1536], P(None, 'shard'), may hold values from -0.09375 to 0.09375
- filter_decay: bfloat16 [1536], P('shard'), may hold values from 0.5 to 25
- out_weight: bfloat16 [768, 768], P('shard'), may hold values from -0.21875 to 0.21875
- out_bias: bfloat16 [768], P('shard'), may hold values from -1.75 to 1.75
- norm2_gain: bfloat16 [768], P('shard'), may hold values from 0.25 to 1.75
- norm2_bias: bfloat16 [768], P('shard'), may hold values from -1.75 to 1.75
- up_weight: bfloat16 [768, 3072], P('shard'), may hold values from -0.21875 to 0.21875
- up_bias: bfloat16 [3072], P('shard'), may hold values from -1.75 to 1.75
- down_weight: bfloat16 [3072, 768], P('shard'), may hold values from -0.109375 to 0.109375
- down_bias: bfloat16 [768], P('shard'), may hold values from -1.75 to 1.75
Outputs:
- prompt_out: bfloat16 [2, 32, 256, 768], P(None, ('rep', 'shard'))
- cont_out: bfloat16 [2, 32, 2, 128, 768], P(None, ('rep', 'shard'))
- prompt_grad: bfloat16 [2, 32, 256, 768], P(None, ('rep', 'shard'))
- cont_grad: bfloat16 [2, 32, 2, 128, 768], P(None, ('rep', 'shard'))
- grad_norm1_gain: float32 [768], P('shard')
- grad_norm1_bias: float32 [768], P('shard')
- grad_in_weight: float32 [768, 2304], P('shard')
- grad_in_bias: float32 [2304], P('shard')
- grad_short_weight: float32 [3, 2304], P(None, 'shard')
- grad_short_bias: float32 [2304], P('shard')
- grad_long_bias: float32 [2, 768], P(None, 'shard')
- grad_filter_w1: float32 [33, 64], P(None, 'shard')
- grad_filter_b1: float32 [64], P('shard')
- grad_filter_w2: float32 [64, 64], P(None, 'shard')
- grad_filter_b2: float32 [64], P('shard')
- grad_filter_w3: float32 [64, 1536], P(None, 'shard')
- grad_out_weight: float32 [768, 768], P('shard')
- grad_out_bias: float32 [768], P('shard')
- grad_norm2_gain: float32 [768], P('shard')
- grad_norm2_bias: float32 [768], P('shard')
- grad_up_weight: float32 [768, 3072], P('shard')
- grad_up_bias: float32 [3072], P('shard')
- grad_down_weight: float32 [3072, 768], P('shard')
- grad_down_bias: float32 [768], P('shard')
The draws below stay inside these ranges and needn't reach their ends.
All inputs are finite; a program needn't handle non-finite values.
Results may differ from the reference program's by a relative error of at most 0.0071.
Values may be sent and summed in bfloat16 or wider, within the bound.
A program may use at most 320 MiB of HBM per device.

```python
import math
import jax
import jax.numpy as jnp
from jax import lax

D = 768
FF = 3072
FH = 64
BANDS = 16
BLOCK = 128
PROMPT = 256
CONTS = 2
MICRO = 2
FE = 33
D3 = 2304
FOUT = 1536
SEQ = 384
GROUPS = 32


def block_scale(stream_key, shape, cuts, least, high):
    def one(dim, shards_of):
        draws = jax.random.uniform(jax.random.fold_in(jax.random.fold_in(stream_key, 6), dim), (shards_of,), jnp.float32, least / len(cuts), high / len(cuts))
        return jnp.repeat(jnp.exp(draws), shape[dim] // shards_of).reshape((-1,) + (1,) * (len(shape) - dim - 1))

    loudness = one(*cuts[0])
    for cut in cuts[1:]:
        loudness = loudness * one(*cut)
    return loudness


def noise(rng, dims, scale, most, cuts=(), dtype=jnp.bfloat16):
    entries = scale * jax.random.normal(rng, dims, jnp.float32)
    if cuts:
        entries = entries * block_scale(rng, dims, cuts, -0.22, 0.18)
    return jnp.clip(entries, -most, most).astype(dtype)


def setup_inputs(seed: int = 0) -> dict:
    key_list = jax.random.split(jax.random.key(seed), 26)
    return {
        "prompt_x": noise(key_list[0], (MICRO, GROUPS, PROMPT, D), 1.0, 6.0, ((1, 32),)),
        "cont_x": noise(key_list[1], (MICRO, GROUPS, CONTS, BLOCK, D), 1.0, 6.0, ((1, 32),)),
        "prompt_cot": noise(key_list[2], (MICRO, GROUPS, PROMPT, D), 1.0, 6.0, ((1, 32),)),
        "cont_cot": noise(key_list[3], (MICRO, GROUPS, CONTS, BLOCK, D), 1.0, 6.0, ((1, 32),)),
        "norm1_gain": jnp.clip(1.0 + 0.15 * jax.random.normal(key_list[4], (D,), jnp.float32), 0.25, 1.75).astype(jnp.bfloat16),
        "norm1_bias": noise(key_list[5], (D,), 0.3, 1.75, ((0, 2),)),
        "in_weight": noise(key_list[6], (D, D3), D ** -0.5, 0.21875, ((0, 2),)),
        "in_bias": noise(key_list[7], (D3,), 0.3, 1.75, ((0, 2),)),
        "short_weight": noise(key_list[8], (3, D3), 0.5, 3.0, ((1, 2),)),
        "short_bias": noise(key_list[9], (D3,), 0.3, 1.75, ((0, 2),)),
        "long_bias": noise(key_list[10], (2, D), 1.0, 6.0, ((1, 2),)),
        "filter_w1": noise(key_list[11], (FE, FH), FE ** -0.5, 1.0, ((1, 2),)),
        "filter_b1": noise(key_list[12], (FH,), 1.0, 6.0, ((0, 2),)),
        "filter_w2": noise(key_list[13], (FH, FH), FH ** -0.5, 0.75, ((1, 2),)),
        "filter_b2": noise(key_list[14], (FH,), 1.0, 6.0, ((0, 2),)),
        "filter_w3": noise(key_list[15], (FH, FOUT), 0.015, 0.09375, ((1, 2),)),
        "filter_decay": jnp.clip(jnp.exp(math.log(25.0) - 3.912023 * jax.random.uniform(key_list[16], (FOUT,), jnp.float32) ** block_scale(key_list[16], (FOUT,), ((0, 2),), -0.2, 0.2)), 0.5, 25.0).astype(jnp.bfloat16),
        "out_weight": noise(key_list[17], (D, D), D ** -0.5, 0.21875, ((0, 2),)),
        "out_bias": noise(key_list[18], (D,), 0.3, 1.75, ((0, 2),)),
        "norm2_gain": jnp.clip(1.0 + 0.15 * jax.random.normal(key_list[19], (D,), jnp.float32), 0.25, 1.75).astype(jnp.bfloat16),
        "norm2_bias": noise(key_list[20], (D,), 0.3, 1.75, ((0, 2),)),
        "up_weight": noise(key_list[21], (D, FF), D ** -0.5, 0.21875, ((0, 2),)),
        "up_bias": noise(key_list[22], (FF,), 0.3, 1.75, ((0, 2),)),
        "down_weight": noise(key_list[23], (FF, D), FF ** -0.5, 0.109375, ((0, 2),)),
        "down_bias": noise(key_list[24], (D,), 0.3, 1.75, ((0, 2),)),
    }


EPS = 1e-05
HIGH = lax.Precision.HIGHEST

@jax.custom_vjp
def low(v):
    return lax.optimization_barrier(v.astype(jnp.bfloat16)).astype(jnp.float32)

@jax.custom_vjp
def low_back(v):
    return v

def low_keep(v):
    return (low(v), None)

def low_pass(kept, grad):
    return (grad,)

def back_keep(v):
    return (v, None)

def back_low(kept, grad):
    return (low(grad),)
low.defvjp(low_keep, low_pass)
low_back.defvjp(back_keep, back_low)

def matmul(left_op, right_op):
    return jnp.dot(left_op, right_op, precision=HIGH, preferred_element_type=jnp.float32)

def layer_norm(values, norm_gain, norm_shift):
    center_val = values - lax.optimization_barrier(jnp.mean(values, axis=-1, keepdims=True))
    spread = lax.optimization_barrier(jnp.mean(center_val * center_val, axis=-1, keepdims=True))
    return center_val * lax.rsqrt(spread + EPS) * norm_gain + norm_shift

def filter_bank(first_w, first_b, second_w, second_b, third_w, decay):
    place = jnp.arange(SEQ).astype(jnp.float32)
    ratio = place / SEQ
    levels = (jnp.arange(BANDS) + 1).astype(jnp.float32)
    angles = 2.0 * math.pi * ratio[:, None] * levels[None, :]
    embed = jnp.concatenate([ratio[:, None], jnp.cos(angles), jnp.sin(angles)], axis=1)
    first_act = jnp.sin(matmul(embed, first_w) + first_b)
    second_act = jnp.sin(matmul(first_act, second_w) + second_b)
    return matmul(second_act, third_w) * jnp.exp(-ratio[:, None] * decay[None, :])

def long_conv(signal, kernel):
    length = signal.shape[-2]
    signal_freq = jnp.fft.rfft(signal, n=2 * length, axis=-2)
    kernel_freq = jnp.fft.rfft(kernel[:length], n=2 * length, axis=0)
    return jnp.fft.irfft(signal_freq * kernel_freq, n=2 * length, axis=-2)[..., :length, :]

def short_conv(signal, before, taps, shift):
    padded = jnp.concatenate([before, signal], axis=-2)
    return taps[0] * padded[..., 2:, :] + taps[1] * padded[..., 1:-1, :] + taps[2] * padded[..., :-2, :] + shift

def group_forward(params, prompt_val, cont_val, decay):
    gain_one, shift_one, proj_in, proj_in_bias, short_taps, short_shift, long_shift, filt_one, filt_one_bias, filt_two, filt_two_bias, filt_three, proj_out, proj_out_bias, gain_two, shift_two, proj_up, proj_up_bias, proj_down, proj_down_bias = params
    kernels = filter_bank(filt_one, filt_one_bias, filt_two, filt_two_bias, filt_three, decay)

    def project(values):
        return low_back(matmul(low(layer_norm(values, gain_one, shift_one)), proj_in) + proj_in_bias)
    prompt_z = project(prompt_val)
    cont_z = project(cont_val)
    prompt_s = short_conv(prompt_z, jnp.zeros((2, D3), jnp.float32), short_taps, short_shift)
    cont_s = short_conv(cont_z, jnp.broadcast_to(prompt_z[-2:], (CONTS, 2, D3)), short_taps, short_shift)

    def mix_step(sig_prompt, sig_cont, kernel, bias_row):
        out_prompt = long_conv(sig_prompt, kernel) + bias_row * sig_prompt
        whole = jnp.concatenate([jnp.broadcast_to(sig_prompt, (CONTS, PROMPT, D)), sig_cont], axis=1)
        out_cont = long_conv(whole, kernel)[:, PROMPT:] + bias_row * sig_cont
        return (out_prompt, out_cont)
    one_prompt, one_cont = mix_step(prompt_s[:, D:2 * D] * prompt_s[:, 2 * D:], cont_s[..., D:2 * D] * cont_s[..., 2 * D:], kernels[:, :D], long_shift[0])
    two_prompt, two_cont = mix_step(prompt_s[:, :D] * one_prompt, cont_s[..., :D] * one_cont, kernels[:, D:], long_shift[1])

    def finish(values, mixed):
        branch = low_back(matmul(low(mixed), proj_out) + proj_out_bias)
        middle = values + branch
        hidden = low_back(matmul(low(layer_norm(middle, gain_two, shift_two)), proj_up) + proj_up_bias)
        return middle + matmul(low(jax.nn.gelu(hidden, approximate=True)), proj_down) + proj_down_bias
    return (finish(prompt_val, two_prompt), finish(cont_val, two_cont))

def reference(prompt_x, cont_x, prompt_cot, cont_cot, norm1_gain, norm1_bias, in_weight, in_bias, short_weight, short_bias, long_bias, filter_w1, filter_b1, filter_w2, filter_b2, filter_w3, filter_decay, out_weight, out_bias, norm2_gain, norm2_bias, up_weight, up_bias, down_weight, down_bias):
    params = tuple((arr.astype(jnp.float32) for arr in (norm1_gain, norm1_bias, in_weight, in_bias, short_weight, short_bias, long_bias, filter_w1, filter_b1, filter_w2, filter_b2, filter_w3, out_weight, out_bias, norm2_gain, norm2_bias, up_weight, up_bias, down_weight, down_bias)))
    decay = filter_decay.astype(jnp.float32)
    number = MICRO * GROUPS
    records = (prompt_x.reshape(number, PROMPT, D), cont_x.reshape(number, CONTS, BLOCK, D), prompt_cot.reshape(number, PROMPT, D), cont_cot.reshape(number, CONTS, BLOCK, D))

    def group_step(totals, record):
        prompt_val = record[0].astype(jnp.float32)
        cont_val = record[1].astype(jnp.float32)

        def forward(weights, first_in, second_in):
            return group_forward(weights, first_in, second_in, decay)
        results, pullback = jax.vjp(forward, params, prompt_val, cont_val)
        grad_params, grad_prompt, grad_cont = pullback((record[2].astype(jnp.float32), record[3].astype(jnp.float32)))
        totals = jax.tree.map(jnp.add, totals, grad_params)
        return (totals, (results[0].astype(jnp.bfloat16), results[1].astype(jnp.bfloat16), grad_prompt.astype(jnp.bfloat16), grad_cont.astype(jnp.bfloat16)))
    start = jax.tree.map(jnp.zeros_like, params)
    grads, outputs = lax.scan(group_step, start, records)
    prompt_out = outputs[0].reshape(MICRO, GROUPS, PROMPT, D)
    cont_out = outputs[1].reshape(MICRO, GROUPS, CONTS, BLOCK, D)
    prompt_grad = outputs[2].reshape(MICRO, GROUPS, PROMPT, D)
    cont_grad = outputs[3].reshape(MICRO, GROUPS, CONTS, BLOCK, D)
    return (prompt_out, cont_out, prompt_grad, cont_grad, grads[0], grads[1], grads[2], grads[3], grads[4], grads[5], grads[6], grads[7], grads[8], grads[9], grads[10], grads[11], grads[12], grads[13], grads[14], grads[15], grads[16], grads[17], grads[18], grads[19])
```

```python
from functools import partial
import math

import jax
import jax.numpy as jnp
import numpy as np
from jax import lax
from jax.experimental import pallas as pl
from jax.experimental.pallas import tpu as pltpu
from jax.sharding import PartitionSpec as P

D = 768
D3 = 3 * D
BANDS = 16
BLOCK = 128
PROMPT = 256
CONTS = 2
SEQ = 384
SPAN = PROMPT + CONTS * BLOCK
TILE = 256
FREQ = 2 * BLOCK

EPS = 1e-05
HIGH = lax.Precision.HIGHEST
f32 = jnp.float32
bf16 = jnp.bfloat16


def matmul(left_op, right_op):
    return jnp.dot(left_op, right_op, precision=HIGH, preferred_element_type=f32)


def lowmul(left_op, right_op):
    return jnp.dot(left_op, right_op, preferred_element_type=f32)


def inner_rows(left_op, right_op):
    return lax.dot_general(
        left_op, right_op, (((0,), (0,)), ((), ())), preferred_element_type=f32
    )


def times_t(left_op, right_op):
    return lax.dot_general(
        left_op, right_op, (((1,), (1,)), ((), ())), preferred_element_type=f32
    )


def layer_norm(values, norm_gain, norm_shift):
    center_val = values - jnp.mean(values, axis=-1, keepdims=True)
    spread = jnp.mean(center_val * center_val, axis=-1, keepdims=True)
    return center_val * lax.rsqrt(spread + EPS) * norm_gain + norm_shift


def dft_matrix():
    freq = np.arange(BLOCK)
    place = np.arange(BLOCK)
    angle = np.pi * ((2 * freq[:, None] + 1) * place[None, :] % (4 * BLOCK)) / FREQ
    return np.concatenate([np.cos(angle), -np.sin(angle)], axis=0)


def split3(matrix):
    matrix = matrix.astype(np.float32)
    high = matrix.astype(jnp.bfloat16)
    rest = (matrix - high.astype(np.float32)).astype(jnp.bfloat16)
    return np.concatenate([high, rest, high], axis=1)


def split_dot(triple, signal):
    high = signal.astype(bf16)
    rest = (signal - high.astype(f32)).astype(bf16)
    return jnp.dot(
        triple, jnp.concatenate([high, high, rest], axis=0), preferred_element_type=f32
    )


def cmul(left, right):
    lr, li = left[:BLOCK], left[BLOCK:]
    rr, ri = right[:BLOCK], right[BLOCK:]
    return jnp.concatenate([lr * rr - li * ri, lr * ri + li * rr], axis=0)


def cmul_conj(left, right):
    lr, li = left[:BLOCK], left[BLOCK:]
    rr, ri = right[:BLOCK], right[BLOCK:]
    return jnp.concatenate([lr * rr + li * ri, lr * ri - li * rr], axis=0)


def row_index():
    return lax.broadcasted_iota(jnp.int32, (BLOCK, TILE), 0)


def delayed(block, before, lag):
    rolled = pltpu.roll(block, lag, 0)
    if before is None:
        return jnp.where(row_index() >= lag, rolled, 0.0)
    return jnp.where(row_index() >= lag, rolled, pltpu.roll(before, lag, 0))


def advanced(block, after, lag):
    rolled = pltpu.roll(block, BLOCK - lag, 0)
    if after is None:
        return jnp.where(row_index() < BLOCK - lag, rolled, 0.0)
    return jnp.where(row_index() < BLOCK - lag, rolled, pltpu.roll(after, BLOCK - lag, 0))


BEFORE = (None, 0, 1, 1)


def load_blocks(ref, base):
    return [ref[pl.ds(base + i * BLOCK, BLOCK), :] for i in range(4)]


def short_blocks(blocks, taps_ref, shift_ref):
    taps = taps_ref[...]
    shift = shift_ref[...]
    outs = []
    for i in range(4):
        before = None if BEFORE[i] is None else blocks[BEFORE[i]]
        outs.append(
            taps[0:1] * blocks[i]
            + taps[1:2] * delayed(blocks[i], before, 1)
            + taps[2:3] * delayed(blocks[i], before, 2)
            + shift
        )
    return outs


def spectra(hats, bank):
    tail = cmul(bank[1], hats[1]) + cmul(bank[2], hats[0])
    return [
        cmul(bank[0], hats[0]),
        cmul(bank[0], hats[1]) + cmul(bank[1], hats[0]),
        cmul(bank[0], hats[2]) + tail,
        cmul(bank[0], hats[3]) + tail,
    ]


def adjoint_spectra(hats, bank):
    tail = hats[2] + hats[3]
    return [
        cmul_conj(bank[0], hats[0]) + cmul_conj(bank[1], hats[1]) + cmul_conj(bank[2], tail),
        cmul_conj(bank[0], hats[1]) + cmul_conj(bank[1], tail),
        cmul_conj(bank[0], hats[2]),
        cmul_conj(bank[0], hats[3]),
    ]


def bank_grads(hats, grads):
    tail = grads[2] + grads[3]
    zero = cmul_conj(hats[0], grads[0])
    for i in range(1, 4):
        zero = zero + cmul_conj(hats[i], grads[i])
    one = cmul_conj(hats[0], grads[1]) + cmul_conj(hats[1], tail)
    return [zero, one, cmul_conj(hats[0], tail)]


def mixer_forward(
    z0, z1, z2, t0, t1, t2, b0, b1, b2, long_ref, bank1, bank2, ahead_ref, back_ref,
    out_ref, hat1_ref, hat2_ref, mid_ref,
):
    ahead = ahead_ref[...]
    back = back_ref[...]
    banks = ([bank1[i] for i in range(3)], [bank2[i] for i in range(3)])

    def step(micro, carry):
        base = pl.multiple_of(micro * SPAN, SPAN)
        gate1 = short_blocks(load_blocks(z1, base), t1, b1)
        value = short_blocks(load_blocks(z2, base), t2, b2)
        sig1 = [gate1[i] * value[i] for i in range(4)]
        hats = []
        for i in range(4):
            hat = split_dot(ahead, sig1[i])
            hat1_ref[micro * 4 + i] = hat
            hats.append(hat)
        wave = spectra(hats, banks[0])
        mid = []
        for i in range(4):
            one = split_dot(back, wave[i]) + long_ref[0:1, :] * sig1[i]
            mid_ref[pl.ds(base + i * BLOCK, BLOCK), :] = one
            mid.append(one)
        gate0 = short_blocks(load_blocks(z0, base), t0, b0)
        sig2 = [gate0[i] * mid[i] for i in range(4)]
        hats = []
        for i in range(4):
            hat = split_dot(ahead, sig2[i])
            hat2_ref[micro * 4 + i] = hat
            hats.append(hat)
        wave = spectra(hats, banks[1])
        for i in range(4):
            two = split_dot(back, wave[i]) + long_ref[1:2, :] * sig2[i]
            out_ref[pl.ds(base + i * BLOCK, BLOCK), :] = two.astype(bf16)
        return carry

    lax.fori_loop(0, z0.shape[0] // SPAN, step, 0)


def mixer_backward(
    grad_ref, z0, z1, z2, t0, t1, t2, b0, b1, b2, long_ref, bank1, bank2, hat1_ref, hat2_ref, mid_ref,
    ahead_ref, back_ref,
    dz_ref, dtap_ref, dlong_ref, dbank1_ref, dbank2_ref,
):
    tile = pl.program_id(0)
    ahead = ahead_ref[...]
    back = back_ref[...]
    banks = ([bank1[i] for i in range(3)], [bank2[i] for i in range(3)])
    width = dz_ref.shape[1] // 3

    dbank1_ref[...] = jnp.zeros_like(dbank1_ref)
    dbank2_ref[...] = jnp.zeros_like(dbank2_ref)
    dlong_ref[...] = jnp.zeros_like(dlong_ref)
    for part in range(3):
        cols = pl.ds(pl.multiple_of(part * width + tile * TILE, TILE), TILE)
        dtap_ref[:, cols] = jnp.zeros((8, TILE), f32)

    def total(values):
        acc = values[0]
        for one in values[1:]:
            acc = acc + one
        return jnp.sum(acc, axis=0, keepdims=True)

    def step(micro, carry):
        base = pl.multiple_of(micro * SPAN, SPAN)
        gate0 = short_blocks(load_blocks(z0, base), t0, b0)
        grad2 = load_blocks(grad_ref, base)
        mid = load_blocks(mid_ref, base)
        dhats = [split_dot(ahead, grad2[i]) for i in range(4)]
        new = bank_grads([hat2_ref[micro * 4 + i] for i in range(4)], dhats)
        for i in range(3):
            dbank2_ref[i] += new[i]
        wave = adjoint_spectra(dhats, banks[1])
        dsig2 = [split_dot(back, wave[i]) + long_ref[1:2, :] * grad2[i] for i in range(4)]
        dlong1 = total([grad2[i] * gate0[i] * mid[i] for i in range(4)])
        dgate0 = [dsig2[i] * mid[i] for i in range(4)]
        grad1 = [dsig2[i] * gate0[i] for i in range(4)]
        dhats = [split_dot(ahead, grad1[i]) for i in range(4)]
        new = bank_grads([hat1_ref[micro * 4 + i] for i in range(4)], dhats)
        for i in range(3):
            dbank1_ref[i] += new[i]
        wave = adjoint_spectra(dhats, banks[0])
        dsig1 = [split_dot(back, wave[i]) + long_ref[0:1, :] * grad1[i] for i in range(4)]
        gate1 = short_blocks(load_blocks(z1, base), t1, b1)
        value = short_blocks(load_blocks(z2, base), t2, b2)
        dlong0 = total([grad1[i] * gate1[i] * value[i] for i in range(4)])
        dlong_ref[0:1, :] += dlong0
        dlong_ref[1:2, :] += dlong1
        dgate1 = [dsig1[i] * value[i] for i in range(4)]
        dvalue = [dsig1[i] * gate1[i] for i in range(4)]
        for part, (z_ref, t_ref, grads) in enumerate(
            ((z0, t0, dgate0), (z1, t1, dgate1), (z2, t2, dvalue))
        ):
            cols = pl.ds(pl.multiple_of(part * width + tile * TILE, TILE), TILE)
            taps = t_ref[...]
            blocks = load_blocks(z_ref, base)
            after = (grads[1], grads[2] + grads[3], None, None)
            dz = []
            for i in range(4):
                one = (
                    taps[0:1] * grads[i]
                    + taps[1:2] * advanced(grads[i], after[i], 1)
                    + taps[2:3] * advanced(grads[i], after[i], 2)
                ).astype(bf16)
                dz_ref[pl.ds(base + i * BLOCK, BLOCK), cols] = one
                dz.append(one.astype(f32))
            dtap_ref[4:5, cols] += total(dz)
            dtap_ref[3:4, cols] += total(grads)
            dtap_ref[0:1, cols] += total([grads[i] * blocks[i] for i in range(4)])
            for lag in (1, 2):
                dtap_ref[lag : lag + 1, cols] += total(
                    [
                        grads[i]
                        * delayed(blocks[i], None if BEFORE[i] is None else blocks[BEFORE[i]], lag)
                        for i in range(4)
                    ]
                )
        return carry

    lax.fori_loop(0, z0.shape[0] // SPAN, step, 0)


def part_specs(rows):
    steps = D // TILE
    return [pl.BlockSpec((rows, TILE), partial(lambda i, p: (0, p * steps + i), p=p)) for p in range(3)]


def constants():
    matrix = dft_matrix()
    return jnp.asarray(split3(matrix)), jnp.asarray(split3(matrix.T))


def const_specs():
    return [
        pl.BlockSpec((FREQ, 3 * BLOCK), lambda i: (0, 0)),
        pl.BlockSpec((BLOCK, 3 * FREQ), lambda i: (0, 0)),
    ]


def bank_specs():
    steps = D // TILE
    return [
        pl.BlockSpec((3, FREQ, TILE), lambda i: (0, 0, i)),
        pl.BlockSpec((3, FREQ, TILE), lambda i: (0, 0, steps + i)),
    ]


def run_forward(z, taps, shift, long_shift, bank):
    rows = z.shape[0]
    blocks = rows // BLOCK
    hat_spec = pl.BlockSpec((blocks, FREQ, TILE), lambda i: (0, 0, i))
    row_spec = pl.BlockSpec((rows, TILE), lambda i: (0, i))
    hat_shape = jax.ShapeDtypeStruct((blocks, FREQ, D), f32)
    return pl.pallas_call(
        mixer_forward,
        grid=(D // TILE,),
        in_specs=part_specs(rows) + part_specs(3) + part_specs(1)
        + [pl.BlockSpec((2, TILE), lambda i: (0, i))] + bank_specs() + const_specs(),
        out_specs=[row_spec, hat_spec, hat_spec, row_spec],
        out_shape=[
            jax.ShapeDtypeStruct((rows, D), bf16), hat_shape, hat_shape,
            jax.ShapeDtypeStruct((rows, D), f32),
        ],
        compiler_params=pltpu.CompilerParams(vmem_limit_bytes=56 * 2**20),
        cost_estimate=pl.CostEstimate(
            flops=32 * blocks * FREQ * 3 * BLOCK * D // 4, bytes_accessed=32 * 2**20, transcendentals=0
        ),
        name="mixer_forward",
    )(z, z, z, taps, taps, taps, shift, shift, shift, long_shift, bank, bank, *constants())


def run_backward(grad, z, taps, shift, long_shift, bank, hat1, hat2, mid):
    rows = z.shape[0]
    blocks = rows // BLOCK
    hat_spec = pl.BlockSpec((blocks, FREQ, TILE), lambda i: (0, 0, i))
    row_spec = pl.BlockSpec((rows, TILE), lambda i: (0, i))
    bank_spec = pl.BlockSpec((3, FREQ, TILE), lambda i: (0, 0, i))
    bank_shape = jax.ShapeDtypeStruct((3, FREQ, D), f32)
    return pl.pallas_call(
        mixer_backward,
        grid=(D // TILE,),
        in_specs=[row_spec] + part_specs(rows) + part_specs(3) + part_specs(1)
        + [pl.BlockSpec((2, TILE), lambda i: (0, i))] + bank_specs()
        + [hat_spec, hat_spec, row_spec] + const_specs(),
        out_specs=[
            pl.BlockSpec((rows, D3), lambda i: (0, 0)),
            pl.BlockSpec((8, D3), lambda i: (0, 0)),
            pl.BlockSpec((2, TILE), lambda i: (0, i)),
            bank_spec, bank_spec,
        ],
        out_shape=[
            jax.ShapeDtypeStruct((rows, D3), bf16), jax.ShapeDtypeStruct((8, D3), f32),
            jax.ShapeDtypeStruct((2, D), f32), bank_shape, bank_shape,
        ],
        compiler_params=pltpu.CompilerParams(vmem_limit_bytes=60 * 2**20),
        cost_estimate=pl.CostEstimate(
            flops=48 * blocks * FREQ * 3 * BLOCK * D // 4, bytes_accessed=48 * 2**20, transcendentals=0
        ),
        name="mixer_backward",
    )(grad, z, z, z, taps, taps, taps, shift, shift, shift, long_shift, bank, bank, hat1, hat2, mid, *constants())


def filter_bank(first_w, first_b, second_w, second_b, third_w, decay):
    place = np.arange(SEQ).astype(np.float32)
    ratio_c = place / np.float32(SEQ)
    levels = (np.arange(BANDS) + 1).astype(np.float32)
    ratio = jnp.asarray(ratio_c)
    angles = 2.0 * math.pi * ratio[:, None] * jnp.asarray(levels)[None, :]
    embed = jnp.concatenate([ratio[:, None], jnp.cos(angles), jnp.sin(angles)], axis=1)
    first_act = jnp.sin(matmul(embed, first_w) + first_b)
    second_act = jnp.sin(matmul(first_act, second_w) + second_b)
    kernels = matmul(second_act, third_w) * jnp.exp(-ratio[:, None] * decay[None, :])
    parts = kernels.reshape(SEQ // BLOCK, BLOCK, kernels.shape[1])
    table = jnp.asarray((dft_matrix() / BLOCK).astype(np.float32))
    hats = [matmul(table, parts[i]) for i in range(SEQ // BLOCK)]
    sign = jnp.asarray(np.where(np.arange(BLOCK) % 2 == 0, 1.0, -1.0).astype(np.float32))[:, None]

    def turned(hat):
        return jnp.concatenate([-sign * hat[BLOCK:], sign * hat[:BLOCK]], axis=0)

    return jnp.stack([hats[0], hats[1] + turned(hats[0]), hats[2] + turned(hats[1])])


def swap(value, axis, mask, size):
    return lax.ppermute(value, axis, [(i, i ^ mask) for i in range(size)])


def bits(size):
    return [1 << i for i in range(size.bit_length() - 1)]


def gather_rows(weight, reps, shards):
    if shards != 2 or reps % 4:
        return lax.all_gather(weight, "shard", axis=0, tiled=True)
    rows, width = weight.shape
    quarter = rows // 4
    place = lax.axis_index("rep") % 4
    shard = lax.axis_index("shard")
    piece = lax.dynamic_slice(weight, (place * quarter, 0), (quarter, width))
    got = swap(piece, "shard", 1, shards)
    side = swap(got, "rep", 2, reps)
    twin = swap(got, "rep", 1, reps)
    twin_side = swap(side, "rep", 1, reps)
    whole = jnp.zeros((2 * rows, width), weight.dtype)
    whole = lax.dynamic_update_slice(whole, weight, (shard * rows, 0))
    for part, mask in ((got, 0), (side, 2), (twin, 1), (twin_side, 3)):
        start = (1 - shard) * rows + (place ^ mask) * quarter
        whole = lax.dynamic_update_slice(whole, part, (start, 0))
    return whole


def reduce_rows(value, reps, shards):
    rep = lax.axis_index("rep")
    shard = lax.axis_index("shard")
    kind = value.dtype

    def halve(halves, axis, name, mask, where, size):
        bit = (where // mask) % 2
        sent = lax.dynamic_index_in_dim(halves, 1 - bit, axis, keepdims=False)
        kept = lax.dynamic_index_in_dim(halves, bit, axis, keepdims=False)
        return (kept.astype(f32) + swap(sent, name, mask, size).astype(f32)).astype(kind)

    rep_masks = bits(reps)
    first, others = rep_masks[:1], rep_masks[1:]
    for mask in first:
        s, rows, width = value.shape
        value = halve(value.reshape(s, 2, rows // 2, width), 1, "rep", mask, rep, reps)
    for mask in reversed(bits(shards)):
        s, rows, width = value.shape
        value = halve(value.reshape(2, s // 2, rows, width), 0, "shard", mask, shard, shards)
    value = value.reshape(value.shape[1:])
    for mask in others:
        rows, width = value.shape
        value = halve(value.reshape(2, rows // 2, width), 0, "rep", mask, rep, reps)
    for mask in reversed(rep_masks):
        got = swap(value, "rep", mask, reps)
        low = (rep // mask) % 2 == 0
        value = jnp.where(
            low, jnp.concatenate([value, got], axis=0), jnp.concatenate([got, value], axis=0)
        )
    return value.astype(f32)


def gather_small(value, axis=0):
    return lax.all_gather(value, "shard", axis=axis, tiled=True).astype(f32)


def per_device(
    prompt_x, cont_x, prompt_cot, cont_cot, norm1_gain, norm1_bias, in_weight, in_bias, short_weight,
    short_bias, long_bias, filter_w1, filter_b1, filter_w2, filter_b2, filter_w3, filter_decay, out_weight,
    out_bias, norm2_gain, norm2_bias, up_weight, up_bias, down_weight, down_bias, *, reps, shards,
):
    micros = prompt_x.shape[0]
    groups = prompt_x.shape[1]
    count = micros * groups * SPAN

    def tokens_of(prompt, cont):
        return jnp.concatenate(
            [
                prompt.reshape(micros * groups, PROMPT, D),
                cont.reshape(micros * groups, CONTS * BLOCK, D),
            ],
            axis=1,
        ).reshape(count, D)

    def parts_of(rows):
        rows = rows.reshape(micros, groups, SPAN, D)
        return rows[:, :, :PROMPT], rows[:, :, PROMPT:].reshape(micros, groups, CONTS, BLOCK, D)

    gain1, shift1 = gather_small(norm1_gain), gather_small(norm1_bias)
    in_shift = gather_small(in_bias)
    taps, short_shift = gather_small(short_weight, 1), gather_small(short_bias)
    long_shift = gather_small(long_bias, 1)
    fw1, fb1 = gather_small(filter_w1, 1), gather_small(filter_b1)
    fw2, fb2 = gather_small(filter_w2, 1), gather_small(filter_b2)
    fw3, decay = gather_small(filter_w3, 1), gather_small(filter_decay)
    out_shift = gather_small(out_bias)
    gain2, shift2 = gather_small(norm2_gain), gather_small(norm2_bias)
    up_shift, down_shift = gather_small(up_bias), gather_small(down_bias)
    in_full = gather_rows(in_weight, reps, shards)
    out_full = gather_rows(out_weight, reps, shards)
    up_full = gather_rows(up_weight, reps, shards)
    down_full = gather_rows(down_weight, reps, shards)

    tokens = tokens_of(prompt_x, cont_x).astype(f32)
    upstream = tokens_of(prompt_cot, cont_cot)
    upstream_f = upstream.astype(f32)

    bank, bank_pull = jax.vjp(partial(filter_bank, decay=decay), fw1, fb1, fw2, fb2, fw3)
    normed, norm_pull = jax.vjp(layer_norm, tokens, gain1, shift1)
    normed_low = normed.astype(bf16)
    projected = lowmul(normed_low, in_full) + in_shift
    mixed_low, hat1, hat2, mid = run_forward(projected, taps, short_shift[None], long_shift, bank)
    middle = tokens + lowmul(mixed_low, out_full) + out_shift
    normed_two, norm_two_pull = jax.vjp(layer_norm, middle, gain2, shift2)
    second_low = normed_two.astype(bf16)
    hidden = lowmul(second_low, up_full) + up_shift
    active, gelu_pull = jax.vjp(partial(jax.nn.gelu, approximate=True), hidden)
    active_low = active.astype(bf16)
    result = (middle + lowmul(active_low, down_full) + down_shift).astype(bf16)
    prompt_out, cont_out = parts_of(result)

    def reduce_weight(left_op, right_op):
        grad = inner_rows(left_op, right_op).astype(bf16)
        return reduce_rows(grad.reshape(shards, grad.shape[0] // shards, grad.shape[1]), reps, shards)

    grad_down = reduce_weight(active_low, upstream)
    d_active = times_t(upstream, down_full)
    d_hidden = gelu_pull(d_active)[0].astype(bf16)
    grad_up = reduce_weight(second_low, d_hidden)
    d_second = times_t(d_hidden, up_full)
    d_middle, grad_gain2, grad_shift2 = norm_two_pull(d_second)
    d_middle = d_middle + upstream_f
    d_branch = d_middle.astype(bf16)
    grad_out = reduce_weight(mixed_low, d_branch)
    d_mixed = times_t(d_branch, out_full)
    d_proj, d_taps, d_long, d_bank1, d_bank2 = run_backward(
        d_mixed, projected, taps, short_shift[None], long_shift, bank, hat1, hat2, mid
    )
    grad_in = reduce_weight(normed_low, d_proj)
    d_normed = times_t(d_proj, in_full)
    d_tokens, grad_gain1, grad_shift1 = norm_pull(d_normed)
    prompt_grad, cont_grad = parts_of((d_tokens + d_middle).astype(bf16))
    grad_f1, grad_fb1, grad_f2, grad_fb2, grad_f3 = bank_pull(
        jnp.concatenate([d_bank1, d_bank2], axis=-1)
    )

    width = D // shards
    packed = []
    sizes = []

    def pack(value):
        lead = value.shape[0] if value.ndim == 2 else 1
        rows = value.reshape(lead, shards, value.size // (lead * shards * width), width)
        rows = rows.transpose(1, 0, 2, 3).reshape(shards, -1, width)
        packed.append(rows)
        sizes.append(rows.shape[1])

    for value in (
        grad_gain1, grad_shift1, d_taps[4], d_taps[:3], d_taps[3], d_long, grad_f3,
        jnp.sum(d_branch.astype(f32), axis=0), grad_gain2, grad_shift2,
        jnp.sum(d_hidden.astype(f32), axis=0), jnp.sum(upstream_f, axis=0),
    ):
        pack(value)
    filters = [grad_f1, grad_fb1[None], grad_f2, grad_fb2[None]]
    loose = jnp.concatenate(filters, axis=0)
    loose = loose.reshape(loose.shape[0], shards, -1).transpose(1, 0, 2).reshape(shards, -1)
    loose_size = loose.shape[1]
    loose_rows = -(-loose_size // width)
    loose = jnp.pad(loose, ((0, 0), (0, loose_rows * width - loose_size)))
    packed.append(loose.reshape(shards, loose_rows, width))
    used = sum(sizes) + loose_rows
    unit = 8 * reps
    spare = -used % unit
    packed.append(jnp.zeros((shards, spare, width), f32))
    small = reduce_rows(jnp.concatenate(packed, axis=1), reps, shards)

    pieces = []
    start = 0
    for size in sizes:
        pieces.append(small[start : start + size])
        start += size
    loose = small[start : start + loose_rows].reshape(-1)[:loose_size].reshape(-1, fw1.shape[1] // shards)
    places = np.cumsum([0] + [one.shape[0] for one in filters])
    loose = [loose[places[i] : places[i + 1]] for i in range(4)]

    return (
        prompt_out,
        cont_out,
        prompt_grad,
        cont_grad,
        pieces[0].reshape(-1),
        pieces[1].reshape(-1),
        grad_in,
        pieces[2].reshape(-1),
        pieces[3].reshape(short_weight.shape),
        pieces[4].reshape(-1),
        pieces[5].reshape(long_bias.shape),
        loose[0],
        loose[1].reshape(-1),
        loose[2],
        loose[3].reshape(-1),
        pieces[6].reshape(filter_w3.shape),
        grad_out,
        pieces[7].reshape(-1),
        pieces[8].reshape(-1),
        pieces[9].reshape(-1),
        grad_up,
        pieces[10].reshape(-1),
        grad_down,
        pieces[11].reshape(-1),
    )


def solution(mesh):
    group4 = P(None, ("rep", "shard"), None, None)
    group5 = P(None, ("rep", "shard"), None, None, None)
    one, row, col = P("shard"), P("shard", None), P(None, "shard")
    grads = (one, one, row, one, col, one, col, col, one, col, one, col)
    rest = (row, one, one, one, row, one, row, one)
    return jax.shard_map(
        partial(per_device, reps=mesh.shape["rep"], shards=mesh.shape["shard"]),
        mesh=mesh,
        in_specs=(group4, group5, group4, group5) + grads + (one,) + rest,
        out_specs=(group4, group5, group4, group5) + grads + rest,
        check_vma=False,
    )
```

```python
from functools import partial
import math

import jax
import jax.numpy as jnp
import numpy as np
from jax import lax
from jax.experimental import pallas as pl
from jax.experimental.pallas import tpu as pltpu
from jax.sharding import PartitionSpec as P

D = 768
D3 = 3 * D
BANDS = 16
BLOCK = 128
PROMPT = 256
CONTS = 2
SEQ = 384
SPAN = PROMPT + CONTS * BLOCK
TILE = 256
FREQ = 2 * BLOCK

EPS = 1e-05
HIGH = lax.Precision.HIGHEST
f32 = jnp.float32
bf16 = jnp.bfloat16


def matmul(left_op, right_op):
    return jnp.dot(left_op, right_op, precision=HIGH, preferred_element_type=f32)


def lowmul(left_op, right_op):
    return jnp.dot(left_op, right_op, preferred_element_type=f32)


def inner_rows(left_op, right_op):
    return lax.dot_general(
        left_op, right_op, (((0,), (0,)), ((), ())), preferred_element_type=f32
    )


def times_t(left_op, right_op):
    return lax.dot_general(
        left_op, right_op, (((1,), (1,)), ((), ())), preferred_element_type=f32
    )


def layer_norm(values, norm_gain, norm_shift):
    center_val = values - jnp.mean(values, axis=-1, keepdims=True)
    spread = jnp.mean(center_val * center_val, axis=-1, keepdims=True)
    return center_val * lax.rsqrt(spread + EPS) * norm_gain + norm_shift


def dft_matrix():
    freq = np.arange(BLOCK)
    place = np.arange(BLOCK)
    angle = np.pi * ((2 * freq[:, None] + 1) * place[None, :] % (4 * BLOCK)) / FREQ
    return np.concatenate([np.cos(angle), -np.sin(angle)], axis=0)


def split3(matrix):
    matrix = matrix.astype(np.float32)
    high = matrix.astype(jnp.bfloat16)
    rest = (matrix - high.astype(np.float32)).astype(jnp.bfloat16)
    return np.concatenate([high, rest, high], axis=1)


def split_dot(triple, signal):
    high = signal.astype(bf16)
    rest = (signal - high.astype(f32)).astype(bf16)
    return jnp.dot(
        triple, jnp.concatenate([high, high, rest], axis=0), preferred_element_type=f32
    )


def cmul(left, right):
    lr, li = left[:BLOCK], left[BLOCK:]
    rr, ri = right[:BLOCK], right[BLOCK:]
    return jnp.concatenate([lr * rr - li * ri, lr * ri + li * rr], axis=0)


def cmul_conj(left, right):
    lr, li = left[:BLOCK], left[BLOCK:]
    rr, ri = right[:BLOCK], right[BLOCK:]
    return jnp.concatenate([lr * rr + li * ri, lr * ri - li * rr], axis=0)


def row_index():
    return lax.broadcasted_iota(jnp.int32, (BLOCK, TILE), 0)


def delayed(block, before, lag):
    rolled = pltpu.roll(block, lag, 0)
    if before is None:
        return jnp.where(row_index() >= lag, rolled, 0.0)
    return jnp.where(row_index() >= lag, rolled, pltpu.roll(before, lag, 0))


def advanced(block, after, lag):
    rolled = pltpu.roll(block, BLOCK - lag, 0)
    if after is None:
        return jnp.where(row_index() < BLOCK - lag, rolled, 0.0)
    return jnp.where(row_index() < BLOCK - lag, rolled, pltpu.roll(after, BLOCK - lag, 0))


BEFORE = (None, 0, 1, 1)


def part(index):
    return slice(index * TILE, (index + 1) * TILE)


def load_blocks(ref, cols=slice(None)):
    return [ref[i * BLOCK : (i + 1) * BLOCK, cols] for i in range(4)]


def short_blocks(z_ref, taps_ref, shift_ref, index):
    blocks = load_blocks(z_ref, part(index))
    taps = taps_ref[:, part(index)]
    shift = shift_ref[:, part(index)]
    outs = []
    for i in range(4):
        before = None if BEFORE[i] is None else blocks[BEFORE[i]]
        outs.append(
            taps[0:1] * blocks[i]
            + taps[1:2] * delayed(blocks[i], before, 1)
            + taps[2:3] * delayed(blocks[i], before, 2)
            + shift
        )
    return outs


def spectra(hats, bank):
    tail = cmul(bank[1], hats[1]) + cmul(bank[2], hats[0])
    return [
        cmul(bank[0], hats[0]),
        cmul(bank[0], hats[1]) + cmul(bank[1], hats[0]),
        cmul(bank[0], hats[2]) + tail,
        cmul(bank[0], hats[3]) + tail,
    ]


def adjoint_spectra(hats, bank):
    tail = hats[2] + hats[3]
    return [
        cmul_conj(bank[0], hats[0]) + cmul_conj(bank[1], hats[1]) + cmul_conj(bank[2], tail),
        cmul_conj(bank[0], hats[1]) + cmul_conj(bank[1], tail),
        cmul_conj(bank[0], hats[2]),
        cmul_conj(bank[0], hats[3]),
    ]


def bank_grads(hats, grads):
    tail = grads[2] + grads[3]
    zero = cmul_conj(hats[0], grads[0])
    for i in range(1, 4):
        zero = zero + cmul_conj(hats[i], grads[i])
    one = cmul_conj(hats[0], grads[1]) + cmul_conj(hats[1], tail)
    return [zero, one, cmul_conj(hats[0], tail)]


def signs():
    odd = lax.broadcasted_iota(jnp.int32, (BLOCK, TILE), 0) % 2
    return (1 - 2 * odd).astype(f32)


def make_bank(ahead, taps_ref, bank_ref):
    hats = [
        split_dot(ahead, taps_ref[o * BLOCK : (o + 1) * BLOCK, :] * (1.0 / BLOCK)) for o in range(3)
    ]
    sign = signs()
    bank = [hats[0]]
    for o in (1, 2):
        prev = hats[o - 1]
        turned = jnp.concatenate([-sign * prev[BLOCK:], sign * prev[:BLOCK]], axis=0)
        bank.append(hats[o] + turned)
    for o in range(3):
        bank_ref[o] = bank[o]


def filter_grads(back, grads, out_ref):
    sign = signs()
    for o in range(3):
        one = grads[o]
        if o < 2:
            after = grads[o + 1]
            one = one + jnp.concatenate([sign * after[BLOCK:], -sign * after[:BLOCK]], axis=0)
        out_ref[o * BLOCK : (o + 1) * BLOCK, :] = split_dot(back, one) * (1.0 / BLOCK)


def mixer_forward(
    z_ref, taps_ref, shift_ref, long_ref, filter1, filter2, ahead_ref, back_ref,
    out_ref, hat1_ref, hat2_ref, mid_ref, bank1, bank2,
):
    ahead = ahead_ref[...]
    back = back_ref[...]

    @pl.when(pl.program_id(1) == 0)
    def _():
        make_bank(ahead, filter1, bank1)
        make_bank(ahead, filter2, bank2)

    gate1 = short_blocks(z_ref, taps_ref, shift_ref, 1)
    value = short_blocks(z_ref, taps_ref, shift_ref, 2)
    sig1 = [gate1[i] * value[i] for i in range(4)]
    hats = []
    for i in range(4):
        hat = split_dot(ahead, sig1[i])
        hat1_ref[i] = hat
        hats.append(hat)
    wave = spectra(hats, [bank1[i] for i in range(3)])
    mid = []
    for i in range(4):
        one = split_dot(back, wave[i]) + long_ref[0:1, :] * sig1[i]
        mid_ref[i * BLOCK : (i + 1) * BLOCK, :] = one
        mid.append(one)
    gate0 = short_blocks(z_ref, taps_ref, shift_ref, 0)
    sig2 = [gate0[i] * mid[i] for i in range(4)]
    hats = []
    for i in range(4):
        hat = split_dot(ahead, sig2[i])
        hat2_ref[i] = hat
        hats.append(hat)
    wave = spectra(hats, [bank2[i] for i in range(3)])
    for i in range(4):
        two = split_dot(back, wave[i]) + long_ref[1:2, :] * sig2[i]
        out_ref[i * BLOCK : (i + 1) * BLOCK, :] = two.astype(bf16)


def mixer_backward(
    grad_ref, z_ref, taps_ref, shift_ref, long_ref, bank1, bank2, hat1_ref, hat2_ref, mid_ref,
    ahead_ref, back_ref,
    dz_ref, dtap_ref, dlong_ref, dfilt1_ref, dfilt2_ref, dbank1, dbank2,
):
    ahead = ahead_ref[...]
    back = back_ref[...]
    micro = pl.program_id(1)

    @pl.when(micro == 0)
    def _():
        dbank1[...] = jnp.zeros_like(dbank1)
        dbank2[...] = jnp.zeros_like(dbank2)
        dlong_ref[...] = jnp.zeros_like(dlong_ref)
        dtap_ref[...] = jnp.zeros_like(dtap_ref)

    def total(values):
        acc = values[0]
        for one in values[1:]:
            acc = acc + one
        return jnp.sum(acc, axis=0, keepdims=True)

    gate0 = short_blocks(z_ref, taps_ref, shift_ref, 0)
    grad2 = load_blocks(grad_ref)
    mid = load_blocks(mid_ref)
    dhats = [split_dot(ahead, grad2[i]) for i in range(4)]
    new = bank_grads([hat2_ref[i] for i in range(4)], dhats)
    for i in range(3):
        dbank2[i] += new[i]
    wave = adjoint_spectra(dhats, [bank2[i] for i in range(3)])
    dsig2 = [split_dot(back, wave[i]) + long_ref[1:2, :] * grad2[i] for i in range(4)]
    dlong_ref[1:2, :] += total([grad2[i] * gate0[i] * mid[i] for i in range(4)])
    dgate0 = [dsig2[i] * mid[i] for i in range(4)]
    grad1 = [dsig2[i] * gate0[i] for i in range(4)]
    dhats = [split_dot(ahead, grad1[i]) for i in range(4)]
    new = bank_grads([hat1_ref[i] for i in range(4)], dhats)
    for i in range(3):
        dbank1[i] += new[i]
    wave = adjoint_spectra(dhats, [bank1[i] for i in range(3)])
    dsig1 = [split_dot(back, wave[i]) + long_ref[0:1, :] * grad1[i] for i in range(4)]
    gate1 = short_blocks(z_ref, taps_ref, shift_ref, 1)
    value = short_blocks(z_ref, taps_ref, shift_ref, 2)
    dlong_ref[0:1, :] += total([grad1[i] * gate1[i] * value[i] for i in range(4)])
    dgate1 = [dsig1[i] * value[i] for i in range(4)]
    dvalue = [dsig1[i] * gate1[i] for i in range(4)]
    for index, grads in enumerate((dgate0, dgate1, dvalue)):
        cols = part(index)
        taps = taps_ref[:, cols]
        blocks = load_blocks(z_ref, cols)
        after = (grads[1], grads[2] + grads[3], None, None)
        dz = []
        for i in range(4):
            one = (
                taps[0:1] * grads[i]
                + taps[1:2] * advanced(grads[i], after[i], 1)
                + taps[2:3] * advanced(grads[i], after[i], 2)
            ).astype(bf16)
            dz_ref[i * BLOCK : (i + 1) * BLOCK, cols] = one
            dz.append(one.astype(f32))
        dtap_ref[4:5, cols] += total(dz)
        dtap_ref[3:4, cols] += total(grads)
        dtap_ref[0:1, cols] += total([grads[i] * blocks[i] for i in range(4)])
        for lag in (1, 2):
            dtap_ref[lag : lag + 1, cols] += total(
                [
                    grads[i]
                    * delayed(blocks[i], None if BEFORE[i] is None else blocks[BEFORE[i]], lag)
                    for i in range(4)
                ]
            )

    @pl.when(micro == pl.num_programs(1) - 1)
    def _():
        filter_grads(back, [dbank1[i] for i in range(3)], dfilt1_ref)
        filter_grads(back, [dbank2[i] for i in range(3)], dfilt2_ref)


def constants():
    matrix = dft_matrix()
    return jnp.asarray(split3(matrix)), jnp.asarray(split3(matrix.T))


STEPS = D // TILE
AHEAD = (FREQ, 3 * BLOCK)
BACK = (BLOCK, 3 * FREQ)


def run_forward(z, taps, shift, long_shift, filters):
    rows = z.shape[0]
    blocks = rows // BLOCK

    def spec(shape, index):
        return pl.BlockSpec(shape, lambda t, m: index(m, t))

    hat_spec = spec((4, FREQ, TILE), lambda m, t: (m, 0, t))
    row_spec = spec((SPAN, TILE), lambda m, t: (m, t))
    bank_spec = spec((3, FREQ, TILE), lambda m, t: (0, 0, t))
    hat_shape = jax.ShapeDtypeStruct((blocks, FREQ, D), f32)
    bank_shape = jax.ShapeDtypeStruct((3, FREQ, D), f32)
    return pl.pallas_call(
        mixer_forward,
        grid=(STEPS, rows // SPAN),
        in_specs=[
            spec((SPAN, 3 * TILE), lambda m, t: (m, t)),
            spec((3, 3 * TILE), lambda m, t: (0, t)),
            spec((1, 3 * TILE), lambda m, t: (0, t)),
            spec((2, TILE), lambda m, t: (0, t)),
            spec((SEQ, TILE), lambda m, t: (0, t)),
            spec((SEQ, TILE), lambda m, t: (0, STEPS + t)),
            spec(AHEAD, lambda m, t: (0, 0)),
            spec(BACK, lambda m, t: (0, 0)),
        ],
        out_specs=[row_spec, hat_spec, hat_spec, row_spec, bank_spec, bank_spec],
        out_shape=[
            jax.ShapeDtypeStruct((rows, D), bf16), hat_shape, hat_shape,
            jax.ShapeDtypeStruct((rows, D), f32), bank_shape, bank_shape,
        ],
        compiler_params=pltpu.CompilerParams(vmem_limit_bytes=40 * 2**20),
        cost_estimate=pl.CostEstimate(flops=10 * 10**9, bytes_accessed=32 * 2**20, transcendentals=0),
        name="mixer_forward",
    )(z, taps, shift, long_shift, filters, filters, *constants())


def run_backward(grad, z, taps, shift, long_shift, bank1, bank2, hat1, hat2, mid):
    rows = z.shape[0]

    def spec(shape, index):
        return pl.BlockSpec(shape, lambda t, m: index(m, t))

    hat_spec = spec((4, FREQ, TILE), lambda m, t: (m, 0, t))
    row_spec = spec((SPAN, TILE), lambda m, t: (m, t))
    bank_spec = spec((3, FREQ, TILE), lambda m, t: (0, 0, t))
    z_spec = spec((SPAN, 3 * TILE), lambda m, t: (m, t))
    column_spec = spec((SEQ, TILE), lambda m, t: (0, t))
    return pl.pallas_call(
        mixer_backward,
        grid=(STEPS, rows // SPAN),
        in_specs=[
            row_spec,
            z_spec,
            spec((3, 3 * TILE), lambda m, t: (0, t)),
            spec((1, 3 * TILE), lambda m, t: (0, t)),
            spec((2, TILE), lambda m, t: (0, t)),
            bank_spec, bank_spec, hat_spec, hat_spec, row_spec,
            spec(AHEAD, lambda m, t: (0, 0)),
            spec(BACK, lambda m, t: (0, 0)),
        ],
        out_specs=[
            z_spec,
            spec((8, 3 * TILE), lambda m, t: (0, t)),
            spec((2, TILE), lambda m, t: (0, t)),
            column_spec,
            column_spec,
        ],
        out_shape=[
            jax.ShapeDtypeStruct((rows, D3), bf16), jax.ShapeDtypeStruct((8, D3), f32),
            jax.ShapeDtypeStruct((2, D), f32), jax.ShapeDtypeStruct((SEQ, D), f32),
            jax.ShapeDtypeStruct((SEQ, D), f32),
        ],
        scratch_shapes=[pltpu.VMEM((3, FREQ, TILE), f32), pltpu.VMEM((3, FREQ, TILE), f32)],
        compiler_params=pltpu.CompilerParams(vmem_limit_bytes=40 * 2**20),
        cost_estimate=pl.CostEstimate(flops=24 * 10**9, bytes_accessed=36 * 2**20, transcendentals=0),
        name="mixer_backward",
    )(grad, z, taps, shift, long_shift, bank1, bank2, hat1, hat2, mid, *constants())


def filter_taps(first_w, first_b, second_w, second_b, third_w, decay):
    place = np.arange(SEQ).astype(np.float32)
    ratio_c = place / np.float32(SEQ)
    levels = (np.arange(BANDS) + 1).astype(np.float32)
    ratio = jnp.asarray(ratio_c)
    angles = 2.0 * math.pi * ratio[:, None] * jnp.asarray(levels)[None, :]
    embed = jnp.concatenate([ratio[:, None], jnp.cos(angles), jnp.sin(angles)], axis=1)
    first_act = jnp.sin(matmul(embed, first_w) + first_b)
    second_act = jnp.sin(matmul(first_act, second_w) + second_b)
    return matmul(second_act, third_w) * jnp.exp(-ratio[:, None] * decay[None, :])


def by_tile(value):
    shape = value.shape
    return value.reshape(*shape[:-1], 3, STEPS, TILE).swapaxes(-3, -2).reshape(shape)


def by_part(value):
    shape = value.shape
    return value.reshape(*shape[:-1], STEPS, 3, TILE).swapaxes(-3, -2).reshape(shape)


MESH = pl.DeviceIdType.MESH


class Place:
    def __init__(self):
        rep = lax.axis_index("rep")
        self.rep = rep
        self.shard = lax.axis_index("shard")
        self.core = rep % 2
        self.side = (rep // 2) % 2
        self.depth = rep // 4
        self.quad = rep % 4

    def other_shard(self):
        return (self.rep, 1 - self.shard)

    def other_side(self):
        return (self.rep + 2 - 4 * self.side, self.shard)

    def other_core(self):
        return (self.rep + 1 - 2 * self.core, self.shard)

    def other_depth(self, step):
        return (((self.depth + step) % 4) * 4 + self.quad, self.shard)


def greet(devices):
    barrier = pltpu.get_barrier_semaphore()
    for device in devices:
        pl.semaphore_signal(barrier, inc=1, device_id=device, device_id_type=MESH)
    pl.semaphore_wait(barrier, len(devices))


def remote(src, dst, send, recv, device):
    return pltpu.make_async_remote_copy(
        src_ref=src, dst_ref=dst, send_sem=send, recv_sem=recv, device_id=device, device_id_type=MESH
    )


UNITS = (
    (0, 0, 96), (1, 0, 96), (2, 0, 48), (2, 48, 48), (3, 0, 96), (3, 96, 96), (3, 192, 96), (3, 288, 96),
)


def gather_kernel(
    flat, narrow, third, w_in, w_out, w_up, w_down,
    flat_all, narrow_all, third_all, f_in, f_out, f_up, f_down,
    small_send, small_recv, own_sem, ysend, yrecv, xsend, xrecv, csend, crecv, dsend, drecv,
):
    place = Place()
    shard, quad = place.shard, place.quad
    greet([place.other_shard(), place.other_side(), place.other_core()])
    locals_ = (w_in, w_out, w_up, w_down)
    fulls = (f_in, f_out, f_up, f_down)
    smalls = []
    for i, (one, both) in enumerate(((flat, flat_all), (narrow, narrow_all), (third, third_all))):
        smalls.append(
            remote(one, both.at[shard], small_send.at[i], small_recv.at[i], place.other_shard())
        )
        smalls[-1].start()

    def rows_of(unit, shard_of, quad_of):
        weight, start, size = unit
        half = locals_[weight].shape[0]
        unit_rows = 16 if size % 16 == 0 else 8
        return pl.ds(pl.multiple_of(shard_of * half + quad_of * (half // 4) + start, unit_rows), size)

    def local_rows(unit):
        weight, start, size = unit
        quarter = locals_[weight].shape[0] // 4
        return pl.ds(pl.multiple_of(quad * quarter + start, 16), size)

    def column_pairs(weight):
        if weight:
            width = locals_[weight].shape[1]
            return [(slice(0, width), slice(0, width))]
        return [
            (part(p * STEPS + t), part(t * 3 + p)) for t in range(STEPS) for p in range(3)
        ]

    for u, unit in enumerate(UNITS):
        weight = unit[0]
        for src, dst in column_pairs(weight):
            remote(
                locals_[weight].at[local_rows(unit), src],
                fulls[weight].at[rows_of(unit, shard, quad), dst],
                ysend.at[u], yrecv.at[u], place.other_shard(),
            ).start()
    owns = []
    for weight in range(4):
        half = locals_[weight].shape[0]
        rows = pl.ds(pl.multiple_of(shard * half, 16), half)
        for src, dst in column_pairs(weight):
            owns.append(
                pltpu.make_async_copy(
                    locals_[weight].at[:, src], fulls[weight].at[rows, dst], own_sem.at[len(owns)]
                )
            )
            owns[-1].start()
    flat_all[shard] = flat[...]
    narrow_all[shard] = narrow[...]
    third_all[shard] = third[...]

    def moved(u, quad_of, sems, device):
        unit = UNITS[u]
        region = fulls[unit[0]].at[rows_of(unit, 1 - shard, quad_of), :]
        return remote(region, region, sems[0].at[u], sems[1].at[u], device)

    def arrivals(u):
        moved(u, quad, (ysend, yrecv), place.other_shard()).wait_recv()
        moved(u, quad, (xsend, xrecv), place.other_side()).start()
        moved(u, quad, (csend, crecv), place.other_core()).start()

    def second(u):
        moved(u, quad + 2 - 4 * (quad // 2), (xsend, xrecv), place.other_side()).wait_recv()
        moved(u, quad + 2 - 4 * (quad // 2), (dsend, drecv), place.other_core()).start()

    for u in range(len(UNITS)):
        arrivals(u)
        if u:
            second(u - 1)
    second(len(UNITS) - 1)
    for u in range(len(UNITS)):
        moved(u, quad, (csend, crecv), place.other_core()).wait()
        moved(u, quad, (dsend, drecv), place.other_core()).wait()
        moved(u, quad, (xsend, xrecv), place.other_side()).wait_send()
        moved(u, quad, (ysend, yrecv), place.other_shard()).wait_send()
    for one in owns:
        one.wait()
    for one in smalls:
        one.wait()


def gather_weights(flat, narrow, third, w_in, w_out, w_up, w_down):
    vmem = pl.BlockSpec(memory_space=pltpu.VMEM)
    hbm = pl.BlockSpec(memory_space=pl.ANY)
    units = len(UNITS)

    def doubled(value):
        return jax.ShapeDtypeStruct((2 * value.shape[0], *value.shape[1:]), value.dtype)

    def both(value):
        return jax.ShapeDtypeStruct((2, *value.shape), value.dtype)

    return pl.pallas_call(
        gather_kernel,
        in_specs=[vmem] * 7,
        out_specs=[vmem] * 3 + [hbm] * 4,
        out_shape=[both(one) for one in (flat, narrow, third)]
        + [doubled(one) for one in (w_in, w_out, w_up, w_down)],
        scratch_shapes=[pltpu.SemaphoreType.DMA((3,))] * 2
        + [pltpu.SemaphoreType.DMA((3 + 3 * STEPS,))]
        + [pltpu.SemaphoreType.DMA((units,))] * 8,
        compiler_params=pltpu.CompilerParams(
            collective_id=0, has_side_effects=True, vmem_limit_bytes=24 * 2**20
        ),
        name="gather_weights",
    )(flat, narrow, third, w_in, w_out, w_up, w_down)


class Reduction:
    def __init__(self, place, first, count, rows, bufs, sems, out):
        self.place = place
        self.first = first
        self.count = count
        self.rows = rows
        self.dtype = bufs[0].dtype
        self.whole, self.from_core, self.half, self.from_shard, self.own, self.from_side, self.mine, self.from_depth, self.back = bufs
        (self.s_core, self.r_core, self.s_shard, self.r_shard, self.s_side, self.r_side, self.s_depth, self.r_depth,
         self.s_gd, self.r_gd, self.s_gs, self.r_gs, self.s_gc, self.r_gc, self.s_own) = sems
        self.out = out

    def when(self, tick, lag, body):
        k = tick - self.first - lag

        @pl.when((k >= 0) & (k < self.count))
        def _():
            body(k, k % 2)

    def rows_at(self, index, size):
        return pl.ds(pl.multiple_of(index * size, size), size)

    def core_copy(self, k, slot):
        p = self.place
        return remote(
            self.whole.at[slot, :, self.rows_at(1 - p.core, self.rows // 2), :],
            self.from_core.at[k], self.s_core.at[k], self.r_core.at[k], p.other_core(),
        )

    def shard_copy(self, k, slot):
        p = self.place
        return remote(
            self.half.at[slot, 1 - p.shard], self.from_shard.at[k], self.s_shard.at[k], self.r_shard.at[k],
            p.other_shard(),
        )

    def side_copy(self, k, slot):
        p = self.place
        return remote(
            self.own.at[slot, self.rows_at(1 - p.side, self.rows // 4), :],
            self.from_side.at[k], self.s_side.at[k], self.r_side.at[k], p.other_side(),
        )

    def quarter(self, base, index):
        rows = self.rows // 8
        return (
            pl.ds(pl.multiple_of(base + (index // 2) * rows, rows), rows),
            pl.ds(pl.multiple_of((index % 2) * (D // 2), D // 2), D // 2),
        )

    def depth_copy(self, k, slot, step):
        p = self.place
        rows, cols = self.quarter(0, (p.depth + step) % 4)
        return remote(
            self.mine.at[slot, rows, cols], self.from_depth.at[k, step - 1],
            self.s_depth.at[k, step - 1], self.r_depth.at[k, step - 1], p.other_depth(step),
        )

    def depth_back(self, k, step):
        p = self.place
        rows, cols = self.quarter(p.side * (self.rows // 4), p.depth)
        region = self.back.at[k, rows, cols]
        return remote(
            region, region, self.s_gd.at[k, step - 1], self.r_gd.at[k, step - 1], p.other_depth(step)
        )

    def side_back(self, k):
        p = self.place
        region = self.back.at[k, self.rows_at(p.side, self.rows // 4), :]
        return remote(region, region, self.s_gs.at[k], self.r_gs.at[k], p.other_side())

    def homes(self, k, place_in):
        rows = pl.ds(pl.multiple_of(self.place.core * (self.rows // 2), self.rows // 2), self.rows // 2)
        return [(cols, ref.at[(*lead, rows, *tail)]) for cols, ref, lead, tail in place_in]

    def send_home(self, k, place_in):
        p = self.place
        for cols, region in self.homes(k, place_in):
            piece = self.back.at[k, :, cols]
            remote(piece, region, self.s_gc.at[k], self.r_gc.at[k], p.other_core()).start()
            pltpu.make_async_copy(piece, region, self.s_own.at[k]).start()

    def wait_home(self, k):
        whole = self.back.at[k]
        remote(whole, whole, self.s_gc.at[k], self.r_gc.at[k], self.place.other_core()).wait()
        pltpu.make_async_copy(whole, whole, self.s_own.at[k]).wait()

    def add(self, left, right):
        return (left.astype(f32) + right.astype(f32)).astype(self.dtype)

    def send(self, tick):
        self.when(tick, 0, lambda k, slot: self.core_copy(k, slot).start())

    def advance(self, tick):
        p = self.place

        def after_core(k, slot):
            self.core_copy(k, slot).wait()
            for s in range(2):
                self.half[slot, s] = self.add(
                    self.whole[slot, s, self.rows_at(p.core, self.rows // 2), :], self.from_core[k, s]
                )
            self.shard_copy(k, slot).start()

        def after_shard(k, slot):
            self.shard_copy(k, slot).wait()
            self.own[slot] = self.add(self.half[slot, p.shard], self.from_shard[k])
            self.side_copy(k, slot).start()

        def after_side(k, slot):
            self.side_copy(k, slot).wait()
            self.mine[slot] = self.add(
                self.own[slot, self.rows_at(p.side, self.rows // 4), :], self.from_side[k]
            )
            for step in range(1, 4):
                self.depth_copy(k, slot, step).start()

        def after_depth(k, slot):
            for step in range(1, 4):
                self.depth_copy(k, slot, step).wait()
            rows, cols = self.quarter(0, p.depth)
            total = self.mine[slot, rows, cols].astype(f32)
            for step in range(3):
                total = total + self.from_depth[k, step].astype(f32)
            rows, cols = self.quarter(p.side * (self.rows // 4), p.depth)
            self.back[k, rows, cols] = total.astype(self.dtype)
            for step in range(1, 4):
                self.depth_back(k, step).start()

        def after_depth_back(k, slot):
            for step in range(1, 4):
                self.depth_back(k, step).wait()
            self.side_back(k).start()

        def after_side_back(k, slot):
            self.side_back(k).wait()
            self.out(self, k)

        def after_core_back(k, slot):
            self.wait_home(k)

        for lag, body in enumerate(
            (after_core, after_shard, after_side, after_depth, after_depth_back, after_side_back, after_core_back), 1
        ):
            self.when(tick, lag, body)


LAGS = 7
DOWN, UP, OUT, IN = 4, 4, 1, STEPS
CHUNKS = DOWN + UP + OUT + IN
SMALL_ROWS = 128


def reduce_kernel(small, active0, active1, upstream, second, d_hidden, mixed, d_branch, normed, d_proj, small_out, g_down, g_up, g_out, g_in, *scratch):
    tick = pl.program_id(0)
    place = Place()
    bufs, sems = scratch[:9], scratch[9:24]
    small_bufs, small_sems = scratch[24:33], scratch[33:48]
    everything = slice(None)

    def little_home(chain, k):
        chain.send_home(k, [(everything, small_out, (k,), (everything,))])

    def big_home(chain, k):
        @pl.when(k < DOWN)
        def _():
            chain.send_home(k, [(everything, g_down, (k,), (everything,))])

        @pl.when((k >= DOWN) & (k < DOWN + UP))
        def _():
            cols = pl.ds(pl.multiple_of((k - DOWN) * D, D), D)
            chain.send_home(k, [(everything, g_up, (), (cols,))])

        @pl.when(k == DOWN + UP)
        def _():
            chain.send_home(k, [(everything, g_out, (), (everything,))])

        @pl.when(k > DOWN + UP)
        def _():
            tile = k - (DOWN + UP + OUT)
            chain.send_home(
                k,
                [
                    (part(p), g_in, (), (pl.ds(pl.multiple_of(p * D + tile * TILE, TILE), TILE),))
                    for p in range(3)
                ],
            )

    little = Reduction(place, 0, 1, SMALL_ROWS, small_bufs, small_sems, little_home)
    big = Reduction(place, 1, CHUNKS, D // 2, bufs, sems, big_home)

    @pl.when(tick == 0)
    def _():
        greet(
            [place.other_shard(), place.other_side(), place.other_core()]
            + [place.other_depth(step) for step in range(1, 4)]
        )
        little.whole[0] = small[...]

    little.advance(tick)
    big.advance(tick)

    def compute(k, slot):
        def chunk(lefts, right):
            for s in range(2):
                big.whole[slot, s] = inner_rows(lefts[s], right[...]).astype(bf16)

        def halves(left):
            return left[:, : D // 2], left[:, D // 2 :]

        @pl.when(k < DOWN)
        def _():
            chunk((active0[...], active1[...]), upstream)

        @pl.when((k >= DOWN) & (k < DOWN + UP))
        def _():
            chunk(halves(second), d_hidden)

        @pl.when(k == DOWN + UP)
        def _():
            chunk(halves(mixed), d_branch)

        @pl.when(k > DOWN + UP)
        def _():
            chunk(halves(normed), d_proj)

    little.send(tick)
    big.when(tick, 0, compute)
    big.send(tick)


def reduce_grads(small, active, upstream, second, d_hidden, mixed, d_branch, normed, d_proj):
    count = upstream.shape[0]
    half = D // 2

    def clamp(tick, low, high):
        return jnp.minimum(jnp.maximum(tick - 1 - low, 0), high - 1)

    def fixed(shape):
        return pl.BlockSpec(shape, lambda t: (0,) * len(shape), pipeline_mode=pl.Buffered(1))

    def buffers(n, rows, kind):
        return [
            pltpu.VMEM((2, 2, rows, D), kind),
            pltpu.VMEM((n, 2, rows // 2, D), kind),
            pltpu.VMEM((2, 2, rows // 2, D), kind),
            pltpu.VMEM((n, rows // 2, D), kind),
            pltpu.VMEM((2, rows // 2, D), kind),
            pltpu.VMEM((n, rows // 4, D), kind),
            pltpu.VMEM((2, rows // 4, D), kind),
            pltpu.VMEM((n, 3, rows // 8, D // 2), kind),
            pltpu.VMEM((n, rows // 2, D), kind),
        ]

    def semaphores(n):
        one = pltpu.SemaphoreType.DMA((n,))
        three = pltpu.SemaphoreType.DMA((n, 3))
        return [one] * 6 + [three] * 4 + [one] * 5

    return pl.pallas_call(
        reduce_kernel,
        grid=(1 + CHUNKS + LAGS,),
        in_specs=[
            fixed(small.shape),
            pl.BlockSpec((count, half), lambda t: (0, clamp(t, 0, DOWN))),
            pl.BlockSpec((count, half), lambda t: (0, DOWN + clamp(t, 0, DOWN))),
            fixed((count, D)),
            fixed((count, D)),
            pl.BlockSpec((count, D), lambda t: (0, clamp(t, DOWN, UP))),
            fixed((count, D)),
            fixed((count, D)),
            fixed((count, D)),
            pl.BlockSpec((count, D), lambda t: (0, clamp(t, DOWN + UP + OUT, IN))),
        ],
        out_specs=[pl.BlockSpec(memory_space=pl.ANY)] * 5,
        out_shape=[
            jax.ShapeDtypeStruct((1, SMALL_ROWS, D), f32),
            jax.ShapeDtypeStruct((DOWN, half, D), bf16),
            jax.ShapeDtypeStruct((half, UP * D), bf16),
            jax.ShapeDtypeStruct((half, D), bf16),
            jax.ShapeDtypeStruct((half, D3), bf16),
        ],
        scratch_shapes=buffers(CHUNKS, half, bf16) + semaphores(CHUNKS) + buffers(1, SMALL_ROWS, f32) + semaphores(1),
        compiler_params=pltpu.CompilerParams(
            collective_id=1, has_side_effects=True, vmem_limit_bytes=63 * 2**20
        ),
        name="reduce_grads",
    )(small, active, active, upstream, second, d_hidden, mixed, d_branch, normed, d_proj)


def pack_rows(values):
    rows = [one.reshape(-1, 128) for one in values]
    groups = [jnp.concatenate(rows[i : i + 4], axis=0) for i in range(0, len(rows), 4)]
    return jnp.concatenate(groups, axis=0)


def per_device(
    prompt_x, cont_x, prompt_cot, cont_cot, norm1_gain, norm1_bias, in_weight, in_bias, short_weight,
    short_bias, long_bias, filter_w1, filter_b1, filter_w2, filter_b2, filter_w3, filter_decay, out_weight,
    out_bias, norm2_gain, norm2_bias, up_weight, up_bias, down_weight, down_bias, *, reps, shards,
):
    own_kernels = reps == 16 and shards == 2
    micros = prompt_x.shape[0]
    groups = prompt_x.shape[1]
    count = micros * groups * SPAN

    def tokens_of(prompt, cont):
        return jnp.concatenate(
            [
                prompt.reshape(micros * groups, PROMPT, D),
                cont.reshape(micros * groups, CONTS * BLOCK, D),
            ],
            axis=1,
        ).reshape(count, D)

    def parts_of(rows):
        rows = rows.reshape(micros, groups, SPAN, D)
        return rows[:, :, :PROMPT], rows[:, :, PROMPT:].reshape(micros, groups, CONTS, BLOCK, D)

    narrow = jnp.concatenate([filter_w1, filter_b1[None], filter_w2, filter_b2[None]], axis=0)
    vectors = (
        norm1_gain, norm1_bias, in_bias, short_weight, short_bias, long_bias, filter_decay, out_bias,
        norm2_gain, norm2_bias, up_bias, down_bias,
    )
    if own_kernels:
        flat, narrow_all, third_all, in_full, out_full, up_full, down_full = gather_weights(
            pack_rows(vectors), narrow, filter_w3, in_weight, out_weight, up_weight, down_weight
        )
        flat = flat.reshape(shards, -1)
    else:
        gather = partial(lax.all_gather, axis_name="shard", axis=0)
        flat = gather(jnp.concatenate([one.reshape(-1) for one in vectors]))
        narrow_all, third_all = gather(narrow), gather(filter_w3)
        in_full, out_full, up_full, down_full = (
            gather(one, tiled=True) for one in (by_tile(in_weight), out_weight, up_weight, down_weight)
        )
    flat, narrow_all, third_all = flat.astype(f32), narrow_all.astype(f32), third_all.astype(f32)
    wide = []
    start = 0
    for one in vectors:
        lead = one.shape[0] if one.ndim == 2 else 1
        value = flat[:, start : start + one.size].reshape(shards, lead, -1)
        value = value.swapaxes(0, 1).reshape(lead, -1)
        wide.append(value if one.ndim == 2 else value[0])
        start += one.size
    gain1, shift1, in_shift, taps, short_shift, long_shift, decay, out_shift, gain2, shift2, up_shift, down_shift = wide
    narrow_all = narrow_all.swapaxes(0, 1).reshape(narrow.shape[0], -1)
    n1 = filter_w1.shape[0]
    n2 = filter_w2.shape[0]
    fw1, fb1 = narrow_all[:n1], narrow_all[n1]
    fw2, fb2 = narrow_all[n1 + 1 : n1 + 1 + n2], narrow_all[n1 + 1 + n2]
    fw3 = third_all.swapaxes(0, 1).reshape(filter_w3.shape[0], -1)
    in_shift, short_shift, taps = by_tile(in_shift), by_tile(short_shift), by_tile(taps)

    tokens = tokens_of(prompt_x, cont_x).astype(f32)
    upstream = tokens_of(prompt_cot, cont_cot)
    upstream_f = upstream.astype(f32)

    filters, filter_pull = jax.vjp(partial(filter_taps, decay=decay), fw1, fb1, fw2, fb2, fw3)
    normed, norm_pull = jax.vjp(layer_norm, tokens, gain1, shift1)
    normed_low = normed.astype(bf16)
    projected = lowmul(normed_low, in_full) + in_shift
    mixed_low, hat1, hat2, mid, bank1, bank2 = run_forward(
        projected, taps, short_shift[None], long_shift, filters
    )
    middle = tokens + lowmul(mixed_low, out_full) + out_shift
    normed_two, norm_two_pull = jax.vjp(layer_norm, middle, gain2, shift2)
    second_low = normed_two.astype(bf16)
    hidden = lowmul(second_low, up_full) + up_shift
    active, gelu_pull = jax.vjp(partial(jax.nn.gelu, approximate=True), hidden)
    active_low = active.astype(bf16)
    result = (middle + lowmul(active_low, down_full) + down_shift).astype(bf16)
    prompt_out, cont_out = parts_of(result)

    d_active = times_t(upstream, down_full)
    d_hidden = gelu_pull(d_active)[0].astype(bf16)
    d_second = times_t(d_hidden, up_full)
    d_middle, grad_gain2, grad_shift2 = norm_two_pull(d_second)
    d_middle = d_middle + upstream_f
    d_branch = d_middle.astype(bf16)
    d_mixed = times_t(d_branch, out_full)
    d_proj, d_taps, d_long, d_filter1, d_filter2 = run_backward(
        d_mixed, projected, taps, short_shift[None], long_shift, bank1, bank2, hat1, hat2, mid
    )
    d_normed = times_t(d_proj, in_full)
    d_tokens, grad_gain1, grad_shift1 = norm_pull(d_normed)
    prompt_grad, cont_grad = parts_of((d_tokens + d_middle).astype(bf16))
    grad_f1, grad_fb1, grad_f2, grad_fb2, grad_f3 = filter_pull(
        jnp.concatenate([d_filter1, d_filter2], axis=-1)
    )

    width = D // shards
    d_taps = by_part(d_taps[:5])
    narrow_grad = jnp.concatenate([grad_f1, grad_fb1[None], grad_f2, grad_fb2[None]], axis=0)
    narrow_grad = narrow_grad.reshape(narrow.shape[0], shards, -1).swapaxes(0, 1).reshape(shards, -1)
    narrow_size = narrow_grad.shape[1]
    narrow_rows = -(-narrow_size // width)
    singles = jnp.stack(
        [
            grad_gain1, grad_shift1, jnp.sum(d_branch.astype(f32), axis=0), grad_gain2, grad_shift2,
            jnp.sum(upstream_f, axis=0),
        ]
    )

    def by_shard(value):
        rows = value.shape[0]
        return value.reshape(rows, shards, -1).swapaxes(0, 1).reshape(shards, -1, width)

    rows = [
        by_shard(d_taps),
        by_shard(d_long),
        by_shard(singles),
        by_shard(jnp.sum(d_hidden.astype(f32), axis=0)[None]),
        jnp.pad(narrow_grad, ((0, 0), (0, narrow_rows * width - narrow_size))).reshape(shards, -1, width),
    ]
    places = np.cumsum([0] + [one.shape[1] for one in rows])
    rows = jnp.concatenate(rows, axis=1)
    third_grad = grad_f3.reshape(filter_w3.shape[0], shards, -1).swapaxes(0, 1)
    if own_kernels:
        heads = third_grad.shape[1]
        small = jnp.concatenate(
            [third_grad, jnp.pad(rows, ((0, 0), (0, SMALL_ROWS - heads - rows.shape[1]), (0, D - width)))], axis=1
        )
        small, grad_down, grad_up, grad_out, grad_in = reduce_grads(
            small, active_low, upstream, second_low, d_hidden, mixed_low, d_branch, normed_low, d_proj
        )
        third_grad = small[0, :heads]
        rows = small[0, heads : heads + places[-1], :width]
        grad_down = grad_down.reshape(-1, D).astype(f32)
        grad_up, grad_out, grad_in = grad_up.astype(f32), grad_out.astype(f32), grad_in.astype(f32)
    else:
        def reduce(value):
            value = lax.psum_scatter(value, "shard", scatter_dimension=0, tiled=True)
            return lax.psum(value, "rep")

        third_grad, rows = reduce(third_grad)[0], reduce(rows)[0]
        grad_down = reduce(inner_rows(active_low, upstream))
        grad_up = reduce(inner_rows(second_low, d_hidden))
        grad_out = reduce(inner_rows(mixed_low, d_branch))
        grad_in = by_part(reduce(inner_rows(normed_low, d_proj)))
    tap_rows, long_rows, single_rows, up_rows, narrow_rows = (
        rows[places[i] : places[i + 1]] for i in range(5)
    )
    tap_rows = tap_rows.reshape(5, -1)
    narrow_own = narrow_rows.reshape(-1)[:narrow_size].reshape(narrow.shape)
    return (
        prompt_out,
        cont_out,
        prompt_grad,
        cont_grad,
        single_rows[0],
        single_rows[1],
        grad_in,
        tap_rows[4],
        tap_rows[:3],
        tap_rows[3],
        long_rows.reshape(2, -1),
        narrow_own[:n1],
        narrow_own[n1],
        narrow_own[n1 + 1 : n1 + 1 + n2],
        narrow_own[n1 + 1 + n2],
        third_grad,
        grad_out,
        single_rows[2],
        single_rows[3],
        single_rows[4],
        grad_up,
        up_rows.reshape(-1),
        grad_down,
        single_rows[5],
    )


def solution(mesh):
    group4 = P(None, ("rep", "shard"), None, None)
    group5 = P(None, ("rep", "shard"), None, None, None)
    one, row, col = P("shard"), P("shard", None), P(None, "shard")
    grads = (one, one, row, one, col, one, col, col, one, col, one, col)
    rest = (row, one, one, one, row, one, row, one)
    return jax.shard_map(
        partial(per_device, reps=mesh.shape["rep"], shards=mesh.shape["shard"]),
        mesh=mesh,
        in_specs=(group4, group5, group4, group5) + grads + (one,) + rest,
        out_specs=(group4, group5, group4, group5) + grads + rest,
        check_vma=False,
    )
```

```python
from functools import partial
import math

import jax
import jax.numpy as jnp
import numpy as np
from jax import lax
from jax.experimental import pallas as pl
from jax.experimental.pallas import tpu as pltpu
from jax.sharding import PartitionSpec as P

D = 768
D3 = 3 * D
BANDS = 16
BLOCK = 128
PROMPT = 256
CONTS = 2
SEQ = 384
SPAN = PROMPT + CONTS * BLOCK
TILE = 256
FREQ = 2 * BLOCK

EPS = 1e-05
HIGH = lax.Precision.HIGHEST
f32 = jnp.float32
bf16 = jnp.bfloat16


def matmul(left_op, right_op):
    return jnp.dot(left_op, right_op, precision=HIGH, preferred_element_type=f32)


def lowmul(left_op, right_op):
    return jnp.dot(left_op, right_op, preferred_element_type=f32)


def inner_rows(left_op, right_op):
    return lax.dot_general(
        left_op, right_op, (((0,), (0,)), ((), ())), preferred_element_type=f32
    )


def times_t(left_op, right_op):
    return lax.dot_general(
        left_op, right_op, (((1,), (1,)), ((), ())), preferred_element_type=f32
    )


def layer_norm(values, norm_gain, norm_shift):
    center_val = values - jnp.mean(values, axis=-1, keepdims=True)
    spread = jnp.mean(center_val * center_val, axis=-1, keepdims=True)
    return center_val * lax.rsqrt(spread + EPS) * norm_gain + norm_shift


def dft_matrix():
    freq = np.arange(BLOCK)
    place = np.arange(BLOCK)
    angle = np.pi * ((2 * freq[:, None] + 1) * place[None, :] % (4 * BLOCK)) / FREQ
    return np.concatenate([np.cos(angle), -np.sin(angle)], axis=0)


def split3(matrix):
    matrix = matrix.astype(np.float32)
    high = matrix.astype(jnp.bfloat16)
    rest = (matrix - high.astype(np.float32)).astype(jnp.bfloat16)
    return np.concatenate([high, rest, high], axis=1)


def split_dot(triple, signal):
    high = signal.astype(bf16)
    rest = (signal - high.astype(f32)).astype(bf16)
    return jnp.dot(
        triple, jnp.concatenate([high, high, rest], axis=0), preferred_element_type=f32
    )


def cmul(left, right):
    lr, li = left[:BLOCK], left[BLOCK:]
    rr, ri = right[:BLOCK], right[BLOCK:]
    return jnp.concatenate([lr * rr - li * ri, lr * ri + li * rr], axis=0)


def cmul_conj(left, right):
    lr, li = left[:BLOCK], left[BLOCK:]
    rr, ri = right[:BLOCK], right[BLOCK:]
    return jnp.concatenate([lr * rr + li * ri, lr * ri - li * rr], axis=0)


def row_index():
    return lax.broadcasted_iota(jnp.int32, (BLOCK, TILE), 0)


def delayed(block, before, lag):
    rolled = pltpu.roll(block, lag, 0)
    if before is None:
        return jnp.where(row_index() >= lag, rolled, 0.0)
    return jnp.where(row_index() >= lag, rolled, pltpu.roll(before, lag, 0))


def advanced(block, after, lag):
    rolled = pltpu.roll(block, BLOCK - lag, 0)
    if after is None:
        return jnp.where(row_index() < BLOCK - lag, rolled, 0.0)
    return jnp.where(row_index() < BLOCK - lag, rolled, pltpu.roll(after, BLOCK - lag, 0))


BEFORE = (None, 0, 1, 1)


def part(index):
    return slice(index * TILE, (index + 1) * TILE)


def load_blocks(ref, cols=slice(None)):
    return [ref[i * BLOCK : (i + 1) * BLOCK, cols] for i in range(4)]


def short_blocks(z_ref, rows_ref, index):
    blocks = load_blocks(z_ref, part(index))
    taps = rows_ref[0:3, part(index)]
    shift = rows_ref[3:4, part(index)]
    outs = []
    for i in range(4):
        before = None if BEFORE[i] is None else blocks[BEFORE[i]]
        outs.append(
            taps[0:1] * blocks[i]
            + taps[1:2] * delayed(blocks[i], before, 1)
            + taps[2:3] * delayed(blocks[i], before, 2)
            + shift
        )
    return outs


def spectra(hats, bank):
    tail = cmul(bank[1], hats[1]) + cmul(bank[2], hats[0])
    return [
        cmul(bank[0], hats[0]),
        cmul(bank[0], hats[1]) + cmul(bank[1], hats[0]),
        cmul(bank[0], hats[2]) + tail,
        cmul(bank[0], hats[3]) + tail,
    ]


def adjoint_spectra(hats, bank):
    tail = hats[2] + hats[3]
    return [
        cmul_conj(bank[0], hats[0]) + cmul_conj(bank[1], hats[1]) + cmul_conj(bank[2], tail),
        cmul_conj(bank[0], hats[1]) + cmul_conj(bank[1], tail),
        cmul_conj(bank[0], hats[2]),
        cmul_conj(bank[0], hats[3]),
    ]


def bank_grads(hats, grads):
    tail = grads[2] + grads[3]
    zero = cmul_conj(hats[0], grads[0])
    for i in range(1, 4):
        zero = zero + cmul_conj(hats[i], grads[i])
    one = cmul_conj(hats[0], grads[1]) + cmul_conj(hats[1], tail)
    return [zero, one, cmul_conj(hats[0], tail)]


def signs():
    odd = lax.broadcasted_iota(jnp.int32, (BLOCK, TILE), 0) % 2
    return (1 - 2 * odd).astype(f32)


LONG1, LONG2 = slice(6, 7), slice(7, 8)


def make_bank(ahead, taps, bank_ref):
    hats = [split_dot(ahead, taps[o * BLOCK : (o + 1) * BLOCK, :] * (1.0 / BLOCK)) for o in range(3)]
    sign = signs()
    bank = [hats[0]]
    for o in (1, 2):
        prev = hats[o - 1]
        turned = jnp.concatenate([-sign * prev[BLOCK:], sign * prev[:BLOCK]], axis=0)
        bank.append(hats[o] + turned)
    for o in range(3):
        bank_ref[o] = bank[o]


def filter_grads(back, grads, out_ref):
    sign = signs()
    for o in range(3):
        one = grads[o]
        if o < 2:
            after = grads[o + 1]
            one = one + jnp.concatenate([sign * after[BLOCK:], -sign * after[:BLOCK]], axis=0)
        out_ref[o * BLOCK : (o + 1) * BLOCK, :] = split_dot(back, one) * (1.0 / BLOCK)


def mixer_forward(
    z_ref, rows_ref, long_ref, filter1, filter2, ahead_ref, back_ref,
    out_ref, hat1_ref, hat2_ref, mid_ref, bank1, bank2,
):
    @pl.when(pl.program_id(1) == 0)
    def _():
        make_bank(ahead_ref[...], filter1[...], bank1)
        make_bank(ahead_ref[...], filter2[...], bank2)

    forward_step(
        z_ref, rows_ref, long_ref, ahead_ref, back_ref, out_ref, hat1_ref, hat2_ref, mid_ref, bank1, bank2
    )


def forward_step(
    z_ref, rows_ref, long_ref, ahead_ref, back_ref, out_ref, hat1_ref, hat2_ref, mid_ref, bank1, bank2
):
    ahead = ahead_ref[...]
    back = back_ref[...]
    gate1 = short_blocks(z_ref, rows_ref, 1)
    value = short_blocks(z_ref, rows_ref, 2)
    sig1 = [gate1[i] * value[i] for i in range(4)]
    hats = []
    for i in range(4):
        hat = split_dot(ahead, sig1[i])
        hat1_ref[i] = hat
        hats.append(hat)
    wave = spectra(hats, [bank1[i] for i in range(3)])
    mid = []
    for i in range(4):
        one = split_dot(back, wave[i]) + long_ref[LONG1, :] * sig1[i]
        mid_ref[i * BLOCK : (i + 1) * BLOCK, :] = one
        mid.append(one)
    gate0 = short_blocks(z_ref, rows_ref, 0)
    sig2 = [gate0[i] * mid[i] for i in range(4)]
    hats = []
    for i in range(4):
        hat = split_dot(ahead, sig2[i])
        hat2_ref[i] = hat
        hats.append(hat)
    wave = spectra(hats, [bank2[i] for i in range(3)])
    for i in range(4):
        two = split_dot(back, wave[i]) + long_ref[LONG2, :] * sig2[i]
        out_ref[i * BLOCK : (i + 1) * BLOCK, :] = two.astype(bf16)


def mixer_backward(
    grad_ref, z_ref, rows_ref, long_ref, bank1, bank2, hat1_ref, hat2_ref, mid_ref,
    ahead_ref, back_ref,
    dz_ref, dtap_ref, dlong_ref, dfilt1_ref, dfilt2_ref, dbank1, dbank2,
):
    micro = pl.program_id(1)
    backward_step(
        micro == 0, micro == pl.num_programs(1) - 1, grad_ref, z_ref, rows_ref, long_ref, bank1, bank2,
        hat1_ref, hat2_ref, mid_ref, ahead_ref, back_ref,
        dz_ref, dtap_ref, dlong_ref, dfilt1_ref, dfilt2_ref, dbank1, dbank2,
    )


def backward_step(
    first, last, grad_ref, z_ref, rows_ref, long_ref, bank1, bank2, hat1_ref, hat2_ref, mid_ref,
    ahead_ref, back_ref,
    dz_ref, dtap_ref, dlong_ref, dfilt1_ref, dfilt2_ref, dbank1, dbank2,
):
    ahead = ahead_ref[...]
    back = back_ref[...]

    @pl.when(first)
    def _():
        dbank1[...] = jnp.zeros_like(dbank1)
        dbank2[...] = jnp.zeros_like(dbank2)
        dlong_ref[...] = jnp.zeros_like(dlong_ref)
        dtap_ref[...] = jnp.zeros_like(dtap_ref)

    def total(values):
        acc = values[0]
        for one in values[1:]:
            acc = acc + one
        return jnp.sum(acc, axis=0, keepdims=True)

    gate0 = short_blocks(z_ref, rows_ref, 0)
    grad2 = load_blocks(grad_ref)
    mid = load_blocks(mid_ref)
    dhats = [split_dot(ahead, grad2[i]) for i in range(4)]
    new = bank_grads([hat2_ref[i] for i in range(4)], dhats)
    for i in range(3):
        dbank2[i] += new[i]
    wave = adjoint_spectra(dhats, [bank2[i] for i in range(3)])
    dsig2 = [split_dot(back, wave[i]) + long_ref[LONG2, :] * grad2[i] for i in range(4)]
    dlong_ref[1:2, :] += total([grad2[i] * gate0[i] * mid[i] for i in range(4)])
    dgate0 = [dsig2[i] * mid[i] for i in range(4)]
    grad1 = [dsig2[i] * gate0[i] for i in range(4)]
    dhats = [split_dot(ahead, grad1[i]) for i in range(4)]
    new = bank_grads([hat1_ref[i] for i in range(4)], dhats)
    for i in range(3):
        dbank1[i] += new[i]
    wave = adjoint_spectra(dhats, [bank1[i] for i in range(3)])
    dsig1 = [split_dot(back, wave[i]) + long_ref[LONG1, :] * grad1[i] for i in range(4)]
    gate1 = short_blocks(z_ref, rows_ref, 1)
    value = short_blocks(z_ref, rows_ref, 2)
    dlong_ref[0:1, :] += total([grad1[i] * gate1[i] * value[i] for i in range(4)])
    dgate1 = [dsig1[i] * value[i] for i in range(4)]
    dvalue = [dsig1[i] * gate1[i] for i in range(4)]
    for index, grads in enumerate((dgate0, dgate1, dvalue)):
        cols = part(index)
        taps = rows_ref[0:3, cols]
        blocks = load_blocks(z_ref, cols)
        after = (grads[1], grads[2] + grads[3], None, None)
        dz = []
        for i in range(4):
            one = (
                taps[0:1] * grads[i]
                + taps[1:2] * advanced(grads[i], after[i], 1)
                + taps[2:3] * advanced(grads[i], after[i], 2)
            ).astype(bf16)
            dz_ref[i * BLOCK : (i + 1) * BLOCK, cols] = one
            dz.append(one.astype(f32))
        dtap_ref[4:5, cols] += total(dz)
        dtap_ref[3:4, cols] += total(grads)
        dtap_ref[0:1, cols] += total([grads[i] * blocks[i] for i in range(4)])
        for lag in (1, 2):
            dtap_ref[lag : lag + 1, cols] += total(
                [
                    grads[i]
                    * delayed(blocks[i], None if BEFORE[i] is None else blocks[BEFORE[i]], lag)
                    for i in range(4)
                ]
            )

    @pl.when(last)
    def _():
        filter_grads(back, [dbank1[i] for i in range(3)], dfilt1_ref)
        filter_grads(back, [dbank2[i] for i in range(3)], dfilt2_ref)


def constants():
    matrix = dft_matrix()
    return jnp.asarray(split3(matrix)), jnp.asarray(split3(matrix.T))


STEPS = D // TILE
AHEAD = (FREQ, 3 * BLOCK)
BACK = (BLOCK, 3 * FREQ)


def run_forward(z, lines, vecs, filters):
    rows = z.shape[0]
    blocks = rows // BLOCK

    def spec(shape, index):
        return pl.BlockSpec(shape, lambda t, m: index(m, t))

    hat_spec = spec((4, FREQ, TILE), lambda m, t: (m, 0, t))
    row_spec = spec((SPAN, TILE), lambda m, t: (m, t))
    bank_spec = spec((3, FREQ, TILE), lambda m, t: (0, 0, t))
    hat_shape = jax.ShapeDtypeStruct((blocks, FREQ, D), f32)
    bank_shape = jax.ShapeDtypeStruct((3, FREQ, D), f32)
    return pl.pallas_call(
        mixer_forward,
        grid=(STEPS, rows // SPAN),
        in_specs=[
            spec((SPAN, 3 * TILE), lambda m, t: (m, t)),
            spec((8, 3 * TILE), lambda m, t: (0, t)),
            spec((8, TILE), lambda m, t: (0, t)),
            spec((SEQ, TILE), lambda m, t: (0, t)),
            spec((SEQ, TILE), lambda m, t: (0, STEPS + t)),
            spec(AHEAD, lambda m, t: (0, 0)),
            spec(BACK, lambda m, t: (0, 0)),
        ],
        out_specs=[row_spec, hat_spec, hat_spec, row_spec, bank_spec, bank_spec],
        out_shape=[
            jax.ShapeDtypeStruct((rows, D), bf16), hat_shape, hat_shape,
            jax.ShapeDtypeStruct((rows, D), f32), bank_shape, bank_shape,
        ],
        compiler_params=pltpu.CompilerParams(vmem_limit_bytes=40 * 2**20),
        cost_estimate=pl.CostEstimate(flops=10 * 10**9, bytes_accessed=32 * 2**20, transcendentals=0),
        name="mixer_forward",
    )(z, lines, vecs, filters, filters, *constants())


def run_backward(grad, z, lines, vecs, bank1, bank2, hat1, hat2, mid):
    rows = z.shape[0]

    def spec(shape, index):
        return pl.BlockSpec(shape, lambda t, m: index(m, t))

    hat_spec = spec((4, FREQ, TILE), lambda m, t: (m, 0, t))
    row_spec = spec((SPAN, TILE), lambda m, t: (m, t))
    bank_spec = spec((3, FREQ, TILE), lambda m, t: (0, 0, t))
    z_spec = spec((SPAN, 3 * TILE), lambda m, t: (m, t))
    column_spec = spec((SEQ, TILE), lambda m, t: (0, t))
    return pl.pallas_call(
        mixer_backward,
        grid=(STEPS, rows // SPAN),
        in_specs=[
            row_spec,
            z_spec,
            spec((8, 3 * TILE), lambda m, t: (0, t)),
            spec((8, TILE), lambda m, t: (0, t)),
            bank_spec, bank_spec, hat_spec, hat_spec, row_spec,
            spec(AHEAD, lambda m, t: (0, 0)),
            spec(BACK, lambda m, t: (0, 0)),
        ],
        out_specs=[
            z_spec,
            spec((8, 3 * TILE), lambda m, t: (0, t)),
            spec((2, TILE), lambda m, t: (0, t)),
            column_spec,
            column_spec,
        ],
        out_shape=[
            jax.ShapeDtypeStruct((rows, D3), bf16), jax.ShapeDtypeStruct((8, D3), f32),
            jax.ShapeDtypeStruct((2, D), f32), jax.ShapeDtypeStruct((SEQ, D), f32),
            jax.ShapeDtypeStruct((SEQ, D), f32),
        ],
        scratch_shapes=[pltpu.VMEM((3, FREQ, TILE), f32), pltpu.VMEM((3, FREQ, TILE), f32)],
        compiler_params=pltpu.CompilerParams(vmem_limit_bytes=40 * 2**20),
        cost_estimate=pl.CostEstimate(flops=24 * 10**9, bytes_accessed=36 * 2**20, transcendentals=0),
        name="mixer_backward",
    )(grad, z, lines, vecs, bank1, bank2, hat1, hat2, mid, *constants())


def place_ratio():
    return (np.arange(SEQ).astype(np.float32) / np.float32(SEQ))[:, None]


def filter_states(first_w, first_b, second_w, second_b):
    levels = (np.arange(BANDS) + 1).astype(np.float32)
    ratio = jnp.asarray(place_ratio())
    angles = 2.0 * math.pi * ratio * jnp.asarray(levels)[None, :]
    embed = jnp.concatenate([ratio, jnp.cos(angles), jnp.sin(angles)], axis=1)
    first_pre = matmul(embed, first_w) + first_b
    first_act = jnp.sin(first_pre)
    second_pre = matmul(first_act, second_w) + second_b
    return embed, first_pre, first_act, second_pre, jnp.sin(second_pre)


def filter_taps(first_w, first_b, second_w, second_b, third_w, decay):
    second_act = filter_states(first_w, first_b, second_w, second_b)[-1]
    return matmul(second_act, third_w) * jnp.exp(-jnp.asarray(place_ratio()) * decay[None, :])


def by_tile(value):
    shape = value.shape
    return value.reshape(*shape[:-1], 3, STEPS, TILE).swapaxes(-3, -2).reshape(shape)


def by_part(value):
    shape = value.shape
    return value.reshape(*shape[:-1], STEPS, 3, TILE).swapaxes(-3, -2).reshape(shape)


MESH = pl.DeviceIdType.MESH


class Place:
    def __init__(self):
        rep = lax.axis_index("rep")
        self.rep = rep
        self.shard = lax.axis_index("shard")
        self.core = rep % 2
        self.side = (rep // 2) % 2
        self.depth = rep // 4
        self.quad = rep % 4

    def other_shard(self):
        return (self.rep, 1 - self.shard)

    def other_side(self):
        return (self.rep + 2 - 4 * self.side, self.shard)

    def other_core(self):
        return (self.rep + 1 - 2 * self.core, self.shard)

    def other_depth(self, step):
        return (((self.depth + step) % 4) * 4 + self.quad, self.shard)


def greet(devices):
    barrier = pltpu.get_barrier_semaphore()
    for device in devices:
        pl.semaphore_signal(barrier, inc=1, device_id=device, device_id_type=MESH)
    pl.semaphore_wait(barrier, len(devices))


def remote(src, dst, send, recv, device):
    return pltpu.make_async_remote_copy(
        src_ref=src, dst_ref=dst, send_sem=send, recv_sem=recv, device_id=device, device_id_type=MESH
    )


UNITS = (
    (0, 0, 32), (0, 32, 32), (0, 64, 32), (1, 0, 96), (2, 0, 48), (2, 48, 48),
    (3, 0, 96), (3, 96, 96), (3, 192, 96), (3, 288, 96),
)
ARRIVALS = ((0, 1, 2, 3), (4,), (5,), (6,), (7,), (8, 9), ())
SECONDS = ((0, 1, 2), (3,), (4,), (), (5,), (6,), (7, 8, 9))
PACK_ROWS = 96
UP_ROW, DECAY_ROW, FIRST_ROW, SECOND_ROW = 23, 27, 32, 32


def column_moves():
    for s in range(2):
        for a in range(3):
            for b in range(3):
                at = s * (D3 // 2) + a * (D // 2) + b * 128
                yield s, a, b * 128, (at % D // TILE * 3 + at // D) * TILE + at % TILE


def gather_kernel(
    gain1, shift1, in_shift, short_w, short_b, long_b, w1, b1, w2, b2, third, decay, out_b, gain2, shift2, up_b,
    down_b, w_in, w_out, w_up, w_down, tokens, embed_ref, ratio_ref, ahead_ref, back_ref,
    z_ref, mixed_ref, hat1_ref, hat2_ref, mid_ref, bank1, bank2,
    vecs, lines, up_all, decay_all, second_all, third_all, pre1, act1, pre2, act2,
    normed_out, f_in, f_out, f_up, f_down,
    pack, packed, packs, thirds, in_v, normed_v,
    small_send, small_recv, own_sem, ysend, yrecv, xsend, xrecv, csend, crecv, dsend, drecv,
):
    tick = pl.program_id(0)
    place = Place()
    shard, quad = place.shard, place.quad
    locals_ = (w_in, w_out, w_up, w_down)
    fulls = (in_v, f_out, f_up, f_down)

    def rows_of(unit, shard_of, quad_of):
        weight, start, size = unit
        half = locals_[weight].shape[0]
        return pl.ds(pl.multiple_of(shard_of * half + quad_of * (half // 4) + start, 16), size)

    def local_rows(unit):
        weight, start, size = unit
        quarter = locals_[weight].shape[0] // 4
        return pl.ds(pl.multiple_of(quad * quarter + start, 16), size)

    def column_pairs(weight):
        if weight:
            width = locals_[weight].shape[1]
            return [(slice(0, width), slice(0, width))]
        return [(part(p * STEPS + t), part(t * 3 + p)) for t in range(STEPS) for p in range(3)]

    def smalls():
        return [
            remote(packed, packs.at[shard], small_send.at[0], small_recv.at[0], place.other_shard()),
            remote(third, thirds.at[shard], small_send.at[1], small_recv.at[1], place.other_shard()),
        ]

    def own_copies():
        copies = []
        for weight in range(1, 4):
            half = locals_[weight].shape[0]
            rows = pl.ds(pl.multiple_of(shard * half, 16), half)
            copies.append(pltpu.make_async_copy(locals_[weight], fulls[weight].at[rows, :], own_sem.at[weight]))
        return copies

    def normed_copy():
        return pltpu.make_async_copy(normed_v, normed_out, own_sem.at[0])

    def in_copy():
        return pltpu.make_async_copy(in_v, f_in, own_sem.at[4])

    def moved(u, quad_of, sems, device):
        unit = UNITS[u]
        region = fulls[unit[0]].at[rows_of(unit, 1 - shard, quad_of), :]
        return remote(region, region, sems[0].at[u], sems[1].at[u], device)

    other_quad = quad + 2 - 4 * (quad // 2)

    def arrivals(u):
        moved(u, quad, (ysend, yrecv), place.other_shard()).wait_recv()
        moved(u, quad, (xsend, xrecv), place.other_side()).start()
        moved(u, quad, (csend, crecv), place.other_core()).start()

    def second(u):
        moved(u, other_quad, (xsend, xrecv), place.other_side()).wait_recv()
        moved(u, other_quad, (dsend, drecv), place.other_core()).start()

    def finish(u):
        moved(u, quad, (csend, crecv), place.other_core()).wait()
        moved(u, quad, (dsend, drecv), place.other_core()).wait()
        moved(u, quad, (xsend, xrecv), place.other_side()).wait_send()
        moved(u, quad, (ysend, yrecv), place.other_shard()).wait_send()

    def exchanges(index):
        waiting = list(SECONDS[index])
        for u in ARRIVALS[index]:
            arrivals(u)
            if waiting and waiting[0] < u:
                second(waiting.pop(0))
        for u in waiting:
            second(u)

    @pl.when(tick == 0)
    def _():
        greet([place.other_shard(), place.other_side(), place.other_core()])
        pack[...] = jnp.zeros_like(pack)
        half = D // 2

        def row(ref):
            return ref[...].astype(f32).reshape(1, ref.shape[0])

        for i, ref in enumerate((gain1, shift1, out_b, gain2, shift2, down_b)):
            pack[i : i + 1, :] = row(ref)
        pack[6:8, :] = long_b[...].astype(f32)
        taps = short_w[...].astype(f32)
        for i, value in enumerate((row(in_shift), row(short_b), taps[0:1], taps[1:2], taps[2:3])):
            for a in range(3):
                pack[8 + 3 * i + a : 9 + 3 * i + a, :] = value[:, a * half : (a + 1) * half]
        value = row(up_b)
        for a in range(4):
            pack[UP_ROW + a : UP_ROW + a + 1, :] = value[:, a * half : (a + 1) * half]
        value = row(decay)
        for a in range(2):
            pack[DECAY_ROW + a : DECAY_ROW + a + 1, :] = value[:, a * half : (a + 1) * half]
        wide = w1.shape[1]
        n1, n2 = w1.shape[0], w2.shape[0]
        pack[FIRST_ROW : FIRST_ROW + n1, 0:wide] = w1[...].astype(f32)
        pack[FIRST_ROW + n1 : FIRST_ROW + n1 + 1, 0:wide] = row(b1)
        pack[FIRST_ROW + n1 + 1 : FIRST_ROW + n1 + 2, 0:wide] = row(b2)
        pack[SECOND_ROW : SECOND_ROW + n2, 128 : 128 + wide] = w2[...].astype(f32)
        packed[...] = pack[...].astype(bf16)
        for one in smalls():
            one.start()
        for u, unit in enumerate(UNITS):
            weight = unit[0]
            for src, dst in column_pairs(weight):
                remote(
                    locals_[weight].at[local_rows(unit), src],
                    fulls[weight].at[rows_of(unit, shard, quad), dst],
                    ysend.at[u], yrecv.at[u], place.other_shard(),
                ).start()
        for one in own_copies():
            one.start()
        rows = pl.ds(pl.multiple_of(shard * (D // 2), 16), D // 2)
        for src, dst in column_pairs(0):
            in_v[rows, dst] = w_in[:, src]
        packs[shard] = packed[...]
        thirds[shard] = third[...]
        for one in smalls():
            one.wait()

        both = [packs[s].astype(f32) for s in range(2)]
        for i in range(8):
            for s in range(2):
                vecs[i : i + 1, s * half : (s + 1) * half] = both[s][i : i + 1]
        lines[...] = jnp.zeros_like(lines)
        for s, a, b, to in column_moves():
            for i, line in enumerate((4, 3, 0, 1, 2)):
                at = 8 + 3 * i + a
                lines[line : line + 1, to : to + 128] = both[s][at : at + 1, b : b + 128]
        for s in range(2):
            for a in range(4):
                to = s * (2 * D) + a * half
                up_all[0:1, to : to + half] = both[s][UP_ROW + a : UP_ROW + a + 1]
            for a in range(2):
                to = s * D + a * half
                decay_all[0:1, to : to + half] = both[s][DECAY_ROW + a : DECAY_ROW + a + 1]
            third_all[:, s * D : (s + 1) * D] = thirds[s].astype(f32)

        def narrow(rows, cols):
            return jnp.concatenate([both[s][rows, cols] for s in range(2)], axis=1)

        first_w = narrow(slice(FIRST_ROW, FIRST_ROW + n1), slice(0, wide))
        first_b = narrow(slice(FIRST_ROW + n1, FIRST_ROW + n1 + 1), slice(0, wide))
        second_b = narrow(slice(FIRST_ROW + n1 + 1, FIRST_ROW + n1 + 2), slice(0, wide))
        second_w = narrow(slice(SECOND_ROW, SECOND_ROW + n2), slice(128, 128 + wide))
        second_all[...] = second_w
        straight = ((1,), (0,))
        pre1[...] = exact(embed_ref[...], first_w, straight) + first_b
        act1[...] = jnp.sin(pre1[...])
        pre2[...] = exact(act1[...], second_w, straight) + second_b
        act2[...] = jnp.sin(pre2[...])

        def norm_rows(i, carry):
            rows = pl.ds(pl.multiple_of(i * 128, 128), 128)
            values = tokens[rows, :].astype(f32)
            normed_v[rows, :] = layer_norm(values, vecs[0:1, :], vecs[1:2, :]).astype(bf16)
            return carry

        lax.fori_loop(0, tokens.shape[0] // 128, norm_rows, 0)
        normed_copy().start()
        exchanges(0)
        for u in range(3):
            finish(u)
        in_copy().start()

    for index in range(1, 2 * STEPS + 1):
        @pl.when(tick == index + 1)
        def _():
            exchanges(index)

    @pl.when(tick > 0)
    def _():
        step = jnp.maximum(tick - 1, 0)
        tile = step // 2
        micro = step % 2
        cols = pl.ds(pl.multiple_of(tile * 3 * TILE, 3 * TILE), 3 * TILE)
        few = pl.ds(pl.multiple_of(tile * TILE, TILE), TILE)
        rows = pl.ds(pl.multiple_of(micro * SPAN, SPAN), SPAN)

        @pl.when(tick <= 2 * STEPS)
        def _():
            @pl.when(micro == 0)
            def _():
                for q, bank in enumerate((bank1, bank2)):
                    those = pl.ds(pl.multiple_of(q * D + tile * TILE, TILE), TILE)
                    window = jnp.exp(-ratio_ref[...] * decay_all[:, those])
                    taps = exact(act2[...], third_all[:, those], ((1,), (0,))) * window
                    make_bank(ahead_ref[...], taps, bank)

            z_ref[...] = lowmul(normed_v[rows, :], in_v[:, cols]) + lines[4:5, cols]
            forward_step(
                z_ref, lines.at[:, cols], vecs.at[:, few], ahead_ref, back_ref,
                mixed_ref, hat1_ref, hat2_ref, mid_ref, bank1, bank2,
            )

    @pl.when(tick == 2 * STEPS + 1)
    def _():
        for u in range(3, len(UNITS)):
            finish(u)
        normed_copy().wait()
        in_copy().wait()
        for one in own_copies():
            one.wait()


def embed_table():
    ratio = place_ratio()
    angles = 2.0 * math.pi * ratio * (np.arange(BANDS) + 1).astype(np.float32)[None, :]
    return np.concatenate([ratio, np.cos(angles), np.sin(angles)], axis=1).astype(np.float32)


def gather_weights(*values):
    w1, w2, w3 = values[6], values[8], values[10]
    weights = values[17:21]
    tokens = values[21]
    count = tokens.shape[0]
    hidden = w2.shape[0]
    vmem = lambda one: pl.BlockSpec(one.shape, lambda t: (0,) * one.ndim, pipeline_mode=pl.Buffered(1))
    hbm = pl.BlockSpec(memory_space=pl.ANY)
    units = len(UNITS)
    embed, ratio = jnp.asarray(embed_table()), jnp.asarray(place_ratio())
    inputs = (*values, embed, ratio, *constants())

    def at_tile(shape, where):
        def index(t):
            step = jnp.minimum(jnp.maximum(t - 1, 0), 2 * STEPS - 1)
            return where(step % 2, step // 2)

        return pl.BlockSpec(shape, index)

    def doubled(value):
        return jax.ShapeDtypeStruct((2 * value.shape[0], *value.shape[1:]), value.dtype)

    def shape(*dims, kind=f32):
        return jax.ShapeDtypeStruct(dims, kind)

    fixed = [
        shape(8, D), shape(8, D3), shape(1, weights[2].shape[1]), shape(1, 2 * w3.shape[1]), shape(hidden, hidden),
        shape(hidden, 2 * w3.shape[1]),
    ] + [shape(SEQ, hidden)] * 4
    blocks = count // BLOCK
    hat_spec = at_tile((4, FREQ, TILE), lambda m, t: (m, 0, t))
    row_spec = at_tile((SPAN, TILE), lambda m, t: (m, t))
    bank_spec = at_tile((3, FREQ, TILE), lambda m, t: (0, 0, t))
    return pl.pallas_call(
        gather_kernel,
        grid=(2 * STEPS + 2,),
        in_specs=[vmem(one) for one in inputs],
        out_specs=[
            at_tile((SPAN, 3 * TILE), lambda m, t: (m, t)), row_spec, hat_spec, hat_spec, row_spec, bank_spec,
            bank_spec,
        ]
        + [vmem(one) for one in fixed] + [hbm] * 5,
        out_shape=[
            shape(count, D3), shape(count, D, kind=bf16), shape(blocks, FREQ, D), shape(blocks, FREQ, D),
            shape(count, D), shape(3, FREQ, D), shape(3, FREQ, D),
        ]
        + fixed + [shape(count, D, kind=bf16)] + [doubled(one) for one in weights],
        scratch_shapes=[
            pltpu.VMEM((PACK_ROWS, D // 2), f32),
            pltpu.VMEM((PACK_ROWS, D // 2), bf16),
            pltpu.VMEM((2, PACK_ROWS, D // 2), bf16),
            pltpu.VMEM((2, *w3.shape), bf16),
            pltpu.VMEM((D, D3), bf16),
            pltpu.VMEM((count, D), bf16),
        ]
        + [pltpu.SemaphoreType.DMA((2,))] * 2
        + [pltpu.SemaphoreType.DMA((5,))]
        + [pltpu.SemaphoreType.DMA((units,))] * 8,
        compiler_params=pltpu.CompilerParams(
            collective_id=0, has_side_effects=True, vmem_limit_bytes=56 * 2**20
        ),
        name="gather_weights",
    )(*inputs)


class Reduction:
    def __init__(self, place, first, count, rows, bufs, sems, out):
        self.place = place
        self.first = first
        self.count = count
        self.rows = rows
        self.dtype = bufs[0].dtype
        self.whole, self.from_core, self.half, self.from_shard, self.own, self.from_side, self.mine, self.from_depth, self.back = bufs
        (self.s_core, self.r_core, self.s_shard, self.r_shard, self.s_side, self.r_side, self.s_depth, self.r_depth,
         self.s_gd, self.r_gd, self.s_gs, self.r_gs, self.s_gc, self.r_gc, self.s_own) = sems
        self.out = out

    def when(self, tick, lag, body):
        k = tick - self.first - lag

        @pl.when((k >= 0) & (k < self.count))
        def _():
            body(k, k % 2)

    def slot(self, ref, k):
        return ref.at[k % ref.shape[0]]

    def rows_at(self, index, size):
        return pl.ds(pl.multiple_of(index * size, size), size)

    def core_copy(self, k, slot):
        p = self.place
        return remote(
            self.whole.at[slot, :, self.rows_at(1 - p.core, self.rows // 2), :],
            self.slot(self.from_core, k), self.s_core.at[k], self.r_core.at[k], p.other_core(),
        )

    def shard_copy(self, k, slot):
        p = self.place
        return remote(
            self.half.at[slot, 1 - p.shard], self.slot(self.from_shard, k), self.s_shard.at[k], self.r_shard.at[k],
            p.other_shard(),
        )

    def side_copy(self, k, slot):
        p = self.place
        return remote(
            self.own.at[slot, self.rows_at(1 - p.side, self.rows // 4), :],
            self.slot(self.from_side, k), self.s_side.at[k], self.r_side.at[k], p.other_side(),
        )

    def quarter(self, base, index):
        rows = self.rows // 8
        return (
            pl.ds(pl.multiple_of(base + (index // 2) * rows, rows), rows),
            pl.ds(pl.multiple_of((index % 2) * (D // 2), D // 2), D // 2),
        )

    def depth_copy(self, k, slot, step):
        p = self.place
        rows, cols = self.quarter(0, (p.depth + step) % 4)
        return remote(
            self.mine.at[slot, rows, cols], self.from_depth.at[k % self.from_depth.shape[0], step - 1],
            self.s_depth.at[k, step - 1], self.r_depth.at[k, step - 1], p.other_depth(step),
        )

    def depth_back(self, k, step):
        p = self.place
        rows, cols = self.quarter(p.side * (self.rows // 4), p.depth)
        region = self.back.at[k % self.back.shape[0], rows, cols]
        return remote(
            region, region, self.s_gd.at[k, step - 1], self.r_gd.at[k, step - 1], p.other_depth(step)
        )

    def side_back(self, k):
        p = self.place
        region = self.back.at[k % self.back.shape[0], self.rows_at(p.side, self.rows // 4), :]
        return remote(region, region, self.s_gs.at[k], self.r_gs.at[k], p.other_side())

    def homes(self, k, place_in):
        rows = pl.ds(pl.multiple_of(self.place.core * (self.rows // 2), self.rows // 2), self.rows // 2)
        return [(cols, ref.at[(*lead, rows, *tail)]) for cols, ref, lead, tail in place_in]

    def send_home(self, k, place_in):
        p = self.place
        for cols, region in self.homes(k, place_in):
            piece = self.back.at[k % self.back.shape[0], :, cols]
            remote(piece, region, self.s_gc.at[k], self.r_gc.at[k], p.other_core()).start()
            pltpu.make_async_copy(piece, region, self.s_own.at[k]).start()

    def wait_home(self, k):
        whole = self.slot(self.back, k)
        remote(whole, whole, self.s_gc.at[k], self.r_gc.at[k], self.place.other_core()).wait()
        pltpu.make_async_copy(whole, whole, self.s_own.at[k]).wait()

    def add(self, left, right):
        return (left.astype(f32) + right.astype(f32)).astype(self.dtype)

    def send(self, tick):
        self.when(tick, 0, lambda k, slot: self.core_copy(k, slot).start())

    def advance(self, tick):
        p = self.place

        def after_core(k, slot):
            self.core_copy(k, slot).wait()
            for s in range(2):
                self.half[slot, s] = self.add(
                    self.whole[slot, s, self.rows_at(p.core, self.rows // 2), :], self.from_core[k % self.from_core.shape[0], s]
                )
            self.shard_copy(k, slot).start()

        def after_shard(k, slot):
            self.shard_copy(k, slot).wait()
            self.own[slot] = self.add(self.half[slot, p.shard], self.from_shard[k % self.from_shard.shape[0]])
            self.side_copy(k, slot).start()

        def after_side(k, slot):
            self.side_copy(k, slot).wait()
            self.mine[slot] = self.add(
                self.own[slot, self.rows_at(p.side, self.rows // 4), :], self.from_side[k % self.from_side.shape[0]]
            )
            for step in range(1, 4):
                self.depth_copy(k, slot, step).start()

        def after_depth(k, slot):
            for step in range(1, 4):
                self.depth_copy(k, slot, step).wait()
            rows, cols = self.quarter(0, p.depth)
            total = self.mine[slot, rows, cols].astype(f32)
            for step in range(3):
                total = total + self.from_depth[k % self.from_depth.shape[0], step].astype(f32)
            rows, cols = self.quarter(p.side * (self.rows // 4), p.depth)
            self.back[k % self.back.shape[0], rows, cols] = total.astype(self.dtype)
            for step in range(1, 4):
                self.depth_back(k, step).start()

        def after_depth_back(k, slot):
            for step in range(1, 4):
                self.depth_back(k, step).wait()
            self.side_back(k).start()

        def after_side_back(k, slot):
            self.side_back(k).wait()
            self.out(self, k)

        def after_core_back(k, slot):
            self.wait_home(k)

        for lag, body in enumerate(
            (after_core, after_shard, after_side, after_depth, after_depth_back, after_side_back, after_core_back), 1
        ):
            self.when(tick, lag, body)


LAGS = 7
DOWN, UP, OUT, IN = 4, 4, 1, STEPS
CHUNKS = DOWN + UP + OUT + IN
SMALL_ROWS = 128
SMALL_TICK = 9
ROW_BLOCK = 128


GIVEN_ROW, TAP_ROW, LONG_ROW, NORM_ROW = 64, 72, 96, 98


def exact(left, right, dims):
    return lax.dot_general(left, right, (dims, ((), ())), precision=HIGH, preferred_element_type=f32)


def reduce_kernel(
    given, active0, active1, upstream, second, d_hidden, mixed, d_middle, normed, tokens, gain,
    grad_ref, z_ref, rows_ref, long_ref, bank1, bank2, hat1_ref, hat2_ref, mid_ref, ahead_ref, back_ref,
    in_ref, decay_ref, decay2_ref, third1_ref, third2_ref, ratio_ref, embed_ref, pre1_ref, act1_ref, pre2_ref, act2_ref,
    second_w_ref,
    small_out, g_down, g_up, g_out, g_in, tokens_out,
    d_proj, dtap, dtaps, dlong, dlongs, dfilt1, dfilt2, dbank1, dbank2, d_normed, d_act, out_rows, out_sem, *scratch,
):
    tick = pl.program_id(0)
    place = Place()
    bufs, sems = scratch[:9], scratch[9:24]
    small_bufs, small_sems = scratch[24:33], scratch[33:48]
    everything = slice(None)
    is_in = (tick % 3 == 2) & (tick < 9)
    tile = tick // 3

    def little_home(chain, k):
        chain.send_home(k, [(everything, small_out, (k,), (everything,))])

    def kinds(k):
        down = (k < 5) & (k % 3 < 2)
        up = ((k >= 6) & (k < 8)) | (k >= 10)
        return down, up, k == 9, (k < 9) & (k % 3 == 2)

    def big_home(chain, k):
        down, up, out, inward = kinds(k)

        @pl.when(down)
        def _():
            chain.send_home(k, [(everything, g_down, (k - k // 3,), (everything,))])

        @pl.when(up)
        def _():
            index = k - 6 - 2 * (k // 9)
            cols = pl.ds(pl.multiple_of(index * D, D), D)
            chain.send_home(k, [(everything, g_up, (), (cols,))])

        @pl.when(out)
        def _():
            chain.send_home(k, [(everything, g_out, (), (everything,))])

        @pl.when(inward)
        def _():
            chain.send_home(
                k,
                [
                    (part(p), g_in, (), (pl.ds(pl.multiple_of(p * D + (k // 3) * TILE, TILE), TILE),))
                    for p in range(3)
                ],
            )

    little = Reduction(place, SMALL_TICK, 1, SMALL_ROWS, small_bufs, small_sems, little_home)
    big = Reduction(place, 0, CHUNKS, D // 2, bufs, sems, big_home)
    pack = little.whole

    @pl.when(tick == 0)
    def _():
        greet(
            [place.other_shard(), place.other_side(), place.other_core()]
            + [place.other_depth(step) for step in range(1, 4)]
        )
        pack[...] = jnp.zeros_like(pack)
        pack[0, :, GIVEN_ROW : GIVEN_ROW + 8, D // 2 :] = given[...]
        d_act[...] = jnp.zeros_like(d_act)

    little.advance(tick)
    big.advance(tick)

    def chunk(slot, lefts, right):
        for s in range(2):
            big.whole[slot, s] = inner_rows(lefts[s], right).astype(bf16)

    def halves(left):
        return left[:, : D // 2], left[:, D // 2 :]

    def compute(k, slot):
        down, up, out, inward = kinds(k)

        @pl.when(down)
        def _():
            chunk(slot, (active0[...], active1[...]), upstream[...])

        @pl.when(up)
        def _():
            chunk(slot, halves(second), d_hidden[...])

        @pl.when(out)
        def _():
            chunk(slot, halves(mixed), d_middle[...].astype(bf16))

        @pl.when(inward)
        def _():
            chunk(slot, halves(normed), d_proj[...])

    big.when(tick, 0, compute)
    big.send(tick)

    @pl.when((tick < 8) & (tick % 3 < 2))
    def _():
        micro = tick % 3
        backward_step(
            micro == 0, micro == 1, grad_ref, z_ref, rows_ref, long_ref, bank1, bank2,
            hat1_ref, hat2_ref, mid_ref, ahead_ref, back_ref,
            d_proj.at[pl.ds(pl.multiple_of(micro * SPAN, SPAN), SPAN), :], dtap, dlong, dfilt1, dfilt2, dbank1, dbank2,
        )

    @pl.when(is_in)
    def _():
        cols = pl.ds(pl.multiple_of(tile * TILE, TILE), TILE)
        dtaps[tile] = dtap[...]
        dlongs[:, cols] = dlong[...]
        step = times_t(d_proj[...], in_ref[...])

        @pl.when(tile == 0)
        def _():
            d_normed[...] = step

        @pl.when(tile > 0)
        def _():
            d_normed[...] += step

        for q, (grads, decay, third) in enumerate(
            ((dfilt1, decay_ref, third1_ref), (dfilt2, decay2_ref, third2_ref))
        ):
            window = jnp.exp(-ratio_ref[...] * decay[...])
            d_taps = grads[...] * window
            pack[0, q, 0 : act2_ref.shape[1], cols] = exact(act2_ref[...], d_taps, ((0,), (0,)))
            d_act[...] += exact(d_taps, third[...], ((1,), (1,)))

    @pl.when(tick == SMALL_TICK)
    def _():
        for s in range(2):
            for a in range(3):
                for b in range(3):
                    at = s * (D3 // 2) + a * (D // 2) + b * 128
                    p, t, o = at // D, at % D // TILE, at % TILE
                    pack[0, s, TAP_ROW + 8 * a : TAP_ROW + 8 * a + 8, D // 2 + b * 128 : D // 2 + b * 128 + 128] = dtaps[
                        t, :, p * TILE + o : p * TILE + o + 128
                    ]
            pack[0, s, LONG_ROW : LONG_ROW + 2, D // 2 :] = dlongs[:, s * (D // 2) : (s + 1) * (D // 2)]

        def norm_rows(i, sums):
            rows = pl.ds(pl.multiple_of(i * ROW_BLOCK, ROW_BLOCK), ROW_BLOCK)
            values = tokens[rows, :].astype(f32)
            grads = d_normed[rows, :]
            center = values - jnp.mean(values, axis=-1, keepdims=True)
            scale = lax.rsqrt(jnp.mean(center * center, axis=-1, keepdims=True) + EPS)
            unit = center * scale
            scaled = grads * gain[0:1, :]
            inner = scaled - jnp.mean(scaled, axis=-1, keepdims=True)
            inner = inner - unit * jnp.mean(scaled * unit, axis=-1, keepdims=True)
            out_rows[rows, :] = (scale * inner + d_middle[rows, :]).astype(bf16)
            return (
                sums[0] + jnp.sum(grads * unit, axis=0, keepdims=True),
                sums[1] + jnp.sum(grads, axis=0, keepdims=True),
            )

        zero = jnp.zeros((1, D), f32)
        sums = lax.fori_loop(0, tokens.shape[0] // ROW_BLOCK, norm_rows, (zero, zero))
        d_pre2 = d_act[...] * jnp.cos(pre2_ref[...])
        g_second = exact(act1_ref[...], d_pre2, ((0,), (0,)))
        g_b2 = jnp.sum(d_pre2, axis=0, keepdims=True)
        d_pre1 = exact(d_pre2, second_w_ref[...], ((1,), (1,))) * jnp.cos(pre1_ref[...])
        g_first = exact(embed_ref[...], d_pre1, ((0,), (0,)))
        g_b1 = jnp.sum(d_pre1, axis=0, keepdims=True)
        wide = g_second.shape[1] // 2
        for s in range(2):
            own = slice(s * wide, (s + 1) * wide)
            for i in range(2):
                pack[0, s, NORM_ROW + i : NORM_ROW + i + 1, D // 2 :] = sums[i][:, s * (D // 2) : (s + 1) * (D // 2)]
            pack[0, s, 64 : 64 + g_first.shape[0], 0:wide] = g_first[:, own]
            pack[0, s, 64 + g_first.shape[0] : 65 + g_first.shape[0], 0:wide] = g_b1[:, own]
            pack[0, s, 65 + g_first.shape[0] : 66 + g_first.shape[0], 0:wide] = g_b2[:, own]
            pack[0, s, 64 : 64 + g_second.shape[0], 128 : 128 + wide] = g_second[:, own]
        pltpu.make_async_copy(out_rows, tokens_out, out_sem).start()

    little.send(tick)

    @pl.when(tick == SMALL_TICK + 2)
    def _():
        pltpu.make_async_copy(out_rows, tokens_out, out_sem).wait()


def reduce_grads(
    given, active, upstream, second, d_hidden, mixed, d_middle, normed, tokens,
    d_mixed, z, lines, vecs, bank1, bank2, hat1, hat2, mid, in_full, decay, third_w, states, second_w,
):
    count = upstream.shape[0]
    half = D // 2
    hidden = second_w.shape[0]
    embed, pre1, act1, pre2, act2 = states

    def fixed(shape):
        return pl.BlockSpec(shape, lambda t: (0,) * len(shape), pipeline_mode=pl.Buffered(1))

    def at_tile(shape, where):
        def index(t):
            tick = jnp.minimum(t, 8)
            return where(jnp.minimum(tick % 3, 1), tick // 3)

        return pl.BlockSpec(shape, index)

    def down_index(t):
        tick = jnp.minimum(t, 4)
        return tick - tick // 3

    def up_index(t):
        return jnp.minimum(jnp.maximum(t - 6, 0), 2) + jnp.minimum(jnp.maximum(t - 10, 0), 1)

    hat_spec = at_tile((4, FREQ, TILE), lambda m, t: (m, 0, t))
    row_spec = at_tile((SPAN, TILE), lambda m, t: (m, t))
    bank_spec = at_tile((3, FREQ, TILE), lambda m, t: (0, 0, t))
    decay_shape = (1, TILE)

    def buffers(n, rows, kind):
        few, many = min(n, 4), min(n, 8)
        return [
            pltpu.VMEM((min(n, 2), 2, rows, D), kind),
            pltpu.VMEM((few, 2, rows // 2, D), kind),
            pltpu.VMEM((min(n, 2), 2, rows // 2, D), kind),
            pltpu.VMEM((few, rows // 2, D), kind),
            pltpu.VMEM((min(n, 2), rows // 2, D), kind),
            pltpu.VMEM((few, rows // 4, D), kind),
            pltpu.VMEM((min(n, 2), rows // 4, D), kind),
            pltpu.VMEM((few, 3, rows // 8, D // 2), kind),
            pltpu.VMEM((many, rows // 2, D), kind),
        ]

    def semaphores(n):
        one = pltpu.SemaphoreType.DMA((n,))
        three = pltpu.SemaphoreType.DMA((n, 3))
        return [one] * 6 + [three] * 4 + [one] * 5

    return pl.pallas_call(
        reduce_kernel,
        grid=(CHUNKS + LAGS,),
        in_specs=[
            fixed((2, 8, half)),
            pl.BlockSpec((count, half), lambda t: (0, down_index(t))),
            pl.BlockSpec((count, half), lambda t: (0, DOWN + down_index(t))),
            fixed((count, D)),
            fixed((count, D)),
            pl.BlockSpec((count, D), lambda t: (0, up_index(t))),
            fixed((count, D)),
            fixed((count, D)),
            fixed((count, D)),
            fixed((count, D)),
            fixed((8, D)),
            row_spec,
            at_tile((SPAN, 3 * TILE), lambda m, t: (m, t)),
            at_tile((8, 3 * TILE), lambda m, t: (0, t)),
            at_tile((8, TILE), lambda m, t: (0, t)),
            bank_spec, bank_spec, hat_spec, hat_spec, row_spec,
            fixed(AHEAD),
            fixed(BACK),
            at_tile((D, 3 * TILE), lambda m, t: (0, t)),
            at_tile(decay_shape, lambda m, t: (0, t)),
            at_tile(decay_shape, lambda m, t: (0, STEPS + t)),
            at_tile((hidden, TILE), lambda m, t: (0, t)),
            at_tile((hidden, TILE), lambda m, t: (0, STEPS + t)),
            fixed((SEQ, 1)),
            fixed(embed.shape),
            fixed(pre1.shape),
            fixed(act1.shape),
            fixed(pre2.shape),
            fixed(act2.shape),
            fixed(second_w.shape),
        ],
        out_specs=[pl.BlockSpec(memory_space=pl.ANY)] * 6,
        out_shape=[
            jax.ShapeDtypeStruct((1, SMALL_ROWS, D), f32),
            jax.ShapeDtypeStruct((DOWN, half, D), bf16),
            jax.ShapeDtypeStruct((half, UP * D), bf16),
            jax.ShapeDtypeStruct((half, D), bf16),
            jax.ShapeDtypeStruct((half, D3), bf16),
            jax.ShapeDtypeStruct((count, D), bf16),
        ],
        scratch_shapes=[
            pltpu.VMEM((count, 3 * TILE), bf16),
            pltpu.VMEM((8, 3 * TILE), f32),
            pltpu.VMEM((STEPS, 8, 3 * TILE), f32),
            pltpu.VMEM((2, TILE), f32),
            pltpu.VMEM((2, D), f32),
            pltpu.VMEM((SEQ, TILE), f32),
            pltpu.VMEM((SEQ, TILE), f32),
            pltpu.VMEM((3, FREQ, TILE), f32),
            pltpu.VMEM((3, FREQ, TILE), f32),
            pltpu.VMEM((count, D), f32),
            pltpu.VMEM((SEQ, hidden), f32),
            pltpu.VMEM((count, D), bf16),
            pltpu.SemaphoreType.DMA(()),
        ]
        + buffers(CHUNKS, half, bf16) + semaphores(CHUNKS) + buffers(1, SMALL_ROWS, f32) + semaphores(1),
        compiler_params=pltpu.CompilerParams(
            collective_id=1, has_side_effects=True, vmem_limit_bytes=63 * 2**20
        ),
        name="reduce_grads",
    )(
        given, active, active, upstream, second, d_hidden, mixed, d_middle, normed, tokens, vecs,
        d_mixed, z, lines, vecs, bank1, bank2, hat1, hat2, mid, *constants(), in_full,
        decay, decay, third_w, third_w, jnp.asarray(place_ratio()), embed, pre1, act1, pre2, act2, second_w,
    )


def per_device(
    prompt_x, cont_x, prompt_cot, cont_cot, norm1_gain, norm1_bias, in_weight, in_bias, short_weight,
    short_bias, long_bias, filter_w1, filter_b1, filter_w2, filter_b2, filter_w3, filter_decay, out_weight,
    out_bias, norm2_gain, norm2_bias, up_weight, up_bias, down_weight, down_bias, *, reps, shards,
):
    own_kernels = reps == 16 and shards == 2
    micros = prompt_x.shape[0]
    groups = prompt_x.shape[1]
    count = micros * groups * SPAN

    def tokens_of(prompt, cont):
        return jnp.concatenate(
            [
                prompt.reshape(micros * groups, PROMPT, D),
                cont.reshape(micros * groups, CONTS * BLOCK, D),
            ],
            axis=1,
        ).reshape(count, D)

    def parts_of(rows):
        rows = rows.reshape(micros, groups, SPAN, D)
        return rows[:, :, :PROMPT], rows[:, :, PROMPT:].reshape(micros, groups, CONTS, BLOCK, D)

    n1 = filter_w1.shape[0]
    n2 = filter_w2.shape[0]
    tokens_low = tokens_of(prompt_x, cont_x)
    tokens = tokens_low.astype(f32)
    upstream = tokens_of(prompt_cot, cont_cot)
    upstream_f = upstream.astype(f32)
    if own_kernels:
        (projected, mixed_low, hat1, hat2, mid, bank1, bank2, vecs, lines, up_shift, decay, fw2, fw3,
         pre1, act1, pre2, act2, normed_low, in_full, out_full, up_full, down_full) = gather_weights(
            norm1_gain, norm1_bias, in_bias, short_weight, short_bias, long_bias, filter_w1, filter_b1, filter_w2,
            filter_b2, filter_w3, filter_decay, out_bias, norm2_gain, norm2_bias, up_bias, down_bias,
            in_weight, out_weight, up_weight, down_weight, tokens_low,
        )
        states = (jnp.asarray(embed_table()), pre1, act1, pre2, act2)
        out_shift, gain2, shift2, down_shift = vecs[2], vecs[3], vecs[4], vecs[5]
        up_shift = up_shift[0]
    else:
        def gather(value, axis=0):
            return lax.all_gather(value, "shard", axis=axis, tiled=True)

        gain1, shift1, out_shift, gain2, shift2, down_shift, in_shift, short_shift, up_shift, decay, fb1, fb2 = (
            gather(one).astype(f32)
            for one in (norm1_gain, norm1_bias, out_bias, norm2_gain, norm2_bias, down_bias, in_bias, short_bias,
                        up_bias, filter_decay, filter_b1, filter_b2)
        )
        taps, long_shift, fw1, fw2, fw3 = (
            gather(one, 1).astype(f32) for one in (short_weight, long_bias, filter_w1, filter_w2, filter_w3)
        )
        in_full, out_full, up_full, down_full = (
            gather(one) for one in (by_tile(in_weight), out_weight, up_weight, down_weight)
        )
        lines = by_tile(jnp.concatenate([taps, short_shift[None], in_shift[None], jnp.zeros((3, D3), f32)], axis=0))
        vecs = jnp.concatenate([jnp.zeros((6, D), f32), long_shift], axis=0)
        filters, filter_pull = jax.vjp(partial(filter_taps, decay=decay), fw1, fb1, fw2, fb2, fw3)
        normed, norm_pull = jax.vjp(layer_norm, tokens, gain1, shift1)
        normed_low = normed.astype(bf16)
        projected = lowmul(normed_low, in_full) + lines[4]
        mixed_low, hat1, hat2, mid, bank1, bank2 = run_forward(projected, lines, vecs, filters)
    middle = tokens + lowmul(mixed_low, out_full) + out_shift
    normed_two, norm_two_pull = jax.vjp(layer_norm, middle, gain2, shift2)
    second_low = normed_two.astype(bf16)
    hidden = lowmul(second_low, up_full) + up_shift
    active, gelu_pull = jax.vjp(partial(jax.nn.gelu, approximate=True), hidden)
    active_low = active.astype(bf16)
    result = (middle + lowmul(active_low, down_full) + down_shift).astype(bf16)
    prompt_out, cont_out = parts_of(result)

    d_active = times_t(upstream, down_full)
    d_hidden = gelu_pull(d_active)[0].astype(bf16)
    d_second = times_t(d_hidden, up_full)
    d_middle, grad_gain2, grad_shift2 = norm_two_pull(d_second)
    d_middle = d_middle + upstream_f
    d_branch = d_middle.astype(bf16)
    d_mixed = times_t(d_branch, out_full)
    width = D // shards

    def by_shard(value):
        rows = value.shape[0]
        return value.reshape(rows, shards, -1).swapaxes(0, 1).reshape(shards, -1, width)

    singles = jnp.stack(
        [jnp.sum(d_branch.astype(f32), axis=0), grad_gain2, grad_shift2, jnp.sum(upstream_f, axis=0)]
    )
    given = jnp.concatenate(
        [by_shard(singles), by_shard(jnp.sum(d_hidden.astype(f32), axis=0)[None])], axis=1
    )
    if own_kernels:
        small, grad_down, grad_up, grad_out, grad_in, d_tokens = reduce_grads(
            given, active_low, upstream, second_low, d_hidden, mixed_low, d_middle, normed_low,
            tokens_low, d_mixed, projected, lines, vecs, bank1, bank2, hat1, hat2, mid, in_full, decay, fw3, states, fw2,
        )
        prompt_grad, cont_grad = parts_of(d_tokens)
        small = small[0]
        half = small[:, width:]
        given = half[GIVEN_ROW : GIVEN_ROW + 8]
        tap_rows = half[TAP_ROW : TAP_ROW + 24].reshape(3, 8, width).swapaxes(0, 1)[:5].reshape(5, -1)
        long_rows = half[LONG_ROW : LONG_ROW + 2]
        norm_rows = half[NORM_ROW : NORM_ROW + 2]
        third_grad = small[: filter_w3.shape[0]]
        cols = filter_w1.shape[1]
        narrow_own = [
            small[64 : 64 + n1, :cols], small[64 + n1, :cols], small[64 : 64 + n2, 128 : 128 + cols],
            small[65 + n1, :cols],
        ]
        grad_down = grad_down.reshape(-1, D).astype(f32)
        grad_up, grad_out, grad_in = grad_up.astype(f32), grad_out.astype(f32), grad_in.astype(f32)
    else:
        def reduce(value, axis=0):
            value = lax.psum_scatter(value, "shard", scatter_dimension=axis, tiled=True)
            return lax.psum(value, "rep")

        d_proj, d_taps, d_long, d_filter1, d_filter2 = run_backward(
            d_mixed, projected, lines, vecs, bank1, bank2, hat1, hat2, mid
        )
        d_tokens, grad_gain1, grad_shift1 = norm_pull(times_t(d_proj, in_full))
        prompt_grad, cont_grad = parts_of((d_tokens + d_middle).astype(bf16))
        filter_grads_all = filter_pull(jnp.concatenate([d_filter1, d_filter2], axis=-1))
        narrow_own = [reduce(one, one.ndim - 1) for one in filter_grads_all[:4]]
        third_grad = reduce(filter_grads_all[4], 1)
        given = reduce(given)[0]
        tap_rows = reduce(by_part(d_taps[:5]), 1)
        long_rows = reduce(d_long, 1)
        norm_rows = reduce(jnp.stack([grad_gain1, grad_shift1]), 1)
        grad_down = reduce(inner_rows(active_low, upstream))
        grad_up = reduce(inner_rows(second_low, d_hidden))
        grad_out = reduce(inner_rows(mixed_low, d_branch))
        grad_in = by_part(reduce(inner_rows(normed_low, d_proj)))
    return (
        prompt_out,
        cont_out,
        prompt_grad,
        cont_grad,
        norm_rows[0],
        norm_rows[1],
        grad_in,
        tap_rows[4],
        tap_rows[:3],
        tap_rows[3],
        long_rows,
        *narrow_own,
        third_grad,
        grad_out,
        given[0],
        given[1],
        given[2],
        grad_up,
        given[4:].reshape(-1),
        grad_down,
        given[3],
    )


def solution(mesh):
    group4 = P(None, ("rep", "shard"), None, None)
    group5 = P(None, ("rep", "shard"), None, None, None)
    one, row, col = P("shard"), P("shard", None), P(None, "shard")
    grads = (one, one, row, one, col, one, col, col, one, col, one, col)
    rest = (row, one, one, one, row, one, row, one)
    return jax.shard_map(
        partial(per_device, reps=mesh.shape["rep"], shards=mesh.shape["shard"]),
        mesh=mesh,
        in_specs=(group4, group5, group4, group5) + grads + (one,) + rest,
        out_specs=(group4, group5, group4, group5) + grads + rest,
        check_vma=False,
    )
```

```python
from functools import partial
import math

import jax
import jax.numpy as jnp
import numpy as np
from jax import lax
from jax.experimental import pallas as pl
from jax.experimental.pallas import tpu as pltpu
from jax.sharding import PartitionSpec as P

D = 768
D3 = 3 * D
BANDS = 16
BLOCK = 128
PROMPT = 256
CONTS = 2
SEQ = 384
SPAN = PROMPT + CONTS * BLOCK
TILE = 256
FREQ = 2 * BLOCK

EPS = 1e-05
HIGH = lax.Precision.HIGHEST
f32 = jnp.float32
bf16 = jnp.bfloat16


def matmul(left_op, right_op):
    return jnp.dot(left_op, right_op, precision=HIGH, preferred_element_type=f32)


def lowmul(left_op, right_op):
    return jnp.dot(left_op, right_op, preferred_element_type=f32)


def inner_rows(left_op, right_op):
    return lax.dot_general(
        left_op, right_op, (((0,), (0,)), ((), ())), preferred_element_type=f32
    )


def times_t(left_op, right_op):
    return lax.dot_general(
        left_op, right_op, (((1,), (1,)), ((), ())), preferred_element_type=f32
    )


def layer_norm(values, norm_gain, norm_shift):
    center_val = values - jnp.mean(values, axis=-1, keepdims=True)
    spread = jnp.mean(center_val * center_val, axis=-1, keepdims=True)
    return center_val * lax.rsqrt(spread + EPS) * norm_gain + norm_shift


def dft_matrix():
    freq = np.arange(BLOCK)
    place = np.arange(BLOCK)
    angle = np.pi * ((2 * freq[:, None] + 1) * place[None, :] % (4 * BLOCK)) / FREQ
    return np.concatenate([np.cos(angle), -np.sin(angle)], axis=0)


def split3(matrix):
    matrix = matrix.astype(np.float32)
    high = matrix.astype(jnp.bfloat16)
    rest = (matrix - high.astype(np.float32)).astype(jnp.bfloat16)
    return np.concatenate([high, rest, high], axis=1)


def split_dot(triple, signal):
    high = signal.astype(bf16)
    rest = (signal - high.astype(f32)).astype(bf16)
    return jnp.dot(
        triple, jnp.concatenate([high, high, rest], axis=0), preferred_element_type=f32
    )


def cmul(left, right):
    lr, li = left[:BLOCK], left[BLOCK:]
    rr, ri = right[:BLOCK], right[BLOCK:]
    return jnp.concatenate([lr * rr - li * ri, lr * ri + li * rr], axis=0)


def cmul_conj(left, right):
    lr, li = left[:BLOCK], left[BLOCK:]
    rr, ri = right[:BLOCK], right[BLOCK:]
    return jnp.concatenate([lr * rr + li * ri, lr * ri - li * rr], axis=0)


def row_index():
    return lax.broadcasted_iota(jnp.int32, (BLOCK, TILE), 0)


def delayed(block, before, lag):
    rolled = pltpu.roll(block, lag, 0)
    if before is None:
        return jnp.where(row_index() >= lag, rolled, 0.0)
    return jnp.where(row_index() >= lag, rolled, pltpu.roll(before, lag, 0))


def advanced(block, after, lag):
    rolled = pltpu.roll(block, BLOCK - lag, 0)
    if after is None:
        return jnp.where(row_index() < BLOCK - lag, rolled, 0.0)
    return jnp.where(row_index() < BLOCK - lag, rolled, pltpu.roll(after, BLOCK - lag, 0))


BEFORE = (None, 0, 1, 1)


def part(index):
    return slice(index * TILE, (index + 1) * TILE)


def load_blocks(ref, cols=slice(None)):
    return [ref[i * BLOCK : (i + 1) * BLOCK, cols] for i in range(4)]


def short_blocks(z_ref, rows_ref, index):
    blocks = load_blocks(z_ref, part(index))
    taps = rows_ref[0:3, part(index)]
    shift = rows_ref[3:4, part(index)]
    outs = []
    for i in range(4):
        before = None if BEFORE[i] is None else blocks[BEFORE[i]]
        outs.append(
            taps[0:1] * blocks[i]
            + taps[1:2] * delayed(blocks[i], before, 1)
            + taps[2:3] * delayed(blocks[i], before, 2)
            + shift
        )
    return outs


def spectra(hats, bank):
    tail = cmul(bank[1], hats[1]) + cmul(bank[2], hats[0])
    return [
        cmul(bank[0], hats[0]),
        cmul(bank[0], hats[1]) + cmul(bank[1], hats[0]),
        cmul(bank[0], hats[2]) + tail,
        cmul(bank[0], hats[3]) + tail,
    ]


def adjoint_spectra(hats, bank):
    tail = hats[2] + hats[3]
    return [
        cmul_conj(bank[0], hats[0]) + cmul_conj(bank[1], hats[1]) + cmul_conj(bank[2], tail),
        cmul_conj(bank[0], hats[1]) + cmul_conj(bank[1], tail),
        cmul_conj(bank[0], hats[2]),
        cmul_conj(bank[0], hats[3]),
    ]


def bank_grads(hats, grads):
    tail = grads[2] + grads[3]
    zero = cmul_conj(hats[0], grads[0])
    for i in range(1, 4):
        zero = zero + cmul_conj(hats[i], grads[i])
    one = cmul_conj(hats[0], grads[1]) + cmul_conj(hats[1], tail)
    return [zero, one, cmul_conj(hats[0], tail)]


def signs():
    odd = lax.broadcasted_iota(jnp.int32, (BLOCK, TILE), 0) % 2
    return (1 - 2 * odd).astype(f32)


LONG1, LONG2 = slice(6, 7), slice(7, 8)


def make_bank(ahead, taps, bank_ref):
    hats = [split_dot(ahead, taps[o * BLOCK : (o + 1) * BLOCK, :] * (1.0 / BLOCK)) for o in range(3)]
    sign = signs()
    bank = [hats[0]]
    for o in (1, 2):
        prev = hats[o - 1]
        turned = jnp.concatenate([-sign * prev[BLOCK:], sign * prev[:BLOCK]], axis=0)
        bank.append(hats[o] + turned)
    for o in range(3):
        bank_ref[o] = bank[o]


def filter_grads(back, grads, out_ref):
    sign = signs()
    for o in range(3):
        one = grads[o]
        if o < 2:
            after = grads[o + 1]
            one = one + jnp.concatenate([sign * after[BLOCK:], -sign * after[:BLOCK]], axis=0)
        out_ref[o * BLOCK : (o + 1) * BLOCK, :] = split_dot(back, one) * (1.0 / BLOCK)


def mixer_forward(
    z_ref, rows_ref, long_ref, filter1, filter2, ahead_ref, back_ref,
    out_ref, hat1_ref, hat2_ref, mid_ref, bank1, bank2,
):
    @pl.when(pl.program_id(1) == 0)
    def _():
        make_bank(ahead_ref[...], filter1[...], bank1)
        make_bank(ahead_ref[...], filter2[...], bank2)

    forward_step(
        z_ref, rows_ref, long_ref, ahead_ref, back_ref, out_ref, hat1_ref, hat2_ref, mid_ref, bank1, bank2
    )


def forward_step(
    z_ref, rows_ref, long_ref, ahead_ref, back_ref, out_ref, hat1_ref, hat2_ref, mid_ref, bank1, bank2
):
    ahead = ahead_ref[...]
    back = back_ref[...]
    gate1 = short_blocks(z_ref, rows_ref, 1)
    value = short_blocks(z_ref, rows_ref, 2)
    sig1 = [gate1[i] * value[i] for i in range(4)]
    hats = []
    for i in range(4):
        hat = split_dot(ahead, sig1[i])
        hat1_ref[i] = hat
        hats.append(hat)
    wave = spectra(hats, [bank1[i] for i in range(3)])
    mid = []
    for i in range(4):
        one = split_dot(back, wave[i]) + long_ref[LONG1, :] * sig1[i]
        mid_ref[i * BLOCK : (i + 1) * BLOCK, :] = one
        mid.append(one)
    gate0 = short_blocks(z_ref, rows_ref, 0)
    sig2 = [gate0[i] * mid[i] for i in range(4)]
    hats = []
    for i in range(4):
        hat = split_dot(ahead, sig2[i])
        hat2_ref[i] = hat
        hats.append(hat)
    wave = spectra(hats, [bank2[i] for i in range(3)])
    for i in range(4):
        two = split_dot(back, wave[i]) + long_ref[LONG2, :] * sig2[i]
        out_ref[i * BLOCK : (i + 1) * BLOCK, :] = two.astype(bf16)


def mixer_backward(
    grad_ref, z_ref, rows_ref, long_ref, bank1, bank2, hat1_ref, hat2_ref, mid_ref,
    ahead_ref, back_ref,
    dz_ref, dtap_ref, dlong_ref, dfilt1_ref, dfilt2_ref, dbank1, dbank2,
):
    micro = pl.program_id(1)
    backward_step(
        micro == 0, micro == pl.num_programs(1) - 1, grad_ref, z_ref, rows_ref, long_ref, bank1, bank2,
        hat1_ref, hat2_ref, mid_ref, ahead_ref, back_ref,
        dz_ref, dtap_ref, dlong_ref, dfilt1_ref, dfilt2_ref, dbank1, dbank2,
    )


def backward_step(
    first, last, grad_ref, z_ref, rows_ref, long_ref, bank1, bank2, hat1_ref, hat2_ref, mid_ref,
    ahead_ref, back_ref,
    dz_ref, dtap_ref, dlong_ref, dfilt1_ref, dfilt2_ref, dbank1, dbank2,
):
    ahead = ahead_ref[...]
    back = back_ref[...]

    @pl.when(first)
    def _():
        dbank1[...] = jnp.zeros_like(dbank1)
        dbank2[...] = jnp.zeros_like(dbank2)
        dlong_ref[...] = jnp.zeros_like(dlong_ref)
        dtap_ref[...] = jnp.zeros_like(dtap_ref)

    def total(values):
        acc = values[0]
        for one in values[1:]:
            acc = acc + one
        return jnp.sum(acc, axis=0, keepdims=True)

    gate0 = short_blocks(z_ref, rows_ref, 0)
    grad2 = load_blocks(grad_ref)
    mid = load_blocks(mid_ref)
    dhats = [split_dot(ahead, grad2[i]) for i in range(4)]
    new = bank_grads([hat2_ref[i] for i in range(4)], dhats)
    for i in range(3):
        dbank2[i] += new[i]
    wave = adjoint_spectra(dhats, [bank2[i] for i in range(3)])
    dsig2 = [split_dot(back, wave[i]) + long_ref[LONG2, :] * grad2[i] for i in range(4)]
    dlong_ref[1:2, :] += total([grad2[i] * gate0[i] * mid[i] for i in range(4)])
    dgate0 = [dsig2[i] * mid[i] for i in range(4)]
    grad1 = [dsig2[i] * gate0[i] for i in range(4)]
    dhats = [split_dot(ahead, grad1[i]) for i in range(4)]
    new = bank_grads([hat1_ref[i] for i in range(4)], dhats)
    for i in range(3):
        dbank1[i] += new[i]
    wave = adjoint_spectra(dhats, [bank1[i] for i in range(3)])
    dsig1 = [split_dot(back, wave[i]) + long_ref[LONG1, :] * grad1[i] for i in range(4)]
    gate1 = short_blocks(z_ref, rows_ref, 1)
    value = short_blocks(z_ref, rows_ref, 2)
    dlong_ref[0:1, :] += total([grad1[i] * gate1[i] * value[i] for i in range(4)])
    dgate1 = [dsig1[i] * value[i] for i in range(4)]
    dvalue = [dsig1[i] * gate1[i] for i in range(4)]
    for index, grads in enumerate((dgate0, dgate1, dvalue)):
        cols = part(index)
        taps = rows_ref[0:3, cols]
        blocks = load_blocks(z_ref, cols)
        after = (grads[1], grads[2] + grads[3], None, None)
        dz = []
        for i in range(4):
            one = (
                taps[0:1] * grads[i]
                + taps[1:2] * advanced(grads[i], after[i], 1)
                + taps[2:3] * advanced(grads[i], after[i], 2)
            ).astype(bf16)
            dz_ref[i * BLOCK : (i + 1) * BLOCK, cols] = one
            dz.append(one.astype(f32))
        dtap_ref[4:5, cols] += total(dz)
        dtap_ref[3:4, cols] += total(grads)
        dtap_ref[0:1, cols] += total([grads[i] * blocks[i] for i in range(4)])
        for lag in (1, 2):
            dtap_ref[lag : lag + 1, cols] += total(
                [
                    grads[i]
                    * delayed(blocks[i], None if BEFORE[i] is None else blocks[BEFORE[i]], lag)
                    for i in range(4)
                ]
            )

    @pl.when(last)
    def _():
        filter_grads(back, [dbank1[i] for i in range(3)], dfilt1_ref)
        filter_grads(back, [dbank2[i] for i in range(3)], dfilt2_ref)


def constants():
    matrix = dft_matrix()
    return jnp.asarray(split3(matrix)), jnp.asarray(split3(matrix.T))


STEPS = D // TILE
AHEAD = (FREQ, 3 * BLOCK)
BACK = (BLOCK, 3 * FREQ)


def run_forward(z, lines, vecs, filters):
    rows = z.shape[0]
    blocks = rows // BLOCK

    def spec(shape, index):
        return pl.BlockSpec(shape, lambda t, m: index(m, t))

    hat_spec = spec((4, FREQ, TILE), lambda m, t: (m, 0, t))
    row_spec = spec((SPAN, TILE), lambda m, t: (m, t))
    bank_spec = spec((3, FREQ, TILE), lambda m, t: (0, 0, t))
    hat_shape = jax.ShapeDtypeStruct((blocks, FREQ, D), f32)
    bank_shape = jax.ShapeDtypeStruct((3, FREQ, D), f32)
    return pl.pallas_call(
        mixer_forward,
        grid=(STEPS, rows // SPAN),
        in_specs=[
            spec((SPAN, 3 * TILE), lambda m, t: (m, t)),
            spec((8, 3 * TILE), lambda m, t: (0, t)),
            spec((8, TILE), lambda m, t: (0, t)),
            spec((SEQ, TILE), lambda m, t: (0, t)),
            spec((SEQ, TILE), lambda m, t: (0, STEPS + t)),
            spec(AHEAD, lambda m, t: (0, 0)),
            spec(BACK, lambda m, t: (0, 0)),
        ],
        out_specs=[row_spec, hat_spec, hat_spec, row_spec, bank_spec, bank_spec],
        out_shape=[
            jax.ShapeDtypeStruct((rows, D), bf16), hat_shape, hat_shape,
            jax.ShapeDtypeStruct((rows, D), f32), bank_shape, bank_shape,
        ],
        compiler_params=pltpu.CompilerParams(vmem_limit_bytes=40 * 2**20),
        cost_estimate=pl.CostEstimate(flops=10 * 10**9, bytes_accessed=32 * 2**20, transcendentals=0),
        name="mixer_forward",
    )(z, lines, vecs, filters, filters, *constants())


def run_backward(grad, z, lines, vecs, bank1, bank2, hat1, hat2, mid):
    rows = z.shape[0]

    def spec(shape, index):
        return pl.BlockSpec(shape, lambda t, m: index(m, t))

    hat_spec = spec((4, FREQ, TILE), lambda m, t: (m, 0, t))
    row_spec = spec((SPAN, TILE), lambda m, t: (m, t))
    bank_spec = spec((3, FREQ, TILE), lambda m, t: (0, 0, t))
    z_spec = spec((SPAN, 3 * TILE), lambda m, t: (m, t))
    column_spec = spec((SEQ, TILE), lambda m, t: (0, t))
    return pl.pallas_call(
        mixer_backward,
        grid=(STEPS, rows // SPAN),
        in_specs=[
            row_spec,
            z_spec,
            spec((8, 3 * TILE), lambda m, t: (0, t)),
            spec((8, TILE), lambda m, t: (0, t)),
            bank_spec, bank_spec, hat_spec, hat_spec, row_spec,
            spec(AHEAD, lambda m, t: (0, 0)),
            spec(BACK, lambda m, t: (0, 0)),
        ],
        out_specs=[
            z_spec,
            spec((8, 3 * TILE), lambda m, t: (0, t)),
            spec((2, TILE), lambda m, t: (0, t)),
            column_spec,
            column_spec,
        ],
        out_shape=[
            jax.ShapeDtypeStruct((rows, D3), bf16), jax.ShapeDtypeStruct((8, D3), f32),
            jax.ShapeDtypeStruct((2, D), f32), jax.ShapeDtypeStruct((SEQ, D), f32),
            jax.ShapeDtypeStruct((SEQ, D), f32),
        ],
        scratch_shapes=[pltpu.VMEM((3, FREQ, TILE), f32), pltpu.VMEM((3, FREQ, TILE), f32)],
        compiler_params=pltpu.CompilerParams(vmem_limit_bytes=40 * 2**20),
        cost_estimate=pl.CostEstimate(flops=24 * 10**9, bytes_accessed=36 * 2**20, transcendentals=0),
        name="mixer_backward",
    )(grad, z, lines, vecs, bank1, bank2, hat1, hat2, mid, *constants())


def place_ratio():
    return (np.arange(SEQ).astype(np.float32) / np.float32(SEQ))[:, None]


def filter_states(first_w, first_b, second_w, second_b):
    levels = (np.arange(BANDS) + 1).astype(np.float32)
    ratio = jnp.asarray(place_ratio())
    angles = 2.0 * math.pi * ratio * jnp.asarray(levels)[None, :]
    embed = jnp.concatenate([ratio, jnp.cos(angles), jnp.sin(angles)], axis=1)
    first_pre = matmul(embed, first_w) + first_b
    first_act = jnp.sin(first_pre)
    second_pre = matmul(first_act, second_w) + second_b
    return embed, first_pre, first_act, second_pre, jnp.sin(second_pre)


def filter_taps(first_w, first_b, second_w, second_b, third_w, decay):
    second_act = filter_states(first_w, first_b, second_w, second_b)[-1]
    return matmul(second_act, third_w) * jnp.exp(-jnp.asarray(place_ratio()) * decay[None, :])


def by_tile(value):
    shape = value.shape
    return value.reshape(*shape[:-1], 3, STEPS, TILE).swapaxes(-3, -2).reshape(shape)


def by_part(value):
    shape = value.shape
    return value.reshape(*shape[:-1], STEPS, 3, TILE).swapaxes(-3, -2).reshape(shape)


MESH = pl.DeviceIdType.MESH


class Place:
    def __init__(self):
        rep = lax.axis_index("rep")
        self.rep = rep
        self.shard = lax.axis_index("shard")
        self.core = rep % 2
        self.side = (rep // 2) % 2
        self.depth = rep // 4
        self.quad = rep % 4
        self.eighth = rep % 8
        self.to_side = 2 - 4 * self.side
        self.to_depth = 4 - 8 * (self.depth % 2)

    def other_shard(self):
        return (self.rep, 1 - self.shard)

    def other_side(self):
        return (self.rep + 2 - 4 * self.side, self.shard)

    def near_depth(self):
        return (self.rep + self.to_depth, self.shard)

    def diagonal(self):
        return (self.rep + (1 - self.core) * self.to_side + self.core * self.to_depth, self.shard)

    def other_core(self):
        return (self.rep + 1 - 2 * self.core, self.shard)

    def other_depth(self, step):
        return (((self.depth + step) % 4) * 4 + self.quad, self.shard)


def greet(devices):
    barrier = pltpu.get_barrier_semaphore()
    for device in devices:
        pl.semaphore_signal(barrier, inc=1, device_id=device, device_id_type=MESH)
    pl.semaphore_wait(barrier, len(devices))


def remote(src, dst, send, recv, device):
    return pltpu.make_async_remote_copy(
        src_ref=src, dst_ref=dst, send_sem=send, recv_sem=recv, device_id=device, device_id_type=MESH
    )


UNITS = (
    (0, 0, 16), (0, 16, 16), (0, 32, 16), (1, 0, 48), (2, 0, 16), (2, 16, 16), (2, 32, 16), (3, 0, 96), (3, 96, 96),
)
STAGES = ("", "A3 A4", "A5 B3 B4", "A6 A7 B5 C3 C4", "A8 B6 B7 C5", "B8 C6 C7", "C8", "")
PACK_ROWS = 96
UP_ROW, DECAY_ROW, FIRST_ROW, SECOND_ROW = 23, 27, 32, 32


def column_moves():
    for s in range(2):
        for a in range(3):
            for b in range(3):
                at = s * (D3 // 2) + a * (D // 2) + b * 128
                yield s, a, b * 128, (at % D // TILE * 3 + at // D) * TILE + at % TILE


def gather_kernel(
    gain1, shift1, in_shift, short_w, short_b, long_b, w1, b1, w2, b2, third, decay, out_b, gain2, shift2, up_b,
    down_b, w_in, w_out, w_up, w_down, tokens, embed_ref, ratio_ref, ahead_ref, back_ref,
    z_ref, mixed_ref, hat1_ref, hat2_ref, mid_ref, bank1, bank2,
    vecs, lines, up_all, decay_all, second_all, third_all, pre1, act1, pre2, act2,
    normed_out, f_in, f_out, f_up, f_down,
    pack, packed, packs, thirds, in_v, normed_v,
    small_send, small_recv, own_sem, ysend, yrecv, xsend, xrecv, zsend, zrecv, dsend, drecv, csend, crecv,
):
    tick = pl.program_id(0)
    place = Place()
    shard, mine = place.shard, place.eighth
    by_side, by_depth = mine + place.to_side, mine + place.to_depth
    by_both = by_side + place.to_depth
    locals_ = (w_in, w_out, w_up, w_down)
    fulls = (in_v, f_out, f_up, f_down)

    def rows_of(unit, shard_of, piece):
        weight, start, size = unit
        half = locals_[weight].shape[0]
        return pl.ds(pl.multiple_of(shard_of * half + piece * (half // 8) + start, 16), size)

    def local_rows(unit):
        weight, start, size = unit
        return pl.ds(pl.multiple_of(mine * (locals_[weight].shape[0] // 8) + start, 16), size)

    def smalls():
        return [
            remote(packed, packs.at[shard], small_send.at[0], small_recv.at[0], place.other_shard()),
            remote(third, thirds.at[shard], small_send.at[1], small_recv.at[1], place.other_shard()),
        ]

    def own_copies():
        copies = []
        for weight in range(1, 4):
            half = locals_[weight].shape[0]
            rows = pl.ds(pl.multiple_of(shard * half, 16), half)
            copies.append(pltpu.make_async_copy(locals_[weight], fulls[weight].at[rows, :], own_sem.at[weight]))
        return copies

    def normed_copy():
        return pltpu.make_async_copy(normed_v, normed_out, own_sem.at[0])

    def in_copy():
        return pltpu.make_async_copy(in_v, f_in, own_sem.at[4])

    def moved(u, piece, send, recv, device):
        unit = UNITS[u]
        region = fulls[unit[0]].at[rows_of(unit, 1 - shard, piece), :]
        return remote(region, region, send, recv, device)

    def from_shard(u):
        return moved(u, mine, ysend.at[u], yrecv.at[u], place.other_shard())

    def side(u, piece):
        return moved(u, piece, xsend.at[u], xrecv.at[u], place.other_side())

    def depth(u, piece):
        return moved(u, piece, zsend.at[u], zrecv.at[u], place.near_depth())

    def diagonal(u, piece):
        return moved(u, piece, dsend.at[u], drecv.at[u], place.diagonal())

    def twin(u, index, piece):
        return moved(u, piece, csend.at[u, index], crecv.at[u, index], place.other_core())

    def exchanges(stages):
        for stage in stages.split():
            kind, u = stage[0], int(stage[1:])
            if kind == "A":
                from_shard(u).wait_recv()
                side(u, mine).start()
                depth(u, mine).start()
                twin(u, 0, mine).start()
            elif kind == "B":
                side(u, by_side).wait_recv()
                twin(u, 1, by_side).start()
                depth(u, by_depth).wait_recv()
                twin(u, 2, by_depth).start()
                diagonal(u, (1 - place.core) * by_depth + place.core * by_side).start()
            else:
                diagonal(u, by_both).wait_recv()
                twin(u, 3, by_both).start()

    def finish(u):
        for index, piece in enumerate((mine, by_side, by_depth, by_both)):
            twin(u, index, piece).wait()
        from_shard(u).wait_send()
        side(u, mine).wait_send()
        depth(u, mine).wait_send()
        diagonal(u, mine).wait_send()

    @pl.when(tick == 0)
    def _():
        greet([place.other_shard(), place.other_side(), place.near_depth(), place.other_core()])
        rows = pl.ds(pl.multiple_of(shard * (D // 2), 16), D // 2)
        for p in range(3):
            for t in range(STEPS):
                in_v[rows, part(t * 3 + p)] = w_in[:, part(p * STEPS + t)]

        def send_units(units):
            for u in units:
                weight = UNITS[u][0]
                to = fulls[weight].at[rows_of(UNITS[u], shard, mine), :]
                source = to if weight == 0 else locals_[weight].at[local_rows(UNITS[u]), :]
                remote(source, to, ysend.at[u], yrecv.at[u], place.other_shard()).start()

        send_units(range(3))
        pack[...] = jnp.zeros_like(pack)
        half = D // 2

        def row(ref):
            return ref[...].astype(f32).reshape(1, ref.shape[0])

        for i, ref in enumerate((gain1, shift1, out_b, gain2, shift2, down_b)):
            pack[i : i + 1, :] = row(ref)
        pack[6:8, :] = long_b[...].astype(f32)
        taps = short_w[...].astype(f32)
        for i, value in enumerate((row(in_shift), row(short_b), taps[0:1], taps[1:2], taps[2:3])):
            for a in range(3):
                pack[8 + 3 * i + a : 9 + 3 * i + a, :] = value[:, a * half : (a + 1) * half]
        value = row(up_b)
        for a in range(4):
            pack[UP_ROW + a : UP_ROW + a + 1, :] = value[:, a * half : (a + 1) * half]
        value = row(decay)
        for a in range(2):
            pack[DECAY_ROW + a : DECAY_ROW + a + 1, :] = value[:, a * half : (a + 1) * half]
        wide = w1.shape[1]
        n1, n2 = w1.shape[0], w2.shape[0]
        pack[FIRST_ROW : FIRST_ROW + n1, 0:wide] = w1[...].astype(f32)
        pack[FIRST_ROW + n1 : FIRST_ROW + n1 + 1, 0:wide] = row(b1)
        pack[FIRST_ROW + n1 + 1 : FIRST_ROW + n1 + 2, 0:wide] = row(b2)
        pack[SECOND_ROW : SECOND_ROW + n2, 128 : 128 + wide] = w2[...].astype(f32)
        packed[...] = pack[...].astype(bf16)
        for one in smalls():
            one.start()
        send_units(range(3, len(UNITS)))
        for one in own_copies():
            one.start()
        packs[shard] = packed[...]
        thirds[shard] = third[...]
        exchanges("A0 A1 A2")
        for one in smalls():
            one.wait()

        both = [packs[s].astype(f32) for s in range(2)]
        for i in range(8):
            for s in range(2):
                vecs[i : i + 1, s * half : (s + 1) * half] = both[s][i : i + 1]
        lines[...] = jnp.zeros_like(lines)
        for s, a, b, to in column_moves():
            for i, line in enumerate((4, 3, 0, 1, 2)):
                at = 8 + 3 * i + a
                lines[line : line + 1, to : to + 128] = both[s][at : at + 1, b : b + 128]
        for s in range(2):
            for a in range(4):
                to = s * (2 * D) + a * half
                up_all[0:1, to : to + half] = both[s][UP_ROW + a : UP_ROW + a + 1]
            for a in range(2):
                to = s * D + a * half
                decay_all[0:1, to : to + half] = both[s][DECAY_ROW + a : DECAY_ROW + a + 1]
            third_all[:, s * D : (s + 1) * D] = thirds[s].astype(f32)

        def narrow(rows, cols):
            return jnp.concatenate([both[s][rows, cols] for s in range(2)], axis=1)

        first_w = narrow(slice(FIRST_ROW, FIRST_ROW + n1), slice(0, wide))
        first_b = narrow(slice(FIRST_ROW + n1, FIRST_ROW + n1 + 1), slice(0, wide))
        second_b = narrow(slice(FIRST_ROW + n1 + 1, FIRST_ROW + n1 + 2), slice(0, wide))
        second_w = narrow(slice(SECOND_ROW, SECOND_ROW + n2), slice(128, 128 + wide))
        second_all[...] = second_w
        exchanges("B0 B1 B2")
        straight = ((1,), (0,))
        pre1[...] = exact(embed_ref[...], first_w, straight) + first_b
        act1[...] = jnp.sin(pre1[...])
        pre2[...] = exact(act1[...], second_w, straight) + second_b
        act2[...] = jnp.sin(pre2[...])

        exchanges("C0 C1 C2")

        def norm_rows(i, carry):
            rows = pl.ds(pl.multiple_of(i * 128, 128), 128)
            values = tokens[rows, :].astype(f32)
            normed_v[rows, :] = layer_norm(values, vecs[0:1, :], vecs[1:2, :]).astype(bf16)
            return carry

        lax.fori_loop(0, tokens.shape[0] // 128, norm_rows, 0)
        normed_copy().start()
        for u in range(3):
            finish(u)
        in_copy().start()

    for index in range(1, len(STAGES)):
        @pl.when(tick == index)
        def _():
            exchanges(STAGES[index])

    @pl.when(tick > 0)
    def _():
        step = jnp.maximum(tick - 1, 0)
        tile = step // 2
        micro = step % 2
        cols = pl.ds(pl.multiple_of(tile * 3 * TILE, 3 * TILE), 3 * TILE)
        few = pl.ds(pl.multiple_of(tile * TILE, TILE), TILE)
        rows = pl.ds(pl.multiple_of(micro * SPAN, SPAN), SPAN)

        @pl.when(tick <= 2 * STEPS)
        def _():
            @pl.when(micro == 0)
            def _():
                for q, bank in enumerate((bank1, bank2)):
                    those = pl.ds(pl.multiple_of(q * D + tile * TILE, TILE), TILE)
                    window = jnp.exp(-ratio_ref[...] * decay_all[:, those])
                    taps = exact(act2[...], third_all[:, those], ((1,), (0,))) * window
                    make_bank(ahead_ref[...], taps, bank)

            z_ref[...] = lowmul(normed_v[rows, :], in_v[:, cols]) + lines[4:5, cols]
            forward_step(
                z_ref, lines.at[:, cols], vecs.at[:, few], ahead_ref, back_ref,
                mixed_ref, hat1_ref, hat2_ref, mid_ref, bank1, bank2,
            )

    @pl.when(tick == 2 * STEPS + 1)
    def _():
        for u in range(3, len(UNITS)):
            finish(u)
        normed_copy().wait()
        in_copy().wait()
        for one in own_copies():
            one.wait()


def embed_table():
    ratio = place_ratio()
    angles = 2.0 * math.pi * ratio * (np.arange(BANDS) + 1).astype(np.float32)[None, :]
    return np.concatenate([ratio, np.cos(angles), np.sin(angles)], axis=1).astype(np.float32)


def gather_weights(*values):
    w1, w2, w3 = values[6], values[8], values[10]
    weights = values[17:21]
    tokens = values[21]
    count = tokens.shape[0]
    hidden = w2.shape[0]
    vmem = lambda one: pl.BlockSpec(one.shape, lambda t: (0,) * one.ndim, pipeline_mode=pl.Buffered(1))
    hbm = pl.BlockSpec(memory_space=pl.ANY)
    units = len(UNITS)
    embed, ratio = jnp.asarray(embed_table()), jnp.asarray(place_ratio())
    inputs = (*values, embed, ratio, *constants())

    def at_tile(shape, where):
        def index(t):
            step = jnp.minimum(jnp.maximum(t - 1, 0), 2 * STEPS - 1)
            return where(step % 2, step // 2)

        return pl.BlockSpec(shape, index)

    def doubled(value):
        return jax.ShapeDtypeStruct((2 * value.shape[0], *value.shape[1:]), value.dtype)

    def shape(*dims, kind=f32):
        return jax.ShapeDtypeStruct(dims, kind)

    fixed = [
        shape(8, D), shape(8, D3), shape(1, weights[2].shape[1]), shape(1, 2 * w3.shape[1]), shape(hidden, hidden),
        shape(hidden, 2 * w3.shape[1]),
    ] + [shape(SEQ, hidden)] * 4
    blocks = count // BLOCK
    hat_spec = at_tile((4, FREQ, TILE), lambda m, t: (m, 0, t))
    row_spec = at_tile((SPAN, TILE), lambda m, t: (m, t))
    bank_spec = at_tile((3, FREQ, TILE), lambda m, t: (0, 0, t))
    return pl.pallas_call(
        gather_kernel,
        grid=(2 * STEPS + 2,),
        in_specs=[vmem(one) for one in inputs],
        out_specs=[
            at_tile((SPAN, 3 * TILE), lambda m, t: (m, t)), row_spec, hat_spec, hat_spec, row_spec, bank_spec,
            bank_spec,
        ]
        + [vmem(one) for one in fixed] + [hbm] * 5,
        out_shape=[
            shape(count, D3), shape(count, D, kind=bf16), shape(blocks, FREQ, D), shape(blocks, FREQ, D),
            shape(count, D), shape(3, FREQ, D), shape(3, FREQ, D),
        ]
        + fixed + [shape(count, D, kind=bf16)] + [doubled(one) for one in weights],
        scratch_shapes=[
            pltpu.VMEM((PACK_ROWS, D // 2), f32),
            pltpu.VMEM((PACK_ROWS, D // 2), bf16),
            pltpu.VMEM((2, PACK_ROWS, D // 2), bf16),
            pltpu.VMEM((2, *w3.shape), bf16),
            pltpu.VMEM((D, D3), bf16),
            pltpu.VMEM((count, D), bf16),
        ]
        + [pltpu.SemaphoreType.DMA((2,))] * 2
        + [pltpu.SemaphoreType.DMA((5,))]
        + [pltpu.SemaphoreType.DMA((units,))] * 8
        + [pltpu.SemaphoreType.DMA((units, 4))] * 2,
        compiler_params=pltpu.CompilerParams(
            collective_id=0, has_side_effects=True, vmem_limit_bytes=63 * 2**20
        ),
        name="gather_weights",
    )(*inputs)


class Reduction:
    def __init__(self, place, first, count, rows, bufs, sems, out):
        self.place = place
        self.first = first
        self.count = count
        self.rows = rows
        self.dtype = bufs[0].dtype
        self.whole, self.from_core, self.half, self.from_shard, self.own, self.from_side, self.mine, self.from_depth, self.back = bufs
        (self.s_core, self.r_core, self.s_shard, self.r_shard, self.s_side, self.r_side, self.s_depth, self.r_depth,
         self.s_gd, self.r_gd, self.s_gs, self.r_gs, self.s_gc, self.r_gc, self.s_own) = sems
        self.out = out

    def when(self, tick, lag, body):
        k = tick - self.first - lag

        @pl.when((k >= 0) & (k < self.count))
        def _():
            body(k, k % 2)

    def slot(self, ref, k):
        return ref.at[k % ref.shape[0]]

    def rows_at(self, index, size):
        return pl.ds(pl.multiple_of(index * size, size), size)

    def core_copy(self, k, slot):
        p = self.place
        return remote(
            self.whole.at[slot, :, self.rows_at(1 - p.core, self.rows // 2), :],
            self.slot(self.from_core, k), self.s_core.at[k], self.r_core.at[k], p.other_core(),
        )

    def shard_copy(self, k, slot):
        p = self.place
        return remote(
            self.half.at[slot, 1 - p.shard], self.slot(self.from_shard, k), self.s_shard.at[k], self.r_shard.at[k],
            p.other_shard(),
        )

    def side_copy(self, k, slot):
        p = self.place
        return remote(
            self.own.at[slot, self.rows_at(1 - p.side, self.rows // 4), :],
            self.slot(self.from_side, k), self.s_side.at[k], self.r_side.at[k], p.other_side(),
        )

    def quarter(self, base, index):
        rows = self.rows // 8
        return (
            pl.ds(pl.multiple_of(base + (index // 2) * rows, rows), rows),
            pl.ds(pl.multiple_of((index % 2) * (D // 2), D // 2), D // 2),
        )

    def depth_copy(self, k, slot, step):
        p = self.place
        rows, cols = self.quarter(0, (p.depth + step) % 4)
        return remote(
            self.mine.at[slot, rows, cols], self.from_depth.at[k % self.from_depth.shape[0], step - 1],
            self.s_depth.at[k, step - 1], self.r_depth.at[k, step - 1], p.other_depth(step),
        )

    def depth_back(self, k, step):
        p = self.place
        rows, cols = self.quarter(p.side * (self.rows // 4), p.depth)
        region = self.back.at[k % self.back.shape[0], rows, cols]
        return remote(
            region, region, self.s_gd.at[k, step - 1], self.r_gd.at[k, step - 1], p.other_depth(step)
        )

    def side_back(self, k):
        p = self.place
        region = self.back.at[k % self.back.shape[0], self.rows_at(p.side, self.rows // 4), :]
        return remote(region, region, self.s_gs.at[k], self.r_gs.at[k], p.other_side())

    def homes(self, k, place_in):
        rows = pl.ds(pl.multiple_of(self.place.core * (self.rows // 2), self.rows // 2), self.rows // 2)
        return [(cols, ref.at[(*lead, rows, *tail)]) for cols, ref, lead, tail in place_in]

    def send_home(self, k, place_in):
        p = self.place
        for cols, region in self.homes(k, place_in):
            piece = self.back.at[k % self.back.shape[0], :, cols]
            remote(piece, region, self.s_gc.at[k], self.r_gc.at[k], p.other_core()).start()
            pltpu.make_async_copy(piece, region, self.s_own.at[k]).start()

    def wait_home(self, k):
        whole = self.slot(self.back, k)
        remote(whole, whole, self.s_gc.at[k], self.r_gc.at[k], self.place.other_core()).wait()
        pltpu.make_async_copy(whole, whole, self.s_own.at[k]).wait()

    def add(self, left, right):
        return (left.astype(f32) + right.astype(f32)).astype(self.dtype)

    def send(self, tick):
        self.when(tick, 0, lambda k, slot: self.core_copy(k, slot).start())

    def advance(self, tick):
        p = self.place

        def after_core(k, slot):
            self.core_copy(k, slot).wait()
            for s in range(2):
                self.half[slot, s] = self.add(
                    self.whole[slot, s, self.rows_at(p.core, self.rows // 2), :], self.from_core[k % self.from_core.shape[0], s]
                )
            self.shard_copy(k, slot).start()

        def after_shard(k, slot):
            self.shard_copy(k, slot).wait()
            self.own[slot] = self.add(self.half[slot, p.shard], self.from_shard[k % self.from_shard.shape[0]])
            self.side_copy(k, slot).start()

        def after_side(k, slot):
            self.side_copy(k, slot).wait()
            self.mine[slot] = self.add(
                self.own[slot, self.rows_at(p.side, self.rows // 4), :], self.from_side[k % self.from_side.shape[0]]
            )
            for step in range(1, 4):
                self.depth_copy(k, slot, step).start()

        def after_depth(k, slot):
            for step in range(1, 4):
                self.depth_copy(k, slot, step).wait()
            rows, cols = self.quarter(0, p.depth)
            total = self.mine[slot, rows, cols].astype(f32)
            for step in range(3):
                total = total + self.from_depth[k % self.from_depth.shape[0], step].astype(f32)
            rows, cols = self.quarter(p.side * (self.rows // 4), p.depth)
            self.back[k % self.back.shape[0], rows, cols] = total.astype(self.dtype)
            for step in range(1, 4):
                self.depth_back(k, step).start()

        def after_depth_back(k, slot):
            for step in range(1, 4):
                self.depth_back(k, step).wait()
            self.side_back(k).start()

        def after_side_back(k, slot):
            self.side_back(k).wait()
            self.out(self, k)

        def after_core_back(k, slot):
            self.wait_home(k)

        for lag, body in enumerate(
            (after_core, after_shard, after_side, after_depth, after_depth_back, after_side_back, after_core_back), 1
        ):
            self.when(tick, lag, body)


LAGS = 7
DOWN, UP, OUT, IN = 4, 4, 1, STEPS
CHUNKS = DOWN + UP + OUT + IN
SMALL_ROWS = 128
SMALL_TICK = 9
ROW_BLOCK = 128


GIVEN_ROW, TAP_ROW, LONG_ROW, NORM_ROW = 64, 72, 96, 98


def exact(left, right, dims):
    return lax.dot_general(left, right, (dims, ((), ())), precision=HIGH, preferred_element_type=f32)


def reduce_kernel(
    given, active0, active1, upstream, second, d_hidden, mixed, d_middle, normed, tokens, gain, middle, down0, down1,
    grad_ref, z_ref, rows_ref, long_ref, bank1, bank2, hat1_ref, hat2_ref, mid_ref, ahead_ref, back_ref,
    in_ref, decay_ref, decay2_ref, third1_ref, third2_ref, ratio_ref, embed_ref, pre1_ref, act1_ref, pre2_ref, act2_ref,
    second_w_ref,
    small_out, g_down, g_up, g_out, g_in, tokens_out, result_out,
    d_proj, dtap, dtaps, dlong, dlongs, dfilt1, dfilt2, dbank1, dbank2, d_normed, d_act, out_rows, out_sem, middle_sem, *scratch,
):
    tick = pl.program_id(0)
    place = Place()
    bufs, sems = scratch[:9], scratch[9:24]
    small_bufs, small_sems = scratch[24:33], scratch[33:48]
    everything = slice(None)
    is_in = (tick % 3 == 2) & (tick < 9)
    tile = tick // 3

    def little_home(chain, k):
        chain.send_home(k, [(everything, small_out, (k,), (everything,))])

    def kinds(k):
        down = (k < 5) & (k % 3 < 2)
        up = ((k >= 6) & (k < 8)) | (k >= 10)
        return down, up, k == 9, (k < 9) & (k % 3 == 2)

    def big_home(chain, k):
        down, up, out, inward = kinds(k)

        @pl.when(down)
        def _():
            chain.send_home(k, [(everything, g_down, (k - k // 3,), (everything,))])

        @pl.when(up)
        def _():
            index = k - 6 - 2 * (k // 9)
            cols = pl.ds(pl.multiple_of(index * D, D), D)
            chain.send_home(k, [(everything, g_up, (), (cols,))])

        @pl.when(out)
        def _():
            chain.send_home(k, [(everything, g_out, (), (everything,))])

        @pl.when(inward)
        def _():
            chain.send_home(
                k,
                [
                    (part(p), g_in, (), (pl.ds(pl.multiple_of(p * D + (k // 3) * TILE, TILE), TILE),))
                    for p in range(3)
                ],
            )

    little = Reduction(place, SMALL_TICK, 1, SMALL_ROWS, small_bufs, small_sems, little_home)
    big = Reduction(place, 0, CHUNKS, D // 2, bufs, sems, big_home)
    pack = little.whole

    @pl.when(tick == 0)
    def _():
        greet(
            [place.other_shard(), place.other_side(), place.other_core()]
            + [place.other_depth(step) for step in range(1, 4)]
        )
        pack[...] = jnp.zeros_like(pack)
        pack[0, :, GIVEN_ROW : GIVEN_ROW + 8, D // 2 :] = given[...]
        d_act[...] = jnp.zeros_like(d_act)

    little.advance(tick)
    big.advance(tick)

    def chunk(slot, lefts, right):
        for s in range(2):
            big.whole[slot, s] = inner_rows(lefts[s], right).astype(bf16)

    def halves(left):
        return left[:, : D // 2], left[:, D // 2 :]

    def compute(k, slot):
        down, up, out, inward = kinds(k)

        @pl.when(down)
        def _():
            chunk(slot, (active0[...], active1[...]), upstream[...])

        @pl.when(up)
        def _():
            chunk(slot, halves(second), d_hidden[...])

        @pl.when(out)
        def _():
            chunk(slot, halves(mixed), d_middle[...].astype(bf16))

        @pl.when(inward)
        def _():
            chunk(slot, halves(normed), d_proj[...])

    big.when(tick, 0, compute)
    big.send(tick)

    @pl.when((tick < 8) & (tick % 3 < 2))
    def _():
        micro = tick % 3
        backward_step(
            micro == 0, micro == 1, grad_ref, z_ref, rows_ref, long_ref, bank1, bank2,
            hat1_ref, hat2_ref, mid_ref, ahead_ref, back_ref,
            d_proj.at[pl.ds(pl.multiple_of(micro * SPAN, SPAN), SPAN), :], dtap, dlong, dfilt1, dfilt2, dbank1, dbank2,
        )

    @pl.when(is_in)
    def _():
        cols = pl.ds(pl.multiple_of(tile * TILE, TILE), TILE)
        dtaps[tile] = dtap[...]
        dlongs[:, cols] = dlong[...]
        step = times_t(d_proj[...], in_ref[...])

        @pl.when(tile == 0)
        def _():
            d_normed[...] = step

        @pl.when(tile > 0)
        def _():
            d_normed[...] += step

        for q, (grads, decay, third) in enumerate(
            ((dfilt1, decay_ref, third1_ref), (dfilt2, decay2_ref, third2_ref))
        ):
            window = jnp.exp(-ratio_ref[...] * decay[...])
            d_taps = grads[...] * window
            pack[0, q, 0 : act2_ref.shape[1], cols] = exact(act2_ref[...], d_taps, ((0,), (0,)))
            d_act[...] += exact(d_taps, third[...], ((1,), (1,)))

    @pl.when(tick == SMALL_TICK)
    def _():
        for s in range(2):
            for a in range(3):
                for b in range(3):
                    at = s * (D3 // 2) + a * (D // 2) + b * 128
                    p, t, o = at // D, at % D // TILE, at % TILE
                    pack[0, s, TAP_ROW + 8 * a : TAP_ROW + 8 * a + 8, D // 2 + b * 128 : D // 2 + b * 128 + 128] = dtaps[
                        t, :, p * TILE + o : p * TILE + o + 128
                    ]
            pack[0, s, LONG_ROW : LONG_ROW + 2, D // 2 :] = dlongs[:, s * (D // 2) : (s + 1) * (D // 2)]

        def norm_rows(i, sums):
            rows = pl.ds(pl.multiple_of(i * ROW_BLOCK, ROW_BLOCK), ROW_BLOCK)
            values = tokens[rows, :].astype(f32)
            grads = d_normed[rows, :]
            center = values - jnp.mean(values, axis=-1, keepdims=True)
            scale = lax.rsqrt(jnp.mean(center * center, axis=-1, keepdims=True) + EPS)
            unit = center * scale
            scaled = grads * gain[0:1, :]
            inner = scaled - jnp.mean(scaled, axis=-1, keepdims=True)
            inner = inner - unit * jnp.mean(scaled * unit, axis=-1, keepdims=True)
            out_rows[rows, :] = (scale * inner + d_middle[rows, :]).astype(bf16)
            return (
                sums[0] + jnp.sum(grads * unit, axis=0, keepdims=True),
                sums[1] + jnp.sum(grads, axis=0, keepdims=True),
            )

        zero = jnp.zeros((1, D), f32)
        sums = lax.fori_loop(0, tokens.shape[0] // ROW_BLOCK, norm_rows, (zero, zero))
        d_pre2 = d_act[...] * jnp.cos(pre2_ref[...])
        g_second = exact(act1_ref[...], d_pre2, ((0,), (0,)))
        g_b2 = jnp.sum(d_pre2, axis=0, keepdims=True)
        d_pre1 = exact(d_pre2, second_w_ref[...], ((1,), (1,))) * jnp.cos(pre1_ref[...])
        g_first = exact(embed_ref[...], d_pre1, ((0,), (0,)))
        g_b1 = jnp.sum(d_pre1, axis=0, keepdims=True)
        wide = g_second.shape[1] // 2
        for s in range(2):
            own = slice(s * wide, (s + 1) * wide)
            for i in range(2):
                pack[0, s, NORM_ROW + i : NORM_ROW + i + 1, D // 2 :] = sums[i][:, s * (D // 2) : (s + 1) * (D // 2)]
            pack[0, s, 64 : 64 + g_first.shape[0], 0:wide] = g_first[:, own]
            pack[0, s, 64 + g_first.shape[0] : 65 + g_first.shape[0], 0:wide] = g_b1[:, own]
            pack[0, s, 65 + g_first.shape[0] : 66 + g_first.shape[0], 0:wide] = g_b2[:, own]
            pack[0, s, 64 : 64 + g_second.shape[0], 128 : 128 + wide] = g_second[:, own]
        pltpu.make_async_copy(out_rows, tokens_out, out_sem).start()

    little.send(tick)

    @pl.when(tick == SMALL_TICK + 2)
    def _():
        pltpu.make_async_copy(out_rows, tokens_out, out_sem).wait()
        pltpu.make_async_copy(middle, d_normed, middle_sem).start()

    @pl.when((tick >= CHUNKS) & (tick < CHUNKS + DOWN))
    def _():
        @pl.when(tick == CHUNKS)
        def _():
            pltpu.make_async_copy(middle, d_normed, middle_sem).wait()

        def result_rows(i, carry):
            rows = pl.ds(pl.multiple_of(i * 256, 256), 256)
            total = d_normed[rows, :] + lowmul(active0[rows, :], down0[...]) + lowmul(active1[rows, :], down1[...])
            d_normed[rows, :] = total

            @pl.when(tick == CHUNKS + DOWN - 1)
            def _():
                out_rows[rows, :] = (total + gain[5:6, :]).astype(bf16)

            return carry

        lax.fori_loop(0, out_rows.shape[0] // 256, result_rows, 0)

        @pl.when(tick == CHUNKS + DOWN - 1)
        def _():
            pltpu.make_async_copy(out_rows, result_out, out_sem).start()

    @pl.when(tick == CHUNKS + LAGS - 1)
    def _():
        pltpu.make_async_copy(out_rows, result_out, out_sem).wait()


def reduce_grads(
    given, active, upstream, second, d_hidden, mixed, d_middle, normed, tokens, middle, down_full,
    d_mixed, z, lines, vecs, bank1, bank2, hat1, hat2, mid, in_full, decay, third_w, states, second_w,
):
    count = upstream.shape[0]
    half = D // 2
    hidden = second_w.shape[0]
    embed, pre1, act1, pre2, act2 = states

    def fixed(shape):
        return pl.BlockSpec(shape, lambda t: (0,) * len(shape), pipeline_mode=pl.Buffered(1))

    def at_tile(shape, where):
        def index(t):
            tick = jnp.minimum(t, 8)
            return where(jnp.minimum(tick % 3, 1), tick // 3)

        return pl.BlockSpec(shape, index)

    def down_index(t):
        tick = jnp.minimum(t, 4)
        late = jnp.minimum(jnp.maximum(t - (CHUNKS - 1), 0), 1)
        return tick - tick // 3 - 3 * late + late_index(t)

    def late_index(t):
        return jnp.minimum(jnp.maximum(t - CHUNKS, 0), DOWN - 1)

    def up_index(t):
        return jnp.minimum(jnp.maximum(t - 6, 0), 2) + jnp.minimum(jnp.maximum(t - 10, 0), 1)

    hat_spec = at_tile((4, FREQ, TILE), lambda m, t: (m, 0, t))
    row_spec = at_tile((SPAN, TILE), lambda m, t: (m, t))
    bank_spec = at_tile((3, FREQ, TILE), lambda m, t: (0, 0, t))
    decay_shape = (1, TILE)

    def buffers(n, rows, kind):
        few, many = min(n, 4), min(n, 8)
        return [
            pltpu.VMEM((min(n, 2), 2, rows, D), kind),
            pltpu.VMEM((few, 2, rows // 2, D), kind),
            pltpu.VMEM((min(n, 2), 2, rows // 2, D), kind),
            pltpu.VMEM((few, rows // 2, D), kind),
            pltpu.VMEM((min(n, 2), rows // 2, D), kind),
            pltpu.VMEM((few, rows // 4, D), kind),
            pltpu.VMEM((min(n, 2), rows // 4, D), kind),
            pltpu.VMEM((few, 3, rows // 8, D // 2), kind),
            pltpu.VMEM((many, rows // 2, D), kind),
        ]

    def semaphores(n):
        one = pltpu.SemaphoreType.DMA((n,))
        three = pltpu.SemaphoreType.DMA((n, 3))
        return [one] * 6 + [three] * 4 + [one] * 5

    return pl.pallas_call(
        reduce_kernel,
        grid=(CHUNKS + LAGS,),
        in_specs=[
            fixed((2, 8, half)),
            pl.BlockSpec((count, half), lambda t: (0, down_index(t))),
            pl.BlockSpec((count, half), lambda t: (0, DOWN + down_index(t))),
            fixed((count, D)),
            fixed((count, D)),
            pl.BlockSpec((count, D), lambda t: (0, up_index(t))),
            fixed((count, D)),
            fixed((count, D)),
            fixed((count, D)),
            fixed((count, D)),
            fixed((8, D)),
            pl.BlockSpec(memory_space=pl.ANY),
            pl.BlockSpec((half, D), lambda t: (late_index(t), 0)),
            pl.BlockSpec((half, D), lambda t: (DOWN + late_index(t), 0)),
            row_spec,
            at_tile((SPAN, 3 * TILE), lambda m, t: (m, t)),
            at_tile((8, 3 * TILE), lambda m, t: (0, t)),
            at_tile((8, TILE), lambda m, t: (0, t)),
            bank_spec, bank_spec, hat_spec, hat_spec, row_spec,
            fixed(AHEAD),
            fixed(BACK),
            at_tile((D, 3 * TILE), lambda m, t: (0, t)),
            at_tile(decay_shape, lambda m, t: (0, t)),
            at_tile(decay_shape, lambda m, t: (0, STEPS + t)),
            at_tile((hidden, TILE), lambda m, t: (0, t)),
            at_tile((hidden, TILE), lambda m, t: (0, STEPS + t)),
            fixed((SEQ, 1)),
            fixed(embed.shape),
            fixed(pre1.shape),
            fixed(act1.shape),
            fixed(pre2.shape),
            fixed(act2.shape),
            fixed(second_w.shape),
        ],
        out_specs=[pl.BlockSpec(memory_space=pl.ANY)] * 7,
        out_shape=[
            jax.ShapeDtypeStruct((1, SMALL_ROWS, D), f32),
            jax.ShapeDtypeStruct((DOWN, half, D), bf16),
            jax.ShapeDtypeStruct((half, UP * D), bf16),
            jax.ShapeDtypeStruct((half, D), bf16),
            jax.ShapeDtypeStruct((half, D3), bf16),
            jax.ShapeDtypeStruct((count, D), bf16),
            jax.ShapeDtypeStruct((count, D), bf16),
        ],
        scratch_shapes=[
            pltpu.VMEM((count, 3 * TILE), bf16),
            pltpu.VMEM((8, 3 * TILE), f32),
            pltpu.VMEM((STEPS, 8, 3 * TILE), f32),
            pltpu.VMEM((2, TILE), f32),
            pltpu.VMEM((2, D), f32),
            pltpu.VMEM((SEQ, TILE), f32),
            pltpu.VMEM((SEQ, TILE), f32),
            pltpu.VMEM((3, FREQ, TILE), f32),
            pltpu.VMEM((3, FREQ, TILE), f32),
            pltpu.VMEM((count, D), f32),
            pltpu.VMEM((SEQ, hidden), f32),
            pltpu.VMEM((count, D), bf16),
            pltpu.SemaphoreType.DMA(()),
            pltpu.SemaphoreType.DMA(()),
        ]
        + buffers(CHUNKS, half, bf16) + semaphores(CHUNKS) + buffers(1, SMALL_ROWS, f32) + semaphores(1),
        compiler_params=pltpu.CompilerParams(
            collective_id=1, has_side_effects=True, vmem_limit_bytes=63 * 2**20
        ),
        name="reduce_grads",
    )(
        given, active, active, upstream, second, d_hidden, mixed, d_middle, normed, tokens, vecs, middle, down_full, down_full,
        d_mixed, z, lines, vecs, bank1, bank2, hat1, hat2, mid, *constants(), in_full,
        decay, decay, third_w, third_w, jnp.asarray(place_ratio()), embed, pre1, act1, pre2, act2, second_w,
    )


HID = 512
GELU_A = math.sqrt(2.0 / math.pi)
GELU_B = 0.044715


def middle_kernel(
    mixed, tokens, upstream, out_ref, vecs, up_ref, shift_ref, down_ref,
    middle_ref, second, active_ref, d_hidden_ref, d_middle_ref, d_mixed_ref, sums_ref, d_shift_ref, d_second_ref,
):
    first = pl.program_id(0) == 0
    last = pl.program_id(0) == pl.num_programs(0) - 1
    steps = second.shape[0] // 256

    def rows_of(i):
        return pl.ds(pl.multiple_of(i * 256, 256), 256)

    @pl.when(first)
    def _():
        def front(i, carry):
            rows = rows_of(i)
            value = tokens[rows, :].astype(f32) + lowmul(mixed[rows, :], out_ref[...]) + vecs[2:3, :]
            middle_ref[rows, :] = value
            second[rows, :] = layer_norm(value, vecs[3:4, :], vecs[4:5, :]).astype(bf16)
            return carry

        lax.fori_loop(0, steps, front, 0)
        d_second_ref[...] = jnp.zeros_like(d_second_ref)

    def block(i, total):
        rows = rows_of(i)
        hidden = lowmul(second[rows, :], up_ref[...]) + shift_ref[...]
        d_active = times_t(upstream[rows, :], down_ref[...])
        square = hidden * hidden
        curve = jnp.tanh(GELU_A * hidden * (1.0 + GELU_B * square))
        half = 0.5 * (1.0 + curve)
        active_ref[rows, :] = (hidden * half).astype(bf16)
        slope = half + 0.5 * hidden * (1.0 - curve * curve) * (GELU_A * (1.0 + 3.0 * GELU_B * square))
        d_hidden = (d_active * slope).astype(bf16)
        d_hidden_ref[rows, :] = d_hidden
        d_second_ref[rows, :] += times_t(d_hidden, up_ref[...])
        return total + jnp.sum(d_hidden.astype(f32), axis=0, keepdims=True)

    d_shift_ref[...] = lax.fori_loop(0, steps, block, jnp.zeros(d_shift_ref.shape, f32))

    @pl.when(last)
    def _():
        def back(i, sums):
            rows = rows_of(i)
            values = middle_ref[rows, :]
            grads = d_second_ref[rows, :]
            given = upstream[rows, :].astype(f32)
            center = values - jnp.mean(values, axis=-1, keepdims=True)
            scale = lax.rsqrt(jnp.mean(center * center, axis=-1, keepdims=True) + EPS)
            unit = center * scale
            scaled = grads * vecs[3:4, :]
            inner = scaled - jnp.mean(scaled, axis=-1, keepdims=True)
            inner = inner - unit * jnp.mean(scaled * unit, axis=-1, keepdims=True)
            value = scale * inner + given
            d_middle_ref[rows, :] = value
            branch = value.astype(bf16)
            d_mixed_ref[rows, :] = times_t(branch, out_ref[...])
            new = (branch.astype(f32), grads * unit, grads, given)
            return tuple(old + jnp.sum(one, axis=0, keepdims=True) for old, one in zip(sums, new))

        zero = jnp.zeros((1, D), f32)
        sums_ref[...] = jnp.zeros_like(sums_ref)
        for i, one in enumerate(lax.fori_loop(0, steps, back, (zero,) * 4)):
            sums_ref[i : i + 1, :] = one


def run_middle(mixed, tokens, upstream, out_full, vecs, up_full, up_shift, down_full):
    count = tokens.shape[0]
    units = up_full.shape[1]

    def fixed(*shape):
        return pl.BlockSpec(shape, lambda j: (0,) * len(shape), pipeline_mode=pl.Buffered(1))

    columns = pl.BlockSpec((count, HID), lambda j: (0, j))
    row = pl.BlockSpec((1, HID), lambda j: (0, j))
    tall = fixed(count, D)
    wide = jax.ShapeDtypeStruct((count, units), bf16)
    full = jax.ShapeDtypeStruct((count, D), f32)
    return pl.pallas_call(
        middle_kernel,
        grid=(units // HID,),
        in_specs=[
            tall, tall, tall, fixed(D, D), fixed(8, D), pl.BlockSpec((D, HID), lambda j: (0, j)), row,
            pl.BlockSpec((HID, D), lambda j: (j, 0)),
        ],
        out_specs=[tall, tall, columns, columns, tall, tall, fixed(8, D), row],
        out_shape=[
            full, jax.ShapeDtypeStruct((count, D), bf16), wide, wide, full, full, jax.ShapeDtypeStruct((8, D), f32),
            jax.ShapeDtypeStruct((1, units), f32),
        ],
        scratch_shapes=[pltpu.VMEM((count, D), f32)],
        compiler_params=pltpu.CompilerParams(vmem_limit_bytes=63 * 2**20),
        cost_estimate=pl.CostEstimate(
            flops=6 * count * D * units, bytes_accessed=40 * 2**20, transcendentals=count * units
        ),
        name="middle",
    )(mixed, tokens, upstream, out_full, vecs, up_full, up_shift, down_full)


def finish_kernel(
    small, result, d_tokens, down, up, out, inward,
    prompt_out, cont_out, prompt_grad, cont_grad,
    g_gain1, g_shift1, g_in, g_in_b, g_taps, g_short_b, g_long, g_w1, g_b1, g_w2, g_b2, g_w3,
    g_out, g_out_b, g_gain2, g_shift2, g_up, g_up_b, g_down, g_down_b,
):
    step = pl.program_id(0)
    for src, dst in ((down, g_down), (up, g_up), (out, g_out), (inward, g_in)):
        dst[...] = src[...].astype(f32)

    @pl.when(step % 2 == 0)
    def _():
        prompt_out[0, 0] = result[...]
        prompt_grad[0, 0] = d_tokens[...]

    @pl.when(step % 2 == 1)
    def _():
        for c in range(CONTS):
            cont_out[0, 0, c] = result[c * BLOCK : (c + 1) * BLOCK, :]
            cont_grad[0, 0, c] = d_tokens[c * BLOCK : (c + 1) * BLOCK, :]

    @pl.when(step == 0)
    def _():
        half = slice(D // 2, D)

        def lines(start, count, stride=1):
            rows = [small[0, start + stride * i : start + stride * i + 1, half] for i in range(count)]
            return jnp.concatenate(rows, axis=1)

        def put(ref, value):
            ref[...] = value.reshape(ref.shape)

        for i, ref in enumerate((g_out_b, g_gain2, g_shift2, g_down_b)):
            put(ref, lines(GIVEN_ROW + i, 1))
        put(g_up_b, lines(GIVEN_ROW + 4, 4))
        for i in range(3):
            g_taps[i : i + 1, :] = lines(TAP_ROW + i, 3, 8)
        put(g_short_b, lines(TAP_ROW + 3, 3, 8))
        put(g_in_b, lines(TAP_ROW + 4, 3, 8))
        g_long[...] = small[0, LONG_ROW : LONG_ROW + 2, half]
        put(g_gain1, lines(NORM_ROW, 1))
        put(g_shift1, lines(NORM_ROW + 1, 1))
        g_w3[...] = small[0, 0 : g_w3.shape[0], :]
        n1, wide = g_w1.shape
        g_w1[...] = small[0, 64 : 64 + n1, 0:wide]
        put(g_b1, small[0, 64 + n1 : 65 + n1, 0:wide])
        put(g_b2, small[0, 65 + n1 : 66 + n1, 0:wide])
        g_w2[...] = small[0, 64 : 64 + g_w2.shape[0], 128 : 128 + wide]


def finish(shapes, micros, small, result, d_tokens, down, up, out, inward):
    steps = 2 * micros

    def rows(value):
        return pl.BlockSpec((value.shape[0] // steps, value.shape[1]), lambda i: (i, 0))

    def fixed(value):
        return pl.BlockSpec(value.shape, lambda i: (0,) * len(value.shape))

    inputs = (small, result, d_tokens, down.reshape(-1, D), up, out, inward)
    prompt = pl.BlockSpec((1, 1, PROMPT, D), lambda i: (i // 2, 0, 0, 0))
    cont = pl.BlockSpec((1, 1, CONTS, BLOCK, D), lambda i: (i // 2, 0, 0, 0, 0))
    big = {6: inward, 16: out, 20: up, 22: down}
    specs = [prompt, cont, prompt, cont] + [rows(one) if i in big else fixed(one) for i, one in enumerate(shapes) if i > 3]
    return pl.pallas_call(
        finish_kernel,
        grid=(steps,),
        in_specs=[fixed(small)] + [rows(one) for one in inputs[1:]],
        out_specs=specs,
        out_shape=shapes,
        compiler_params=pltpu.CompilerParams(vmem_limit_bytes=63 * 2**20),
        name="finish",
    )(*inputs)


def per_device(
    prompt_x, cont_x, prompt_cot, cont_cot, norm1_gain, norm1_bias, in_weight, in_bias, short_weight,
    short_bias, long_bias, filter_w1, filter_b1, filter_w2, filter_b2, filter_w3, filter_decay, out_weight,
    out_bias, norm2_gain, norm2_bias, up_weight, up_bias, down_weight, down_bias, *, reps, shards,
):
    own_kernels = reps == 16 and shards == 2 and prompt_x.shape[1] == 1
    micros = prompt_x.shape[0]
    groups = prompt_x.shape[1]
    count = micros * groups * SPAN

    def tokens_of(prompt, cont):
        return jnp.concatenate(
            [
                prompt.reshape(micros * groups, PROMPT, D),
                cont.reshape(micros * groups, CONTS * BLOCK, D),
            ],
            axis=1,
        ).reshape(count, D)

    def parts_of(rows):
        rows = rows.reshape(micros, groups, SPAN, D)
        return rows[:, :, :PROMPT], rows[:, :, PROMPT:].reshape(micros, groups, CONTS, BLOCK, D)

    n1 = filter_w1.shape[0]
    n2 = filter_w2.shape[0]
    tokens_low = tokens_of(prompt_x, cont_x)
    upstream = tokens_of(prompt_cot, cont_cot)
    if own_kernels:
        (projected, mixed_low, hat1, hat2, mid, bank1, bank2, vecs, lines, up_shift, decay, fw2, fw3,
         pre1, act1, pre2, act2, normed_low, in_full, out_full, up_full, down_full) = gather_weights(
            norm1_gain, norm1_bias, in_bias, short_weight, short_bias, long_bias, filter_w1, filter_b1, filter_w2,
            filter_b2, filter_w3, filter_decay, out_bias, norm2_gain, norm2_bias, up_bias, down_bias,
            in_weight, out_weight, up_weight, down_weight, tokens_low,
        )
        states = (jnp.asarray(embed_table()), pre1, act1, pre2, act2)
    else:
        def gather(value, axis=0):
            return lax.all_gather(value, "shard", axis=axis, tiled=True)

        gain1, shift1, out_shift, gain2, shift2, down_shift, in_shift, short_shift, up_shift, decay, fb1, fb2 = (
            gather(one).astype(f32)
            for one in (norm1_gain, norm1_bias, out_bias, norm2_gain, norm2_bias, down_bias, in_bias, short_bias,
                        up_bias, filter_decay, filter_b1, filter_b2)
        )
        taps, long_shift, fw1, fw2, fw3 = (
            gather(one, 1).astype(f32) for one in (short_weight, long_bias, filter_w1, filter_w2, filter_w3)
        )
        in_full, out_full, up_full, down_full = (
            gather(one) for one in (by_tile(in_weight), out_weight, up_weight, down_weight)
        )
        up_shift = up_shift[None]
        lines = by_tile(jnp.concatenate([taps, short_shift[None], in_shift[None], jnp.zeros((3, D3), f32)], axis=0))
        vecs = jnp.stack([gain1, shift1, out_shift, gain2, shift2, down_shift])
        vecs = jnp.concatenate([vecs, long_shift], axis=0)
        filters, filter_pull = jax.vjp(partial(filter_taps, decay=decay), fw1, fb1, fw2, fb2, fw3)
        normed, norm_pull = jax.vjp(layer_norm, tokens_low.astype(f32), gain1, shift1)
        normed_low = normed.astype(bf16)
        projected = lowmul(normed_low, in_full) + lines[4]
        mixed_low, hat1, hat2, mid, bank1, bank2 = run_forward(projected, lines, vecs, filters)
    middle, second_low, active_low, d_hidden, d_middle, d_mixed, sums, d_up_shift = run_middle(
        mixed_low, tokens_low, upstream, out_full, vecs, up_full, up_shift, down_full
    )
    width = D // shards

    def by_shard(value):
        rows = value.shape[0]
        return value.reshape(rows, shards, -1).swapaxes(0, 1).reshape(shards, -1, width)

    given = jnp.concatenate(
        [by_shard(sums[:4]), by_shard(d_up_shift)], axis=1
    )
    if own_kernels:
        small, grad_down, grad_up, grad_out, grad_in, d_tokens, result = reduce_grads(
            given, active_low, upstream, second_low, d_hidden, mixed_low, d_middle, normed_low,
            tokens_low, middle, down_full, d_mixed, projected, lines, vecs, bank1, bank2, hat1, hat2, mid, in_full, decay, fw3, states, fw2,
        )
        args = (norm1_gain, norm1_bias, in_weight, in_bias, short_weight, short_bias, long_bias, filter_w1, filter_b1,
                filter_w2, filter_b2, filter_w3, out_weight, out_bias, norm2_gain, norm2_bias, up_weight, up_bias,
                down_weight, down_bias)
        shapes = [jax.ShapeDtypeStruct(one.shape, bf16) for one in (prompt_x, cont_x) * 2]
        shapes += [jax.ShapeDtypeStruct(one.shape, f32) for one in args]
        return tuple(finish(shapes, micros, small, result, d_tokens, grad_down, grad_up, grad_out, grad_in))
    else:
        def reduce(value, axis=0):
            value = lax.psum_scatter(value, "shard", scatter_dimension=axis, tiled=True)
            return lax.psum(value, "rep")

        result = (middle + lowmul(active_low, down_full) + down_shift).astype(bf16)
        prompt_out, cont_out = parts_of(result)
        d_proj, d_taps, d_long, d_filter1, d_filter2 = run_backward(
            d_mixed, projected, lines, vecs, bank1, bank2, hat1, hat2, mid
        )
        d_tokens, grad_gain1, grad_shift1 = norm_pull(times_t(d_proj, in_full))
        prompt_grad, cont_grad = parts_of((d_tokens + d_middle).astype(bf16))
        filter_grads_all = filter_pull(jnp.concatenate([d_filter1, d_filter2], axis=-1))
        narrow_own = [reduce(one, one.ndim - 1) for one in filter_grads_all[:4]]
        third_grad = reduce(filter_grads_all[4], 1)
        given = reduce(given)[0]
        tap_rows = reduce(by_part(d_taps[:5]), 1)
        long_rows = reduce(d_long, 1)
        norm_rows = reduce(jnp.stack([grad_gain1, grad_shift1]), 1)
        grad_down = reduce(inner_rows(active_low, upstream))
        grad_up = reduce(inner_rows(second_low, d_hidden))
        grad_out = reduce(inner_rows(mixed_low, d_middle.astype(bf16)))
        grad_in = by_part(reduce(inner_rows(normed_low, d_proj)))
    return (
        prompt_out,
        cont_out,
        prompt_grad,
        cont_grad,
        norm_rows[0],
        norm_rows[1],
        grad_in,
        tap_rows[4],
        tap_rows[:3],
        tap_rows[3],
        long_rows,
        *narrow_own,
        third_grad,
        grad_out,
        given[0],
        given[1],
        given[2],
        grad_up,
        given[4:].reshape(-1),
        grad_down,
        given[3],
    )


def solution(mesh):
    group4 = P(None, ("rep", "shard"), None, None)
    group5 = P(None, ("rep", "shard"), None, None, None)
    one, row, col = P("shard"), P("shard", None), P(None, "shard")
    grads = (one, one, row, one, col, one, col, col, one, col, one, col)
    rest = (row, one, one, one, row, one, row, one)
    return jax.shard_map(
        partial(per_device, reps=mesh.shape["rep"], shards=mesh.shape["shard"]),
        mesh=mesh,
        in_specs=(group4, group5, group4, group5) + grads + (one,) + rest,
        out_specs=(group4, group5, group4, group5) + grads + rest,
        check_vma=False,
    )
```

```python
from functools import partial
import math

import jax
import jax.numpy as jnp
import numpy as np
from jax import lax
from jax.experimental import pallas as pl
from jax.experimental.pallas import tpu as pltpu
from jax.sharding import PartitionSpec as P

D = 768
D3 = 3 * D
BANDS = 16
BLOCK = 128
PROMPT = 256
CONTS = 2
SEQ = 384
SPAN = PROMPT + CONTS * BLOCK
TILE = 256
FREQ = 2 * BLOCK

EPS = 1e-05
HIGH = lax.Precision.HIGHEST
f32 = jnp.float32
bf16 = jnp.bfloat16


def matmul(left_op, right_op):
    return jnp.dot(left_op, right_op, precision=HIGH, preferred_element_type=f32)


def lowmul(left_op, right_op):
    return jnp.dot(left_op, right_op, preferred_element_type=f32)


def inner_rows(left_op, right_op):
    return lax.dot_general(
        left_op, right_op, (((0,), (0,)), ((), ())), preferred_element_type=f32
    )


def times_t(left_op, right_op):
    return lax.dot_general(
        left_op, right_op, (((1,), (1,)), ((), ())), preferred_element_type=f32
    )


def layer_norm(values, norm_gain, norm_shift):
    center_val = values - jnp.mean(values, axis=-1, keepdims=True)
    spread = jnp.mean(center_val * center_val, axis=-1, keepdims=True)
    return center_val * lax.rsqrt(spread + EPS) * norm_gain + norm_shift


def dft_matrix():
    freq = np.arange(BLOCK)
    place = np.arange(BLOCK)
    angle = np.pi * ((2 * freq[:, None] + 1) * place[None, :] % (4 * BLOCK)) / FREQ
    return np.concatenate([np.cos(angle), -np.sin(angle)], axis=0)


def split3(matrix):
    matrix = matrix.astype(np.float32)
    high = matrix.astype(jnp.bfloat16)
    rest = (matrix - high.astype(np.float32)).astype(jnp.bfloat16)
    return np.concatenate([high, rest, high], axis=1)


def split_dot(triple, signal):
    high = signal.astype(bf16)
    rest = (signal - high.astype(f32)).astype(bf16)
    return jnp.dot(
        triple, jnp.concatenate([high, high, rest], axis=0), preferred_element_type=f32
    )


def cmul(left, right):
    lr, li = left[:BLOCK], left[BLOCK:]
    rr, ri = right[:BLOCK], right[BLOCK:]
    return jnp.concatenate([lr * rr - li * ri, lr * ri + li * rr], axis=0)


def cmul_conj(left, right):
    lr, li = left[:BLOCK], left[BLOCK:]
    rr, ri = right[:BLOCK], right[BLOCK:]
    return jnp.concatenate([lr * rr + li * ri, lr * ri - li * rr], axis=0)


def row_index():
    return lax.broadcasted_iota(jnp.int32, (BLOCK, TILE), 0)


def delayed(block, before, lag):
    rolled = pltpu.roll(block, lag, 0)
    if before is None:
        return jnp.where(row_index() >= lag, rolled, 0.0)
    return jnp.where(row_index() >= lag, rolled, pltpu.roll(before, lag, 0))


def advanced(block, after, lag):
    rolled = pltpu.roll(block, BLOCK - lag, 0)
    if after is None:
        return jnp.where(row_index() < BLOCK - lag, rolled, 0.0)
    return jnp.where(row_index() < BLOCK - lag, rolled, pltpu.roll(after, BLOCK - lag, 0))


BEFORE = (None, 0, 1, 1)


def part(index):
    return slice(index * TILE, (index + 1) * TILE)


def load_blocks(ref, cols=slice(None)):
    return [ref[i * BLOCK : (i + 1) * BLOCK, cols] for i in range(4)]


def short_blocks(z_ref, rows_ref, index):
    blocks = load_blocks(z_ref, part(index))
    taps = rows_ref[0:3, part(index)]
    shift = rows_ref[3:4, part(index)]
    outs = []
    for i in range(4):
        before = None if BEFORE[i] is None else blocks[BEFORE[i]]
        outs.append(
            taps[0:1] * blocks[i]
            + taps[1:2] * delayed(blocks[i], before, 1)
            + taps[2:3] * delayed(blocks[i], before, 2)
            + shift
        )
    return outs


def spectra(hats, bank):
    tail = cmul(bank[1], hats[1]) + cmul(bank[2], hats[0])
    return [
        cmul(bank[0], hats[0]),
        cmul(bank[0], hats[1]) + cmul(bank[1], hats[0]),
        cmul(bank[0], hats[2]) + tail,
        cmul(bank[0], hats[3]) + tail,
    ]


def adjoint_spectra(hats, bank):
    tail = hats[2] + hats[3]
    return [
        cmul_conj(bank[0], hats[0]) + cmul_conj(bank[1], hats[1]) + cmul_conj(bank[2], tail),
        cmul_conj(bank[0], hats[1]) + cmul_conj(bank[1], tail),
        cmul_conj(bank[0], hats[2]),
        cmul_conj(bank[0], hats[3]),
    ]


def bank_grads(hats, grads):
    tail = grads[2] + grads[3]
    zero = cmul_conj(hats[0], grads[0])
    for i in range(1, 4):
        zero = zero + cmul_conj(hats[i], grads[i])
    one = cmul_conj(hats[0], grads[1]) + cmul_conj(hats[1], tail)
    return [zero, one, cmul_conj(hats[0], tail)]


def signs():
    odd = lax.broadcasted_iota(jnp.int32, (BLOCK, TILE), 0) % 2
    return (1 - 2 * odd).astype(f32)


LONG1, LONG2 = slice(6, 7), slice(7, 8)


def make_bank(ahead, taps, bank_ref):
    hats = [split_dot(ahead, taps[o * BLOCK : (o + 1) * BLOCK, :] * (1.0 / BLOCK)) for o in range(3)]
    sign = signs()
    bank = [hats[0]]
    for o in (1, 2):
        prev = hats[o - 1]
        turned = jnp.concatenate([-sign * prev[BLOCK:], sign * prev[:BLOCK]], axis=0)
        bank.append(hats[o] + turned)
    for o in range(3):
        bank_ref[o] = bank[o]


def filter_grads(back, grads, out_ref):
    sign = signs()
    for o in range(3):
        one = grads[o]
        if o < 2:
            after = grads[o + 1]
            one = one + jnp.concatenate([sign * after[BLOCK:], -sign * after[:BLOCK]], axis=0)
        out_ref[o * BLOCK : (o + 1) * BLOCK, :] = split_dot(back, one) * (1.0 / BLOCK)


def mixer_forward(
    z_ref, rows_ref, long_ref, filter1, filter2, ahead_ref, back_ref,
    out_ref, hat1_ref, hat2_ref, mid_ref, bank1, bank2,
):
    @pl.when(pl.program_id(1) == 0)
    def _():
        make_bank(ahead_ref[...], filter1[...], bank1)
        make_bank(ahead_ref[...], filter2[...], bank2)

    forward_step(
        z_ref, rows_ref, long_ref, ahead_ref, back_ref, out_ref, hat1_ref, hat2_ref, mid_ref, bank1, bank2
    )


def forward_step(
    z_ref, rows_ref, long_ref, ahead_ref, back_ref, out_ref, hat1_ref, hat2_ref, mid_ref, bank1, bank2
):
    ahead = ahead_ref[...]
    back = back_ref[...]
    gate1 = short_blocks(z_ref, rows_ref, 1)
    value = short_blocks(z_ref, rows_ref, 2)
    sig1 = [gate1[i] * value[i] for i in range(4)]
    hats = []
    for i in range(4):
        hat = split_dot(ahead, sig1[i])
        hat1_ref[i] = hat
        hats.append(hat)
    wave = spectra(hats, [bank1[i] for i in range(3)])
    mid = []
    for i in range(4):
        one = split_dot(back, wave[i]) + long_ref[LONG1, :] * sig1[i]
        mid_ref[i * BLOCK : (i + 1) * BLOCK, :] = one
        mid.append(one)
    gate0 = short_blocks(z_ref, rows_ref, 0)
    sig2 = [gate0[i] * mid[i] for i in range(4)]
    hats = []
    for i in range(4):
        hat = split_dot(ahead, sig2[i])
        hat2_ref[i] = hat
        hats.append(hat)
    wave = spectra(hats, [bank2[i] for i in range(3)])
    for i in range(4):
        two = split_dot(back, wave[i]) + long_ref[LONG2, :] * sig2[i]
        out_ref[i * BLOCK : (i + 1) * BLOCK, :] = two.astype(bf16)


def mixer_backward(
    grad_ref, z_ref, rows_ref, long_ref, bank1, bank2, hat1_ref, hat2_ref, mid_ref,
    ahead_ref, back_ref,
    dz_ref, dtap_ref, dlong_ref, dfilt1_ref, dfilt2_ref, dbank1, dbank2,
):
    micro = pl.program_id(1)
    backward_step(
        micro == 0, micro == pl.num_programs(1) - 1, grad_ref, z_ref, rows_ref, long_ref, bank1, bank2,
        hat1_ref, hat2_ref, mid_ref, ahead_ref, back_ref,
        dz_ref, dtap_ref, dlong_ref, dfilt1_ref, dfilt2_ref, dbank1, dbank2,
    )


def backward_step(
    first, last, grad_ref, z_ref, rows_ref, long_ref, bank1, bank2, hat1_ref, hat2_ref, mid_ref,
    ahead_ref, back_ref,
    dz_ref, dtap_ref, dlong_ref, dfilt1_ref, dfilt2_ref, dbank1, dbank2,
):
    ahead = ahead_ref[...]
    back = back_ref[...]

    @pl.when(first)
    def _():
        dbank1[...] = jnp.zeros_like(dbank1)
        dbank2[...] = jnp.zeros_like(dbank2)
        dlong_ref[...] = jnp.zeros_like(dlong_ref)
        dtap_ref[...] = jnp.zeros_like(dtap_ref)

    def total(values):
        acc = values[0]
        for one in values[1:]:
            acc = acc + one
        return jnp.sum(acc, axis=0, keepdims=True)

    gate0 = short_blocks(z_ref, rows_ref, 0)
    grad2 = load_blocks(grad_ref)
    mid = load_blocks(mid_ref)
    dhats = [split_dot(ahead, grad2[i]) for i in range(4)]
    new = bank_grads([hat2_ref[i] for i in range(4)], dhats)
    for i in range(3):
        dbank2[i] += new[i]
    wave = adjoint_spectra(dhats, [bank2[i] for i in range(3)])
    dsig2 = [split_dot(back, wave[i]) + long_ref[LONG2, :] * grad2[i] for i in range(4)]
    dlong_ref[1:2, :] += total([grad2[i] * gate0[i] * mid[i] for i in range(4)])
    dgate0 = [dsig2[i] * mid[i] for i in range(4)]
    grad1 = [dsig2[i] * gate0[i] for i in range(4)]
    dhats = [split_dot(ahead, grad1[i]) for i in range(4)]
    new = bank_grads([hat1_ref[i] for i in range(4)], dhats)
    for i in range(3):
        dbank1[i] += new[i]
    wave = adjoint_spectra(dhats, [bank1[i] for i in range(3)])
    dsig1 = [split_dot(back, wave[i]) + long_ref[LONG1, :] * grad1[i] for i in range(4)]
    gate1 = short_blocks(z_ref, rows_ref, 1)
    value = short_blocks(z_ref, rows_ref, 2)
    dlong_ref[0:1, :] += total([grad1[i] * gate1[i] * value[i] for i in range(4)])
    dgate1 = [dsig1[i] * value[i] for i in range(4)]
    dvalue = [dsig1[i] * gate1[i] for i in range(4)]
    for index, grads in enumerate((dgate0, dgate1, dvalue)):
        cols = part(index)
        taps = rows_ref[0:3, cols]
        blocks = load_blocks(z_ref, cols)
        after = (grads[1], grads[2] + grads[3], None, None)
        dz = []
        for i in range(4):
            one = (
                taps[0:1] * grads[i]
                + taps[1:2] * advanced(grads[i], after[i], 1)
                + taps[2:3] * advanced(grads[i], after[i], 2)
            ).astype(bf16)
            dz_ref[i * BLOCK : (i + 1) * BLOCK, cols] = one
            dz.append(one.astype(f32))
        dtap_ref[4:5, cols] += total(dz)
        dtap_ref[3:4, cols] += total(grads)
        dtap_ref[0:1, cols] += total([grads[i] * blocks[i] for i in range(4)])
        for lag in (1, 2):
            dtap_ref[lag : lag + 1, cols] += total(
                [
                    grads[i]
                    * delayed(blocks[i], None if BEFORE[i] is None else blocks[BEFORE[i]], lag)
                    for i in range(4)
                ]
            )

    @pl.when(last)
    def _():
        filter_grads(back, [dbank1[i] for i in range(3)], dfilt1_ref)
        filter_grads(back, [dbank2[i] for i in range(3)], dfilt2_ref)


def constants():
    matrix = dft_matrix()
    return jnp.asarray(split3(matrix)), jnp.asarray(split3(matrix.T))


STEPS = D // TILE
AHEAD = (FREQ, 3 * BLOCK)
BACK = (BLOCK, 3 * FREQ)


def run_forward(z, lines, vecs, filters):
    rows = z.shape[0]
    blocks = rows // BLOCK

    def spec(shape, index):
        return pl.BlockSpec(shape, lambda t, m: index(m, t))

    hat_spec = spec((4, FREQ, TILE), lambda m, t: (m, 0, t))
    row_spec = spec((SPAN, TILE), lambda m, t: (m, t))
    bank_spec = spec((3, FREQ, TILE), lambda m, t: (0, 0, t))
    hat_shape = jax.ShapeDtypeStruct((blocks, FREQ, D), f32)
    bank_shape = jax.ShapeDtypeStruct((3, FREQ, D), f32)
    return pl.pallas_call(
        mixer_forward,
        grid=(STEPS, rows // SPAN),
        in_specs=[
            spec((SPAN, 3 * TILE), lambda m, t: (m, t)),
            spec((8, 3 * TILE), lambda m, t: (0, t)),
            spec((8, TILE), lambda m, t: (0, t)),
            spec((SEQ, TILE), lambda m, t: (0, t)),
            spec((SEQ, TILE), lambda m, t: (0, STEPS + t)),
            spec(AHEAD, lambda m, t: (0, 0)),
            spec(BACK, lambda m, t: (0, 0)),
        ],
        out_specs=[row_spec, hat_spec, hat_spec, row_spec, bank_spec, bank_spec],
        out_shape=[
            jax.ShapeDtypeStruct((rows, D), bf16), hat_shape, hat_shape,
            jax.ShapeDtypeStruct((rows, D), f32), bank_shape, bank_shape,
        ],
        compiler_params=pltpu.CompilerParams(vmem_limit_bytes=40 * 2**20),
        cost_estimate=pl.CostEstimate(flops=10 * 10**9, bytes_accessed=32 * 2**20, transcendentals=0),
        name="mixer_forward",
    )(z, lines, vecs, filters, filters, *constants())


def run_backward(grad, z, lines, vecs, bank1, bank2, hat1, hat2, mid):
    rows = z.shape[0]

    def spec(shape, index):
        return pl.BlockSpec(shape, lambda t, m: index(m, t))

    hat_spec = spec((4, FREQ, TILE), lambda m, t: (m, 0, t))
    row_spec = spec((SPAN, TILE), lambda m, t: (m, t))
    bank_spec = spec((3, FREQ, TILE), lambda m, t: (0, 0, t))
    z_spec = spec((SPAN, 3 * TILE), lambda m, t: (m, t))
    column_spec = spec((SEQ, TILE), lambda m, t: (0, t))
    return pl.pallas_call(
        mixer_backward,
        grid=(STEPS, rows // SPAN),
        in_specs=[
            row_spec,
            z_spec,
            spec((8, 3 * TILE), lambda m, t: (0, t)),
            spec((8, TILE), lambda m, t: (0, t)),
            bank_spec, bank_spec, hat_spec, hat_spec, row_spec,
            spec(AHEAD, lambda m, t: (0, 0)),
            spec(BACK, lambda m, t: (0, 0)),
        ],
        out_specs=[
            z_spec,
            spec((8, 3 * TILE), lambda m, t: (0, t)),
            spec((2, TILE), lambda m, t: (0, t)),
            column_spec,
            column_spec,
        ],
        out_shape=[
            jax.ShapeDtypeStruct((rows, D3), bf16), jax.ShapeDtypeStruct((8, D3), f32),
            jax.ShapeDtypeStruct((2, D), f32), jax.ShapeDtypeStruct((SEQ, D), f32),
            jax.ShapeDtypeStruct((SEQ, D), f32),
        ],
        scratch_shapes=[pltpu.VMEM((3, FREQ, TILE), f32), pltpu.VMEM((3, FREQ, TILE), f32)],
        compiler_params=pltpu.CompilerParams(vmem_limit_bytes=40 * 2**20),
        cost_estimate=pl.CostEstimate(flops=24 * 10**9, bytes_accessed=36 * 2**20, transcendentals=0),
        name="mixer_backward",
    )(grad, z, lines, vecs, bank1, bank2, hat1, hat2, mid, *constants())


def place_ratio():
    return (np.arange(SEQ).astype(np.float32) / np.float32(SEQ))[:, None]


def filter_states(first_w, first_b, second_w, second_b):
    levels = (np.arange(BANDS) + 1).astype(np.float32)
    ratio = jnp.asarray(place_ratio())
    angles = 2.0 * math.pi * ratio * jnp.asarray(levels)[None, :]
    embed = jnp.concatenate([ratio, jnp.cos(angles), jnp.sin(angles)], axis=1)
    first_pre = matmul(embed, first_w) + first_b
    first_act = jnp.sin(first_pre)
    second_pre = matmul(first_act, second_w) + second_b
    return embed, first_pre, first_act, second_pre, jnp.sin(second_pre)


def filter_taps(first_w, first_b, second_w, second_b, third_w, decay):
    second_act = filter_states(first_w, first_b, second_w, second_b)[-1]
    return matmul(second_act, third_w) * jnp.exp(-jnp.asarray(place_ratio()) * decay[None, :])


def by_tile(value):
    shape = value.shape
    return value.reshape(*shape[:-1], 3, STEPS, TILE).swapaxes(-3, -2).reshape(shape)


def by_part(value):
    shape = value.shape
    return value.reshape(*shape[:-1], STEPS, 3, TILE).swapaxes(-3, -2).reshape(shape)


MESH = pl.DeviceIdType.MESH


class Place:
    def __init__(self):
        rep = lax.axis_index("rep")
        self.rep = rep
        self.shard = lax.axis_index("shard")
        self.core = rep % 2
        self.side = (rep // 2) % 2
        self.depth = rep // 4
        self.quad = rep % 4
        self.eighth = rep % 8
        self.to_side = 2 - 4 * self.side
        self.to_depth = 4 - 8 * (self.depth % 2)

    def other_shard(self):
        return (self.rep, 1 - self.shard)

    def other_side(self):
        return (self.rep + 2 - 4 * self.side, self.shard)

    def near_depth(self):
        return (self.rep + self.to_depth, self.shard)

    def diagonal(self):
        return (self.rep + (1 - self.core) * self.to_side + self.core * self.to_depth, self.shard)

    def other_core(self):
        return (self.rep + 1 - 2 * self.core, self.shard)

    def other_depth(self, step):
        return (((self.depth + step) % 4) * 4 + self.quad, self.shard)


def greet(devices):
    barrier = pltpu.get_barrier_semaphore()
    for device in devices:
        pl.semaphore_signal(barrier, inc=1, device_id=device, device_id_type=MESH)
    pl.semaphore_wait(barrier, len(devices))


def remote(src, dst, send, recv, device):
    return pltpu.make_async_remote_copy(
        src_ref=src, dst_ref=dst, send_sem=send, recv_sem=recv, device_id=device, device_id_type=MESH
    )


UNITS = (
    (0, 0, 16), (0, 16, 16), (0, 32, 16), (1, 0, 48), (2, 0, 16), (2, 16, 16), (2, 32, 16), (3, 0, 96), (3, 96, 96),
)
STAGES = ("", "A3 A4", "A5 B3 B4", "A6 A7 B5 C3 C4", "A8 B6 B7 C5", "B8 C6 C7", "C8", "")
PACK_ROWS = 96
UP_ROW, DECAY_ROW, FIRST_ROW, SECOND_ROW = 23, 27, 32, 32


def column_moves():
    for s in range(2):
        for a in range(3):
            for b in range(3):
                at = s * (D3 // 2) + a * (D // 2) + b * 128
                yield s, a, b * 128, (at % D // TILE * 3 + at // D) * TILE + at % TILE


def gather_kernel(
    gain1, shift1, in_shift, short_w, short_b, long_b, w1, b1, w2, b2, third, decay, out_b, gain2, shift2, up_b,
    down_b, w_in, w_out, w_up, w_down, prompt_x, cont_x, prompt_g, cont_g, embed_ref, ratio_ref, ahead_ref, back_ref,
    z_ref, mixed_ref, hat1_ref, hat2_ref, mid_ref, bank1, bank2,
    vecs, lines, up_all, decay_all, second_all, third_all, pre1, act1, pre2, act2,
    normed_out, tokens_out, upstream_out, f_in, f_out, f_up, f_down,
    pack, packed, packs, thirds, in_v, normed_v,
    small_send, small_recv, own_sem, token_sem, ysend, yrecv, xsend, xrecv, zsend, zrecv, dsend, drecv, csend, crecv,
):
    tick = pl.program_id(0)
    place = Place()
    shard, mine = place.shard, place.eighth
    by_side, by_depth = mine + place.to_side, mine + place.to_depth
    by_both = by_side + place.to_depth
    locals_ = (w_in, w_out, w_up, w_down)
    fulls = (in_v, f_out, f_up, f_down)

    def rows_of(unit, shard_of, piece):
        weight, start, size = unit
        half = locals_[weight].shape[0]
        return pl.ds(pl.multiple_of(shard_of * half + piece * (half // 8) + start, 16), size)

    def local_rows(unit):
        weight, start, size = unit
        return pl.ds(pl.multiple_of(mine * (locals_[weight].shape[0] // 8) + start, 16), size)

    def smalls():
        return [
            remote(packed, packs.at[shard], small_send.at[0], small_recv.at[0], place.other_shard()),
            remote(third, thirds.at[shard], small_send.at[1], small_recv.at[1], place.other_shard()),
        ]

    def own_copies():
        copies = []
        for weight in range(1, 4):
            half = locals_[weight].shape[0]
            rows = pl.ds(pl.multiple_of(shard * half, 16), half)
            copies.append(pltpu.make_async_copy(locals_[weight], fulls[weight].at[rows, :], own_sem.at[weight]))
        return copies

    def token_copies():
        copies = []
        for to, parts in ((tokens_out, (prompt_x, cont_x)), (upstream_out, (prompt_g, cont_g))):
            for m in range(prompt_x.shape[0]):
                for i, ref in enumerate(parts):
                    rows = slice(m * SPAN + i * PROMPT, m * SPAN + (i + 1) * PROMPT)
                    copies.append(pltpu.make_async_copy(ref.at[m], to.at[rows, :], token_sem.at[len(copies)]))
        return copies

    def normed_copy():
        return pltpu.make_async_copy(normed_v, normed_out, own_sem.at[0])

    def in_copy():
        return pltpu.make_async_copy(in_v, f_in, own_sem.at[4])

    def moved(u, piece, send, recv, device):
        unit = UNITS[u]
        region = fulls[unit[0]].at[rows_of(unit, 1 - shard, piece), :]
        return remote(region, region, send, recv, device)

    def from_shard(u):
        return moved(u, mine, ysend.at[u], yrecv.at[u], place.other_shard())

    def side(u, piece):
        return moved(u, piece, xsend.at[u], xrecv.at[u], place.other_side())

    def depth(u, piece):
        return moved(u, piece, zsend.at[u], zrecv.at[u], place.near_depth())

    def diagonal(u, piece):
        return moved(u, piece, dsend.at[u], drecv.at[u], place.diagonal())

    def twin(u, index, piece):
        return moved(u, piece, csend.at[u, index], crecv.at[u, index], place.other_core())

    def exchanges(stages):
        for stage in stages.split():
            kind, u = stage[0], int(stage[1:])
            if kind == "A":
                from_shard(u).wait_recv()
                side(u, mine).start()
                depth(u, mine).start()
                twin(u, 0, mine).start()
            elif kind == "B":
                side(u, by_side).wait_recv()
                twin(u, 1, by_side).start()
                depth(u, by_depth).wait_recv()
                twin(u, 2, by_depth).start()
                diagonal(u, (1 - place.core) * by_depth + place.core * by_side).start()
            else:
                diagonal(u, by_both).wait_recv()
                twin(u, 3, by_both).start()

    def finish(u):
        for index, piece in enumerate((mine, by_side, by_depth, by_both)):
            twin(u, index, piece).wait()
        from_shard(u).wait_send()
        side(u, mine).wait_send()
        depth(u, mine).wait_send()
        diagonal(u, mine).wait_send()

    @pl.when(tick == 0)
    def _():
        greet([place.other_shard(), place.other_side(), place.near_depth(), place.other_core()])
        rows = pl.ds(pl.multiple_of(shard * (D // 2), 16), D // 2)
        for p in range(3):
            for t in range(STEPS):
                in_v[rows, part(t * 3 + p)] = w_in[:, part(p * STEPS + t)]

        def send_units(units):
            for u in units:
                weight = UNITS[u][0]
                to = fulls[weight].at[rows_of(UNITS[u], shard, mine), :]
                source = to if weight == 0 else locals_[weight].at[local_rows(UNITS[u]), :]
                remote(source, to, ysend.at[u], yrecv.at[u], place.other_shard()).start()

        send_units(range(3))
        pack[...] = jnp.zeros_like(pack)
        half = D // 2

        def row(ref):
            return ref[...].astype(f32).reshape(1, ref.shape[0])

        for i, ref in enumerate((gain1, shift1, out_b, gain2, shift2, down_b)):
            pack[i : i + 1, :] = row(ref)
        pack[6:8, :] = long_b[...].astype(f32)
        taps = short_w[...].astype(f32)
        for i, value in enumerate((row(in_shift), row(short_b), taps[0:1], taps[1:2], taps[2:3])):
            for a in range(3):
                pack[8 + 3 * i + a : 9 + 3 * i + a, :] = value[:, a * half : (a + 1) * half]
        value = row(up_b)
        for a in range(4):
            pack[UP_ROW + a : UP_ROW + a + 1, :] = value[:, a * half : (a + 1) * half]
        value = row(decay)
        for a in range(2):
            pack[DECAY_ROW + a : DECAY_ROW + a + 1, :] = value[:, a * half : (a + 1) * half]
        wide, n1 = w1.shape
        n2 = w2.shape[1]
        pack[FIRST_ROW : FIRST_ROW + n1, 0:wide] = w1[...].astype(f32).T
        pack[FIRST_ROW + n1 : FIRST_ROW + n1 + 1, 0:wide] = row(b1)
        pack[FIRST_ROW + n1 + 1 : FIRST_ROW + n1 + 2, 0:wide] = row(b2)
        pack[SECOND_ROW : SECOND_ROW + n2, 128 : 128 + wide] = w2[...].astype(f32).T
        packed[...] = pack[...].astype(bf16)
        for one in smalls():
            one.start()
        send_units(range(3, len(UNITS)))
        for one in own_copies() + token_copies():
            one.start()
        packs[shard] = packed[...]
        thirds[shard] = third[...]
        exchanges("A0 A1 A2")
        for one in smalls():
            one.wait()

        both = [packs[s].astype(f32) for s in range(2)]
        for i in range(8):
            for s in range(2):
                vecs[i : i + 1, s * half : (s + 1) * half] = both[s][i : i + 1]
        lines[...] = jnp.zeros_like(lines)
        for s, a, b, to in column_moves():
            for i, line in enumerate((4, 3, 0, 1, 2)):
                at = 8 + 3 * i + a
                lines[line : line + 1, to : to + 128] = both[s][at : at + 1, b : b + 128]
        for s in range(2):
            for a in range(4):
                to = s * (2 * D) + a * half
                up_all[0:1, to : to + half] = both[s][UP_ROW + a : UP_ROW + a + 1]
            for a in range(2):
                to = s * D + a * half
                decay_all[0:1, to : to + half] = both[s][DECAY_ROW + a : DECAY_ROW + a + 1]
            third_all[:, s * D : (s + 1) * D] = thirds[s].astype(f32)

        def narrow(rows, cols):
            return jnp.concatenate([both[s][rows, cols] for s in range(2)], axis=1)

        first_w = narrow(slice(FIRST_ROW, FIRST_ROW + n1), slice(0, wide))
        first_b = narrow(slice(FIRST_ROW + n1, FIRST_ROW + n1 + 1), slice(0, wide))
        second_b = narrow(slice(FIRST_ROW + n1 + 1, FIRST_ROW + n1 + 2), slice(0, wide))
        second_w = narrow(slice(SECOND_ROW, SECOND_ROW + n2), slice(128, 128 + wide))
        second_all[...] = second_w
        exchanges("B0 B1 B2")
        straight = ((1,), (0,))
        pre1[...] = exact(embed_ref[...], first_w, straight) + first_b
        act1[...] = jnp.sin(pre1[...])
        pre2[...] = exact(act1[...], second_w, straight) + second_b
        act2[...] = jnp.sin(pre2[...])

        exchanges("C0 C1 C2")

        for i, ref in enumerate((prompt_x, cont_x)):
            def norm_rows(step, carry):
                m, h = step // 2, step % 2
                values = ref[m, pl.ds(pl.multiple_of(h * 128, 128), 128), :].astype(f32)
                rows = pl.ds(pl.multiple_of(m * SPAN + i * PROMPT + h * 128, 128), 128)
                normed_v[rows, :] = layer_norm(values, vecs[0:1, :], vecs[1:2, :]).astype(bf16)
                return carry

            lax.fori_loop(0, 2 * ref.shape[0], norm_rows, 0)
        normed_copy().start()
        for u in range(3):
            finish(u)
        in_copy().start()

    for index in range(1, len(STAGES)):
        @pl.when(tick == index)
        def _():
            exchanges(STAGES[index])

    @pl.when(tick > 0)
    def _():
        step = jnp.maximum(tick - 1, 0)
        tile = step // 2
        micro = step % 2
        cols = pl.ds(pl.multiple_of(tile * 3 * TILE, 3 * TILE), 3 * TILE)
        few = pl.ds(pl.multiple_of(tile * TILE, TILE), TILE)
        rows = pl.ds(pl.multiple_of(micro * SPAN, SPAN), SPAN)

        @pl.when(tick <= 2 * STEPS)
        def _():
            @pl.when(micro == 0)
            def _():
                for q, bank in enumerate((bank1, bank2)):
                    those = pl.ds(pl.multiple_of(q * D + tile * TILE, TILE), TILE)
                    window = jnp.exp(-ratio_ref[...] * decay_all[:, those])
                    taps = exact(act2[...], third_all[:, those], ((1,), (0,))) * window
                    make_bank(ahead_ref[...], taps, bank)

            z_ref[...] = lowmul(normed_v[rows, :], in_v[:, cols]) + lines[4:5, cols]
            forward_step(
                z_ref, lines.at[:, cols], vecs.at[:, few], ahead_ref, back_ref,
                mixed_ref, hat1_ref, hat2_ref, mid_ref, bank1, bank2,
            )

    @pl.when(tick == 2 * STEPS + 1)
    def _():
        for u in range(3, len(UNITS)):
            finish(u)
        normed_copy().wait()
        in_copy().wait()
        for one in own_copies() + token_copies():
            one.wait()


def embed_table():
    ratio = place_ratio()
    angles = 2.0 * math.pi * ratio * (np.arange(BANDS) + 1).astype(np.float32)[None, :]
    return np.concatenate([ratio, np.cos(angles), np.sin(angles)], axis=1).astype(np.float32)


def gather_weights(*values):
    w1, w2, w3 = values[6], values[8], values[10]
    weights = values[17:21]
    micros = values[21].shape[0]
    count = micros * SPAN
    hidden = w2.shape[1]
    vmem = lambda one: pl.BlockSpec(one.shape, lambda t: (0,) * one.ndim, pipeline_mode=pl.Buffered(1))
    hbm = pl.BlockSpec(memory_space=pl.ANY)
    units = len(UNITS)
    embed, ratio = jnp.asarray(embed_table()), jnp.asarray(place_ratio())
    inputs = (*values, embed, ratio, *constants())

    def at_tile(shape, where):
        def index(t):
            step = jnp.minimum(jnp.maximum(t - 1, 0), 2 * STEPS - 1)
            return where(step % 2, step // 2)

        return pl.BlockSpec(shape, index)

    def doubled(value):
        return jax.ShapeDtypeStruct((2 * value.shape[0], *value.shape[1:]), value.dtype)

    def shape(*dims, kind=f32):
        return jax.ShapeDtypeStruct(dims, kind)

    fixed = [
        shape(8, D), shape(8, D3), shape(1, weights[2].shape[1]), shape(1, 2 * w3.shape[1]), shape(hidden, hidden),
        shape(hidden, 2 * w3.shape[1]),
    ] + [shape(SEQ, hidden)] * 4
    blocks = count // BLOCK
    hat_spec = at_tile((4, FREQ, TILE), lambda m, t: (m, 0, t))
    row_spec = at_tile((SPAN, TILE), lambda m, t: (m, t))
    bank_spec = at_tile((3, FREQ, TILE), lambda m, t: (0, 0, t))
    return pl.pallas_call(
        gather_kernel,
        grid=(2 * STEPS + 2,),
        in_specs=[vmem(one) for one in inputs],
        out_specs=[
            at_tile((SPAN, 3 * TILE), lambda m, t: (m, t)), row_spec, hat_spec, hat_spec, row_spec, bank_spec,
            bank_spec,
        ]
        + [vmem(one) for one in fixed] + [hbm] * 7,
        out_shape=[
            shape(count, D3), shape(count, D, kind=bf16), shape(blocks, FREQ, D), shape(blocks, FREQ, D),
            shape(count, D), shape(3, FREQ, D), shape(3, FREQ, D),
        ]
        + fixed + [shape(count, D, kind=bf16)] * 3 + [doubled(one) for one in weights],
        scratch_shapes=[
            pltpu.VMEM((PACK_ROWS, D // 2), f32),
            pltpu.VMEM((PACK_ROWS, D // 2), bf16),
            pltpu.VMEM((2, PACK_ROWS, D // 2), bf16),
            pltpu.VMEM((2, *w3.shape), bf16),
            pltpu.VMEM((D, D3), bf16),
            pltpu.VMEM((count, D), bf16),
        ]
        + [pltpu.SemaphoreType.DMA((2,))] * 2
        + [pltpu.SemaphoreType.DMA((5,)), pltpu.SemaphoreType.DMA((4 * micros,))]
        + [pltpu.SemaphoreType.DMA((units,))] * 8
        + [pltpu.SemaphoreType.DMA((units, 4))] * 2,
        compiler_params=pltpu.CompilerParams(
            collective_id=0, has_side_effects=True, vmem_limit_bytes=63 * 2**20
        ),
        name="gather_weights",
    )(*inputs)


class Reduction:
    def __init__(self, place, first, count, rows, bufs, sems, out):
        self.place = place
        self.first = first
        self.count = count
        self.rows = rows
        self.dtype = bufs[0].dtype
        self.whole, self.from_core, self.half, self.from_shard, self.own, self.from_side, self.mine, self.from_depth, self.back = bufs
        (self.s_core, self.r_core, self.s_shard, self.r_shard, self.s_side, self.r_side, self.s_depth, self.r_depth,
         self.s_gd, self.r_gd, self.s_gs, self.r_gs, self.s_gc, self.r_gc, self.s_own) = sems
        self.out = out

    def when(self, tick, lag, body):
        k = tick - self.first - lag

        @pl.when((k >= 0) & (k < self.count))
        def _():
            body(k, k % 2)

    def slot(self, ref, k):
        return ref.at[k % ref.shape[0]]

    def rows_at(self, index, size):
        return pl.ds(pl.multiple_of(index * size, size), size)

    def core_copy(self, k, slot):
        p = self.place
        return remote(
            self.whole.at[slot, :, self.rows_at(1 - p.core, self.rows // 2), :],
            self.slot(self.from_core, k), self.s_core.at[k], self.r_core.at[k], p.other_core(),
        )

    def shard_copy(self, k, slot):
        p = self.place
        return remote(
            self.half.at[slot, 1 - p.shard], self.slot(self.from_shard, k), self.s_shard.at[k], self.r_shard.at[k],
            p.other_shard(),
        )

    def side_copy(self, k, slot):
        p = self.place
        return remote(
            self.own.at[slot, self.rows_at(1 - p.side, self.rows // 4), :],
            self.slot(self.from_side, k), self.s_side.at[k], self.r_side.at[k], p.other_side(),
        )

    def quarter(self, base, index):
        rows = self.rows // 8
        return (
            pl.ds(pl.multiple_of(base + (index // 2) * rows, rows), rows),
            pl.ds(pl.multiple_of((index % 2) * (D // 2), D // 2), D // 2),
        )

    def depth_copy(self, k, slot, step):
        p = self.place
        rows, cols = self.quarter(0, (p.depth + step) % 4)
        return remote(
            self.mine.at[slot, rows, cols], self.from_depth.at[k % self.from_depth.shape[0], step - 1],
            self.s_depth.at[k, step - 1], self.r_depth.at[k, step - 1], p.other_depth(step),
        )

    def depth_back(self, k, step):
        p = self.place
        rows, cols = self.quarter(p.side * (self.rows // 4), p.depth)
        region = self.back.at[k % self.back.shape[0], rows, cols]
        return remote(
            region, region, self.s_gd.at[k, step - 1], self.r_gd.at[k, step - 1], p.other_depth(step)
        )

    def side_back(self, k):
        p = self.place
        region = self.back.at[k % self.back.shape[0], self.rows_at(p.side, self.rows // 4), :]
        return remote(region, region, self.s_gs.at[k], self.r_gs.at[k], p.other_side())

    def homes(self, k, place_in):
        rows = pl.ds(pl.multiple_of(self.place.core * (self.rows // 2), self.rows // 2), self.rows // 2)
        return [(cols, ref.at[(*lead, rows, *tail)]) for cols, ref, lead, tail in place_in]

    def send_home(self, k, place_in):
        p = self.place
        for cols, region in self.homes(k, place_in):
            piece = self.back.at[k % self.back.shape[0], :, cols]
            remote(piece, region, self.s_gc.at[k], self.r_gc.at[k], p.other_core()).start()
            pltpu.make_async_copy(piece, region, self.s_own.at[k]).start()

    def wait_home(self, k):
        whole = self.slot(self.back, k)
        remote(whole, whole, self.s_gc.at[k], self.r_gc.at[k], self.place.other_core()).wait()
        pltpu.make_async_copy(whole, whole, self.s_own.at[k]).wait()

    def add(self, left, right):
        return (left.astype(f32) + right.astype(f32)).astype(self.dtype)

    def send(self, tick):
        self.when(tick, 0, lambda k, slot: self.core_copy(k, slot).start())

    def advance(self, tick):
        p = self.place

        def after_core(k, slot):
            self.core_copy(k, slot).wait()
            for s in range(2):
                self.half[slot, s] = self.add(
                    self.whole[slot, s, self.rows_at(p.core, self.rows // 2), :], self.from_core[k % self.from_core.shape[0], s]
                )
            self.shard_copy(k, slot).start()

        def after_shard(k, slot):
            self.shard_copy(k, slot).wait()
            self.own[slot] = self.add(self.half[slot, p.shard], self.from_shard[k % self.from_shard.shape[0]])
            self.side_copy(k, slot).start()

        def after_side(k, slot):
            self.side_copy(k, slot).wait()
            self.mine[slot] = self.add(
                self.own[slot, self.rows_at(p.side, self.rows // 4), :], self.from_side[k % self.from_side.shape[0]]
            )
            for step in range(1, 4):
                self.depth_copy(k, slot, step).start()

        def after_depth(k, slot):
            for step in range(1, 4):
                self.depth_copy(k, slot, step).wait()
            rows, cols = self.quarter(0, p.depth)
            total = self.mine[slot, rows, cols].astype(f32)
            for step in range(3):
                total = total + self.from_depth[k % self.from_depth.shape[0], step].astype(f32)
            rows, cols = self.quarter(p.side * (self.rows // 4), p.depth)
            self.back[k % self.back.shape[0], rows, cols] = total.astype(self.dtype)
            for step in range(1, 4):
                self.depth_back(k, step).start()

        def after_depth_back(k, slot):
            for step in range(1, 4):
                self.depth_back(k, step).wait()
            self.side_back(k).start()

        def after_side_back(k, slot):
            self.side_back(k).wait()
            self.out(self, k)

        def after_core_back(k, slot):
            self.wait_home(k)

        for lag, body in enumerate(
            (after_core, after_shard, after_side, after_depth, after_depth_back, after_side_back, after_core_back), 1
        ):
            self.when(tick, lag, body)


LAGS = 7
DOWN, UP, OUT, IN = 4, 4, 1, STEPS
CHUNKS = DOWN + UP + OUT + IN
SMALL_ROWS = 128
SMALL_TICK = 9
ROW_BLOCK = 128


GIVEN_ROW, TAP_ROW, LONG_ROW, NORM_ROW = 64, 72, 96, 98


def exact(left, right, dims):
    return lax.dot_general(left, right, (dims, ((), ())), precision=HIGH, preferred_element_type=f32)


def reduce_kernel(
    sums, d_shift, active0, active1, upstream, second_h, d_hidden, mixed_h, d_middle_h, normed_h, tokens_h, gain, middle, down0, down1,
    grad_ref, z_ref, rows_ref, long_ref, bank1, bank2, hat1_ref, hat2_ref, mid_ref, ahead_ref, back_ref,
    in_ref, decay_ref, decay2_ref, third1_ref, third2_ref, ratio_ref, embed_ref, pre1_ref, act1_ref, pre2_ref, act2_ref,
    second_w_ref,
    small_out, g_down, g_up, g_out, g_in, tokens_out, result_out,
    d_proj, dtap, dtaps, dlong, dlongs, dfilt1, dfilt2, dbank1, dbank2, d_normed, d_act, out_rows, out_sem, middle_sem,
    second, mixed, d_middle, normed, tokens, late_sem, *scratch,
):
    tick = pl.program_id(0)
    place = Place()
    bufs, sems = scratch[:9], scratch[9:24]
    small_bufs, small_sems = scratch[24:33], scratch[33:48]
    everything = slice(None)
    is_in = (tick % 3 == 2) & (tick < 9)
    tile = tick // 3

    def little_home(chain, k):
        chain.send_home(k, [(everything, small_out, (k,), (everything,))])

    def kinds(k):
        down = (k < 5) & (k % 3 < 2)
        up = ((k >= 6) & (k < 8)) | (k >= 10)
        return down, up, k == 9, (k < 9) & (k % 3 == 2)

    def big_home(chain, k):
        down, up, out, inward = kinds(k)

        @pl.when(down)
        def _():
            chain.send_home(k, [(everything, g_down, (k - k // 3,), (everything,))])

        @pl.when(up)
        def _():
            index = k - 6 - 2 * (k // 9)
            cols = pl.ds(pl.multiple_of(index * D, D), D)
            chain.send_home(k, [(everything, g_up, (), (cols,))])

        @pl.when(out)
        def _():
            chain.send_home(k, [(everything, g_out, (), (everything,))])

        @pl.when(inward)
        def _():
            chain.send_home(
                k,
                [
                    (part(p), g_in, (), (pl.ds(pl.multiple_of(p * D + (k // 3) * TILE, TILE), TILE),))
                    for p in range(3)
                ],
            )

    little = Reduction(place, SMALL_TICK, 1, SMALL_ROWS, small_bufs, small_sems, little_home)
    big = Reduction(place, 0, CHUNKS, D // 2, bufs, sems, big_home)
    pack = little.whole
    late = [
        pltpu.make_async_copy(src, dst, late_sem.at[i])
        for i, (src, dst) in enumerate(
            ((normed_h, normed), (second_h, second), (mixed_h, mixed), (d_middle_h, d_middle), (tokens_h, tokens))
        )
    ]

    @pl.when(tick == 0)
    def _():
        for one in late:
            one.start()
        greet(
            [place.other_shard(), place.other_side(), place.other_core()]
            + [place.other_depth(step) for step in range(1, 4)]
        )
        pack[...] = jnp.zeros_like(pack)
        for s in range(2):
            pack[0, s, GIVEN_ROW : GIVEN_ROW + 4, D // 2 :] = sums[0:4, s * (D // 2) : (s + 1) * (D // 2)]
            for a in range(4):
                at = s * 2 * D + a * (D // 2)
                pack[0, s, GIVEN_ROW + 4 + a : GIVEN_ROW + 5 + a, D // 2 :] = d_shift[0:1, at : at + D // 2]
        d_act[...] = jnp.zeros_like(d_act)

    little.advance(tick)
    big.advance(tick)

    def chunk(slot, lefts, right):
        for s in range(2):
            big.whole[slot, s] = inner_rows(lefts[s], right).astype(bf16)

    def halves(left):
        return left[:, : D // 2], left[:, D // 2 :]

    def compute(k, slot):
        down, up, out, inward = kinds(k)

        @pl.when(down)
        def _():
            chunk(slot, (active0[...], active1[...]), upstream[...])

        @pl.when(up)
        def _():
            chunk(slot, halves(second), d_hidden[...])

        @pl.when(out)
        def _():
            chunk(slot, halves(mixed), d_middle[...].astype(bf16))

        @pl.when(inward)
        def _():
            chunk(slot, halves(normed), d_proj[...])

    for first, those in ((2, late[:1]), (6, late[1:2]), (SMALL_TICK, late[2:])):
        @pl.when(tick == first)
        def _():
            for one in those:
                one.wait()

    big.when(tick, 0, compute)
    big.send(tick)

    @pl.when((tick < 8) & (tick % 3 < 2))
    def _():
        micro = tick % 3
        backward_step(
            micro == 0, micro == 1, grad_ref, z_ref, rows_ref, long_ref, bank1, bank2,
            hat1_ref, hat2_ref, mid_ref, ahead_ref, back_ref,
            d_proj.at[pl.ds(pl.multiple_of(micro * SPAN, SPAN), SPAN), :], dtap, dlong, dfilt1, dfilt2, dbank1, dbank2,
        )

    @pl.when(is_in)
    def _():
        cols = pl.ds(pl.multiple_of(tile * TILE, TILE), TILE)
        dtaps[tile] = dtap[...]
        dlongs[:, cols] = dlong[...]
        step = times_t(d_proj[...], in_ref[...])

        @pl.when(tile == 0)
        def _():
            d_normed[...] = step

        @pl.when(tile > 0)
        def _():
            d_normed[...] += step

        for q, (grads, decay, third) in enumerate(
            ((dfilt1, decay_ref, third1_ref), (dfilt2, decay2_ref, third2_ref))
        ):
            window = jnp.exp(-ratio_ref[...] * decay[...])
            d_taps = grads[...] * window
            pack[0, q, 0 : act2_ref.shape[1], cols] = exact(act2_ref[...], d_taps, ((0,), (0,)))
            d_act[...] += exact(d_taps, third[...], ((1,), (1,)))

    @pl.when(tick == SMALL_TICK)
    def _():
        for s in range(2):
            for a in range(3):
                for b in range(3):
                    at = s * (D3 // 2) + a * (D // 2) + b * 128
                    p, t, o = at // D, at % D // TILE, at % TILE
                    pack[0, s, TAP_ROW + 8 * a : TAP_ROW + 8 * a + 8, D // 2 + b * 128 : D // 2 + b * 128 + 128] = dtaps[
                        t, :, p * TILE + o : p * TILE + o + 128
                    ]
            pack[0, s, LONG_ROW : LONG_ROW + 2, D // 2 :] = dlongs[:, s * (D // 2) : (s + 1) * (D // 2)]

        def norm_rows(i, sums):
            rows = pl.ds(pl.multiple_of(i * ROW_BLOCK, ROW_BLOCK), ROW_BLOCK)
            values = tokens[rows, :].astype(f32)
            grads = d_normed[rows, :]
            center = values - jnp.mean(values, axis=-1, keepdims=True)
            scale = lax.rsqrt(jnp.mean(center * center, axis=-1, keepdims=True) + EPS)
            unit = center * scale
            scaled = grads * gain[0:1, :]
            inner = scaled - jnp.mean(scaled, axis=-1, keepdims=True)
            inner = inner - unit * jnp.mean(scaled * unit, axis=-1, keepdims=True)
            out_rows[rows, :] = (scale * inner + d_middle[rows, :]).astype(bf16)
            return (
                sums[0] + jnp.sum(grads * unit, axis=0, keepdims=True),
                sums[1] + jnp.sum(grads, axis=0, keepdims=True),
            )

        zero = jnp.zeros((1, D), f32)
        sums = lax.fori_loop(0, tokens.shape[0] // ROW_BLOCK, norm_rows, (zero, zero))
        d_pre2 = d_act[...] * jnp.cos(pre2_ref[...])
        g_second = exact(act1_ref[...], d_pre2, ((0,), (0,)))
        g_b2 = jnp.sum(d_pre2, axis=0, keepdims=True)
        d_pre1 = exact(d_pre2, second_w_ref[...], ((1,), (1,))) * jnp.cos(pre1_ref[...])
        g_first = exact(embed_ref[...], d_pre1, ((0,), (0,)))
        g_b1 = jnp.sum(d_pre1, axis=0, keepdims=True)
        wide = g_second.shape[1] // 2
        for s in range(2):
            own = slice(s * wide, (s + 1) * wide)
            for i in range(2):
                pack[0, s, NORM_ROW + i : NORM_ROW + i + 1, D // 2 :] = sums[i][:, s * (D // 2) : (s + 1) * (D // 2)]
            pack[0, s, 64 : 64 + g_first.shape[0], 0:wide] = g_first[:, own]
            pack[0, s, 64 + g_first.shape[0] : 65 + g_first.shape[0], 0:wide] = g_b1[:, own]
            pack[0, s, 65 + g_first.shape[0] : 66 + g_first.shape[0], 0:wide] = g_b2[:, own]
            pack[0, s, 64 : 64 + g_second.shape[0], 128 : 128 + wide] = g_second[:, own]
        pltpu.make_async_copy(out_rows, tokens_out, out_sem).start()

    little.send(tick)

    @pl.when(tick == SMALL_TICK + 2)
    def _():
        pltpu.make_async_copy(out_rows, tokens_out, out_sem).wait()
        pltpu.make_async_copy(middle, d_normed, middle_sem).start()

    @pl.when((tick >= CHUNKS) & (tick < CHUNKS + DOWN))
    def _():
        @pl.when(tick == CHUNKS)
        def _():
            pltpu.make_async_copy(middle, d_normed, middle_sem).wait()

        def result_rows(i, carry):
            rows = pl.ds(pl.multiple_of(i * 256, 256), 256)
            total = d_normed[rows, :] + lowmul(active0[rows, :], down0[...]) + lowmul(active1[rows, :], down1[...])
            d_normed[rows, :] = total

            @pl.when(tick == CHUNKS + DOWN - 1)
            def _():
                out_rows[rows, :] = (total + gain[5:6, :]).astype(bf16)

            return carry

        lax.fori_loop(0, out_rows.shape[0] // 256, result_rows, 0)

        @pl.when(tick == CHUNKS + DOWN - 1)
        def _():
            pltpu.make_async_copy(out_rows, result_out, out_sem).start()

    @pl.when(tick == CHUNKS + LAGS - 1)
    def _():
        pltpu.make_async_copy(out_rows, result_out, out_sem).wait()


def reduce_grads(
    sums, d_shift, active, upstream, second, d_hidden, mixed, d_middle, normed, tokens, middle, down_full,
    d_mixed, z, lines, vecs, bank1, bank2, hat1, hat2, mid, in_full, decay, third_w, states, second_w,
):
    count = upstream.shape[0]
    half = D // 2
    hidden = second_w.shape[0]
    embed, pre1, act1, pre2, act2 = states

    def fixed(shape):
        return pl.BlockSpec(shape, lambda t: (0,) * len(shape), pipeline_mode=pl.Buffered(1))

    def at_tile(shape, where):
        def index(t):
            tick = jnp.minimum(t, 8)
            return where(jnp.minimum(tick % 3, 1), tick // 3)

        return pl.BlockSpec(shape, index)

    hbm = pl.BlockSpec(memory_space=pl.ANY)

    def down_index(t):
        tick = jnp.minimum(t, 4)
        late = jnp.minimum(jnp.maximum(t - (CHUNKS - 1), 0), 1)
        return tick - tick // 3 - 3 * late + late_index(t)

    def late_index(t):
        return jnp.minimum(jnp.maximum(t - CHUNKS, 0), DOWN - 1)

    def up_index(t):
        return jnp.minimum(jnp.maximum(t - 6, 0), 2) + jnp.minimum(jnp.maximum(t - 10, 0), 1)

    hat_spec = at_tile((4, FREQ, TILE), lambda m, t: (m, 0, t))
    row_spec = at_tile((SPAN, TILE), lambda m, t: (m, t))
    bank_spec = at_tile((3, FREQ, TILE), lambda m, t: (0, 0, t))
    decay_shape = (1, TILE)

    def buffers(n, rows, kind):
        few, many = min(n, 4), min(n, 8)
        return [
            pltpu.VMEM((min(n, 2), 2, rows, D), kind),
            pltpu.VMEM((few, 2, rows // 2, D), kind),
            pltpu.VMEM((min(n, 2), 2, rows // 2, D), kind),
            pltpu.VMEM((few, rows // 2, D), kind),
            pltpu.VMEM((min(n, 2), rows // 2, D), kind),
            pltpu.VMEM((few, rows // 4, D), kind),
            pltpu.VMEM((min(n, 2), rows // 4, D), kind),
            pltpu.VMEM((few, 3, rows // 8, D // 2), kind),
            pltpu.VMEM((many, rows // 2, D), kind),
        ]

    def semaphores(n):
        one = pltpu.SemaphoreType.DMA((n,))
        three = pltpu.SemaphoreType.DMA((n, 3))
        return [one] * 6 + [three] * 4 + [one] * 5

    return pl.pallas_call(
        reduce_kernel,
        grid=(CHUNKS + LAGS,),
        in_specs=[
            fixed(sums.shape),
            fixed(d_shift.shape),
            pl.BlockSpec((count, half), lambda t: (0, down_index(t))),
            pl.BlockSpec((count, half), lambda t: (0, DOWN + down_index(t))),
            fixed((count, D)),
            hbm,
            pl.BlockSpec((count, D), lambda t: (0, up_index(t))),
            hbm, hbm, hbm, hbm,
            fixed((8, D)),
            pl.BlockSpec(memory_space=pl.ANY),
            pl.BlockSpec((half, D), lambda t: (late_index(t), 0)),
            pl.BlockSpec((half, D), lambda t: (DOWN + late_index(t), 0)),
            row_spec,
            at_tile((SPAN, 3 * TILE), lambda m, t: (m, t)),
            at_tile((8, 3 * TILE), lambda m, t: (0, t)),
            at_tile((8, TILE), lambda m, t: (0, t)),
            bank_spec, bank_spec, hat_spec, hat_spec, row_spec,
            fixed(AHEAD),
            fixed(BACK),
            at_tile((D, 3 * TILE), lambda m, t: (0, t)),
            at_tile(decay_shape, lambda m, t: (0, t)),
            at_tile(decay_shape, lambda m, t: (0, STEPS + t)),
            at_tile((hidden, TILE), lambda m, t: (0, t)),
            at_tile((hidden, TILE), lambda m, t: (0, STEPS + t)),
            fixed((SEQ, 1)),
            fixed(embed.shape),
            fixed(pre1.shape),
            fixed(act1.shape),
            fixed(pre2.shape),
            fixed(act2.shape),
            fixed(second_w.shape),
        ],
        out_specs=[pl.BlockSpec(memory_space=pl.ANY)] * 7,
        out_shape=[
            jax.ShapeDtypeStruct((1, SMALL_ROWS, D), f32),
            jax.ShapeDtypeStruct((DOWN, half, D), bf16),
            jax.ShapeDtypeStruct((half, UP * D), bf16),
            jax.ShapeDtypeStruct((half, D), bf16),
            jax.ShapeDtypeStruct((half, D3), bf16),
            jax.ShapeDtypeStruct((count, D), bf16),
            jax.ShapeDtypeStruct((count, D), bf16),
        ],
        scratch_shapes=[
            pltpu.VMEM((count, 3 * TILE), bf16),
            pltpu.VMEM((8, 3 * TILE), f32),
            pltpu.VMEM((STEPS, 8, 3 * TILE), f32),
            pltpu.VMEM((2, TILE), f32),
            pltpu.VMEM((2, D), f32),
            pltpu.VMEM((SEQ, TILE), f32),
            pltpu.VMEM((SEQ, TILE), f32),
            pltpu.VMEM((3, FREQ, TILE), f32),
            pltpu.VMEM((3, FREQ, TILE), f32),
            pltpu.VMEM((count, D), f32),
            pltpu.VMEM((SEQ, hidden), f32),
            pltpu.VMEM((count, D), bf16),
            pltpu.SemaphoreType.DMA(()),
            pltpu.SemaphoreType.DMA(()),
            pltpu.VMEM((count, D), bf16),
            pltpu.VMEM((count, D), bf16),
            pltpu.VMEM((count, D), f32),
            pltpu.VMEM((count, D), bf16),
            pltpu.VMEM((count, D), bf16),
            pltpu.SemaphoreType.DMA((5,)),
        ]
        + buffers(CHUNKS, half, bf16) + semaphores(CHUNKS) + buffers(1, SMALL_ROWS, f32) + semaphores(1),
        compiler_params=pltpu.CompilerParams(
            collective_id=1, has_side_effects=True, vmem_limit_bytes=63 * 2**20
        ),
        name="reduce_grads",
    )(
        sums, d_shift, active, active, upstream, second, d_hidden, mixed, d_middle, normed, tokens, vecs, middle, down_full, down_full,
        d_mixed, z, lines, vecs, bank1, bank2, hat1, hat2, mid, *constants(), in_full,
        decay, decay, third_w, third_w, jnp.asarray(place_ratio()), embed, pre1, act1, pre2, act2, second_w,
    )


HID = 512
GELU_A = math.sqrt(2.0 / math.pi)
GELU_B = 0.044715


def middle_kernel(
    mixed, tokens, upstream, out_ref, vecs, up_ref, shift_ref, down_ref,
    middle_ref, second, active_ref, d_hidden_ref, d_middle_ref, d_mixed_ref, sums_ref, d_shift_ref, d_second_ref,
):
    first = pl.program_id(0) == 0
    last = pl.program_id(0) == pl.num_programs(0) - 1
    steps = second.shape[0] // 256

    def rows_of(i):
        return pl.ds(pl.multiple_of(i * 256, 256), 256)

    @pl.when(first)
    def _():
        def front(i, carry):
            rows = rows_of(i)
            value = tokens[rows, :].astype(f32) + lowmul(mixed[rows, :], out_ref[...]) + vecs[2:3, :]
            middle_ref[rows, :] = value
            second[rows, :] = layer_norm(value, vecs[3:4, :], vecs[4:5, :]).astype(bf16)
            return carry

        lax.fori_loop(0, steps, front, 0)
        d_second_ref[...] = jnp.zeros_like(d_second_ref)

    def block(i, total):
        rows = rows_of(i)
        hidden = lowmul(second[rows, :], up_ref[...]) + shift_ref[...]
        d_active = times_t(upstream[rows, :], down_ref[...])
        square = hidden * hidden
        curve = jnp.tanh(GELU_A * hidden * (1.0 + GELU_B * square))
        half = 0.5 * (1.0 + curve)
        active_ref[rows, :] = (hidden * half).astype(bf16)
        slope = half + 0.5 * hidden * (1.0 - curve * curve) * (GELU_A * (1.0 + 3.0 * GELU_B * square))
        d_hidden = (d_active * slope).astype(bf16)
        d_hidden_ref[rows, :] = d_hidden
        d_second_ref[rows, :] += times_t(d_hidden, up_ref[...])
        return total + jnp.sum(d_hidden.astype(f32), axis=0, keepdims=True)

    d_shift_ref[...] = lax.fori_loop(0, steps, block, jnp.zeros(d_shift_ref.shape, f32), unroll=2)

    @pl.when(last)
    def _():
        def back(i, sums):
            rows = rows_of(i)
            values = middle_ref[rows, :]
            grads = d_second_ref[rows, :]
            given = upstream[rows, :].astype(f32)
            center = values - jnp.mean(values, axis=-1, keepdims=True)
            scale = lax.rsqrt(jnp.mean(center * center, axis=-1, keepdims=True) + EPS)
            unit = center * scale
            scaled = grads * vecs[3:4, :]
            inner = scaled - jnp.mean(scaled, axis=-1, keepdims=True)
            inner = inner - unit * jnp.mean(scaled * unit, axis=-1, keepdims=True)
            value = scale * inner + given
            d_middle_ref[rows, :] = value
            branch = value.astype(bf16)
            d_mixed_ref[rows, :] = times_t(branch, out_ref[...])
            new = (branch.astype(f32), grads * unit, grads, given)
            return tuple(old + jnp.sum(one, axis=0, keepdims=True) for old, one in zip(sums, new))

        zero = jnp.zeros((1, D), f32)
        sums_ref[...] = jnp.zeros_like(sums_ref)
        for i, one in enumerate(lax.fori_loop(0, steps, back, (zero,) * 4)):
            sums_ref[i : i + 1, :] = one


def run_middle(mixed, tokens, upstream, out_full, vecs, up_full, up_shift, down_full):
    count = tokens.shape[0]
    units = up_full.shape[1]

    def fixed(*shape):
        return pl.BlockSpec(shape, lambda j: (0,) * len(shape), pipeline_mode=pl.Buffered(1))

    columns = pl.BlockSpec((count, HID), lambda j: (0, j))
    row = pl.BlockSpec((1, HID), lambda j: (0, j))
    tall = fixed(count, D)
    wide = jax.ShapeDtypeStruct((count, units), bf16)
    full = jax.ShapeDtypeStruct((count, D), f32)
    return pl.pallas_call(
        middle_kernel,
        grid=(units // HID,),
        in_specs=[
            tall, tall, tall, fixed(D, D), fixed(8, D), pl.BlockSpec((D, HID), lambda j: (0, j)), row,
            pl.BlockSpec((HID, D), lambda j: (j, 0)),
        ],
        out_specs=[tall, tall, columns, columns, tall, tall, fixed(8, D), row],
        out_shape=[
            full, jax.ShapeDtypeStruct((count, D), bf16), wide, wide, full, full, jax.ShapeDtypeStruct((8, D), f32),
            jax.ShapeDtypeStruct((1, units), f32),
        ],
        scratch_shapes=[pltpu.VMEM((count, D), f32)],
        compiler_params=pltpu.CompilerParams(vmem_limit_bytes=63 * 2**20),
        cost_estimate=pl.CostEstimate(
            flops=6 * count * D * units, bytes_accessed=40 * 2**20, transcendentals=count * units
        ),
        name="middle",
    )(mixed, tokens, upstream, out_full, vecs, up_full, up_shift, down_full)


def finish_kernel(
    small, result, d_tokens, down, up, out, inward,
    prompt_out, cont_out, prompt_grad, cont_grad,
    g_gain1, g_shift1, g_in, g_in_b, g_taps, g_short_b, g_long, g_w1, g_b1, g_w2, g_b2, g_w3,
    g_out, g_out_b, g_gain2, g_shift2, g_up, g_up_b, g_down, g_down_b,
):
    step = pl.program_id(0)
    for src, dst in ((down, g_down), (up, g_up), (out, g_out), (inward, g_in)):
        dst[...] = src[...].astype(f32)

    @pl.when(step % 4 < 2)
    def _():
        prompt_out[0, 0] = result[...]
        prompt_grad[0, 0] = d_tokens[...]

    @pl.when(step % 4 >= 2)
    def _():
        cont_out[0, 0, 0] = result[...]
        cont_grad[0, 0, 0] = d_tokens[...]

    @pl.when(step == 0)
    def _():
        half = slice(D // 2, D)

        def lines(start, count, stride=1):
            rows = [small[0, start + stride * i : start + stride * i + 1, half] for i in range(count)]
            return jnp.concatenate(rows, axis=1)

        def put(ref, value):
            ref[...] = value.reshape(ref.shape)

        for i, ref in enumerate((g_out_b, g_gain2, g_shift2, g_down_b)):
            put(ref, lines(GIVEN_ROW + i, 1))
        put(g_up_b, lines(GIVEN_ROW + 4, 4))
        for i in range(3):
            g_taps[i : i + 1, :] = lines(TAP_ROW + i, 3, 8)
        put(g_short_b, lines(TAP_ROW + 3, 3, 8))
        put(g_in_b, lines(TAP_ROW + 4, 3, 8))
        g_long[...] = small[0, LONG_ROW : LONG_ROW + 2, half]
        put(g_gain1, lines(NORM_ROW, 1))
        put(g_shift1, lines(NORM_ROW + 1, 1))
        g_w3[...] = small[0, 0 : g_w3.shape[0], :]
        wide, n1 = g_w1.shape
        g_w1[...] = small[0, 64 : 64 + n1, 0:wide].T
        put(g_b1, small[0, 64 + n1 : 65 + n1, 0:wide])
        put(g_b2, small[0, 65 + n1 : 66 + n1, 0:wide])
        g_w2[...] = small[0, 64 : 64 + g_w2.shape[1], 128 : 128 + wide].T


def finish(shapes, micros, small, result, d_tokens, down, up, out, inward):
    steps = 4 * micros

    def rows(value):
        return pl.BlockSpec((value.shape[0] // steps, value.shape[1]), lambda i: (i, 0))

    def fixed(value):
        return pl.BlockSpec(value.shape, lambda i: (0,) * len(value.shape))

    inputs = (small, result, d_tokens, down.reshape(-1, D), up, out, inward)
    prompt = pl.BlockSpec((1, 1, BLOCK, D), lambda i: (i // 4, 0, jnp.minimum(i % 4, 1), 0))
    cont = pl.BlockSpec((1, 1, 1, BLOCK, D), lambda i: (i // 4, 0, jnp.maximum(i % 4 - 2, 0), 0, 0))
    big = {6: inward, 16: out, 20: up, 22: down}
    specs = [prompt, cont, prompt, cont] + [rows(one) if i in big else fixed(one) for i, one in enumerate(shapes) if i > 3]
    return pl.pallas_call(
        finish_kernel,
        grid=(steps,),
        in_specs=[fixed(small)] + [rows(one) for one in inputs[1:]],
        out_specs=specs,
        out_shape=shapes,
        compiler_params=pltpu.CompilerParams(vmem_limit_bytes=63 * 2**20),
        name="finish",
    )(*inputs)


def per_device(
    prompt_x, cont_x, prompt_cot, cont_cot, norm1_gain, norm1_bias, in_weight, in_bias, short_weight,
    short_bias, long_bias, filter_w1, filter_b1, filter_w2, filter_b2, filter_w3, filter_decay, out_weight,
    out_bias, norm2_gain, norm2_bias, up_weight, up_bias, down_weight, down_bias, *, reps, shards,
):
    own_kernels = reps == 16 and shards == 2 and prompt_x.shape[1] == 1
    micros = prompt_x.shape[0]
    groups = prompt_x.shape[1]
    count = micros * groups * SPAN

    def tokens_of(prompt, cont):
        return jnp.concatenate(
            [
                prompt.reshape(micros * groups, PROMPT, D),
                cont.reshape(micros * groups, CONTS * BLOCK, D),
            ],
            axis=1,
        ).reshape(count, D)

    def parts_of(rows):
        rows = rows.reshape(micros, groups, SPAN, D)
        return rows[:, :, :PROMPT], rows[:, :, PROMPT:].reshape(micros, groups, CONTS, BLOCK, D)

    n1 = filter_w1.shape[0]
    n2 = filter_w2.shape[0]
    if own_kernels:
        (projected, mixed_low, hat1, hat2, mid, bank1, bank2, vecs, lines, up_shift, decay, fw2, fw3,
         pre1, act1, pre2, act2, normed_low, tokens_low, upstream, in_full, out_full, up_full, down_full) = gather_weights(
            norm1_gain, norm1_bias, in_bias, short_weight, short_bias, long_bias, filter_w1.T, filter_b1, filter_w2.T,
            filter_b2, filter_w3, filter_decay, out_bias, norm2_gain, norm2_bias, up_bias, down_bias,
            in_weight, out_weight, up_weight, down_weight,
            *(one.reshape(micros, PROMPT, D) for one in (prompt_x, cont_x, prompt_cot, cont_cot)),
        )
        states = (jnp.asarray(embed_table()), pre1, act1, pre2, act2)
    else:
        tokens_low = tokens_of(prompt_x, cont_x)
        upstream = tokens_of(prompt_cot, cont_cot)

        def gather(value, axis=0):
            return lax.all_gather(value, "shard", axis=axis, tiled=True)

        gain1, shift1, out_shift, gain2, shift2, down_shift, in_shift, short_shift, up_shift, decay, fb1, fb2 = (
            gather(one).astype(f32)
            for one in (norm1_gain, norm1_bias, out_bias, norm2_gain, norm2_bias, down_bias, in_bias, short_bias,
                        up_bias, filter_decay, filter_b1, filter_b2)
        )
        taps, long_shift, fw1, fw2, fw3 = (
            gather(one, 1).astype(f32) for one in (short_weight, long_bias, filter_w1, filter_w2, filter_w3)
        )
        in_full, out_full, up_full, down_full = (
            gather(one) for one in (by_tile(in_weight), out_weight, up_weight, down_weight)
        )
        up_shift = up_shift[None]
        lines = by_tile(jnp.concatenate([taps, short_shift[None], in_shift[None], jnp.zeros((3, D3), f32)], axis=0))
        vecs = jnp.stack([gain1, shift1, out_shift, gain2, shift2, down_shift])
        vecs = jnp.concatenate([vecs, long_shift], axis=0)
        filters, filter_pull = jax.vjp(partial(filter_taps, decay=decay), fw1, fb1, fw2, fb2, fw3)
        normed, norm_pull = jax.vjp(layer_norm, tokens_low.astype(f32), gain1, shift1)
        normed_low = normed.astype(bf16)
        projected = lowmul(normed_low, in_full) + lines[4]
        mixed_low, hat1, hat2, mid, bank1, bank2 = run_forward(projected, lines, vecs, filters)
    middle, second_low, active_low, d_hidden, d_middle, d_mixed, sums, d_up_shift = run_middle(
        mixed_low, tokens_low, upstream, out_full, vecs, up_full, up_shift, down_full
    )
    width = D // shards

    def by_shard(value):
        rows = value.shape[0]
        return value.reshape(rows, shards, -1).swapaxes(0, 1).reshape(shards, -1, width)

    if own_kernels:
        small, grad_down, grad_up, grad_out, grad_in, d_tokens, result = reduce_grads(
            sums, d_up_shift, active_low, upstream, second_low, d_hidden, mixed_low, d_middle, normed_low,
            tokens_low, middle, down_full, d_mixed, projected, lines, vecs, bank1, bank2, hat1, hat2, mid, in_full, decay, fw3, states, fw2,
        )
        args = (norm1_gain, norm1_bias, in_weight, in_bias, short_weight, short_bias, long_bias, filter_w1, filter_b1,
                filter_w2, filter_b2, filter_w3, out_weight, out_bias, norm2_gain, norm2_bias, up_weight, up_bias,
                down_weight, down_bias)
        shapes = [jax.ShapeDtypeStruct(one.shape, bf16) for one in (prompt_x, cont_x) * 2]
        shapes += [jax.ShapeDtypeStruct(one.shape, f32) for one in args]
        for i in (11, 13):
            shapes[i] = jax.ShapeDtypeStruct(shapes[i].shape[::-1], f32)
        outs = list(finish(shapes, micros, small, result, d_tokens, grad_down, grad_up, grad_out, grad_in))
        outs[11], outs[13] = outs[11].T, outs[13].T
        return tuple(outs)
    else:
        def reduce(value, axis=0):
            value = lax.psum_scatter(value, "shard", scatter_dimension=axis, tiled=True)
            return lax.psum(value, "rep")

        result = (middle + lowmul(active_low, down_full) + down_shift).astype(bf16)
        prompt_out, cont_out = parts_of(result)
        d_proj, d_taps, d_long, d_filter1, d_filter2 = run_backward(
            d_mixed, projected, lines, vecs, bank1, bank2, hat1, hat2, mid
        )
        d_tokens, grad_gain1, grad_shift1 = norm_pull(times_t(d_proj, in_full))
        prompt_grad, cont_grad = parts_of((d_tokens + d_middle).astype(bf16))
        filter_grads_all = filter_pull(jnp.concatenate([d_filter1, d_filter2], axis=-1))
        narrow_own = [reduce(one, one.ndim - 1) for one in filter_grads_all[:4]]
        third_grad = reduce(filter_grads_all[4], 1)
        given = jnp.concatenate([by_shard(sums[:4]), by_shard(d_up_shift)], axis=1)
        given = reduce(given)[0]
        tap_rows = reduce(by_part(d_taps[:5]), 1)
        long_rows = reduce(d_long, 1)
        norm_rows = reduce(jnp.stack([grad_gain1, grad_shift1]), 1)
        grad_down = reduce(inner_rows(active_low, upstream))
        grad_up = reduce(inner_rows(second_low, d_hidden))
        grad_out = reduce(inner_rows(mixed_low, d_middle.astype(bf16)))
        grad_in = by_part(reduce(inner_rows(normed_low, d_proj)))
    return (
        prompt_out,
        cont_out,
        prompt_grad,
        cont_grad,
        norm_rows[0],
        norm_rows[1],
        grad_in,
        tap_rows[4],
        tap_rows[:3],
        tap_rows[3],
        long_rows,
        *narrow_own,
        third_grad,
        grad_out,
        given[0],
        given[1],
        given[2],
        grad_up,
        given[4:].reshape(-1),
        grad_down,
        given[3],
    )


def solution(mesh):
    group4 = P(None, ("rep", "shard"), None, None)
    group5 = P(None, ("rep", "shard"), None, None, None)
    one, row, col = P("shard"), P("shard", None), P(None, "shard")
    grads = (one, one, row, one, col, one, col, col, one, col, one, col)
    rest = (row, one, one, one, row, one, row, one)
    return jax.shard_map(
        partial(per_device, reps=mesh.shape["rep"], shards=mesh.shape["shard"]),
        mesh=mesh,
        in_specs=(group4, group5, group4, group5) + grads + (one,) + rest,
        out_specs=(group4, group5, group4, group5) + grads + rest,
        check_vma=False,
    )
```

```python
from functools import partial
import math

import jax
import jax.numpy as jnp
import numpy as np
from jax import lax
from jax.experimental import pallas as pl
from jax.experimental.pallas import tpu as pltpu
from jax.sharding import PartitionSpec as P

D = 768
D3 = 3 * D
BANDS = 16
BLOCK = 128
PROMPT = 256
CONTS = 2
SEQ = 384
SPAN = PROMPT + CONTS * BLOCK
TILE = 256
FREQ = 2 * BLOCK

EPS = 1e-05
HIGH = lax.Precision.HIGHEST
f32 = jnp.float32
bf16 = jnp.bfloat16


def matmul(left_op, right_op):
    return jnp.dot(left_op, right_op, precision=HIGH, preferred_element_type=f32)


def lowmul(left_op, right_op):
    return jnp.dot(left_op, right_op, preferred_element_type=f32)


def inner_rows(left_op, right_op):
    return lax.dot_general(
        left_op, right_op, (((0,), (0,)), ((), ())), preferred_element_type=f32
    )


def times_t(left_op, right_op):
    return lax.dot_general(
        left_op, right_op, (((1,), (1,)), ((), ())), preferred_element_type=f32
    )


def layer_norm(values, norm_gain, norm_shift):
    center_val = values - jnp.mean(values, axis=-1, keepdims=True)
    spread = jnp.mean(center_val * center_val, axis=-1, keepdims=True)
    return center_val * lax.rsqrt(spread + EPS) * norm_gain + norm_shift


def dft_matrix():
    freq = np.arange(BLOCK)
    place = np.arange(BLOCK)
    angle = np.pi * ((2 * freq[:, None] + 1) * place[None, :] % (4 * BLOCK)) / FREQ
    return np.concatenate([np.cos(angle), -np.sin(angle)], axis=0)


def split3(matrix):
    matrix = matrix.astype(np.float32)
    high = matrix.astype(jnp.bfloat16)
    rest = (matrix - high.astype(np.float32)).astype(jnp.bfloat16)
    return np.concatenate([high, rest, high], axis=1)


def split_dot(triple, signal):
    high = signal.astype(bf16)
    rest = (signal - high.astype(f32)).astype(bf16)
    return jnp.dot(
        triple, jnp.concatenate([high, high, rest], axis=0), preferred_element_type=f32
    )


def cmul(left, right):
    lr, li = left[:BLOCK], left[BLOCK:]
    rr, ri = right[:BLOCK], right[BLOCK:]
    return jnp.concatenate([lr * rr - li * ri, lr * ri + li * rr], axis=0)


def cmul_conj(left, right):
    lr, li = left[:BLOCK], left[BLOCK:]
    rr, ri = right[:BLOCK], right[BLOCK:]
    return jnp.concatenate([lr * rr + li * ri, lr * ri - li * rr], axis=0)


def row_index():
    return lax.broadcasted_iota(jnp.int32, (BLOCK, TILE), 0)


def delayed(block, before, lag):
    rolled = pltpu.roll(block, lag, 0)
    if before is None:
        return jnp.where(row_index() >= lag, rolled, 0.0)
    return jnp.where(row_index() >= lag, rolled, pltpu.roll(before, lag, 0))


def advanced(block, after, lag):
    rolled = pltpu.roll(block, BLOCK - lag, 0)
    if after is None:
        return jnp.where(row_index() < BLOCK - lag, rolled, 0.0)
    return jnp.where(row_index() < BLOCK - lag, rolled, pltpu.roll(after, BLOCK - lag, 0))


BEFORE = (None, 0, 1, 1)


def part(index):
    return slice(index * TILE, (index + 1) * TILE)


def load_blocks(ref, cols=slice(None)):
    return [ref[i * BLOCK : (i + 1) * BLOCK, cols] for i in range(4)]


def short_blocks(z_ref, rows_ref, index):
    blocks = load_blocks(z_ref, part(index))
    taps = rows_ref[0:3, part(index)]
    shift = rows_ref[3:4, part(index)]
    outs = []
    for i in range(4):
        before = None if BEFORE[i] is None else blocks[BEFORE[i]]
        outs.append(
            taps[0:1] * blocks[i]
            + taps[1:2] * delayed(blocks[i], before, 1)
            + taps[2:3] * delayed(blocks[i], before, 2)
            + shift
        )
    return outs


def spectra(hats, bank):
    tail = cmul(bank[1], hats[1]) + cmul(bank[2], hats[0])
    return [
        cmul(bank[0], hats[0]),
        cmul(bank[0], hats[1]) + cmul(bank[1], hats[0]),
        cmul(bank[0], hats[2]) + tail,
        cmul(bank[0], hats[3]) + tail,
    ]


def adjoint_spectra(hats, bank):
    tail = hats[2] + hats[3]
    return [
        cmul_conj(bank[0], hats[0]) + cmul_conj(bank[1], hats[1]) + cmul_conj(bank[2], tail),
        cmul_conj(bank[0], hats[1]) + cmul_conj(bank[1], tail),
        cmul_conj(bank[0], hats[2]),
        cmul_conj(bank[0], hats[3]),
    ]


def bank_grads(hats, grads):
    tail = grads[2] + grads[3]
    zero = cmul_conj(hats[0], grads[0])
    for i in range(1, 4):
        zero = zero + cmul_conj(hats[i], grads[i])
    one = cmul_conj(hats[0], grads[1]) + cmul_conj(hats[1], tail)
    return [zero, one, cmul_conj(hats[0], tail)]


def signs():
    odd = lax.broadcasted_iota(jnp.int32, (BLOCK, TILE), 0) % 2
    return (1 - 2 * odd).astype(f32)


LONG1, LONG2 = slice(6, 7), slice(7, 8)


def make_bank(ahead, taps, bank_ref):
    hats = [split_dot(ahead, taps[o * BLOCK : (o + 1) * BLOCK, :] * (1.0 / BLOCK)) for o in range(3)]
    sign = signs()
    bank = [hats[0]]
    for o in (1, 2):
        prev = hats[o - 1]
        turned = jnp.concatenate([-sign * prev[BLOCK:], sign * prev[:BLOCK]], axis=0)
        bank.append(hats[o] + turned)
    for o in range(3):
        bank_ref[o] = bank[o]


def filter_grads(back, grads, out_ref):
    sign = signs()
    for o in range(3):
        one = grads[o]
        if o < 2:
            after = grads[o + 1]
            one = one + jnp.concatenate([sign * after[BLOCK:], -sign * after[:BLOCK]], axis=0)
        out_ref[o * BLOCK : (o + 1) * BLOCK, :] = split_dot(back, one) * (1.0 / BLOCK)


def mixer_forward(
    z_ref, rows_ref, long_ref, filter1, filter2, ahead_ref, back_ref,
    out_ref, hat1_ref, hat2_ref, mid_ref, bank1, bank2,
):
    @pl.when(pl.program_id(1) == 0)
    def _():
        make_bank(ahead_ref[...], filter1[...], bank1)
        make_bank(ahead_ref[...], filter2[...], bank2)

    forward_step(
        z_ref, rows_ref, long_ref, ahead_ref, back_ref, out_ref, hat1_ref, hat2_ref, mid_ref, bank1, bank2
    )


def forward_step(
    z_ref, rows_ref, long_ref, ahead_ref, back_ref, out_ref, hat1_ref, hat2_ref, mid_ref, bank1, bank2
):
    ahead = ahead_ref[...]
    back = back_ref[...]
    gate1 = short_blocks(z_ref, rows_ref, 1)
    value = short_blocks(z_ref, rows_ref, 2)
    sig1 = [gate1[i] * value[i] for i in range(4)]
    hats = []
    for i in range(4):
        hat = split_dot(ahead, sig1[i])
        hat1_ref[i] = hat
        hats.append(hat)
    wave = spectra(hats, [bank1[i] for i in range(3)])
    mid = []
    for i in range(4):
        one = split_dot(back, wave[i]) + long_ref[LONG1, :] * sig1[i]
        mid_ref[i * BLOCK : (i + 1) * BLOCK, :] = one
        mid.append(one)
    gate0 = short_blocks(z_ref, rows_ref, 0)
    sig2 = [gate0[i] * mid[i] for i in range(4)]
    hats = []
    for i in range(4):
        hat = split_dot(ahead, sig2[i])
        hat2_ref[i] = hat
        hats.append(hat)
    wave = spectra(hats, [bank2[i] for i in range(3)])
    for i in range(4):
        two = split_dot(back, wave[i]) + long_ref[LONG2, :] * sig2[i]
        out_ref[i * BLOCK : (i + 1) * BLOCK, :] = two.astype(bf16)


def mixer_backward(
    grad_ref, z_ref, rows_ref, long_ref, bank1, bank2, hat1_ref, hat2_ref, mid_ref,
    ahead_ref, back_ref,
    dz_ref, dtap_ref, dlong_ref, dfilt1_ref, dfilt2_ref, dbank1, dbank2,
):
    micro = pl.program_id(1)
    backward_step(
        micro == 0, micro == pl.num_programs(1) - 1, grad_ref, z_ref, rows_ref, long_ref, bank1, bank2,
        hat1_ref, hat2_ref, mid_ref, ahead_ref, back_ref,
        dz_ref, dtap_ref, dlong_ref, dfilt1_ref, dfilt2_ref, dbank1, dbank2,
    )


def backward_step(
    first, last, grad_ref, z_ref, rows_ref, long_ref, bank1, bank2, hat1_ref, hat2_ref, mid_ref,
    ahead_ref, back_ref,
    dz_ref, dtap_ref, dlong_ref, dfilt1_ref, dfilt2_ref, dbank1, dbank2,
):
    ahead = ahead_ref[...]
    back = back_ref[...]

    @pl.when(first)
    def _():
        dbank1[...] = jnp.zeros_like(dbank1)
        dbank2[...] = jnp.zeros_like(dbank2)
        dlong_ref[...] = jnp.zeros_like(dlong_ref)
        dtap_ref[...] = jnp.zeros_like(dtap_ref)

    def total(values):
        acc = values[0]
        for one in values[1:]:
            acc = acc + one
        return jnp.sum(acc, axis=0, keepdims=True)

    gate0 = short_blocks(z_ref, rows_ref, 0)
    grad2 = load_blocks(grad_ref)
    mid = load_blocks(mid_ref)
    dhats = [split_dot(ahead, grad2[i]) for i in range(4)]
    new = bank_grads([hat2_ref[i] for i in range(4)], dhats)
    for i in range(3):
        dbank2[i] += new[i]
    wave = adjoint_spectra(dhats, [bank2[i] for i in range(3)])
    dsig2 = [split_dot(back, wave[i]) + long_ref[LONG2, :] * grad2[i] for i in range(4)]
    dlong_ref[1:2, :] += total([grad2[i] * gate0[i] * mid[i] for i in range(4)])
    dgate0 = [dsig2[i] * mid[i] for i in range(4)]
    grad1 = [dsig2[i] * gate0[i] for i in range(4)]
    dhats = [split_dot(ahead, grad1[i]) for i in range(4)]
    new = bank_grads([hat1_ref[i] for i in range(4)], dhats)
    for i in range(3):
        dbank1[i] += new[i]
    wave = adjoint_spectra(dhats, [bank1[i] for i in range(3)])
    dsig1 = [split_dot(back, wave[i]) + long_ref[LONG1, :] * grad1[i] for i in range(4)]
    gate1 = short_blocks(z_ref, rows_ref, 1)
    value = short_blocks(z_ref, rows_ref, 2)
    dlong_ref[0:1, :] += total([grad1[i] * gate1[i] * value[i] for i in range(4)])
    dgate1 = [dsig1[i] * value[i] for i in range(4)]
    dvalue = [dsig1[i] * gate1[i] for i in range(4)]
    for index, grads in enumerate((dgate0, dgate1, dvalue)):
        cols = part(index)
        taps = rows_ref[0:3, cols]
        blocks = load_blocks(z_ref, cols)
        after = (grads[1], grads[2] + grads[3], None, None)
        dz = []
        for i in range(4):
            one = (
                taps[0:1] * grads[i]
                + taps[1:2] * advanced(grads[i], after[i], 1)
                + taps[2:3] * advanced(grads[i], after[i], 2)
            ).astype(bf16)
            dz_ref[i * BLOCK : (i + 1) * BLOCK, cols] = one
            dz.append(one.astype(f32))
        dtap_ref[4:5, cols] += total(dz)
        dtap_ref[3:4, cols] += total(grads)
        dtap_ref[0:1, cols] += total([grads[i] * blocks[i] for i in range(4)])
        for lag in (1, 2):
            dtap_ref[lag : lag + 1, cols] += total(
                [
                    grads[i]
                    * delayed(blocks[i], None if BEFORE[i] is None else blocks[BEFORE[i]], lag)
                    for i in range(4)
                ]
            )

    @pl.when(last)
    def _():
        filter_grads(back, [dbank1[i] for i in range(3)], dfilt1_ref)
        filter_grads(back, [dbank2[i] for i in range(3)], dfilt2_ref)


def constants():
    matrix = dft_matrix()
    return jnp.asarray(split3(matrix)), jnp.asarray(split3(matrix.T))


STEPS = D // TILE
AHEAD = (FREQ, 3 * BLOCK)
BACK = (BLOCK, 3 * FREQ)


def run_forward(z, lines, vecs, filters):
    rows = z.shape[0]
    blocks = rows // BLOCK

    def spec(shape, index):
        return pl.BlockSpec(shape, lambda t, m: index(m, t))

    hat_spec = spec((4, FREQ, TILE), lambda m, t: (m, 0, t))
    row_spec = spec((SPAN, TILE), lambda m, t: (m, t))
    bank_spec = spec((3, FREQ, TILE), lambda m, t: (0, 0, t))
    hat_shape = jax.ShapeDtypeStruct((blocks, FREQ, D), f32)
    bank_shape = jax.ShapeDtypeStruct((3, FREQ, D), f32)
    return pl.pallas_call(
        mixer_forward,
        grid=(STEPS, rows // SPAN),
        in_specs=[
            spec((SPAN, 3 * TILE), lambda m, t: (m, t)),
            spec((8, 3 * TILE), lambda m, t: (0, t)),
            spec((8, TILE), lambda m, t: (0, t)),
            spec((SEQ, TILE), lambda m, t: (0, t)),
            spec((SEQ, TILE), lambda m, t: (0, STEPS + t)),
            spec(AHEAD, lambda m, t: (0, 0)),
            spec(BACK, lambda m, t: (0, 0)),
        ],
        out_specs=[row_spec, hat_spec, hat_spec, row_spec, bank_spec, bank_spec],
        out_shape=[
            jax.ShapeDtypeStruct((rows, D), bf16), hat_shape, hat_shape,
            jax.ShapeDtypeStruct((rows, D), f32), bank_shape, bank_shape,
        ],
        compiler_params=pltpu.CompilerParams(vmem_limit_bytes=40 * 2**20),
        cost_estimate=pl.CostEstimate(flops=10 * 10**9, bytes_accessed=32 * 2**20, transcendentals=0),
        name="mixer_forward",
    )(z, lines, vecs, filters, filters, *constants())


def run_backward(grad, z, lines, vecs, bank1, bank2, hat1, hat2, mid):
    rows = z.shape[0]

    def spec(shape, index):
        return pl.BlockSpec(shape, lambda t, m: index(m, t))

    hat_spec = spec((4, FREQ, TILE), lambda m, t: (m, 0, t))
    row_spec = spec((SPAN, TILE), lambda m, t: (m, t))
    bank_spec = spec((3, FREQ, TILE), lambda m, t: (0, 0, t))
    z_spec = spec((SPAN, 3 * TILE), lambda m, t: (m, t))
    column_spec = spec((SEQ, TILE), lambda m, t: (0, t))
    return pl.pallas_call(
        mixer_backward,
        grid=(STEPS, rows // SPAN),
        in_specs=[
            row_spec,
            z_spec,
            spec((8, 3 * TILE), lambda m, t: (0, t)),
            spec((8, TILE), lambda m, t: (0, t)),
            bank_spec, bank_spec, hat_spec, hat_spec, row_spec,
            spec(AHEAD, lambda m, t: (0, 0)),
            spec(BACK, lambda m, t: (0, 0)),
        ],
        out_specs=[
            z_spec,
            spec((8, 3 * TILE), lambda m, t: (0, t)),
            spec((2, TILE), lambda m, t: (0, t)),
            column_spec,
            column_spec,
        ],
        out_shape=[
            jax.ShapeDtypeStruct((rows, D3), bf16), jax.ShapeDtypeStruct((8, D3), f32),
            jax.ShapeDtypeStruct((2, D), f32), jax.ShapeDtypeStruct((SEQ, D), f32),
            jax.ShapeDtypeStruct((SEQ, D), f32),
        ],
        scratch_shapes=[pltpu.VMEM((3, FREQ, TILE), f32), pltpu.VMEM((3, FREQ, TILE), f32)],
        compiler_params=pltpu.CompilerParams(vmem_limit_bytes=40 * 2**20),
        cost_estimate=pl.CostEstimate(flops=24 * 10**9, bytes_accessed=36 * 2**20, transcendentals=0),
        name="mixer_backward",
    )(grad, z, lines, vecs, bank1, bank2, hat1, hat2, mid, *constants())


def place_ratio():
    return (np.arange(SEQ).astype(np.float32) / np.float32(SEQ))[:, None]


def filter_states(first_w, first_b, second_w, second_b):
    levels = (np.arange(BANDS) + 1).astype(np.float32)
    ratio = jnp.asarray(place_ratio())
    angles = 2.0 * math.pi * ratio * jnp.asarray(levels)[None, :]
    embed = jnp.concatenate([ratio, jnp.cos(angles), jnp.sin(angles)], axis=1)
    first_pre = matmul(embed, first_w) + first_b
    first_act = jnp.sin(first_pre)
    second_pre = matmul(first_act, second_w) + second_b
    return embed, first_pre, first_act, second_pre, jnp.sin(second_pre)


def filter_taps(first_w, first_b, second_w, second_b, third_w, decay):
    second_act = filter_states(first_w, first_b, second_w, second_b)[-1]
    return matmul(second_act, third_w) * jnp.exp(-jnp.asarray(place_ratio()) * decay[None, :])


def by_tile(value):
    shape = value.shape
    return value.reshape(*shape[:-1], 3, STEPS, TILE).swapaxes(-3, -2).reshape(shape)


def by_part(value):
    shape = value.shape
    return value.reshape(*shape[:-1], STEPS, 3, TILE).swapaxes(-3, -2).reshape(shape)


MESH = pl.DeviceIdType.MESH


class Place:
    def __init__(self):
        rep = lax.axis_index("rep")
        self.rep = rep
        self.shard = lax.axis_index("shard")
        self.core = rep % 2
        self.side = (rep // 2) % 2
        self.depth = rep // 4
        self.quad = rep % 4
        self.eighth = rep % 8
        self.to_side = 2 - 4 * self.side
        self.to_depth = 4 - 8 * (self.depth % 2)

    def other_shard(self):
        return (self.rep, 1 - self.shard)

    def other_side(self):
        return (self.rep + 2 - 4 * self.side, self.shard)

    def near_depth(self):
        return (self.rep + self.to_depth, self.shard)

    def diagonal(self):
        return (self.rep + (1 - self.core) * self.to_side + self.core * self.to_depth, self.shard)

    def other_core(self):
        return (self.rep + 1 - 2 * self.core, self.shard)

    def other_depth(self, step):
        return (((self.depth + step) % 4) * 4 + self.quad, self.shard)


def greet(devices):
    barrier = pltpu.get_barrier_semaphore()
    for device in devices:
        pl.semaphore_signal(barrier, inc=1, device_id=device, device_id_type=MESH)
    pl.semaphore_wait(barrier, len(devices))


def remote(src, dst, send, recv, device):
    return pltpu.make_async_remote_copy(
        src_ref=src, dst_ref=dst, send_sem=send, recv_sem=recv, device_id=device, device_id_type=MESH
    )


UNITS = (
    (0, 0, 16), (0, 16, 16), (0, 32, 16), (1, 0, 48), (2, 0, 16), (2, 16, 16), (2, 32, 16), (3, 0, 96), (3, 96, 96),
)
STRAIGHT = (4, 5, 6)
STAGES = ("", "A3 A4", "A5 B3 B4", "A6 A7 B5 C3 C4", "A8 B6 B7 C5", "B8 C6 C7", "C8", "")
PACK_ROWS = 96
UP_ROW, DECAY_ROW, FIRST_ROW, SECOND_ROW = 23, 27, 32, 32


def column_moves():
    for s in range(2):
        for a in range(3):
            for b in range(3):
                at = s * (D3 // 2) + a * (D // 2) + b * 128
                yield s, a, b * 128, (at % D // TILE * 3 + at // D) * TILE + at % TILE


def gather_kernel(
    gain1, shift1, in_shift, short_w, short_b, long_b, w1, b1, w2, b2, third, decay, out_b, gain2, shift2, up_b,
    down_b, w_in, w_out, w_up, w_down, prompt_x, cont_x, prompt_g, cont_g, embed_ref, ratio_ref, ahead_ref, back_ref,
    z_ref, mixed_ref, hat1_ref, hat2_ref, mid_ref, bank1, bank2,
    vecs, lines, up_all, decay_all, second_all, third_all, pre1, act1, pre2, act2,
    normed_out, tokens_out, upstream_out, f_in, f_out, f_up, f_down,
    pack, packed, packs, thirds, in_v, normed_v,
    small_send, small_recv, own_sem, token_sem, ysend, yrecv, xsend, xrecv, zsend, zrecv, dsend, drecv, ssend, srecv, csend, crecv,
):
    tick = pl.program_id(0)
    place = Place()
    shard, mine = place.shard, place.eighth
    by_side, by_depth = mine + place.to_side, mine + place.to_depth
    by_both = by_side + place.to_depth
    locals_ = (w_in, w_out, w_up, w_down)
    fulls = (in_v, f_out, f_up, f_down)

    def rows_of(unit, shard_of, piece):
        weight, start, size = unit
        half = locals_[weight].shape[0]
        return pl.ds(pl.multiple_of(shard_of * half + piece * (half // 8) + start, 16), size)

    def local_rows(unit, piece):
        weight, start, size = unit
        return pl.ds(pl.multiple_of(piece * (locals_[weight].shape[0] // 8) + start, 16), size)

    def smalls():
        return [
            remote(packed, packs.at[shard], small_send.at[0], small_recv.at[0], place.other_shard()),
            remote(third, thirds.at[shard], small_send.at[1], small_recv.at[1], place.other_shard()),
        ]

    def own_copies():
        copies = []
        for weight in range(1, 4):
            half = locals_[weight].shape[0]
            rows = pl.ds(pl.multiple_of(shard * half, 16), half)
            copies.append(pltpu.make_async_copy(locals_[weight], fulls[weight].at[rows, :], own_sem.at[weight]))
        return copies

    def token_copies():
        copies = []
        for to, parts in ((tokens_out, (prompt_x, cont_x)), (upstream_out, (prompt_g, cont_g))):
            for m in range(prompt_x.shape[0]):
                for i, ref in enumerate(parts):
                    rows = slice(m * SPAN + i * PROMPT, m * SPAN + (i + 1) * PROMPT)
                    copies.append(pltpu.make_async_copy(ref.at[m], to.at[rows, :], token_sem.at[len(copies)]))
        return copies

    def normed_copy():
        return pltpu.make_async_copy(normed_v, normed_out, own_sem.at[0])

    def in_copy():
        return pltpu.make_async_copy(in_v, f_in, own_sem.at[4])

    def moved(u, piece, send, recv, device):
        unit = UNITS[u]
        region = fulls[unit[0]].at[rows_of(unit, 1 - shard, piece), :]
        return remote(region, region, send, recv, device)

    def from_shard(u):
        return moved(u, mine, ysend.at[u], yrecv.at[u], place.other_shard())

    def side(u, piece):
        return moved(u, piece, xsend.at[u], xrecv.at[u], place.other_side())

    def depth(u, piece):
        return moved(u, piece, zsend.at[u], zrecv.at[u], place.near_depth())

    def diagonal(u, piece):
        return moved(u, piece, dsend.at[u], drecv.at[u], place.diagonal())

    def straight(u):
        return moved(u, by_both, ssend.at[u], srecv.at[u], place.other_shard())

    def twin(u, index, piece):
        return moved(u, piece, csend.at[u, index], crecv.at[u, index], place.other_core())

    def exchanges(stages):
        for stage in stages.split():
            kind, u = stage[0], int(stage[1:])
            if kind == "A":
                from_shard(u).wait_recv()
                side(u, mine).start()
                depth(u, mine).start()
                twin(u, 0, mine).start()
            elif kind == "B":
                side(u, by_side).wait_recv()
                twin(u, 1, by_side).start()
                depth(u, by_depth).wait_recv()
                twin(u, 2, by_depth).start()
                if u not in STRAIGHT:
                    diagonal(u, (1 - place.core) * by_depth + place.core * by_side).start()
            else:
                (straight(u) if u in STRAIGHT else diagonal(u, by_both)).wait_recv()
                twin(u, 3, by_both).start()

    def finish(u):
        for index, piece in enumerate((mine, by_side, by_depth, by_both)):
            twin(u, index, piece).wait()
        from_shard(u).wait_send()
        side(u, mine).wait_send()
        depth(u, mine).wait_send()
        (straight(u) if u in STRAIGHT else diagonal(u, mine)).wait_send()

    @pl.when(tick == 0)
    def _():
        greet([place.other_shard(), place.other_side(), place.near_depth(), place.other_core()])
        rows = pl.ds(pl.multiple_of(shard * (D // 2), 16), D // 2)
        for p in range(3):
            for t in range(STEPS):
                in_v[rows, part(t * 3 + p)] = w_in[:, part(p * STEPS + t)]

        def send_units(units):
            for u in units:
                weight = UNITS[u][0]
                to = fulls[weight].at[rows_of(UNITS[u], shard, mine), :]
                source = to if weight == 0 else locals_[weight].at[local_rows(UNITS[u], mine), :]
                remote(source, to, ysend.at[u], yrecv.at[u], place.other_shard()).start()
                if u in STRAIGHT:
                    to = fulls[weight].at[rows_of(UNITS[u], shard, by_both), :]
                    source = locals_[weight].at[local_rows(UNITS[u], by_both), :]
                    remote(source, to, ssend.at[u], srecv.at[u], place.other_shard()).start()

        send_units(range(3))
        pack[...] = jnp.zeros_like(pack)
        half = D // 2

        def row(ref):
            return ref[...].astype(f32).reshape(1, ref.shape[0])

        for i, ref in enumerate((gain1, shift1, out_b, gain2, shift2, down_b)):
            pack[i : i + 1, :] = row(ref)
        pack[6:8, :] = long_b[...].astype(f32)
        taps = short_w[...].astype(f32)
        for i, value in enumerate((row(in_shift), row(short_b), taps[0:1], taps[1:2], taps[2:3])):
            for a in range(3):
                pack[8 + 3 * i + a : 9 + 3 * i + a, :] = value[:, a * half : (a + 1) * half]
        value = row(up_b)
        for a in range(4):
            pack[UP_ROW + a : UP_ROW + a + 1, :] = value[:, a * half : (a + 1) * half]
        value = row(decay)
        for a in range(2):
            pack[DECAY_ROW + a : DECAY_ROW + a + 1, :] = value[:, a * half : (a + 1) * half]
        wide, n1 = w1.shape
        n2 = w2.shape[1]
        pack[FIRST_ROW : FIRST_ROW + n1, 0:wide] = w1[...].astype(f32).T
        pack[FIRST_ROW + n1 : FIRST_ROW + n1 + 1, 0:wide] = row(b1)
        pack[FIRST_ROW + n1 + 1 : FIRST_ROW + n1 + 2, 0:wide] = row(b2)
        pack[SECOND_ROW : SECOND_ROW + n2, 128 : 128 + wide] = w2[...].astype(f32).T
        packed[...] = pack[...].astype(bf16)
        for one in smalls():
            one.start()
        send_units(range(3, len(UNITS)))
        for one in own_copies() + token_copies():
            one.start()
        packs[shard] = packed[...]
        thirds[shard] = third[...]
        exchanges("A0 A1 A2")
        for one in smalls():
            one.wait()

        both = [packs[s].astype(f32) for s in range(2)]
        for i in range(8):
            for s in range(2):
                vecs[i : i + 1, s * half : (s + 1) * half] = both[s][i : i + 1]
        lines[...] = jnp.zeros_like(lines)
        for s, a, b, to in column_moves():
            for i, line in enumerate((4, 3, 0, 1, 2)):
                at = 8 + 3 * i + a
                lines[line : line + 1, to : to + 128] = both[s][at : at + 1, b : b + 128]
        for s in range(2):
            for a in range(4):
                to = s * (2 * D) + a * half
                up_all[0:1, to : to + half] = both[s][UP_ROW + a : UP_ROW + a + 1]
            for a in range(2):
                to = s * D + a * half
                decay_all[0:1, to : to + half] = both[s][DECAY_ROW + a : DECAY_ROW + a + 1]
            third_all[:, s * D : (s + 1) * D] = thirds[s].astype(f32)

        def narrow(rows, cols):
            return jnp.concatenate([both[s][rows, cols] for s in range(2)], axis=1)

        first_w = narrow(slice(FIRST_ROW, FIRST_ROW + n1), slice(0, wide))
        first_b = narrow(slice(FIRST_ROW + n1, FIRST_ROW + n1 + 1), slice(0, wide))
        second_b = narrow(slice(FIRST_ROW + n1 + 1, FIRST_ROW + n1 + 2), slice(0, wide))
        second_w = narrow(slice(SECOND_ROW, SECOND_ROW + n2), slice(128, 128 + wide))
        second_all[...] = second_w
        exchanges("B0 B1 B2")
        straight = ((1,), (0,))
        pre1[...] = exact(embed_ref[...], first_w, straight) + first_b
        act1[...] = jnp.sin(pre1[...])
        pre2[...] = exact(act1[...], second_w, straight) + second_b
        act2[...] = jnp.sin(pre2[...])

        exchanges("C0 C1 C2")

        for i, ref in enumerate((prompt_x, cont_x)):
            def norm_rows(step, carry):
                m, h = step // 2, step % 2
                values = ref[m, pl.ds(pl.multiple_of(h * 128, 128), 128), :].astype(f32)
                rows = pl.ds(pl.multiple_of(m * SPAN + i * PROMPT + h * 128, 128), 128)
                normed_v[rows, :] = layer_norm(values, vecs[0:1, :], vecs[1:2, :]).astype(bf16)
                return carry

            lax.fori_loop(0, 2 * ref.shape[0], norm_rows, 0)
        normed_copy().start()
        for u in range(3):
            finish(u)
        in_copy().start()

    for index in range(1, len(STAGES)):
        @pl.when(tick == index)
        def _():
            exchanges(STAGES[index])

    @pl.when(tick > 0)
    def _():
        step = jnp.maximum(tick - 1, 0)
        tile = step // 2
        micro = step % 2
        cols = pl.ds(pl.multiple_of(tile * 3 * TILE, 3 * TILE), 3 * TILE)
        few = pl.ds(pl.multiple_of(tile * TILE, TILE), TILE)
        rows = pl.ds(pl.multiple_of(micro * SPAN, SPAN), SPAN)

        @pl.when(tick <= 2 * STEPS)
        def _():
            @pl.when(micro == 0)
            def _():
                for q, bank in enumerate((bank1, bank2)):
                    those = pl.ds(pl.multiple_of(q * D + tile * TILE, TILE), TILE)
                    window = jnp.exp(-ratio_ref[...] * decay_all[:, those])
                    taps = exact(act2[...], third_all[:, those], ((1,), (0,))) * window
                    make_bank(ahead_ref[...], taps, bank)

            z_ref[...] = lowmul(normed_v[rows, :], in_v[:, cols]) + lines[4:5, cols]
            forward_step(
                z_ref, lines.at[:, cols], vecs.at[:, few], ahead_ref, back_ref,
                mixed_ref, hat1_ref, hat2_ref, mid_ref, bank1, bank2,
            )

    @pl.when(tick == 2 * STEPS + 1)
    def _():
        for u in range(3, len(UNITS)):
            finish(u)
        normed_copy().wait()
        in_copy().wait()
        for one in own_copies() + token_copies():
            one.wait()


def embed_table():
    ratio = place_ratio()
    angles = 2.0 * math.pi * ratio * (np.arange(BANDS) + 1).astype(np.float32)[None, :]
    return np.concatenate([ratio, np.cos(angles), np.sin(angles)], axis=1).astype(np.float32)


def gather_weights(*values):
    w1, w2, w3 = values[6], values[8], values[10]
    weights = values[17:21]
    micros = values[21].shape[0]
    count = micros * SPAN
    hidden = w2.shape[1]
    vmem = lambda one: pl.BlockSpec(one.shape, lambda t: (0,) * one.ndim, pipeline_mode=pl.Buffered(1))
    hbm = pl.BlockSpec(memory_space=pl.ANY)
    units = len(UNITS)
    embed, ratio = jnp.asarray(embed_table()), jnp.asarray(place_ratio())
    inputs = (*values, embed, ratio, *constants())

    def at_tile(shape, where):
        def index(t):
            step = jnp.minimum(jnp.maximum(t - 1, 0), 2 * STEPS - 1)
            return where(step % 2, step // 2)

        return pl.BlockSpec(shape, index)

    def doubled(value):
        return jax.ShapeDtypeStruct((2 * value.shape[0], *value.shape[1:]), value.dtype)

    def shape(*dims, kind=f32):
        return jax.ShapeDtypeStruct(dims, kind)

    fixed = [
        shape(8, D), shape(8, D3), shape(1, weights[2].shape[1]), shape(1, 2 * w3.shape[1]), shape(hidden, hidden),
        shape(hidden, 2 * w3.shape[1]),
    ] + [shape(SEQ, hidden)] * 4
    blocks = count // BLOCK
    hat_spec = at_tile((4, FREQ, TILE), lambda m, t: (m, 0, t))
    row_spec = at_tile((SPAN, TILE), lambda m, t: (m, t))
    bank_spec = at_tile((3, FREQ, TILE), lambda m, t: (0, 0, t))
    return pl.pallas_call(
        gather_kernel,
        grid=(2 * STEPS + 2,),
        in_specs=[vmem(one) for one in inputs],
        out_specs=[
            at_tile((SPAN, 3 * TILE), lambda m, t: (m, t)), row_spec, hat_spec, hat_spec, row_spec, bank_spec,
            bank_spec,
        ]
        + [vmem(one) for one in fixed] + [hbm] * 7,
        out_shape=[
            shape(count, D3), shape(count, D, kind=bf16), shape(blocks, FREQ, D), shape(blocks, FREQ, D),
            shape(count, D), shape(3, FREQ, D), shape(3, FREQ, D),
        ]
        + fixed + [shape(count, D, kind=bf16)] * 3 + [doubled(one) for one in weights],
        scratch_shapes=[
            pltpu.VMEM((PACK_ROWS, D // 2), f32),
            pltpu.VMEM((PACK_ROWS, D // 2), bf16),
            pltpu.VMEM((2, PACK_ROWS, D // 2), bf16),
            pltpu.VMEM((2, *w3.shape), bf16),
            pltpu.VMEM((D, D3), bf16),
            pltpu.VMEM((count, D), bf16),
        ]
        + [pltpu.SemaphoreType.DMA((2,))] * 2
        + [pltpu.SemaphoreType.DMA((5,)), pltpu.SemaphoreType.DMA((4 * micros,))]
        + [pltpu.SemaphoreType.DMA((units,))] * 10
        + [pltpu.SemaphoreType.DMA((units, 4))] * 2,
        compiler_params=pltpu.CompilerParams(
            collective_id=0, has_side_effects=True, vmem_limit_bytes=63 * 2**20
        ),
        name="gather_weights",
    )(*inputs)


class Reduction:
    def __init__(self, place, first, count, rows, bufs, sems, out):
        self.place = place
        self.first = first
        self.count = count
        self.rows = rows
        self.dtype = bufs[0].dtype
        self.whole, self.from_core, self.half, self.from_shard, self.own, self.from_side, self.mine, self.from_depth, self.back = bufs
        (self.s_core, self.r_core, self.s_shard, self.r_shard, self.s_side, self.r_side, self.s_depth, self.r_depth,
         self.s_gd, self.r_gd, self.s_gs, self.r_gs, self.s_gc, self.r_gc, self.s_own) = sems
        self.out = out

    def when(self, tick, lag, body):
        k = tick - self.first - lag

        @pl.when((k >= 0) & (k < self.count))
        def _():
            body(k, k % 2)

    def slot(self, ref, k):
        return ref.at[k % ref.shape[0]]

    def rows_at(self, index, size):
        return pl.ds(pl.multiple_of(index * size, size), size)

    def core_copy(self, k, slot):
        p = self.place
        return remote(
            self.whole.at[slot, :, self.rows_at(1 - p.core, self.rows // 2), :],
            self.slot(self.from_core, k), self.s_core.at[k], self.r_core.at[k], p.other_core(),
        )

    def shard_copy(self, k, slot):
        p = self.place
        return remote(
            self.half.at[slot, 1 - p.shard], self.slot(self.from_shard, k), self.s_shard.at[k], self.r_shard.at[k],
            p.other_shard(),
        )

    def side_copy(self, k, slot):
        p = self.place
        return remote(
            self.own.at[slot, self.rows_at(1 - p.side, self.rows // 4), :],
            self.slot(self.from_side, k), self.s_side.at[k], self.r_side.at[k], p.other_side(),
        )

    def quarter(self, base, index):
        rows = self.rows // 8
        return (
            pl.ds(pl.multiple_of(base + (index // 2) * rows, rows), rows),
            pl.ds(pl.multiple_of((index % 2) * (D // 2), D // 2), D // 2),
        )

    def depth_copy(self, k, slot, step):
        p = self.place
        rows, cols = self.quarter(0, (p.depth + step) % 4)
        return remote(
            self.mine.at[slot, rows, cols], self.from_depth.at[k % self.from_depth.shape[0], step - 1],
            self.s_depth.at[k, step - 1], self.r_depth.at[k, step - 1], p.other_depth(step),
        )

    def depth_back(self, k, step):
        p = self.place
        rows, cols = self.quarter(p.side * (self.rows // 4), p.depth)
        region = self.back.at[k % self.back.shape[0], rows, cols]
        return remote(
            region, region, self.s_gd.at[k, step - 1], self.r_gd.at[k, step - 1], p.other_depth(step)
        )

    def side_back(self, k):
        p = self.place
        region = self.back.at[k % self.back.shape[0], self.rows_at(p.side, self.rows // 4), :]
        return remote(region, region, self.s_gs.at[k], self.r_gs.at[k], p.other_side())

    def homes(self, k, place_in):
        rows = pl.ds(pl.multiple_of(self.place.core * (self.rows // 2), self.rows // 2), self.rows // 2)
        return [(cols, ref.at[(*lead, rows, *tail)]) for cols, ref, lead, tail in place_in]

    def send_home(self, k, place_in):
        p = self.place
        for cols, region in self.homes(k, place_in):
            piece = self.back.at[k % self.back.shape[0], :, cols]
            remote(piece, region, self.s_gc.at[k], self.r_gc.at[k], p.other_core()).start()
            pltpu.make_async_copy(piece, region, self.s_own.at[k]).start()

    def wait_home(self, k):
        whole = self.slot(self.back, k)
        remote(whole, whole, self.s_gc.at[k], self.r_gc.at[k], self.place.other_core()).wait()
        pltpu.make_async_copy(whole, whole, self.s_own.at[k]).wait()

    def add(self, left, right):
        return (left.astype(f32) + right.astype(f32)).astype(self.dtype)

    def send(self, tick):
        self.when(tick, 0, lambda k, slot: self.core_copy(k, slot).start())

    def advance(self, tick):
        p = self.place

        def after_core(k, slot):
            self.core_copy(k, slot).wait()
            for s in range(2):
                self.half[slot, s] = self.add(
                    self.whole[slot, s, self.rows_at(p.core, self.rows // 2), :], self.from_core[k % self.from_core.shape[0], s]
                )
            self.shard_copy(k, slot).start()

        def after_shard(k, slot):
            self.shard_copy(k, slot).wait()
            self.own[slot] = self.add(self.half[slot, p.shard], self.from_shard[k % self.from_shard.shape[0]])
            self.side_copy(k, slot).start()

        def after_side(k, slot):
            self.side_copy(k, slot).wait()
            self.mine[slot] = self.add(
                self.own[slot, self.rows_at(p.side, self.rows // 4), :], self.from_side[k % self.from_side.shape[0]]
            )
            for step in range(1, 4):
                self.depth_copy(k, slot, step).start()

        def after_depth(k, slot):
            for step in range(1, 4):
                self.depth_copy(k, slot, step).wait()
            rows, cols = self.quarter(0, p.depth)
            total = self.mine[slot, rows, cols].astype(f32)
            for step in range(3):
                total = total + self.from_depth[k % self.from_depth.shape[0], step].astype(f32)
            rows, cols = self.quarter(p.side * (self.rows // 4), p.depth)
            self.back[k % self.back.shape[0], rows, cols] = total.astype(self.dtype)
            for step in range(1, 4):
                self.depth_back(k, step).start()

        def after_depth_back(k, slot):
            for step in range(1, 4):
                self.depth_back(k, step).wait()
            self.side_back(k).start()

        def after_side_back(k, slot):
            self.side_back(k).wait()
            self.out(self, k)

        def after_core_back(k, slot):
            self.wait_home(k)

        for lag, body in enumerate(
            (after_core, after_shard, after_side, after_depth, after_depth_back, after_side_back, after_core_back), 1
        ):
            self.when(tick, lag, body)


LAGS = 7
DOWN, UP, OUT, IN = 4, 4, 1, STEPS
CHUNKS = DOWN + UP + OUT + IN
SMALL_ROWS = 128
SMALL_TICK = 9
ROW_BLOCK = 128


GIVEN_ROW, TAP_ROW, LONG_ROW, NORM_ROW = 64, 72, 96, 98


def exact(left, right, dims):
    return lax.dot_general(left, right, (dims, ((), ())), precision=HIGH, preferred_element_type=f32)


def reduce_kernel(
    sums, d_shift, active0, active1, upstream, second_h, d_hidden, mixed_h, d_middle_h, normed_h, tokens_h, gain, middle, down0, down1,
    grad_ref, z_ref, rows_ref, long_ref, bank1, bank2, hat1_ref, hat2_ref, mid_ref, ahead_ref, back_ref,
    in_ref, decay_ref, decay2_ref, third1_ref, third2_ref, ratio_ref, embed_ref, pre1_ref, act1_ref, pre2_ref, act2_ref,
    second_w_ref,
    small_out, g_down, g_up, g_out, g_in, tokens_out, result_out,
    d_proj, dtap, dtaps, dlong, dlongs, dfilt1, dfilt2, dbank1, dbank2, d_normed, d_act, out_rows, out_sem, middle_sem,
    second, mixed, d_middle, normed, tokens, late_sem, *scratch,
):
    tick = pl.program_id(0)
    place = Place()
    bufs, sems = scratch[:9], scratch[9:24]
    small_bufs, small_sems = scratch[24:33], scratch[33:48]
    everything = slice(None)
    is_in = (tick % 3 == 2) & (tick < 9)
    tile = tick // 3

    def little_home(chain, k):
        chain.send_home(k, [(everything, small_out, (k,), (everything,))])

    def kinds(k):
        down = (k < 5) & (k % 3 < 2)
        up = ((k >= 6) & (k < 8)) | (k >= 10)
        return down, up, k == 9, (k < 9) & (k % 3 == 2)

    def big_home(chain, k):
        down, up, out, inward = kinds(k)

        @pl.when(down)
        def _():
            chain.send_home(k, [(everything, g_down, (k - k // 3,), (everything,))])

        @pl.when(up)
        def _():
            index = k - 6 - 2 * (k // 9)
            cols = pl.ds(pl.multiple_of(index * D, D), D)
            chain.send_home(k, [(everything, g_up, (), (cols,))])

        @pl.when(out)
        def _():
            chain.send_home(k, [(everything, g_out, (), (everything,))])

        @pl.when(inward)
        def _():
            chain.send_home(
                k,
                [
                    (part(p), g_in, (), (pl.ds(pl.multiple_of(p * D + (k // 3) * TILE, TILE), TILE),))
                    for p in range(3)
                ],
            )

    little = Reduction(place, SMALL_TICK, 1, SMALL_ROWS, small_bufs, small_sems, little_home)
    big = Reduction(place, 0, CHUNKS, D // 2, bufs, sems, big_home)
    pack = little.whole
    late = [
        pltpu.make_async_copy(src, dst, late_sem.at[i])
        for i, (src, dst) in enumerate(
            ((normed_h, normed), (second_h, second), (mixed_h, mixed), (d_middle_h, d_middle), (tokens_h, tokens))
        )
    ]

    @pl.when(tick == 0)
    def _():
        for one in late:
            one.start()
        greet(
            [place.other_shard(), place.other_side(), place.other_core()]
            + [place.other_depth(step) for step in range(1, 4)]
        )
        pack[...] = jnp.zeros_like(pack)
        for s in range(2):
            pack[0, s, GIVEN_ROW : GIVEN_ROW + 4, D // 2 :] = sums[0:4, s * (D // 2) : (s + 1) * (D // 2)]
            for a in range(4):
                at = s * 2 * D + a * (D // 2)
                pack[0, s, GIVEN_ROW + 4 + a : GIVEN_ROW + 5 + a, D // 2 :] = d_shift[0:1, at : at + D // 2]
        d_act[...] = jnp.zeros_like(d_act)

    little.advance(tick)
    big.advance(tick)

    def chunk(slot, lefts, right):
        for s in range(2):
            big.whole[slot, s] = inner_rows(lefts[s], right).astype(bf16)

    def halves(left):
        return left[:, : D // 2], left[:, D // 2 :]

    def compute(k, slot):
        down, up, out, inward = kinds(k)

        @pl.when(down)
        def _():
            chunk(slot, (active0[...], active1[...]), upstream[...])

        @pl.when(up)
        def _():
            chunk(slot, halves(second), d_hidden[...])

        @pl.when(out)
        def _():
            chunk(slot, halves(mixed), d_middle[...].astype(bf16))

        @pl.when(inward)
        def _():
            chunk(slot, halves(normed), d_proj[...])

    for first, those in ((2, late[:1]), (6, late[1:2]), (SMALL_TICK, late[2:])):
        @pl.when(tick == first)
        def _():
            for one in those:
                one.wait()

    big.when(tick, 0, compute)
    big.send(tick)

    @pl.when((tick < 8) & (tick % 3 < 2))
    def _():
        micro = tick % 3
        backward_step(
            micro == 0, micro == 1, grad_ref, z_ref, rows_ref, long_ref, bank1, bank2,
            hat1_ref, hat2_ref, mid_ref, ahead_ref, back_ref,
            d_proj.at[pl.ds(pl.multiple_of(micro * SPAN, SPAN), SPAN), :], dtap, dlong, dfilt1, dfilt2, dbank1, dbank2,
        )

    @pl.when(is_in)
    def _():
        cols = pl.ds(pl.multiple_of(tile * TILE, TILE), TILE)
        dtaps[tile] = dtap[...]
        dlongs[:, cols] = dlong[...]
        step = times_t(d_proj[...], in_ref[...])

        @pl.when(tile == 0)
        def _():
            d_normed[...] = step

        @pl.when(tile > 0)
        def _():
            d_normed[...] += step

        for q, (grads, decay, third) in enumerate(
            ((dfilt1, decay_ref, third1_ref), (dfilt2, decay2_ref, third2_ref))
        ):
            window = jnp.exp(-ratio_ref[...] * decay[...])
            d_taps = grads[...] * window
            pack[0, q, 0 : act2_ref.shape[1], cols] = exact(act2_ref[...], d_taps, ((0,), (0,)))
            d_act[...] += exact(d_taps, third[...], ((1,), (1,)))

    @pl.when(tick == SMALL_TICK)
    def _():
        for s in range(2):
            for a in range(3):
                for b in range(3):
                    at = s * (D3 // 2) + a * (D // 2) + b * 128
                    p, t, o = at // D, at % D // TILE, at % TILE
                    pack[0, s, TAP_ROW + 8 * a : TAP_ROW + 8 * a + 8, D // 2 + b * 128 : D // 2 + b * 128 + 128] = dtaps[
                        t, :, p * TILE + o : p * TILE + o + 128
                    ]
            pack[0, s, LONG_ROW : LONG_ROW + 2, D // 2 :] = dlongs[:, s * (D // 2) : (s + 1) * (D // 2)]

        def norm_rows(i, sums):
            rows = pl.ds(pl.multiple_of(i * ROW_BLOCK, ROW_BLOCK), ROW_BLOCK)
            values = tokens[rows, :].astype(f32)
            grads = d_normed[rows, :]
            center = values - jnp.mean(values, axis=-1, keepdims=True)
            scale = lax.rsqrt(jnp.mean(center * center, axis=-1, keepdims=True) + EPS)
            unit = center * scale
            scaled = grads * gain[0:1, :]
            inner = scaled - jnp.mean(scaled, axis=-1, keepdims=True)
            inner = inner - unit * jnp.mean(scaled * unit, axis=-1, keepdims=True)
            out_rows[rows, :] = (scale * inner + d_middle[rows, :]).astype(bf16)
            return (
                sums[0] + jnp.sum(grads * unit, axis=0, keepdims=True),
                sums[1] + jnp.sum(grads, axis=0, keepdims=True),
            )

        zero = jnp.zeros((1, D), f32)
        sums = lax.fori_loop(0, tokens.shape[0] // ROW_BLOCK, norm_rows, (zero, zero))
        d_pre2 = d_act[...] * jnp.cos(pre2_ref[...])
        g_second = exact(act1_ref[...], d_pre2, ((0,), (0,)))
        g_b2 = jnp.sum(d_pre2, axis=0, keepdims=True)
        d_pre1 = exact(d_pre2, second_w_ref[...], ((1,), (1,))) * jnp.cos(pre1_ref[...])
        g_first = exact(embed_ref[...], d_pre1, ((0,), (0,)))
        g_b1 = jnp.sum(d_pre1, axis=0, keepdims=True)
        wide = g_second.shape[1] // 2
        for s in range(2):
            own = slice(s * wide, (s + 1) * wide)
            for i in range(2):
                pack[0, s, NORM_ROW + i : NORM_ROW + i + 1, D // 2 :] = sums[i][:, s * (D // 2) : (s + 1) * (D // 2)]
            pack[0, s, 64 : 64 + g_first.shape[0], 0:wide] = g_first[:, own]
            pack[0, s, 64 + g_first.shape[0] : 65 + g_first.shape[0], 0:wide] = g_b1[:, own]
            pack[0, s, 65 + g_first.shape[0] : 66 + g_first.shape[0], 0:wide] = g_b2[:, own]
            pack[0, s, 64 : 64 + g_second.shape[0], 128 : 128 + wide] = g_second[:, own]
        pltpu.make_async_copy(out_rows, tokens_out, out_sem).start()

    little.send(tick)

    @pl.when(tick == SMALL_TICK + 2)
    def _():
        pltpu.make_async_copy(out_rows, tokens_out, out_sem).wait()
        pltpu.make_async_copy(middle, d_normed, middle_sem).start()

    @pl.when((tick >= CHUNKS) & (tick < CHUNKS + DOWN))
    def _():
        @pl.when(tick == CHUNKS)
        def _():
            pltpu.make_async_copy(middle, d_normed, middle_sem).wait()

        def result_rows(i, carry):
            rows = pl.ds(pl.multiple_of(i * 256, 256), 256)
            total = d_normed[rows, :] + lowmul(active0[rows, :], down0[...]) + lowmul(active1[rows, :], down1[...])
            d_normed[rows, :] = total

            @pl.when(tick == CHUNKS + DOWN - 1)
            def _():
                out_rows[rows, :] = (total + gain[5:6, :]).astype(bf16)

            return carry

        lax.fori_loop(0, out_rows.shape[0] // 256, result_rows, 0)

        @pl.when(tick == CHUNKS + DOWN - 1)
        def _():
            pltpu.make_async_copy(out_rows, result_out, out_sem).start()

    @pl.when(tick == CHUNKS + LAGS - 1)
    def _():
        pltpu.make_async_copy(out_rows, result_out, out_sem).wait()


def reduce_grads(
    sums, d_shift, active, upstream, second, d_hidden, mixed, d_middle, normed, tokens, middle, down_full,
    d_mixed, z, lines, vecs, bank1, bank2, hat1, hat2, mid, in_full, decay, third_w, states, second_w,
):
    count = upstream.shape[0]
    half = D // 2
    hidden = second_w.shape[0]
    embed, pre1, act1, pre2, act2 = states

    def fixed(shape):
        return pl.BlockSpec(shape, lambda t: (0,) * len(shape), pipeline_mode=pl.Buffered(1))

    def at_tile(shape, where):
        def index(t):
            tick = jnp.minimum(t, 8)
            return where(jnp.minimum(tick % 3, 1), tick // 3)

        return pl.BlockSpec(shape, index)

    hbm = pl.BlockSpec(memory_space=pl.ANY)

    def down_index(t):
        tick = jnp.minimum(t, 4)
        late = jnp.minimum(jnp.maximum(t - (CHUNKS - 1), 0), 1)
        return tick - tick // 3 - 3 * late + late_index(t)

    def late_index(t):
        return jnp.minimum(jnp.maximum(t - CHUNKS, 0), DOWN - 1)

    def up_index(t):
        return jnp.minimum(jnp.maximum(t - 6, 0), 2) + jnp.minimum(jnp.maximum(t - 10, 0), 1)

    hat_spec = at_tile((4, FREQ, TILE), lambda m, t: (m, 0, t))
    row_spec = at_tile((SPAN, TILE), lambda m, t: (m, t))
    bank_spec = at_tile((3, FREQ, TILE), lambda m, t: (0, 0, t))
    decay_shape = (1, TILE)

    def buffers(n, rows, kind):
        few, many = min(n, 4), min(n, 8)
        return [
            pltpu.VMEM((min(n, 2), 2, rows, D), kind),
            pltpu.VMEM((few, 2, rows // 2, D), kind),
            pltpu.VMEM((min(n, 2), 2, rows // 2, D), kind),
            pltpu.VMEM((few, rows // 2, D), kind),
            pltpu.VMEM((min(n, 2), rows // 2, D), kind),
            pltpu.VMEM((few, rows // 4, D), kind),
            pltpu.VMEM((min(n, 2), rows // 4, D), kind),
            pltpu.VMEM((few, 3, rows // 8, D // 2), kind),
            pltpu.VMEM((many, rows // 2, D), kind),
        ]

    def semaphores(n):
        one = pltpu.SemaphoreType.DMA((n,))
        three = pltpu.SemaphoreType.DMA((n, 3))
        return [one] * 6 + [three] * 4 + [one] * 5

    return pl.pallas_call(
        reduce_kernel,
        grid=(CHUNKS + LAGS,),
        in_specs=[
            fixed(sums.shape),
            fixed(d_shift.shape),
            pl.BlockSpec((count, half), lambda t: (0, down_index(t))),
            pl.BlockSpec((count, half), lambda t: (0, DOWN + down_index(t))),
            fixed((count, D)),
            hbm,
            pl.BlockSpec((count, D), lambda t: (0, up_index(t))),
            hbm, hbm, hbm, hbm,
            fixed((8, D)),
            pl.BlockSpec(memory_space=pl.ANY),
            pl.BlockSpec((half, D), lambda t: (late_index(t), 0)),
            pl.BlockSpec((half, D), lambda t: (DOWN + late_index(t), 0)),
            row_spec,
            at_tile((SPAN, 3 * TILE), lambda m, t: (m, t)),
            at_tile((8, 3 * TILE), lambda m, t: (0, t)),
            at_tile((8, TILE), lambda m, t: (0, t)),
            bank_spec, bank_spec, hat_spec, hat_spec, row_spec,
            fixed(AHEAD),
            fixed(BACK),
            at_tile((D, 3 * TILE), lambda m, t: (0, t)),
            at_tile(decay_shape, lambda m, t: (0, t)),
            at_tile(decay_shape, lambda m, t: (0, STEPS + t)),
            at_tile((hidden, TILE), lambda m, t: (0, t)),
            at_tile((hidden, TILE), lambda m, t: (0, STEPS + t)),
            fixed((SEQ, 1)),
            fixed(embed.shape),
            fixed(pre1.shape),
            fixed(act1.shape),
            fixed(pre2.shape),
            fixed(act2.shape),
            fixed(second_w.shape),
        ],
        out_specs=[pl.BlockSpec(memory_space=pl.ANY)] * 7,
        out_shape=[
            jax.ShapeDtypeStruct((1, SMALL_ROWS, D), f32),
            jax.ShapeDtypeStruct((DOWN, half, D), bf16),
            jax.ShapeDtypeStruct((half, UP * D), bf16),
            jax.ShapeDtypeStruct((half, D), bf16),
            jax.ShapeDtypeStruct((half, D3), bf16),
            jax.ShapeDtypeStruct((count, D), bf16),
            jax.ShapeDtypeStruct((count, D), bf16),
        ],
        scratch_shapes=[
            pltpu.VMEM((count, 3 * TILE), bf16),
            pltpu.VMEM((8, 3 * TILE), f32),
            pltpu.VMEM((STEPS, 8, 3 * TILE), f32),
            pltpu.VMEM((2, TILE), f32),
            pltpu.VMEM((2, D), f32),
            pltpu.VMEM((SEQ, TILE), f32),
            pltpu.VMEM((SEQ, TILE), f32),
            pltpu.VMEM((3, FREQ, TILE), f32),
            pltpu.VMEM((3, FREQ, TILE), f32),
            pltpu.VMEM((count, D), f32),
            pltpu.VMEM((SEQ, hidden), f32),
            pltpu.VMEM((count, D), bf16),
            pltpu.SemaphoreType.DMA(()),
            pltpu.SemaphoreType.DMA(()),
            pltpu.VMEM((count, D), bf16),
            pltpu.VMEM((count, D), bf16),
            pltpu.VMEM((count, D), f32),
            pltpu.VMEM((count, D), bf16),
            pltpu.VMEM((count, D), bf16),
            pltpu.SemaphoreType.DMA((5,)),
        ]
        + buffers(CHUNKS, half, bf16) + semaphores(CHUNKS) + buffers(1, SMALL_ROWS, f32) + semaphores(1),
        compiler_params=pltpu.CompilerParams(
            collective_id=1, has_side_effects=True, vmem_limit_bytes=63 * 2**20
        ),
        name="reduce_grads",
    )(
        sums, d_shift, active, active, upstream, second, d_hidden, mixed, d_middle, normed, tokens, vecs, middle, down_full, down_full,
        d_mixed, z, lines, vecs, bank1, bank2, hat1, hat2, mid, *constants(), in_full,
        decay, decay, third_w, third_w, jnp.asarray(place_ratio()), embed, pre1, act1, pre2, act2, second_w,
    )


HID = 768
GELU_A = math.sqrt(2.0 / math.pi)
GELU_B = 0.044715


def middle_kernel(
    mixed, tokens, upstream, out_ref, vecs, up_ref, shift_ref, down_ref,
    middle_ref, second, active_ref, d_hidden_ref, d_middle_ref, d_mixed_ref, sums_ref, d_shift_ref, d_second_ref,
):
    first = pl.program_id(0) == 0
    last = pl.program_id(0) == pl.num_programs(0) - 1
    steps = second.shape[0] // 256

    def rows_of(i):
        return pl.ds(pl.multiple_of(i * 256, 256), 256)

    @pl.when(first)
    def _():
        def front(i, carry):
            rows = rows_of(i)
            value = tokens[rows, :].astype(f32) + lowmul(mixed[rows, :], out_ref[...]) + vecs[2:3, :]
            middle_ref[rows, :] = value
            second[rows, :] = layer_norm(value, vecs[3:4, :], vecs[4:5, :]).astype(bf16)
            return carry

        lax.fori_loop(0, steps, front, 0)
        d_second_ref[...] = jnp.zeros_like(d_second_ref)

    def block(i, total):
        rows = rows_of(i)
        hidden = lowmul(second[rows, :], up_ref[...]) + shift_ref[...]
        d_active = times_t(upstream[rows, :], down_ref[...])
        square = hidden * hidden
        curve = jnp.tanh(GELU_A * hidden * (1.0 + GELU_B * square))
        half = 0.5 * (1.0 + curve)
        active_ref[rows, :] = (hidden * half).astype(bf16)
        slope = half + 0.5 * hidden * (1.0 - curve * curve) * (GELU_A * (1.0 + 3.0 * GELU_B * square))
        d_hidden = (d_active * slope).astype(bf16)
        d_hidden_ref[rows, :] = d_hidden
        d_second_ref[rows, :] += times_t(d_hidden, up_ref[...])
        return total + jnp.sum(d_hidden.astype(f32), axis=0, keepdims=True)

    d_shift_ref[...] = lax.fori_loop(0, steps, block, jnp.zeros(d_shift_ref.shape, f32), unroll=2)

    @pl.when(last)
    def _():
        def back(i, sums):
            rows = rows_of(i)
            values = middle_ref[rows, :]
            grads = d_second_ref[rows, :]
            given = upstream[rows, :].astype(f32)
            center = values - jnp.mean(values, axis=-1, keepdims=True)
            scale = lax.rsqrt(jnp.mean(center * center, axis=-1, keepdims=True) + EPS)
            unit = center * scale
            scaled = grads * vecs[3:4, :]
            inner = scaled - jnp.mean(scaled, axis=-1, keepdims=True)
            inner = inner - unit * jnp.mean(scaled * unit, axis=-1, keepdims=True)
            value = scale * inner + given
            d_middle_ref[rows, :] = value
            branch = value.astype(bf16)
            d_mixed_ref[rows, :] = times_t(branch, out_ref[...])
            new = (branch.astype(f32), grads * unit, grads, given)
            return tuple(old + jnp.sum(one, axis=0, keepdims=True) for old, one in zip(sums, new))

        zero = jnp.zeros((1, D), f32)
        sums_ref[...] = jnp.zeros_like(sums_ref)
        for i, one in enumerate(lax.fori_loop(0, steps, back, (zero,) * 4)):
            sums_ref[i : i + 1, :] = one


def run_middle(mixed, tokens, upstream, out_full, vecs, up_full, up_shift, down_full):
    count = tokens.shape[0]
    units = up_full.shape[1]

    def fixed(*shape):
        return pl.BlockSpec(shape, lambda j: (0,) * len(shape), pipeline_mode=pl.Buffered(1))

    columns = pl.BlockSpec((count, HID), lambda j: (0, j))
    row = pl.BlockSpec((1, HID), lambda j: (0, j))
    tall = fixed(count, D)
    wide = jax.ShapeDtypeStruct((count, units), bf16)
    full = jax.ShapeDtypeStruct((count, D), f32)
    return pl.pallas_call(
        middle_kernel,
        grid=(units // HID,),
        in_specs=[
            tall, tall, tall, fixed(D, D), fixed(8, D), pl.BlockSpec((D, HID), lambda j: (0, j)), row,
            pl.BlockSpec((HID, D), lambda j: (j, 0)),
        ],
        out_specs=[tall, tall, columns, columns, tall, tall, fixed(8, D), row],
        out_shape=[
            full, jax.ShapeDtypeStruct((count, D), bf16), wide, wide, full, full, jax.ShapeDtypeStruct((8, D), f32),
            jax.ShapeDtypeStruct((1, units), f32),
        ],
        scratch_shapes=[pltpu.VMEM((count, D), f32)],
        compiler_params=pltpu.CompilerParams(vmem_limit_bytes=63 * 2**20),
        cost_estimate=pl.CostEstimate(
            flops=6 * count * D * units, bytes_accessed=40 * 2**20, transcendentals=count * units
        ),
        name="middle",
    )(mixed, tokens, upstream, out_full, vecs, up_full, up_shift, down_full)


def finish_kernel(
    small, result, d_tokens, down, up, out, inward,
    prompt_out, cont_out, prompt_grad, cont_grad,
    g_gain1, g_shift1, g_in, g_in_b, g_taps, g_short_b, g_long, g_w1, g_b1, g_w2, g_b2, g_w3,
    g_out, g_out_b, g_gain2, g_shift2, g_up, g_up_b, g_down, g_down_b,
):
    step = pl.program_id(0)
    for src, dst in ((down, g_down), (up, g_up), (out, g_out), (inward, g_in)):
        dst[...] = src[...].astype(f32)

    @pl.when(step % 4 < 2)
    def _():
        prompt_out[0, 0] = result[...]
        prompt_grad[0, 0] = d_tokens[...]

    @pl.when(step % 4 >= 2)
    def _():
        cont_out[0, 0, 0] = result[...]
        cont_grad[0, 0, 0] = d_tokens[...]

    @pl.when(step == 0)
    def _():
        half = slice(D // 2, D)

        def lines(start, count, stride=1):
            rows = [small[0, start + stride * i : start + stride * i + 1, half] for i in range(count)]
            return jnp.concatenate(rows, axis=1)

        def put(ref, value):
            ref[...] = value.reshape(ref.shape)

        for i, ref in enumerate((g_out_b, g_gain2, g_shift2, g_down_b)):
            put(ref, lines(GIVEN_ROW + i, 1))
        put(g_up_b, lines(GIVEN_ROW + 4, 4))
        for i in range(3):
            g_taps[i : i + 1, :] = lines(TAP_ROW + i, 3, 8)
        put(g_short_b, lines(TAP_ROW + 3, 3, 8))
        put(g_in_b, lines(TAP_ROW + 4, 3, 8))
        g_long[...] = small[0, LONG_ROW : LONG_ROW + 2, half]
        put(g_gain1, lines(NORM_ROW, 1))
        put(g_shift1, lines(NORM_ROW + 1, 1))
        g_w3[...] = small[0, 0 : g_w3.shape[0], :]
        wide, n1 = g_w1.shape
        g_w1[...] = small[0, 64 : 64 + n1, 0:wide].T
        put(g_b1, small[0, 64 + n1 : 65 + n1, 0:wide])
        put(g_b2, small[0, 65 + n1 : 66 + n1, 0:wide])
        g_w2[...] = small[0, 64 : 64 + g_w2.shape[1], 128 : 128 + wide].T


def finish(shapes, micros, small, result, d_tokens, down, up, out, inward):
    steps = 4 * micros

    def rows(value):
        return pl.BlockSpec((value.shape[0] // steps, value.shape[1]), lambda i: (i, 0))

    def fixed(value):
        return pl.BlockSpec(value.shape, lambda i: (0,) * len(value.shape))

    inputs = (small, result, d_tokens, down.reshape(-1, D), up, out, inward)
    prompt = pl.BlockSpec((1, 1, BLOCK, D), lambda i: (i // 4, 0, jnp.minimum(i % 4, 1), 0))
    cont = pl.BlockSpec((1, 1, 1, BLOCK, D), lambda i: (i // 4, 0, jnp.maximum(i % 4 - 2, 0), 0, 0))
    big = {6: inward, 16: out, 20: up, 22: down}
    specs = [prompt, cont, prompt, cont] + [rows(one) if i in big else fixed(one) for i, one in enumerate(shapes) if i > 3]
    return pl.pallas_call(
        finish_kernel,
        grid=(steps,),
        in_specs=[fixed(small)] + [rows(one) for one in inputs[1:]],
        out_specs=specs,
        out_shape=shapes,
        compiler_params=pltpu.CompilerParams(vmem_limit_bytes=63 * 2**20),
        name="finish",
    )(*inputs)


def per_device(
    prompt_x, cont_x, prompt_cot, cont_cot, norm1_gain, norm1_bias, in_weight, in_bias, short_weight,
    short_bias, long_bias, filter_w1, filter_b1, filter_w2, filter_b2, filter_w3, filter_decay, out_weight,
    out_bias, norm2_gain, norm2_bias, up_weight, up_bias, down_weight, down_bias, *, reps, shards,
):
    own_kernels = reps == 16 and shards == 2 and prompt_x.shape[1] == 1
    micros = prompt_x.shape[0]
    groups = prompt_x.shape[1]
    count = micros * groups * SPAN

    def tokens_of(prompt, cont):
        return jnp.concatenate(
            [
                prompt.reshape(micros * groups, PROMPT, D),
                cont.reshape(micros * groups, CONTS * BLOCK, D),
            ],
            axis=1,
        ).reshape(count, D)

    def parts_of(rows):
        rows = rows.reshape(micros, groups, SPAN, D)
        return rows[:, :, :PROMPT], rows[:, :, PROMPT:].reshape(micros, groups, CONTS, BLOCK, D)

    n1 = filter_w1.shape[0]
    n2 = filter_w2.shape[0]
    if own_kernels:
        (projected, mixed_low, hat1, hat2, mid, bank1, bank2, vecs, lines, up_shift, decay, fw2, fw3,
         pre1, act1, pre2, act2, normed_low, tokens_low, upstream, in_full, out_full, up_full, down_full) = gather_weights(
            norm1_gain, norm1_bias, in_bias, short_weight, short_bias, long_bias, filter_w1.T, filter_b1, filter_w2.T,
            filter_b2, filter_w3, filter_decay, out_bias, norm2_gain, norm2_bias, up_bias, down_bias,
            in_weight, out_weight, up_weight, down_weight,
            *(one.reshape(micros, PROMPT, D) for one in (prompt_x, cont_x, prompt_cot, cont_cot)),
        )
        states = (jnp.asarray(embed_table()), pre1, act1, pre2, act2)
    else:
        tokens_low = tokens_of(prompt_x, cont_x)
        upstream = tokens_of(prompt_cot, cont_cot)

        def gather(value, axis=0):
            return lax.all_gather(value, "shard", axis=axis, tiled=True)

        gain1, shift1, out_shift, gain2, shift2, down_shift, in_shift, short_shift, up_shift, decay, fb1, fb2 = (
            gather(one).astype(f32)
            for one in (norm1_gain, norm1_bias, out_bias, norm2_gain, norm2_bias, down_bias, in_bias, short_bias,
                        up_bias, filter_decay, filter_b1, filter_b2)
        )
        taps, long_shift, fw1, fw2, fw3 = (
            gather(one, 1).astype(f32) for one in (short_weight, long_bias, filter_w1, filter_w2, filter_w3)
        )
        in_full, out_full, up_full, down_full = (
            gather(one) for one in (by_tile(in_weight), out_weight, up_weight, down_weight)
        )
        up_shift = up_shift[None]
        lines = by_tile(jnp.concatenate([taps, short_shift[None], in_shift[None], jnp.zeros((3, D3), f32)], axis=0))
        vecs = jnp.stack([gain1, shift1, out_shift, gain2, shift2, down_shift])
        vecs = jnp.concatenate([vecs, long_shift], axis=0)
        filters, filter_pull = jax.vjp(partial(filter_taps, decay=decay), fw1, fb1, fw2, fb2, fw3)
        normed, norm_pull = jax.vjp(layer_norm, tokens_low.astype(f32), gain1, shift1)
        normed_low = normed.astype(bf16)
        projected = lowmul(normed_low, in_full) + lines[4]
        mixed_low, hat1, hat2, mid, bank1, bank2 = run_forward(projected, lines, vecs, filters)
    middle, second_low, active_low, d_hidden, d_middle, d_mixed, sums, d_up_shift = run_middle(
        mixed_low, tokens_low, upstream, out_full, vecs, up_full, up_shift, down_full
    )
    width = D // shards

    def by_shard(value):
        rows = value.shape[0]
        return value.reshape(rows, shards, -1).swapaxes(0, 1).reshape(shards, -1, width)

    if own_kernels:
        small, grad_down, grad_up, grad_out, grad_in, d_tokens, result = reduce_grads(
            sums, d_up_shift, active_low, upstream, second_low, d_hidden, mixed_low, d_middle, normed_low,
            tokens_low, middle, down_full, d_mixed, projected, lines, vecs, bank1, bank2, hat1, hat2, mid, in_full, decay, fw3, states, fw2,
        )
        args = (norm1_gain, norm1_bias, in_weight, in_bias, short_weight, short_bias, long_bias, filter_w1, filter_b1,
                filter_w2, filter_b2, filter_w3, out_weight, out_bias, norm2_gain, norm2_bias, up_weight, up_bias,
                down_weight, down_bias)
        shapes = [jax.ShapeDtypeStruct(one.shape, bf16) for one in (prompt_x, cont_x) * 2]
        shapes += [jax.ShapeDtypeStruct(one.shape, f32) for one in args]
        for i in (11, 13):
            shapes[i] = jax.ShapeDtypeStruct(shapes[i].shape[::-1], f32)
        outs = list(finish(shapes, micros, small, result, d_tokens, grad_down, grad_up, grad_out, grad_in))
        outs[11], outs[13] = outs[11].T, outs[13].T
        return tuple(outs)
    else:
        def reduce(value, axis=0):
            value = lax.psum_scatter(value, "shard", scatter_dimension=axis, tiled=True)
            return lax.psum(value, "rep")

        result = (middle + lowmul(active_low, down_full) + down_shift).astype(bf16)
        prompt_out, cont_out = parts_of(result)
        d_proj, d_taps, d_long, d_filter1, d_filter2 = run_backward(
            d_mixed, projected, lines, vecs, bank1, bank2, hat1, hat2, mid
        )
        d_tokens, grad_gain1, grad_shift1 = norm_pull(times_t(d_proj, in_full))
        prompt_grad, cont_grad = parts_of((d_tokens + d_middle).astype(bf16))
        filter_grads_all = filter_pull(jnp.concatenate([d_filter1, d_filter2], axis=-1))
        narrow_own = [reduce(one, one.ndim - 1) for one in filter_grads_all[:4]]
        third_grad = reduce(filter_grads_all[4], 1)
        given = jnp.concatenate([by_shard(sums[:4]), by_shard(d_up_shift)], axis=1)
        given = reduce(given)[0]
        tap_rows = reduce(by_part(d_taps[:5]), 1)
        long_rows = reduce(d_long, 1)
        norm_rows = reduce(jnp.stack([grad_gain1, grad_shift1]), 1)
        grad_down = reduce(inner_rows(active_low, upstream))
        grad_up = reduce(inner_rows(second_low, d_hidden))
        grad_out = reduce(inner_rows(mixed_low, d_middle.astype(bf16)))
        grad_in = by_part(reduce(inner_rows(normed_low, d_proj)))
    return (
        prompt_out,
        cont_out,
        prompt_grad,
        cont_grad,
        norm_rows[0],
        norm_rows[1],
        grad_in,
        tap_rows[4],
        tap_rows[:3],
        tap_rows[3],
        long_rows,
        *narrow_own,
        third_grad,
        grad_out,
        given[0],
        given[1],
        given[2],
        grad_up,
        given[4:].reshape(-1),
        grad_down,
        given[3],
    )


def solution(mesh):
    group4 = P(None, ("rep", "shard"), None, None)
    group5 = P(None, ("rep", "shard"), None, None, None)
    one, row, col = P("shard"), P("shard", None), P(None, "shard")
    grads = (one, one, row, one, col, one, col, col, one, col, one, col)
    rest = (row, one, one, one, row, one, row, one)
    return jax.shard_map(
        partial(per_device, reps=mesh.shape["rep"], shards=mesh.shape["shard"]),
        mesh=mesh,
        in_specs=(group4, group5, group4, group5) + grads + (one,) + rest,
        out_specs=(group4, group5, group4, group5) + grads + rest,
        check_vma=False,
    )
```

```python
from functools import partial
import math

import jax
import jax.numpy as jnp
import numpy as np
from jax import lax
from jax.experimental import pallas as pl
from jax.experimental.pallas import tpu as pltpu
from jax.sharding import PartitionSpec as P

D = 768
D3 = 3 * D
BANDS = 16
BLOCK = 128
PROMPT = 256
CONTS = 2
SEQ = 384
SPAN = PROMPT + CONTS * BLOCK
TILE = 256
FREQ = 2 * BLOCK

EPS = 1e-05
HIGH = lax.Precision.HIGHEST
f32 = jnp.float32
bf16 = jnp.bfloat16


def matmul(left_op, right_op):
    return jnp.dot(left_op, right_op, precision=HIGH, preferred_element_type=f32)


def lowmul(left_op, right_op):
    return jnp.dot(left_op, right_op, preferred_element_type=f32)


def inner_rows(left_op, right_op):
    return lax.dot_general(
        left_op, right_op, (((0,), (0,)), ((), ())), preferred_element_type=f32
    )


def times_t(left_op, right_op):
    return lax.dot_general(
        left_op, right_op, (((1,), (1,)), ((), ())), preferred_element_type=f32
    )


def layer_norm(values, norm_gain, norm_shift):
    center_val = values - jnp.mean(values, axis=-1, keepdims=True)
    spread = jnp.mean(center_val * center_val, axis=-1, keepdims=True)
    return center_val * lax.rsqrt(spread + EPS) * norm_gain + norm_shift


def dft_matrix():
    freq = np.arange(BLOCK)
    place = np.arange(BLOCK)
    angle = np.pi * ((2 * freq[:, None] + 1) * place[None, :] % (4 * BLOCK)) / FREQ
    return np.concatenate([np.cos(angle), -np.sin(angle)], axis=0)


def split3(matrix):
    matrix = matrix.astype(np.float32)
    high = matrix.astype(jnp.bfloat16)
    rest = (matrix - high.astype(np.float32)).astype(jnp.bfloat16)
    return np.concatenate([high, rest, high], axis=1)


def split_dot(triple, signal):
    high = signal.astype(bf16)
    rest = (signal - high.astype(f32)).astype(bf16)
    return jnp.dot(
        triple, jnp.concatenate([high, high, rest], axis=0), preferred_element_type=f32
    )


def cmul(left, right):
    lr, li = left[:BLOCK], left[BLOCK:]
    rr, ri = right[:BLOCK], right[BLOCK:]
    return jnp.concatenate([lr * rr - li * ri, lr * ri + li * rr], axis=0)


def cmul_conj(left, right):
    lr, li = left[:BLOCK], left[BLOCK:]
    rr, ri = right[:BLOCK], right[BLOCK:]
    return jnp.concatenate([lr * rr + li * ri, lr * ri - li * rr], axis=0)


def row_index():
    return lax.broadcasted_iota(jnp.int32, (BLOCK, TILE), 0)


def delayed(block, before, lag):
    rolled = pltpu.roll(block, lag, 0)
    if before is None:
        return jnp.where(row_index() >= lag, rolled, 0.0)
    return jnp.where(row_index() >= lag, rolled, pltpu.roll(before, lag, 0))


def advanced(block, after, lag):
    rolled = pltpu.roll(block, BLOCK - lag, 0)
    if after is None:
        return jnp.where(row_index() < BLOCK - lag, rolled, 0.0)
    return jnp.where(row_index() < BLOCK - lag, rolled, pltpu.roll(after, BLOCK - lag, 0))


BEFORE = (None, 0, 1, 1)


def part(index):
    return slice(index * TILE, (index + 1) * TILE)


def load_blocks(ref, cols=slice(None)):
    return [ref[i * BLOCK : (i + 1) * BLOCK, cols] for i in range(4)]


def short_blocks(z_ref, rows_ref, index):
    blocks = load_blocks(z_ref, part(index))
    taps = rows_ref[0:3, part(index)]
    shift = rows_ref[3:4, part(index)]
    outs = []
    for i in range(4):
        before = None if BEFORE[i] is None else blocks[BEFORE[i]]
        outs.append(
            taps[0:1] * blocks[i]
            + taps[1:2] * delayed(blocks[i], before, 1)
            + taps[2:3] * delayed(blocks[i], before, 2)
            + shift
        )
    return outs


def spectra(hats, bank):
    tail = cmul(bank[1], hats[1]) + cmul(bank[2], hats[0])
    return [
        cmul(bank[0], hats[0]),
        cmul(bank[0], hats[1]) + cmul(bank[1], hats[0]),
        cmul(bank[0], hats[2]) + tail,
        cmul(bank[0], hats[3]) + tail,
    ]


def adjoint_spectra(hats, bank):
    tail = hats[2] + hats[3]
    return [
        cmul_conj(bank[0], hats[0]) + cmul_conj(bank[1], hats[1]) + cmul_conj(bank[2], tail),
        cmul_conj(bank[0], hats[1]) + cmul_conj(bank[1], tail),
        cmul_conj(bank[0], hats[2]),
        cmul_conj(bank[0], hats[3]),
    ]


def bank_grads(hats, grads):
    tail = grads[2] + grads[3]
    zero = cmul_conj(hats[0], grads[0])
    for i in range(1, 4):
        zero = zero + cmul_conj(hats[i], grads[i])
    one = cmul_conj(hats[0], grads[1]) + cmul_conj(hats[1], tail)
    return [zero, one, cmul_conj(hats[0], tail)]


def signs():
    odd = lax.broadcasted_iota(jnp.int32, (BLOCK, TILE), 0) % 2
    return (1 - 2 * odd).astype(f32)


LONG1, LONG2 = slice(6, 7), slice(7, 8)


def make_bank(ahead, taps, bank_ref):
    hats = [split_dot(ahead, taps[o * BLOCK : (o + 1) * BLOCK, :] * (1.0 / BLOCK)) for o in range(3)]
    sign = signs()
    bank = [hats[0]]
    for o in (1, 2):
        prev = hats[o - 1]
        turned = jnp.concatenate([-sign * prev[BLOCK:], sign * prev[:BLOCK]], axis=0)
        bank.append(hats[o] + turned)
    for o in range(3):
        bank_ref[o] = bank[o]


def filter_grads(back, grads, out_ref):
    sign = signs()
    for o in range(3):
        one = grads[o]
        if o < 2:
            after = grads[o + 1]
            one = one + jnp.concatenate([sign * after[BLOCK:], -sign * after[:BLOCK]], axis=0)
        out_ref[o * BLOCK : (o + 1) * BLOCK, :] = split_dot(back, one) * (1.0 / BLOCK)


def mixer_forward(
    z_ref, rows_ref, long_ref, filter1, filter2, ahead_ref, back_ref,
    out_ref, hat1_ref, hat2_ref, mid_ref, bank1, bank2,
):
    @pl.when(pl.program_id(1) == 0)
    def _():
        make_bank(ahead_ref[...], filter1[...], bank1)
        make_bank(ahead_ref[...], filter2[...], bank2)

    forward_step(
        z_ref, rows_ref, long_ref, ahead_ref, back_ref, out_ref, hat1_ref, hat2_ref, mid_ref, bank1, bank2
    )


def forward_step(
    z_ref, rows_ref, long_ref, ahead_ref, back_ref, out_ref, hat1_ref, hat2_ref, mid_ref, bank1, bank2
):
    ahead = ahead_ref[...]
    back = back_ref[...]
    gate1 = short_blocks(z_ref, rows_ref, 1)
    value = short_blocks(z_ref, rows_ref, 2)
    sig1 = [gate1[i] * value[i] for i in range(4)]
    hats = []
    for i in range(4):
        hat = split_dot(ahead, sig1[i])
        hat1_ref[i] = hat
        hats.append(hat)
    wave = spectra(hats, [bank1[i] for i in range(3)])
    mid = []
    for i in range(4):
        one = split_dot(back, wave[i]) + long_ref[LONG1, :] * sig1[i]
        mid_ref[i * BLOCK : (i + 1) * BLOCK, :] = one
        mid.append(one)
    gate0 = short_blocks(z_ref, rows_ref, 0)
    sig2 = [gate0[i] * mid[i] for i in range(4)]
    hats = []
    for i in range(4):
        hat = split_dot(ahead, sig2[i])
        hat2_ref[i] = hat
        hats.append(hat)
    wave = spectra(hats, [bank2[i] for i in range(3)])
    for i in range(4):
        two = split_dot(back, wave[i]) + long_ref[LONG2, :] * sig2[i]
        out_ref[i * BLOCK : (i + 1) * BLOCK, :] = two.astype(bf16)


def mixer_backward(
    grad_ref, z_ref, rows_ref, long_ref, bank1, bank2, hat1_ref, hat2_ref, mid_ref,
    ahead_ref, back_ref,
    dz_ref, dtap_ref, dlong_ref, dfilt1_ref, dfilt2_ref, dbank1, dbank2,
):
    micro = pl.program_id(1)
    backward_step(
        micro == 0, micro == pl.num_programs(1) - 1, grad_ref, z_ref, rows_ref, long_ref, bank1, bank2,
        hat1_ref, hat2_ref, mid_ref, ahead_ref, back_ref,
        dz_ref, dtap_ref, dlong_ref, dfilt1_ref, dfilt2_ref, dbank1, dbank2,
    )


def backward_step(
    first, last, grad_ref, z_ref, rows_ref, long_ref, bank1, bank2, hat1_ref, hat2_ref, mid_ref,
    ahead_ref, back_ref,
    dz_ref, dtap_ref, dlong_ref, dfilt1_ref, dfilt2_ref, dbank1, dbank2,
):
    ahead = ahead_ref[...]
    back = back_ref[...]

    @pl.when(first)
    def _():
        dbank1[...] = jnp.zeros_like(dbank1)
        dbank2[...] = jnp.zeros_like(dbank2)
        dlong_ref[...] = jnp.zeros_like(dlong_ref)
        dtap_ref[...] = jnp.zeros_like(dtap_ref)

    def total(values):
        acc = values[0]
        for one in values[1:]:
            acc = acc + one
        return jnp.sum(acc, axis=0, keepdims=True)

    gate0 = short_blocks(z_ref, rows_ref, 0)
    grad2 = load_blocks(grad_ref)
    mid = load_blocks(mid_ref)
    dhats = [split_dot(ahead, grad2[i]) for i in range(4)]
    new = bank_grads([hat2_ref[i] for i in range(4)], dhats)
    for i in range(3):
        dbank2[i] += new[i]
    wave = adjoint_spectra(dhats, [bank2[i] for i in range(3)])
    dsig2 = [split_dot(back, wave[i]) + long_ref[LONG2, :] * grad2[i] for i in range(4)]
    dlong_ref[1:2, :] += total([grad2[i] * gate0[i] * mid[i] for i in range(4)])
    dgate0 = [dsig2[i] * mid[i] for i in range(4)]
    grad1 = [dsig2[i] * gate0[i] for i in range(4)]
    dhats = [split_dot(ahead, grad1[i]) for i in range(4)]
    new = bank_grads([hat1_ref[i] for i in range(4)], dhats)
    for i in range(3):
        dbank1[i] += new[i]
    wave = adjoint_spectra(dhats, [bank1[i] for i in range(3)])
    dsig1 = [split_dot(back, wave[i]) + long_ref[LONG1, :] * grad1[i] for i in range(4)]
    gate1 = short_blocks(z_ref, rows_ref, 1)
    value = short_blocks(z_ref, rows_ref, 2)
    dlong_ref[0:1, :] += total([grad1[i] * gate1[i] * value[i] for i in range(4)])
    dgate1 = [dsig1[i] * value[i] for i in range(4)]
    dvalue = [dsig1[i] * gate1[i] for i in range(4)]
    for index, grads in enumerate((dgate0, dgate1, dvalue)):
        cols = part(index)
        taps = rows_ref[0:3, cols]
        blocks = load_blocks(z_ref, cols)
        after = (grads[1], grads[2] + grads[3], None, None)
        dz = []
        for i in range(4):
            one = (
                taps[0:1] * grads[i]
                + taps[1:2] * advanced(grads[i], after[i], 1)
                + taps[2:3] * advanced(grads[i], after[i], 2)
            ).astype(bf16)
            dz_ref[i * BLOCK : (i + 1) * BLOCK, cols] = one
            dz.append(one.astype(f32))
        dtap_ref[4:5, cols] += total(dz)
        dtap_ref[3:4, cols] += total(grads)
        dtap_ref[0:1, cols] += total([grads[i] * blocks[i] for i in range(4)])
        for lag in (1, 2):
            dtap_ref[lag : lag + 1, cols] += total(
                [
                    grads[i]
                    * delayed(blocks[i], None if BEFORE[i] is None else blocks[BEFORE[i]], lag)
                    for i in range(4)
                ]
            )

    @pl.when(last)
    def _():
        filter_grads(back, [dbank1[i] for i in range(3)], dfilt1_ref)
        filter_grads(back, [dbank2[i] for i in range(3)], dfilt2_ref)


def constants():
    matrix = dft_matrix()
    return jnp.asarray(split3(matrix)), jnp.asarray(split3(matrix.T))


STEPS = D // TILE
AHEAD = (FREQ, 3 * BLOCK)
BACK = (BLOCK, 3 * FREQ)


def run_forward(z, lines, vecs, filters):
    rows = z.shape[0]
    blocks = rows // BLOCK

    def spec(shape, index):
        return pl.BlockSpec(shape, lambda t, m: index(m, t))

    hat_spec = spec((4, FREQ, TILE), lambda m, t: (m, 0, t))
    row_spec = spec((SPAN, TILE), lambda m, t: (m, t))
    bank_spec = spec((3, FREQ, TILE), lambda m, t: (0, 0, t))
    hat_shape = jax.ShapeDtypeStruct((blocks, FREQ, D), f32)
    bank_shape = jax.ShapeDtypeStruct((3, FREQ, D), f32)
    return pl.pallas_call(
        mixer_forward,
        grid=(STEPS, rows // SPAN),
        in_specs=[
            spec((SPAN, 3 * TILE), lambda m, t: (m, t)),
            spec((8, 3 * TILE), lambda m, t: (0, t)),
            spec((8, TILE), lambda m, t: (0, t)),
            spec((SEQ, TILE), lambda m, t: (0, t)),
            spec((SEQ, TILE), lambda m, t: (0, STEPS + t)),
            spec(AHEAD, lambda m, t: (0, 0)),
            spec(BACK, lambda m, t: (0, 0)),
        ],
        out_specs=[row_spec, hat_spec, hat_spec, row_spec, bank_spec, bank_spec],
        out_shape=[
            jax.ShapeDtypeStruct((rows, D), bf16), hat_shape, hat_shape,
            jax.ShapeDtypeStruct((rows, D), f32), bank_shape, bank_shape,
        ],
        compiler_params=pltpu.CompilerParams(vmem_limit_bytes=40 * 2**20),
        cost_estimate=pl.CostEstimate(flops=10 * 10**9, bytes_accessed=32 * 2**20, transcendentals=0),
        name="mixer_forward",
    )(z, lines, vecs, filters, filters, *constants())


def run_backward(grad, z, lines, vecs, bank1, bank2, hat1, hat2, mid):
    rows = z.shape[0]

    def spec(shape, index):
        return pl.BlockSpec(shape, lambda t, m: index(m, t))

    hat_spec = spec((4, FREQ, TILE), lambda m, t: (m, 0, t))
    row_spec = spec((SPAN, TILE), lambda m, t: (m, t))
    bank_spec = spec((3, FREQ, TILE), lambda m, t: (0, 0, t))
    z_spec = spec((SPAN, 3 * TILE), lambda m, t: (m, t))
    column_spec = spec((SEQ, TILE), lambda m, t: (0, t))
    return pl.pallas_call(
        mixer_backward,
        grid=(STEPS, rows // SPAN),
        in_specs=[
            row_spec,
            z_spec,
            spec((8, 3 * TILE), lambda m, t: (0, t)),
            spec((8, TILE), lambda m, t: (0, t)),
            bank_spec, bank_spec, hat_spec, hat_spec, row_spec,
            spec(AHEAD, lambda m, t: (0, 0)),
            spec(BACK, lambda m, t: (0, 0)),
        ],
        out_specs=[
            z_spec,
            spec((8, 3 * TILE), lambda m, t: (0, t)),
            spec((2, TILE), lambda m, t: (0, t)),
            column_spec,
            column_spec,
        ],
        out_shape=[
            jax.ShapeDtypeStruct((rows, D3), bf16), jax.ShapeDtypeStruct((8, D3), f32),
            jax.ShapeDtypeStruct((2, D), f32), jax.ShapeDtypeStruct((SEQ, D), f32),
            jax.ShapeDtypeStruct((SEQ, D), f32),
        ],
        scratch_shapes=[pltpu.VMEM((3, FREQ, TILE), f32), pltpu.VMEM((3, FREQ, TILE), f32)],
        compiler_params=pltpu.CompilerParams(vmem_limit_bytes=40 * 2**20),
        cost_estimate=pl.CostEstimate(flops=24 * 10**9, bytes_accessed=36 * 2**20, transcendentals=0),
        name="mixer_backward",
    )(grad, z, lines, vecs, bank1, bank2, hat1, hat2, mid, *constants())


def place_ratio():
    return (np.arange(SEQ).astype(np.float32) / np.float32(SEQ))[:, None]


def filter_states(first_w, first_b, second_w, second_b):
    levels = (np.arange(BANDS) + 1).astype(np.float32)
    ratio = jnp.asarray(place_ratio())
    angles = 2.0 * math.pi * ratio * jnp.asarray(levels)[None, :]
    embed = jnp.concatenate([ratio, jnp.cos(angles), jnp.sin(angles)], axis=1)
    first_pre = matmul(embed, first_w) + first_b
    first_act = jnp.sin(first_pre)
    second_pre = matmul(first_act, second_w) + second_b
    return embed, first_pre, first_act, second_pre, jnp.sin(second_pre)


def filter_taps(first_w, first_b, second_w, second_b, third_w, decay):
    second_act = filter_states(first_w, first_b, second_w, second_b)[-1]
    return matmul(second_act, third_w) * jnp.exp(-jnp.asarray(place_ratio()) * decay[None, :])


def by_tile(value):
    shape = value.shape
    return value.reshape(*shape[:-1], 3, STEPS, TILE).swapaxes(-3, -2).reshape(shape)


def by_part(value):
    shape = value.shape
    return value.reshape(*shape[:-1], STEPS, 3, TILE).swapaxes(-3, -2).reshape(shape)


MESH = pl.DeviceIdType.MESH


class Place:
    def __init__(self):
        rep = lax.axis_index("rep")
        self.rep = rep
        self.shard = lax.axis_index("shard")
        self.core = rep % 2
        self.side = (rep // 2) % 2
        self.depth = rep // 4
        self.quad = rep % 4
        self.eighth = rep % 8
        self.to_side = 2 - 4 * self.side
        self.to_depth = 4 - 8 * (self.depth % 2)

    def other_shard(self):
        return (self.rep, 1 - self.shard)

    def other_side(self):
        return (self.rep + 2 - 4 * self.side, self.shard)

    def near_depth(self):
        return (self.rep + self.to_depth, self.shard)

    def diagonal(self):
        return (self.rep + (1 - self.core) * self.to_side + self.core * self.to_depth, self.shard)

    def other_core(self):
        return (self.rep + 1 - 2 * self.core, self.shard)

    def other_depth(self, step):
        return (((self.depth + step) % 4) * 4 + self.quad, self.shard)


def greet(devices):
    barrier = pltpu.get_barrier_semaphore()
    for device in devices:
        pl.semaphore_signal(barrier, inc=1, device_id=device, device_id_type=MESH)
    pl.semaphore_wait(barrier, len(devices))


def remote(src, dst, send, recv, device):
    return pltpu.make_async_remote_copy(
        src_ref=src, dst_ref=dst, send_sem=send, recv_sem=recv, device_id=device, device_id_type=MESH
    )


UNITS = (
    (0, 0, 16), (0, 16, 16), (0, 32, 16), (1, 0, 48), (2, 0, 16), (2, 16, 16), (2, 32, 16), (3, 0, 96), (3, 96, 96),
)
STRAIGHT = (4, 5, 6)
STAGES = ("", "A3 A4", "A5 B3 B4", "A6 A7 B5 C3 C4", "A8 B6 B7 C5", "B8 C6 C7", "C8", "")
PACK_ROWS = 96
UP_ROW, DECAY_ROW, FIRST_ROW, SECOND_ROW = 23, 27, 32, 32


def column_moves():
    for s in range(2):
        for a in range(3):
            for b in range(3):
                at = s * (D3 // 2) + a * (D // 2) + b * 128
                yield s, a, b * 128, (at % D // TILE * 3 + at // D) * TILE + at % TILE


def gather_kernel(
    gain1, shift1, in_shift, short_w, short_b, long_b, w1, b1, w2, b2, third, decay, out_b, gain2, shift2, up_b,
    down_b, w_in, w_out, w_up, w_down, prompt_x, cont_x, prompt_g, cont_g, embed_ref, ratio_ref, ahead_ref, back_ref,
    z_ref, mixed_ref, hat1_ref, hat2_ref, mid_ref, bank1, bank2,
    vecs, lines, up_all, decay_all, second_all, third_all, pre1, act1, pre2, act2,
    normed_out, tokens_out, upstream_out, f_in, f_out, f_up, f_down,
    pack, packed, packs, thirds, in_v, normed_v,
    small_send, small_recv, own_sem, token_sem, ysend, yrecv, xsend, xrecv, zsend, zrecv, dsend, drecv, ssend, srecv, csend, crecv,
):
    tick = pl.program_id(0)
    place = Place()
    shard, mine = place.shard, place.eighth
    by_side, by_depth = mine + place.to_side, mine + place.to_depth
    by_both = by_side + place.to_depth
    locals_ = (w_in, w_out, w_up, w_down)
    fulls = (in_v, f_out, f_up, f_down)

    def rows_of(unit, shard_of, piece):
        weight, start, size = unit
        half = locals_[weight].shape[0]
        return pl.ds(pl.multiple_of(shard_of * half + piece * (half // 8) + start, 16), size)

    def local_rows(unit, piece):
        weight, start, size = unit
        return pl.ds(pl.multiple_of(piece * (locals_[weight].shape[0] // 8) + start, 16), size)

    def smalls():
        return [
            remote(packed, packs.at[shard], small_send.at[0], small_recv.at[0], place.other_shard()),
            remote(third, thirds.at[shard], small_send.at[1], small_recv.at[1], place.other_shard()),
        ]

    def own_copies():
        copies = []
        for weight in range(1, 4):
            half = locals_[weight].shape[0]
            rows = pl.ds(pl.multiple_of(shard * half, 16), half)
            copies.append(pltpu.make_async_copy(locals_[weight], fulls[weight].at[rows, :], own_sem.at[weight]))
        return copies

    def token_copies():
        copies = []
        for to, parts in ((tokens_out, (prompt_x, cont_x)), (upstream_out, (prompt_g, cont_g))):
            for m in range(prompt_x.shape[0]):
                for i, ref in enumerate(parts):
                    rows = slice(m * SPAN + i * PROMPT, m * SPAN + (i + 1) * PROMPT)
                    copies.append(pltpu.make_async_copy(ref.at[m], to.at[rows, :], token_sem.at[len(copies)]))
        return copies

    def normed_copy():
        return pltpu.make_async_copy(normed_v, normed_out, own_sem.at[0])

    def in_copy():
        return pltpu.make_async_copy(in_v, f_in, own_sem.at[4])

    def moved(u, piece, send, recv, device):
        unit = UNITS[u]
        region = fulls[unit[0]].at[rows_of(unit, 1 - shard, piece), :]
        return remote(region, region, send, recv, device)

    def from_shard(u):
        return moved(u, mine, ysend.at[u], yrecv.at[u], place.other_shard())

    def side(u, piece):
        return moved(u, piece, xsend.at[u], xrecv.at[u], place.other_side())

    def depth(u, piece):
        return moved(u, piece, zsend.at[u], zrecv.at[u], place.near_depth())

    def diagonal(u, piece):
        return moved(u, piece, dsend.at[u], drecv.at[u], place.diagonal())

    def straight(u):
        return moved(u, by_both, ssend.at[u], srecv.at[u], place.other_shard())

    def twin(u, index, piece):
        return moved(u, piece, csend.at[u, index], crecv.at[u, index], place.other_core())

    def exchanges(stages):
        for stage in stages.split():
            kind, u = stage[0], int(stage[1:])
            if kind == "A":
                from_shard(u).wait_recv()
                side(u, mine).start()
                depth(u, mine).start()
                twin(u, 0, mine).start()
            elif kind == "B":
                side(u, by_side).wait_recv()
                twin(u, 1, by_side).start()
                depth(u, by_depth).wait_recv()
                twin(u, 2, by_depth).start()
                if u not in STRAIGHT:
                    diagonal(u, (1 - place.core) * by_depth + place.core * by_side).start()
            else:
                (straight(u) if u in STRAIGHT else diagonal(u, by_both)).wait_recv()
                twin(u, 3, by_both).start()

    def finish(u):
        for index, piece in enumerate((mine, by_side, by_depth, by_both)):
            twin(u, index, piece).wait()
        from_shard(u).wait_send()
        side(u, mine).wait_send()
        depth(u, mine).wait_send()
        (straight(u) if u in STRAIGHT else diagonal(u, mine)).wait_send()

    @pl.when(tick == 0)
    def _():
        greet([place.other_shard(), place.other_side(), place.near_depth(), place.other_core()])
        rows = pl.ds(pl.multiple_of(shard * (D // 2), 16), D // 2)
        for p in range(3):
            for t in range(STEPS):
                in_v[rows, part(t * 3 + p)] = w_in[:, part(p * STEPS + t)]

        def send_units(units):
            for u in units:
                weight = UNITS[u][0]
                to = fulls[weight].at[rows_of(UNITS[u], shard, mine), :]
                source = to if weight == 0 else locals_[weight].at[local_rows(UNITS[u], mine), :]
                remote(source, to, ysend.at[u], yrecv.at[u], place.other_shard()).start()
                if u in STRAIGHT:
                    to = fulls[weight].at[rows_of(UNITS[u], shard, by_both), :]
                    source = locals_[weight].at[local_rows(UNITS[u], by_both), :]
                    remote(source, to, ssend.at[u], srecv.at[u], place.other_shard()).start()

        send_units(range(3))
        pack[...] = jnp.zeros_like(pack)
        half = D // 2

        def row(ref):
            return ref[...].astype(f32).reshape(1, ref.shape[0])

        for i, ref in enumerate((gain1, shift1, out_b, gain2, shift2, down_b)):
            pack[i : i + 1, :] = row(ref)
        pack[6:8, :] = long_b[...].astype(f32)
        taps = short_w[...].astype(f32)
        for i, value in enumerate((row(in_shift), row(short_b), taps[0:1], taps[1:2], taps[2:3])):
            for a in range(3):
                pack[8 + 3 * i + a : 9 + 3 * i + a, :] = value[:, a * half : (a + 1) * half]
        value = row(up_b)
        for a in range(4):
            pack[UP_ROW + a : UP_ROW + a + 1, :] = value[:, a * half : (a + 1) * half]
        value = row(decay)
        for a in range(2):
            pack[DECAY_ROW + a : DECAY_ROW + a + 1, :] = value[:, a * half : (a + 1) * half]
        wide, n1 = w1.shape
        n2 = w2.shape[1]
        pack[FIRST_ROW : FIRST_ROW + n1, 0:wide] = w1[...].astype(f32).T
        pack[FIRST_ROW + n1 : FIRST_ROW + n1 + 1, 0:wide] = row(b1)
        pack[FIRST_ROW + n1 + 1 : FIRST_ROW + n1 + 2, 0:wide] = row(b2)
        pack[SECOND_ROW : SECOND_ROW + n2, 128 : 128 + wide] = w2[...].astype(f32).T
        packed[...] = pack[...].astype(bf16)
        for one in smalls():
            one.start()
        send_units(range(3, len(UNITS)))
        for one in own_copies() + token_copies():
            one.start()
        packs[shard] = packed[...]
        thirds[shard] = third[...]
        exchanges("A0 A1 A2")
        for one in smalls():
            one.wait()

        both = [packs[s].astype(f32) for s in range(2)]
        for i in range(8):
            for s in range(2):
                vecs[i : i + 1, s * half : (s + 1) * half] = both[s][i : i + 1]
        lines[...] = jnp.zeros_like(lines)
        for s, a, b, to in column_moves():
            for i, line in enumerate((4, 3, 0, 1, 2)):
                at = 8 + 3 * i + a
                lines[line : line + 1, to : to + 128] = both[s][at : at + 1, b : b + 128]
        for s in range(2):
            for a in range(4):
                to = s * (2 * D) + a * half
                up_all[0:1, to : to + half] = both[s][UP_ROW + a : UP_ROW + a + 1]
            for a in range(2):
                to = s * D + a * half
                decay_all[0:1, to : to + half] = both[s][DECAY_ROW + a : DECAY_ROW + a + 1]
            third_all[:, s * D : (s + 1) * D] = thirds[s].astype(f32)

        def narrow(rows, cols):
            return jnp.concatenate([both[s][rows, cols] for s in range(2)], axis=1)

        first_w = narrow(slice(FIRST_ROW, FIRST_ROW + n1), slice(0, wide))
        first_b = narrow(slice(FIRST_ROW + n1, FIRST_ROW + n1 + 1), slice(0, wide))
        second_b = narrow(slice(FIRST_ROW + n1 + 1, FIRST_ROW + n1 + 2), slice(0, wide))
        second_w = narrow(slice(SECOND_ROW, SECOND_ROW + n2), slice(128, 128 + wide))
        second_all[...] = second_w
        exchanges("B0 B1 B2")
        straight = ((1,), (0,))
        pre1[...] = exact(embed_ref[...], first_w, straight) + first_b
        act1[...] = jnp.sin(pre1[...])
        pre2[...] = exact(act1[...], second_w, straight) + second_b
        act2[...] = jnp.sin(pre2[...])

        exchanges("C0 C1 C2")

        for i, ref in enumerate((prompt_x, cont_x)):
            def norm_rows(step, carry):
                m, h = step // 2, step % 2
                values = ref[m, pl.ds(pl.multiple_of(h * 128, 128), 128), :].astype(f32)
                rows = pl.ds(pl.multiple_of(m * SPAN + i * PROMPT + h * 128, 128), 128)
                normed_v[rows, :] = layer_norm(values, vecs[0:1, :], vecs[1:2, :]).astype(bf16)
                return carry

            lax.fori_loop(0, 2 * ref.shape[0], norm_rows, 0)
        normed_copy().start()
        for u in range(3):
            finish(u)
        in_copy().start()

    for index in range(1, len(STAGES)):
        @pl.when(tick == index)
        def _():
            exchanges(STAGES[index])

    @pl.when(tick > 0)
    def _():
        step = jnp.maximum(tick - 1, 0)
        tile = step // 2
        micro = step % 2
        cols = pl.ds(pl.multiple_of(tile * 3 * TILE, 3 * TILE), 3 * TILE)
        few = pl.ds(pl.multiple_of(tile * TILE, TILE), TILE)
        rows = pl.ds(pl.multiple_of(micro * SPAN, SPAN), SPAN)

        @pl.when(tick <= 2 * STEPS)
        def _():
            @pl.when(micro == 0)
            def _():
                for q, bank in enumerate((bank1, bank2)):
                    those = pl.ds(pl.multiple_of(q * D + tile * TILE, TILE), TILE)
                    window = jnp.exp(-ratio_ref[...] * decay_all[:, those])
                    taps = exact(act2[...], third_all[:, those], ((1,), (0,))) * window
                    make_bank(ahead_ref[...], taps, bank)

            z_ref[...] = lowmul(normed_v[rows, :], in_v[:, cols]) + lines[4:5, cols]
            forward_step(
                z_ref, lines.at[:, cols], vecs.at[:, few], ahead_ref, back_ref,
                mixed_ref, hat1_ref, hat2_ref, mid_ref, bank1, bank2,
            )

    @pl.when(tick == 2 * STEPS + 1)
    def _():
        for u in range(3, len(UNITS)):
            finish(u)
        normed_copy().wait()
        in_copy().wait()
        for one in own_copies() + token_copies():
            one.wait()


def embed_table():
    ratio = place_ratio()
    angles = 2.0 * math.pi * ratio * (np.arange(BANDS) + 1).astype(np.float32)[None, :]
    return np.concatenate([ratio, np.cos(angles), np.sin(angles)], axis=1).astype(np.float32)


def gather_weights(*values):
    w1, w2, w3 = values[6], values[8], values[10]
    weights = values[17:21]
    micros = values[21].shape[0]
    count = micros * SPAN
    hidden = w2.shape[1]
    vmem = lambda one: pl.BlockSpec(one.shape, lambda t: (0,) * one.ndim, pipeline_mode=pl.Buffered(1))
    hbm = pl.BlockSpec(memory_space=pl.ANY)
    units = len(UNITS)
    embed, ratio = jnp.asarray(embed_table()), jnp.asarray(place_ratio())
    inputs = (*values, embed, ratio, *constants())

    def at_tile(shape, where):
        def index(t):
            step = jnp.minimum(jnp.maximum(t - 1, 0), 2 * STEPS - 1)
            return where(step % 2, step // 2)

        return pl.BlockSpec(shape, index)

    def doubled(value):
        return jax.ShapeDtypeStruct((2 * value.shape[0], *value.shape[1:]), value.dtype)

    def shape(*dims, kind=f32):
        return jax.ShapeDtypeStruct(dims, kind)

    fixed = [
        shape(8, D), shape(8, D3), shape(1, weights[2].shape[1]), shape(1, 2 * w3.shape[1]), shape(hidden, hidden),
        shape(hidden, 2 * w3.shape[1]),
    ] + [shape(SEQ, hidden)] * 4
    blocks = count // BLOCK
    hat_spec = at_tile((4, FREQ, TILE), lambda m, t: (m, 0, t))
    row_spec = at_tile((SPAN, TILE), lambda m, t: (m, t))
    bank_spec = at_tile((3, FREQ, TILE), lambda m, t: (0, 0, t))
    return pl.pallas_call(
        gather_kernel,
        grid=(2 * STEPS + 2,),
        in_specs=[vmem(one) for one in inputs],
        out_specs=[
            at_tile((SPAN, 3 * TILE), lambda m, t: (m, t)), row_spec, hat_spec, hat_spec, row_spec, bank_spec,
            bank_spec,
        ]
        + [vmem(one) for one in fixed] + [hbm] * 7,
        out_shape=[
            shape(count, D3), shape(count, D, kind=bf16), shape(blocks, FREQ, D), shape(blocks, FREQ, D),
            shape(count, D), shape(3, FREQ, D), shape(3, FREQ, D),
        ]
        + fixed + [shape(count, D, kind=bf16)] * 3 + [doubled(one) for one in weights],
        scratch_shapes=[
            pltpu.VMEM((PACK_ROWS, D // 2), f32),
            pltpu.VMEM((PACK_ROWS, D // 2), bf16),
            pltpu.VMEM((2, PACK_ROWS, D // 2), bf16),
            pltpu.VMEM((2, *w3.shape), bf16),
            pltpu.VMEM((D, D3), bf16),
            pltpu.VMEM((count, D), bf16),
        ]
        + [pltpu.SemaphoreType.DMA((2,))] * 2
        + [pltpu.SemaphoreType.DMA((5,)), pltpu.SemaphoreType.DMA((4 * micros,))]
        + [pltpu.SemaphoreType.DMA((units,))] * 10
        + [pltpu.SemaphoreType.DMA((units, 4))] * 2,
        compiler_params=pltpu.CompilerParams(
            collective_id=0, has_side_effects=True, vmem_limit_bytes=63 * 2**20
        ),
        name="gather_weights",
    )(*inputs)


class Reduction:
    def __init__(self, place, first, count, rows, bufs, sems, out):
        self.place = place
        self.first = first
        self.count = count
        self.rows = rows
        self.dtype = bufs[0].dtype
        self.whole, self.from_core, self.half, self.from_shard, self.own, self.from_side, self.mine, self.from_depth, self.back = bufs
        (self.s_core, self.r_core, self.s_shard, self.r_shard, self.s_side, self.r_side, self.s_depth, self.r_depth,
         self.s_gd, self.r_gd, self.s_gs, self.r_gs, self.s_gc, self.r_gc, self.s_own) = sems
        self.out = out

    def when(self, tick, lag, body):
        k = tick - self.first - lag

        @pl.when((k >= 0) & (k < self.count))
        def _():
            body(k, k % 2)

    def slot(self, ref, k):
        return ref.at[k % ref.shape[0]]

    def rows_at(self, index, size):
        return pl.ds(pl.multiple_of(index * size, size), size)

    def core_copy(self, k, slot):
        p = self.place
        return remote(
            self.whole.at[slot, :, self.rows_at(1 - p.core, self.rows // 2), :],
            self.slot(self.from_core, k), self.s_core.at[k], self.r_core.at[k], p.other_core(),
        )

    def shard_copy(self, k, slot):
        p = self.place
        return remote(
            self.half.at[slot, 1 - p.shard], self.slot(self.from_shard, k), self.s_shard.at[k], self.r_shard.at[k],
            p.other_shard(),
        )

    def side_copy(self, k, slot):
        p = self.place
        return remote(
            self.own.at[slot, self.rows_at(1 - p.side, self.rows // 4), :],
            self.slot(self.from_side, k), self.s_side.at[k], self.r_side.at[k], p.other_side(),
        )

    def quarter(self, base, index):
        rows = self.rows // 8
        return (
            pl.ds(pl.multiple_of(base + (index // 2) * rows, rows), rows),
            pl.ds(pl.multiple_of((index % 2) * (D // 2), D // 2), D // 2),
        )

    def depth_copy(self, k, slot, step):
        p = self.place
        rows, cols = self.quarter(0, (p.depth + step) % 4)
        return remote(
            self.mine.at[slot, rows, cols], self.from_depth.at[k % self.from_depth.shape[0], step - 1],
            self.s_depth.at[k, step - 1], self.r_depth.at[k, step - 1], p.other_depth(step),
        )

    def depth_back(self, k, step):
        p = self.place
        rows, cols = self.quarter(p.side * (self.rows // 4), p.depth)
        region = self.back.at[k % self.back.shape[0], rows, cols]
        return remote(
            region, region, self.s_gd.at[k, step - 1], self.r_gd.at[k, step - 1], p.other_depth(step)
        )

    def side_back(self, k):
        p = self.place
        region = self.back.at[k % self.back.shape[0], self.rows_at(p.side, self.rows // 4), :]
        return remote(region, region, self.s_gs.at[k], self.r_gs.at[k], p.other_side())

    def homes(self, k, place_in):
        rows = pl.ds(pl.multiple_of(self.place.core * (self.rows // 2), self.rows // 2), self.rows // 2)
        return [(cols, ref.at[(*lead, rows, *tail)]) for cols, ref, lead, tail in place_in]

    def send_home(self, k, place_in):
        p = self.place
        for cols, region in self.homes(k, place_in):
            piece = self.back.at[k % self.back.shape[0], :, cols]
            remote(piece, region, self.s_gc.at[k], self.r_gc.at[k], p.other_core()).start()
            pltpu.make_async_copy(piece, region, self.s_own.at[k]).start()

    def wait_home(self, k):
        whole = self.slot(self.back, k)
        remote(whole, whole, self.s_gc.at[k], self.r_gc.at[k], self.place.other_core()).wait()
        pltpu.make_async_copy(whole, whole, self.s_own.at[k]).wait()

    def add(self, left, right):
        return (left.astype(f32) + right.astype(f32)).astype(self.dtype)

    def send(self, tick):
        self.when(tick, 0, lambda k, slot: self.core_copy(k, slot).start())

    def advance(self, tick):
        p = self.place

        def after_core(k, slot):
            self.core_copy(k, slot).wait()
            for s in range(2):
                self.half[slot, s] = self.add(
                    self.whole[slot, s, self.rows_at(p.core, self.rows // 2), :], self.from_core[k % self.from_core.shape[0], s]
                )
            self.shard_copy(k, slot).start()

        def after_shard(k, slot):
            self.shard_copy(k, slot).wait()
            self.own[slot] = self.add(self.half[slot, p.shard], self.from_shard[k % self.from_shard.shape[0]])
            self.side_copy(k, slot).start()

        def after_side(k, slot):
            self.side_copy(k, slot).wait()
            self.mine[slot] = self.add(
                self.own[slot, self.rows_at(p.side, self.rows // 4), :], self.from_side[k % self.from_side.shape[0]]
            )
            for step in range(1, 4):
                self.depth_copy(k, slot, step).start()

        def after_depth(k, slot):
            for step in range(1, 4):
                self.depth_copy(k, slot, step).wait()
            rows, cols = self.quarter(0, p.depth)
            total = self.mine[slot, rows, cols].astype(f32)
            for step in range(3):
                total = total + self.from_depth[k % self.from_depth.shape[0], step].astype(f32)
            rows, cols = self.quarter(p.side * (self.rows // 4), p.depth)
            self.back[k % self.back.shape[0], rows, cols] = total.astype(self.dtype)
            for step in range(1, 4):
                self.depth_back(k, step).start()

        def after_depth_back(k, slot):
            for step in range(1, 4):
                self.depth_back(k, step).wait()
            self.side_back(k).start()

        def after_side_back(k, slot):
            self.side_back(k).wait()
            self.out(self, k)

        def after_core_back(k, slot):
            self.wait_home(k)

        for lag, body in enumerate(
            (after_core, after_shard, after_side, after_depth, after_depth_back, after_side_back, after_core_back), 1
        ):
            self.when(tick, lag, body)


LAGS = 7
DOWN, UP, OUT, IN = 4, 4, 1, STEPS
CHUNKS = DOWN + UP + OUT + IN
SMALL_ROWS = 128
SMALL_TICK = 9
ROW_BLOCK = 128


GIVEN_ROW, TAP_ROW, LONG_ROW, NORM_ROW = 64, 72, 96, 98


def exact(left, right, dims):
    return lax.dot_general(left, right, (dims, ((), ())), precision=HIGH, preferred_element_type=f32)


def reduce_kernel(
    sums, d_shift, active0, active1, upstream, second_h, d_hidden, mixed_h, d_middle_h, normed_h, tokens_h, gain, middle, down0, down1,
    grad_ref, z_ref, rows_ref, long_ref, bank1, bank2, hat1_ref, hat2_ref, mid_ref, ahead_ref, back_ref,
    in_ref, decay_ref, decay2_ref, third1_ref, third2_ref, ratio_ref, embed_ref, pre1_ref, act1_ref, pre2_ref, act2_ref,
    second_w_ref,
    small_out, g_down, g_up, g_out, g_in, tokens_out, result_out,
    d_proj, dtap, dtaps, dlong, dlongs, dfilt1, dfilt2, dbank1, dbank2, d_normed, d_act, out_rows, out_sem, middle_sem,
    second, mixed, d_middle, normed, tokens, late_sem, *scratch,
):
    tick = pl.program_id(0)
    place = Place()
    bufs, sems = scratch[:9], scratch[9:24]
    small_bufs, small_sems = scratch[24:33], scratch[33:48]
    everything = slice(None)
    is_in = (tick % 3 == 2) & (tick < 9)
    tile = tick // 3

    def little_home(chain, k):
        chain.send_home(k, [(everything, small_out, (k,), (everything,))])

    def kinds(k):
        down = (k < 5) & (k % 3 < 2)
        up = ((k >= 6) & (k < 8)) | (k >= 10)
        return down, up, k == 9, (k < 9) & (k % 3 == 2)

    def big_home(chain, k):
        down, up, out, inward = kinds(k)

        @pl.when(down)
        def _():
            chain.send_home(k, [(everything, g_down, (k - k // 3,), (everything,))])

        @pl.when(up)
        def _():
            index = k - 6 - 2 * (k // 9)
            cols = pl.ds(pl.multiple_of(index * D, D), D)
            chain.send_home(k, [(everything, g_up, (), (cols,))])

        @pl.when(out)
        def _():
            chain.send_home(k, [(everything, g_out, (), (everything,))])

        @pl.when(inward)
        def _():
            chain.send_home(
                k,
                [
                    (part(p), g_in, (), (pl.ds(pl.multiple_of(p * D + (k // 3) * TILE, TILE), TILE),))
                    for p in range(3)
                ],
            )

    little = Reduction(place, SMALL_TICK, 1, SMALL_ROWS, small_bufs, small_sems, little_home)
    big = Reduction(place, 0, CHUNKS, D // 2, bufs, sems, big_home)
    pack = little.whole
    late = [
        pltpu.make_async_copy(src, dst, late_sem.at[i])
        for i, (src, dst) in enumerate(
            ((normed_h, normed), (second_h, second), (mixed_h, mixed), (d_middle_h, d_middle), (tokens_h, tokens))
        )
    ]

    @pl.when(tick == 0)
    def _():
        for one in late:
            one.start()
        greet(
            [place.other_shard(), place.other_side(), place.other_core()]
            + [place.other_depth(step) for step in range(1, 4)]
        )
        pack[...] = jnp.zeros_like(pack)
        for s in range(2):
            pack[0, s, GIVEN_ROW : GIVEN_ROW + 4, D // 2 :] = sums[0:4, s * (D // 2) : (s + 1) * (D // 2)]
            for a in range(4):
                at = s * 2 * D + a * (D // 2)
                pack[0, s, GIVEN_ROW + 4 + a : GIVEN_ROW + 5 + a, D // 2 :] = d_shift[0:1, at : at + D // 2]
        d_act[...] = jnp.zeros_like(d_act)

    little.advance(tick)
    big.advance(tick)

    def chunk(slot, lefts, right):
        for s in range(2):
            big.whole[slot, s] = inner_rows(lefts[s], right).astype(bf16)

    def halves(left):
        return left[:, : D // 2], left[:, D // 2 :]

    def compute(k, slot):
        down, up, out, inward = kinds(k)

        @pl.when(down)
        def _():
            chunk(slot, (active0[...], active1[...]), upstream[...])

        @pl.when(up)
        def _():
            chunk(slot, halves(second), d_hidden[...])

        @pl.when(out)
        def _():
            chunk(slot, halves(mixed), d_middle[...].astype(bf16))

        @pl.when(inward)
        def _():
            chunk(slot, halves(normed), d_proj[...])

    for first, those in ((2, late[:1]), (6, late[1:2]), (SMALL_TICK, late[2:])):
        @pl.when(tick == first)
        def _():
            for one in those:
                one.wait()

    big.when(tick, 0, compute)
    big.send(tick)

    @pl.when((tick < 8) & (tick % 3 < 2))
    def _():
        micro = tick % 3
        backward_step(
            micro == 0, micro == 1, grad_ref, z_ref, rows_ref, long_ref, bank1, bank2,
            hat1_ref, hat2_ref, mid_ref, ahead_ref, back_ref,
            d_proj.at[pl.ds(pl.multiple_of(micro * SPAN, SPAN), SPAN), :], dtap, dlong, dfilt1, dfilt2, dbank1, dbank2,
        )

    @pl.when(is_in)
    def _():
        cols = pl.ds(pl.multiple_of(tile * TILE, TILE), TILE)
        dtaps[tile] = dtap[...]
        dlongs[:, cols] = dlong[...]
        step = times_t(d_proj[...], in_ref[...])

        @pl.when(tile == 0)
        def _():
            d_normed[...] = step

        @pl.when(tile > 0)
        def _():
            d_normed[...] += step

        for q, (grads, decay, third) in enumerate(
            ((dfilt1, decay_ref, third1_ref), (dfilt2, decay2_ref, third2_ref))
        ):
            window = jnp.exp(-ratio_ref[...] * decay[...])
            d_taps = grads[...] * window
            pack[0, q, 0 : act2_ref.shape[1], cols] = exact(act2_ref[...], d_taps, ((0,), (0,)))
            d_act[...] += exact(d_taps, third[...], ((1,), (1,)))

    @pl.when(tick == SMALL_TICK)
    def _():
        for s in range(2):
            for a in range(3):
                for b in range(3):
                    at = s * (D3 // 2) + a * (D // 2) + b * 128
                    p, t, o = at // D, at % D // TILE, at % TILE
                    pack[0, s, TAP_ROW + 8 * a : TAP_ROW + 8 * a + 8, D // 2 + b * 128 : D // 2 + b * 128 + 128] = dtaps[
                        t, :, p * TILE + o : p * TILE + o + 128
                    ]
            pack[0, s, LONG_ROW : LONG_ROW + 2, D // 2 :] = dlongs[:, s * (D // 2) : (s + 1) * (D // 2)]

        def norm_rows(i, sums):
            rows = pl.ds(pl.multiple_of(i * ROW_BLOCK, ROW_BLOCK), ROW_BLOCK)
            values = tokens[rows, :].astype(f32)
            grads = d_normed[rows, :]
            center = values - jnp.mean(values, axis=-1, keepdims=True)
            scale = lax.rsqrt(jnp.mean(center * center, axis=-1, keepdims=True) + EPS)
            unit = center * scale
            scaled = grads * gain[0:1, :]
            inner = scaled - jnp.mean(scaled, axis=-1, keepdims=True)
            inner = inner - unit * jnp.mean(scaled * unit, axis=-1, keepdims=True)
            out_rows[rows, :] = (scale * inner + d_middle[rows, :]).astype(bf16)
            return (
                sums[0] + jnp.sum(grads * unit, axis=0, keepdims=True),
                sums[1] + jnp.sum(grads, axis=0, keepdims=True),
            )

        zero = jnp.zeros((1, D), f32)
        sums = lax.fori_loop(0, tokens.shape[0] // ROW_BLOCK, norm_rows, (zero, zero))
        d_pre2 = d_act[...] * jnp.cos(pre2_ref[...])
        g_second = exact(act1_ref[...], d_pre2, ((0,), (0,)))
        g_b2 = jnp.sum(d_pre2, axis=0, keepdims=True)
        d_pre1 = exact(d_pre2, second_w_ref[...], ((1,), (1,))) * jnp.cos(pre1_ref[...])
        g_first = exact(embed_ref[...], d_pre1, ((0,), (0,)))
        g_b1 = jnp.sum(d_pre1, axis=0, keepdims=True)
        wide = g_second.shape[1] // 2
        for s in range(2):
            own = slice(s * wide, (s + 1) * wide)
            for i in range(2):
                pack[0, s, NORM_ROW + i : NORM_ROW + i + 1, D // 2 :] = sums[i][:, s * (D // 2) : (s + 1) * (D // 2)]
            pack[0, s, 64 : 64 + g_first.shape[0], 0:wide] = g_first[:, own]
            pack[0, s, 64 + g_first.shape[0] : 65 + g_first.shape[0], 0:wide] = g_b1[:, own]
            pack[0, s, 65 + g_first.shape[0] : 66 + g_first.shape[0], 0:wide] = g_b2[:, own]
            pack[0, s, 64 : 64 + g_second.shape[0], 128 : 128 + wide] = g_second[:, own]
        pltpu.make_async_copy(out_rows, tokens_out, out_sem).start()

    little.send(tick)

    @pl.when(tick == SMALL_TICK + 2)
    def _():
        pltpu.make_async_copy(out_rows, tokens_out, out_sem).wait()
        pltpu.make_async_copy(middle, d_normed, middle_sem).start()

    @pl.when((tick >= CHUNKS) & (tick < CHUNKS + DOWN))
    def _():
        @pl.when(tick == CHUNKS)
        def _():
            pltpu.make_async_copy(middle, d_normed, middle_sem).wait()

        def result_rows(i, carry):
            rows = pl.ds(pl.multiple_of(i * 256, 256), 256)
            total = d_normed[rows, :] + lowmul(active0[rows, :], down0[...]) + lowmul(active1[rows, :], down1[...])
            d_normed[rows, :] = total

            @pl.when(tick == CHUNKS + DOWN - 1)
            def _():
                out_rows[rows, :] = (total + gain[5:6, :]).astype(bf16)

            return carry

        lax.fori_loop(0, out_rows.shape[0] // 256, result_rows, 0)

        @pl.when(tick == CHUNKS + DOWN - 1)
        def _():
            pltpu.make_async_copy(out_rows, result_out, out_sem).start()

    @pl.when(tick == CHUNKS + LAGS - 1)
    def _():
        pltpu.make_async_copy(out_rows, result_out, out_sem).wait()


def reduce_grads(
    sums, d_shift, active, upstream, second, d_hidden, mixed, d_middle, normed, tokens, middle, down_full,
    d_mixed, z, lines, vecs, bank1, bank2, hat1, hat2, mid, in_full, decay, third_w, states, second_w,
):
    count = upstream.shape[0]
    half = D // 2
    hidden = second_w.shape[0]
    embed, pre1, act1, pre2, act2 = states

    def fixed(shape):
        return pl.BlockSpec(shape, lambda t: (0,) * len(shape), pipeline_mode=pl.Buffered(1))

    def at_tile(shape, where):
        def index(t):
            tick = jnp.minimum(t, 8)
            return where(jnp.minimum(tick % 3, 1), tick // 3)

        return pl.BlockSpec(shape, index)

    hbm = pl.BlockSpec(memory_space=pl.ANY)

    def down_index(t):
        tick = jnp.minimum(t, 4)
        late = jnp.minimum(jnp.maximum(t - (CHUNKS - 1), 0), 1)
        return tick - tick // 3 - 3 * late + late_index(t)

    def late_index(t):
        return jnp.minimum(jnp.maximum(t - CHUNKS, 0), DOWN - 1)

    def up_index(t):
        return jnp.minimum(jnp.maximum(t - 6, 0), 2) + jnp.minimum(jnp.maximum(t - 10, 0), 1)

    hat_spec = at_tile((4, FREQ, TILE), lambda m, t: (m, 0, t))
    row_spec = at_tile((SPAN, TILE), lambda m, t: (m, t))
    bank_spec = at_tile((3, FREQ, TILE), lambda m, t: (0, 0, t))
    decay_shape = (1, TILE)

    def buffers(n, rows, kind):
        few, many = min(n, 4), min(n, 8)
        return [
            pltpu.VMEM((min(n, 2), 2, rows, D), kind),
            pltpu.VMEM((few, 2, rows // 2, D), kind),
            pltpu.VMEM((min(n, 2), 2, rows // 2, D), kind),
            pltpu.VMEM((few, rows // 2, D), kind),
            pltpu.VMEM((min(n, 2), rows // 2, D), kind),
            pltpu.VMEM((few, rows // 4, D), kind),
            pltpu.VMEM((min(n, 2), rows // 4, D), kind),
            pltpu.VMEM((few, 3, rows // 8, D // 2), kind),
            pltpu.VMEM((many, rows // 2, D), kind),
        ]

    def semaphores(n):
        one = pltpu.SemaphoreType.DMA((n,))
        three = pltpu.SemaphoreType.DMA((n, 3))
        return [one] * 6 + [three] * 4 + [one] * 5

    return pl.pallas_call(
        reduce_kernel,
        grid=(CHUNKS + LAGS,),
        in_specs=[
            fixed(sums.shape),
            fixed(d_shift.shape),
            pl.BlockSpec((count, half), lambda t: (0, down_index(t))),
            pl.BlockSpec((count, half), lambda t: (0, DOWN + down_index(t))),
            fixed((count, D)),
            hbm,
            pl.BlockSpec((count, D), lambda t: (0, up_index(t))),
            hbm, hbm, hbm, hbm,
            fixed((8, D)),
            pl.BlockSpec(memory_space=pl.ANY),
            pl.BlockSpec((half, D), lambda t: (late_index(t), 0)),
            pl.BlockSpec((half, D), lambda t: (DOWN + late_index(t), 0)),
            row_spec,
            at_tile((SPAN, 3 * TILE), lambda m, t: (m, t)),
            at_tile((8, 3 * TILE), lambda m, t: (0, t)),
            at_tile((8, TILE), lambda m, t: (0, t)),
            bank_spec, bank_spec, hat_spec, hat_spec, row_spec,
            fixed(AHEAD),
            fixed(BACK),
            at_tile((D, 3 * TILE), lambda m, t: (0, t)),
            at_tile(decay_shape, lambda m, t: (0, t)),
            at_tile(decay_shape, lambda m, t: (0, STEPS + t)),
            at_tile((hidden, TILE), lambda m, t: (0, t)),
            at_tile((hidden, TILE), lambda m, t: (0, STEPS + t)),
            fixed((SEQ, 1)),
            fixed(embed.shape),
            fixed(pre1.shape),
            fixed(act1.shape),
            fixed(pre2.shape),
            fixed(act2.shape),
            fixed(second_w.shape),
        ],
        out_specs=[pl.BlockSpec(memory_space=pl.ANY)] * 7,
        out_shape=[
            jax.ShapeDtypeStruct((1, SMALL_ROWS, D), f32),
            jax.ShapeDtypeStruct((DOWN, half, D), bf16),
            jax.ShapeDtypeStruct((half, UP * D), bf16),
            jax.ShapeDtypeStruct((half, D), bf16),
            jax.ShapeDtypeStruct((half, D3), bf16),
            jax.ShapeDtypeStruct((count, D), bf16),
            jax.ShapeDtypeStruct((count, D), bf16),
        ],
        scratch_shapes=[
            pltpu.VMEM((count, 3 * TILE), bf16),
            pltpu.VMEM((8, 3 * TILE), f32),
            pltpu.VMEM((STEPS, 8, 3 * TILE), f32),
            pltpu.VMEM((2, TILE), f32),
            pltpu.VMEM((2, D), f32),
            pltpu.VMEM((SEQ, TILE), f32),
            pltpu.VMEM((SEQ, TILE), f32),
            pltpu.VMEM((3, FREQ, TILE), f32),
            pltpu.VMEM((3, FREQ, TILE), f32),
            pltpu.VMEM((count, D), f32),
            pltpu.VMEM((SEQ, hidden), f32),
            pltpu.VMEM((count, D), bf16),
            pltpu.SemaphoreType.DMA(()),
            pltpu.SemaphoreType.DMA(()),
            pltpu.VMEM((count, D), bf16),
            pltpu.VMEM((count, D), bf16),
            pltpu.VMEM((count, D), f32),
            pltpu.VMEM((count, D), bf16),
            pltpu.VMEM((count, D), bf16),
            pltpu.SemaphoreType.DMA((5,)),
        ]
        + buffers(CHUNKS, half, bf16) + semaphores(CHUNKS) + buffers(1, SMALL_ROWS, f32) + semaphores(1),
        compiler_params=pltpu.CompilerParams(
            collective_id=1, has_side_effects=True, vmem_limit_bytes=63 * 2**20
        ),
        name="reduce_grads",
    )(
        sums, d_shift, active, active, upstream, second, d_hidden, mixed, d_middle, normed, tokens, vecs, middle, down_full, down_full,
        d_mixed, z, lines, vecs, bank1, bank2, hat1, hat2, mid, *constants(), in_full,
        decay, decay, third_w, third_w, jnp.asarray(place_ratio()), embed, pre1, act1, pre2, act2, second_w,
    )


HID = 1024
GELU_A = math.sqrt(2.0 / math.pi)
GELU_B = 0.044715


def middle_kernel(
    mixed, tokens, upstream, out_ref, vecs, up_ref, shift_ref, down_ref,
    middle_ref, second, active_ref, d_hidden_ref, d_middle_ref, d_mixed_ref, sums_ref, d_shift_ref, d_second_ref,
):
    first = pl.program_id(0) == 0
    last = pl.program_id(0) == pl.num_programs(0) - 1
    steps = second.shape[0] // 256

    def rows_of(i):
        return pl.ds(pl.multiple_of(i * 256, 256), 256)

    @pl.when(first)
    def _():
        def front(i, carry):
            rows = rows_of(i)
            value = tokens[rows, :].astype(f32) + lowmul(mixed[rows, :], out_ref[...]) + vecs[2:3, :]
            middle_ref[rows, :] = value
            second[rows, :] = layer_norm(value, vecs[3:4, :], vecs[4:5, :]).astype(bf16)
            return carry

        lax.fori_loop(0, steps, front, 0)
        d_second_ref[...] = jnp.zeros_like(d_second_ref)

    def block(i, total):
        rows = rows_of(i)
        hidden = lowmul(second[rows, :], up_ref[...]) + shift_ref[...]
        d_active = times_t(upstream[rows, :], down_ref[...])
        square = hidden * hidden
        curve = jnp.tanh(GELU_A * hidden * (1.0 + GELU_B * square))
        half = 0.5 * (1.0 + curve)
        active_ref[rows, :] = (hidden * half).astype(bf16)
        slope = half + 0.5 * hidden * (1.0 - curve * curve) * (GELU_A * (1.0 + 3.0 * GELU_B * square))
        d_hidden = (d_active * slope).astype(bf16)
        d_hidden_ref[rows, :] = d_hidden
        d_second_ref[rows, :] += times_t(d_hidden, up_ref[...])
        return total + jnp.sum(d_hidden.astype(f32), axis=0, keepdims=True)

    d_shift_ref[...] = lax.fori_loop(0, steps, block, jnp.zeros(d_shift_ref.shape, f32), unroll=2)

    @pl.when(last)
    def _():
        def back(i, sums):
            rows = rows_of(i)
            values = middle_ref[rows, :]
            grads = d_second_ref[rows, :]
            given = upstream[rows, :].astype(f32)
            center = values - jnp.mean(values, axis=-1, keepdims=True)
            scale = lax.rsqrt(jnp.mean(center * center, axis=-1, keepdims=True) + EPS)
            unit = center * scale
            scaled = grads * vecs[3:4, :]
            inner = scaled - jnp.mean(scaled, axis=-1, keepdims=True)
            inner = inner - unit * jnp.mean(scaled * unit, axis=-1, keepdims=True)
            value = scale * inner + given
            d_middle_ref[rows, :] = value
            branch = value.astype(bf16)
            d_mixed_ref[rows, :] = times_t(branch, out_ref[...])
            new = (branch.astype(f32), grads * unit, grads, given)
            return tuple(old + jnp.sum(one, axis=0, keepdims=True) for old, one in zip(sums, new))

        zero = jnp.zeros((1, D), f32)
        sums_ref[...] = jnp.zeros_like(sums_ref)
        for i, one in enumerate(lax.fori_loop(0, steps, back, (zero,) * 4)):
            sums_ref[i : i + 1, :] = one


def run_middle(mixed, tokens, upstream, out_full, vecs, up_full, up_shift, down_full):
    count = tokens.shape[0]
    units = up_full.shape[1]

    def fixed(*shape):
        return pl.BlockSpec(shape, lambda j: (0,) * len(shape), pipeline_mode=pl.Buffered(1))

    columns = pl.BlockSpec((count, HID), lambda j: (0, j))
    row = pl.BlockSpec((1, HID), lambda j: (0, j))
    tall = fixed(count, D)
    wide = jax.ShapeDtypeStruct((count, units), bf16)
    full = jax.ShapeDtypeStruct((count, D), f32)
    return pl.pallas_call(
        middle_kernel,
        grid=(units // HID,),
        in_specs=[
            tall, tall, tall, fixed(D, D), fixed(8, D), pl.BlockSpec((D, HID), lambda j: (0, j)), row,
            pl.BlockSpec((HID, D), lambda j: (j, 0)),
        ],
        out_specs=[tall, tall, columns, columns, tall, tall, fixed(8, D), row],
        out_shape=[
            full, jax.ShapeDtypeStruct((count, D), bf16), wide, wide, full, full, jax.ShapeDtypeStruct((8, D), f32),
            jax.ShapeDtypeStruct((1, units), f32),
        ],
        scratch_shapes=[pltpu.VMEM((count, D), f32)],
        compiler_params=pltpu.CompilerParams(vmem_limit_bytes=63 * 2**20),
        cost_estimate=pl.CostEstimate(
            flops=6 * count * D * units, bytes_accessed=40 * 2**20, transcendentals=count * units
        ),
        name="middle",
    )(mixed, tokens, upstream, out_full, vecs, up_full, up_shift, down_full)


def finish_kernel(
    small, result, d_tokens, down, up, out, inward,
    prompt_out, cont_out, prompt_grad, cont_grad,
    g_gain1, g_shift1, g_in, g_in_b, g_taps, g_short_b, g_long, g_w1, g_b1, g_w2, g_b2, g_w3,
    g_out, g_out_b, g_gain2, g_shift2, g_up, g_up_b, g_down, g_down_b,
):
    step = pl.program_id(0)
    for src, dst in ((down, g_down), (up, g_up), (out, g_out), (inward, g_in)):
        dst[...] = src[...].astype(f32)

    @pl.when(step % 4 < 2)
    def _():
        prompt_out[0, 0] = result[...]
        prompt_grad[0, 0] = d_tokens[...]

    @pl.when(step % 4 >= 2)
    def _():
        cont_out[0, 0, 0] = result[...]
        cont_grad[0, 0, 0] = d_tokens[...]

    @pl.when(step == 0)
    def _():
        half = slice(D // 2, D)

        def lines(start, count, stride=1):
            rows = [small[0, start + stride * i : start + stride * i + 1, half] for i in range(count)]
            return jnp.concatenate(rows, axis=1)

        def put(ref, value):
            ref[...] = value.reshape(ref.shape)

        for i, ref in enumerate((g_out_b, g_gain2, g_shift2, g_down_b)):
            put(ref, lines(GIVEN_ROW + i, 1))
        put(g_up_b, lines(GIVEN_ROW + 4, 4))
        for i in range(3):
            g_taps[i : i + 1, :] = lines(TAP_ROW + i, 3, 8)
        put(g_short_b, lines(TAP_ROW + 3, 3, 8))
        put(g_in_b, lines(TAP_ROW + 4, 3, 8))
        g_long[...] = small[0, LONG_ROW : LONG_ROW + 2, half]
        put(g_gain1, lines(NORM_ROW, 1))
        put(g_shift1, lines(NORM_ROW + 1, 1))
        g_w3[...] = small[0, 0 : g_w3.shape[0], :]
        wide, n1 = g_w1.shape
        g_w1[...] = small[0, 64 : 64 + n1, 0:wide].T
        put(g_b1, small[0, 64 + n1 : 65 + n1, 0:wide])
        put(g_b2, small[0, 65 + n1 : 66 + n1, 0:wide])
        g_w2[...] = small[0, 64 : 64 + g_w2.shape[1], 128 : 128 + wide].T


def finish(shapes, micros, small, result, d_tokens, down, up, out, inward):
    steps = 4 * micros

    def rows(value):
        return pl.BlockSpec((value.shape[0] // steps, value.shape[1]), lambda i: (i, 0))

    def fixed(value):
        return pl.BlockSpec(value.shape, lambda i: (0,) * len(value.shape))

    inputs = (small, result, d_tokens, down.reshape(-1, D), up, out, inward)
    prompt = pl.BlockSpec((1, 1, BLOCK, D), lambda i: (i // 4, 0, jnp.minimum(i % 4, 1), 0))
    cont = pl.BlockSpec((1, 1, 1, BLOCK, D), lambda i: (i // 4, 0, jnp.maximum(i % 4 - 2, 0), 0, 0))
    big = {6: inward, 16: out, 20: up, 22: down}
    specs = [prompt, cont, prompt, cont] + [rows(one) if i in big else fixed(one) for i, one in enumerate(shapes) if i > 3]
    return pl.pallas_call(
        finish_kernel,
        grid=(steps,),
        in_specs=[fixed(small)] + [rows(one) for one in inputs[1:]],
        out_specs=specs,
        out_shape=shapes,
        compiler_params=pltpu.CompilerParams(vmem_limit_bytes=63 * 2**20),
        name="finish",
    )(*inputs)


def per_device(
    prompt_x, cont_x, prompt_cot, cont_cot, norm1_gain, norm1_bias, in_weight, in_bias, short_weight,
    short_bias, long_bias, filter_w1, filter_b1, filter_w2, filter_b2, filter_w3, filter_decay, out_weight,
    out_bias, norm2_gain, norm2_bias, up_weight, up_bias, down_weight, down_bias, *, reps, shards,
):
    own_kernels = reps == 16 and shards == 2 and prompt_x.shape[1] == 1
    micros = prompt_x.shape[0]
    groups = prompt_x.shape[1]
    count = micros * groups * SPAN

    def tokens_of(prompt, cont):
        return jnp.concatenate(
            [
                prompt.reshape(micros * groups, PROMPT, D),
                cont.reshape(micros * groups, CONTS * BLOCK, D),
            ],
            axis=1,
        ).reshape(count, D)

    def parts_of(rows):
        rows = rows.reshape(micros, groups, SPAN, D)
        return rows[:, :, :PROMPT], rows[:, :, PROMPT:].reshape(micros, groups, CONTS, BLOCK, D)

    n1 = filter_w1.shape[0]
    n2 = filter_w2.shape[0]
    if own_kernels:
        (projected, mixed_low, hat1, hat2, mid, bank1, bank2, vecs, lines, up_shift, decay, fw2, fw3,
         pre1, act1, pre2, act2, normed_low, tokens_low, upstream, in_full, out_full, up_full, down_full) = gather_weights(
            norm1_gain, norm1_bias, in_bias, short_weight, short_bias, long_bias, filter_w1.T, filter_b1, filter_w2.T,
            filter_b2, filter_w3, filter_decay, out_bias, norm2_gain, norm2_bias, up_bias, down_bias,
            in_weight, out_weight, up_weight, down_weight,
            *(one.reshape(micros, PROMPT, D) for one in (prompt_x, cont_x, prompt_cot, cont_cot)),
        )
        states = (jnp.asarray(embed_table()), pre1, act1, pre2, act2)
    else:
        tokens_low = tokens_of(prompt_x, cont_x)
        upstream = tokens_of(prompt_cot, cont_cot)

        def gather(value, axis=0):
            return lax.all_gather(value, "shard", axis=axis, tiled=True)

        gain1, shift1, out_shift, gain2, shift2, down_shift, in_shift, short_shift, up_shift, decay, fb1, fb2 = (
            gather(one).astype(f32)
            for one in (norm1_gain, norm1_bias, out_bias, norm2_gain, norm2_bias, down_bias, in_bias, short_bias,
                        up_bias, filter_decay, filter_b1, filter_b2)
        )
        taps, long_shift, fw1, fw2, fw3 = (
            gather(one, 1).astype(f32) for one in (short_weight, long_bias, filter_w1, filter_w2, filter_w3)
        )
        in_full, out_full, up_full, down_full = (
            gather(one) for one in (by_tile(in_weight), out_weight, up_weight, down_weight)
        )
        up_shift = up_shift[None]
        lines = by_tile(jnp.concatenate([taps, short_shift[None], in_shift[None], jnp.zeros((3, D3), f32)], axis=0))
        vecs = jnp.stack([gain1, shift1, out_shift, gain2, shift2, down_shift])
        vecs = jnp.concatenate([vecs, long_shift], axis=0)
        filters, filter_pull = jax.vjp(partial(filter_taps, decay=decay), fw1, fb1, fw2, fb2, fw3)
        normed, norm_pull = jax.vjp(layer_norm, tokens_low.astype(f32), gain1, shift1)
        normed_low = normed.astype(bf16)
        projected = lowmul(normed_low, in_full) + lines[4]
        mixed_low, hat1, hat2, mid, bank1, bank2 = run_forward(projected, lines, vecs, filters)
    middle, second_low, active_low, d_hidden, d_middle, d_mixed, sums, d_up_shift = run_middle(
        mixed_low, tokens_low, upstream, out_full, vecs, up_full, up_shift, down_full
    )
    width = D // shards

    def by_shard(value):
        rows = value.shape[0]
        return value.reshape(rows, shards, -1).swapaxes(0, 1).reshape(shards, -1, width)

    if own_kernels:
        small, grad_down, grad_up, grad_out, grad_in, d_tokens, result = reduce_grads(
            sums, d_up_shift, active_low, upstream, second_low, d_hidden, mixed_low, d_middle, normed_low,
            tokens_low, middle, down_full, d_mixed, projected, lines, vecs, bank1, bank2, hat1, hat2, mid, in_full, decay, fw3, states, fw2,
        )
        args = (norm1_gain, norm1_bias, in_weight, in_bias, short_weight, short_bias, long_bias, filter_w1, filter_b1,
                filter_w2, filter_b2, filter_w3, out_weight, out_bias, norm2_gain, norm2_bias, up_weight, up_bias,
                down_weight, down_bias)
        shapes = [jax.ShapeDtypeStruct(one.shape, bf16) for one in (prompt_x, cont_x) * 2]
        shapes += [jax.ShapeDtypeStruct(one.shape, f32) for one in args]
        for i in (11, 13):
            shapes[i] = jax.ShapeDtypeStruct(shapes[i].shape[::-1], f32)
        outs = list(finish(shapes, micros, small, result, d_tokens, grad_down, grad_up, grad_out, grad_in))
        outs[11], outs[13] = outs[11].T, outs[13].T
        return tuple(outs)
    else:
        def reduce(value, axis=0):
            value = lax.psum_scatter(value, "shard", scatter_dimension=axis, tiled=True)
            return lax.psum(value, "rep")

        result = (middle + lowmul(active_low, down_full) + down_shift).astype(bf16)
        prompt_out, cont_out = parts_of(result)
        d_proj, d_taps, d_long, d_filter1, d_filter2 = run_backward(
            d_mixed, projected, lines, vecs, bank1, bank2, hat1, hat2, mid
        )
        d_tokens, grad_gain1, grad_shift1 = norm_pull(times_t(d_proj, in_full))
        prompt_grad, cont_grad = parts_of((d_tokens + d_middle).astype(bf16))
        filter_grads_all = filter_pull(jnp.concatenate([d_filter1, d_filter2], axis=-1))
        narrow_own = [reduce(one, one.ndim - 1) for one in filter_grads_all[:4]]
        third_grad = reduce(filter_grads_all[4], 1)
        given = jnp.concatenate([by_shard(sums[:4]), by_shard(d_up_shift)], axis=1)
        given = reduce(given)[0]
        tap_rows = reduce(by_part(d_taps[:5]), 1)
        long_rows = reduce(d_long, 1)
        norm_rows = reduce(jnp.stack([grad_gain1, grad_shift1]), 1)
        grad_down = reduce(inner_rows(active_low, upstream))
        grad_up = reduce(inner_rows(second_low, d_hidden))
        grad_out = reduce(inner_rows(mixed_low, d_middle.astype(bf16)))
        grad_in = by_part(reduce(inner_rows(normed_low, d_proj)))
    return (
        prompt_out,
        cont_out,
        prompt_grad,
        cont_grad,
        norm_rows[0],
        norm_rows[1],
        grad_in,
        tap_rows[4],
        tap_rows[:3],
        tap_rows[3],
        long_rows,
        *narrow_own,
        third_grad,
        grad_out,
        given[0],
        given[1],
        given[2],
        grad_up,
        given[4:].reshape(-1),
        grad_down,
        given[3],
    )


def solution(mesh):
    group4 = P(None, ("rep", "shard"), None, None)
    group5 = P(None, ("rep", "shard"), None, None, None)
    one, row, col = P("shard"), P("shard", None), P(None, "shard")
    grads = (one, one, row, one, col, one, col, col, one, col, one, col)
    rest = (row, one, one, one, row, one, row, one)
    return jax.shard_map(
        partial(per_device, reps=mesh.shape["rep"], shards=mesh.shape["shard"]),
        mesh=mesh,
        in_specs=(group4, group5, group4, group5) + grads + (one,) + rest,
        out_specs=(group4, group5, group4, group5) + grads + rest,
        check_vma=False,
    )
```
